32 devices in a mesh: dp: 8 (over z, x), band: 4 (over y, core).
Axes of the slice: x: 2, y: 2, z: 4, core: 2. Of those that a mesh axis runs over, the one named last changes fastest.
Arguments:
- inputs: bfloat16 [8, 24, 4, 12, 256], P('dp', 'band'), may hold values from -6 to 6
- targets: bfloat16 [8, 24, 4, 12, 256], P('dp', 'band'), may hold values from -6 to 6
- crop_extent: int32 [8, 2], P('dp'), may hold values from 6 to 24, as said below
- master: float32 [5708800], P(('dp', 'band')), may hold values from -1.5 to 1.5
- moment_one: float32 [5708800], P(('dp', 'band'))
- moment_two: float32 [5708800], P(('dp', 'band')), as said below
- step_count: int32 [1], replicated, may hold values from 1 to 20
Outputs:
- new_master: float32 [5708800], P(('dp', 'band'))
- new_moment_one: float32 [5708800], P(('dp', 'band'))
- new_moment_two: float32 [5708800], P(('dp', 'band'))
- new_copy: bfloat16 [5708800], P(('dp', 'band'))
- loss: float32 [], replicated
- grad_norm: float32 [], replicated
The draws below stay inside these ranges and needn't reach their ends.
Inputs may be any that keep to these rules, and one draw needn't show every extreme that they name: `crop_extent`: latitude extents lie from 12 to 24, longitude extents from 6 to 12; one crop reaches both largest values. `moment_two`: positive.
All inputs are finite; a program needn't handle non-finite values.
Results may differ from the reference program's by a relative error of at most 0.01.
The reference program's roundings to bfloat16 on the way (of `working`) count: a program that leaves them out, or rounds other values in their place, can miss the bound.
Values may be sent and summed in bfloat16 or wider, within the bound.
No kernel may reach another device: no remote copies, remote signals or barrier semaphores. Data moves between devices by JAX's collectives and lax.ppermute only.
A program may use at most 192 MiB of HBM per device.

```python
import math
import jax
import jax.numpy as jnp
from jax import lax

D_ENC = 192
HEADS_ENC = 6
D_TRUNK = 384
HEADS_TRUNK = 12
PIN = 128
GROUPS = 2
LEVELS = 4
LON = 12
CROPS = 8
NLAT = 24
PARAMS = 5708800


CLIP_LEVEL = 0.07


def block_layout_drawn(path_name, group_id, layer_id, n_width):
    prefix = (path_name, group_id, layer_id)
    return [(prefix + ('norm_one',), (2, n_width)), (prefix + ('qkv',), (n_width, 3 * n_width)), (prefix + ('proj',), (n_width, n_width)), (prefix + ('norm_two',), (2, n_width)), (prefix + ('up',), (n_width, 4 * n_width)), (prefix + ('down',), (4 * n_width, n_width))]


def layout_drawn():
    entries = []
    for group_id in range(GROUPS):
        entries.append((('enc', group_id, -1, 'embed'), (PIN, D_ENC)))
        for layer_id in range(2):
            entries += block_layout_drawn('enc', group_id, layer_id, D_ENC)
        entries.append((('top', group_id, -1, 'decode'), (D_TRUNK, D_ENC)))
        entries.append((('top', group_id, -1, 'head'), (D_ENC, PIN)))
        entries.append((('top', group_id, -1, 'scale'), (PIN,)))
    entries.append((('trunk', 0, -1, 'joining'), (GROUPS * D_ENC, D_TRUNK)))
    for layer_id in range(2):
        entries += block_layout_drawn('trunk', 0, layer_id, D_TRUNK)
    entries.append((('trunk', 0, -1, 'final'), (2, D_TRUNK)))
    return entries


def draw_master(key, part):
    pieces = []
    for index_id, (label_key, dims_shape) in enumerate(layout_drawn()):
        sub_key = jax.random.fold_in(key, index_id)
        kind_name = label_key[3]
        if kind_name in ('norm_one', 'norm_two', 'final'):
            gain_row = jax.random.uniform(sub_key, (1, dims_shape[1]), jnp.float32, 0.7, 1.3)
            shift_row = 0.2 * jnp.clip(jax.random.normal(jax.random.fold_in(sub_key, 1), (1, dims_shape[1]), jnp.float32), -4.0, 4.0)
            segment = jnp.concatenate([gain_row, shift_row], 0)
        elif kind_name == 'scale':
            segment = jax.random.uniform(sub_key, dims_shape, jnp.float32, -1.5, -0.5)
        else:
            boost_factor = 2.0 if kind_name == 'proj' else 1.0
            segment = boost_factor * jnp.clip(jax.random.normal(sub_key, dims_shape, jnp.float32), -4.0, 4.0) / math.sqrt(dims_shape[0])
        pieces.append(segment.reshape(-1))
    return jnp.clip(jnp.concatenate(pieces), -1.5, 1.5)


def draw_moment_one(key, part):
    return jax.random.normal(key, (PARAMS,), jnp.float32) * (CLIP_LEVEL / math.sqrt(PARAMS))


def draw_moment_two(key, part):
    spread_vals = jax.random.uniform(key, (PARAMS,), jnp.float32, 0.5, 2.0) * (CLIP_LEVEL / math.sqrt(PARAMS))
    return spread_vals * spread_vals


def draw_crop_extent(key, part):
    lat_key = jax.random.fold_in(key, 11)
    lon_key = jax.random.fold_in(key, 12)
    pick_key = jax.random.fold_in(key, 13)
    lat_rows = jax.random.randint(lat_key, (CROPS,), NLAT // 2, NLAT + 1)
    lon_cols = jax.random.randint(lon_key, (CROPS,), LON // 2, LON + 1)
    chosen = jax.random.randint(pick_key, (), 0, CROPS)
    lat_rows = lat_rows.at[chosen].set(NLAT)
    lon_cols = lon_cols.at[chosen].set(LON)
    return jnp.stack([lat_rows, lon_cols], 1).astype(jnp.int32)


def shard_levels(rng, extent, shards, low, largest):
    def one(position, shards_of):
        draws = jax.random.uniform(jax.random.fold_in(jax.random.fold_in(rng, 6), position), (shards_of,), jnp.float32, low / len(shards), largest / len(shards))
        return jnp.repeat(jnp.exp(draws), extent[position] // shards_of).reshape((-1,) + (1,) * (len(extent) - position - 1))

    loudness = one(*shards[0])
    for cut in shards[1:]:
        loudness = loudness * one(*cut)
    return loudness


def bell_draw(own_key, shape, deviation, most, cuts=(), held_as=jnp.bfloat16):
    factor_of = shard_levels(own_key, shape, cuts, -0.22, 0.18) if cuts else 1.0
    values = jax.random.normal(own_key, shape, jnp.float32) * deviation * factor_of
    return jnp.minimum(jnp.maximum(values, -most), most).astype(held_as)


def setup_inputs(seed: int = 0) -> dict:
    streams_of = jax.random.split(jax.random.key(seed), 8)
    inputs = bell_draw(streams_of[0], (CROPS, NLAT, LEVELS, LON, GROUPS * PIN), 1.0, 6.0, ((0, 8), (1, 4)))
    targets = bell_draw(streams_of[1], (CROPS, NLAT, LEVELS, LON, GROUPS * PIN), 1.0, 6.0, ((0, 8), (1, 4)))
    crop_extent = draw_crop_extent(jax.random.fold_in(streams_of[7], 71), 0)
    master = draw_master(jax.random.fold_in(streams_of[7], 71), 0)
    moment_one = draw_moment_one(jax.random.fold_in(streams_of[7], 71), 0)
    moment_two = draw_moment_two(jax.random.fold_in(streams_of[7], 71), 0)
    step_count = jax.random.randint(streams_of[6], (1,), 1, 21).astype(jnp.int32)
    return {"inputs": inputs, "targets": targets, "crop_extent": crop_extent, "master": master, "moment_one": moment_one, "moment_two": moment_two, "step_count": step_count}


@jax.custom_vjp
def low(v):
    return lax.optimization_barrier(v.astype(jnp.bfloat16)).astype(jnp.float32)

@jax.custom_vjp
def low_back(v):
    return v

def low_keep(v):
    return (low(v), None)

def low_pass(kept, grad):
    return (grad,)

def back_keep(v):
    return (v, None)

def back_low(kept, grad):
    return (low(grad),)
low.defvjp(low_keep, low_pass)
low_back.defvjp(back_keep, back_low)
NEG_FILL = -1000000000.0
BETA_ONE = 0.5
BETA_TWO = 0.5
LEARN_RATE = 0.01
WEIGHT_DECAY = 0.1
CLIP_LEVEL = 0.07
ADAM_EPS = 1e-08
HIGHEST_PRECISION = lax.Precision.HIGHEST

def block_layout(path_name, group_id, layer_id, n_width):
    prefix = (path_name, group_id, layer_id)
    return [(prefix + ('norm_one',), (2, n_width)), (prefix + ('qkv',), (n_width, 3 * n_width)), (prefix + ('proj',), (n_width, n_width)), (prefix + ('norm_two',), (2, n_width)), (prefix + ('up',), (n_width, 4 * n_width)), (prefix + ('down',), (4 * n_width, n_width))]

def layout():
    entries = []
    for group_id in range(GROUPS):
        entries.append((('enc', group_id, -1, 'embed'), (PIN, D_ENC)))
        for layer_id in range(2):
            entries += block_layout('enc', group_id, layer_id, D_ENC)
        entries.append((('top', group_id, -1, 'decode'), (D_TRUNK, D_ENC)))
        entries.append((('top', group_id, -1, 'head'), (D_ENC, PIN)))
        entries.append((('top', group_id, -1, 'scale'), (PIN,)))
    entries.append((('trunk', 0, -1, 'joining'), (GROUPS * D_ENC, D_TRUNK)))
    for layer_id in range(2):
        entries += block_layout('trunk', 0, layer_id, D_TRUNK)
    entries.append((('trunk', 0, -1, 'final'), (2, D_TRUNK)))
    return entries

def unpack(flat_vec):
    weights = {}
    offset = 0
    for label_key, dims_shape in layout():
        length = math.prod(dims_shape)
        weights[label_key] = flat_vec[offset:offset + length].reshape(dims_shape)
        offset += length
    return weights

def layer_norm(values, gain_shift):
    centre = values - lax.optimization_barrier(jnp.mean(values, -1, keepdims=True))
    spread = lax.optimization_barrier(jnp.mean(centre * centre, -1, keepdims=True))
    return centre * lax.rsqrt(spread + 1e-05) * gain_shift[0] + gain_shift[1]

def product(left_op, right_op):
    return jnp.einsum('...w,wc->...c', left_op, right_op, precision=HIGHEST_PRECISION)

def to_windows(grid_field, shifted):
    if shifted:
        grid_field = jnp.roll(grid_field, (-1, -6), axis=(2, 3))
    n_batch, n_rows, n_levels, n_cols, n_chans = grid_field.shape
    grid_field = grid_field.reshape(n_batch, n_rows // 6, 6, n_levels // 2, 2, n_cols // 12, 12, n_chans)
    return grid_field.transpose(0, 1, 3, 5, 2, 4, 6, 7).reshape(-1, 144, n_chans)

def from_windows(windowed, grid_shape, shifted):
    n_batch, n_rows, n_levels, n_cols, n_chans = grid_shape
    grid_field = windowed.reshape(n_batch, n_rows // 6, n_levels // 2, n_cols // 12, 6, 2, 12, n_chans)
    grid_field = grid_field.transpose(0, 1, 4, 2, 5, 3, 6, 7).reshape(grid_shape)
    if shifted:
        grid_field = jnp.roll(grid_field, (1, 6), axis=(2, 3))
    return grid_field

def window_codes(code_grid, shifted):
    return to_windows(code_grid[..., None], shifted)[..., 0]

def attend(windowed, qkv_weight, query_code, key_code, n_heads):
    n_win, n_tok, n_width = windowed.shape
    head_dim = n_width // n_heads
    packed = low_back(low(product(windowed, qkv_weight)))
    packed = packed.reshape(n_win, n_tok, 3, n_heads, head_dim)
    queries, key_rows, value_rows = (packed[:, :, 0], packed[:, :, 1], packed[:, :, 2])
    scores = jnp.einsum('nihd,njhd->nhij', queries, key_rows, precision=HIGHEST_PRECISION) * head_dim ** (-0.5)
    allowed = query_code[:, None, :, None] == key_code[:, None, None, :]
    scores = low_back(jnp.where(allowed, scores, NEG_FILL))
    exp_scores = jnp.exp(scores - lax.optimization_barrier(jnp.max(scores, -1, keepdims=True)))
    attn_probs = low(exp_scores / lax.optimization_barrier(jnp.sum(exp_scores, -1, keepdims=True)))
    mixed_rows = jnp.einsum('nhij,njhd->nihd', attn_probs, value_rows, precision=HIGHEST_PRECISION)
    return low_back(low(mixed_rows.reshape(n_win, n_tok, n_width)))

def block_apply(resid_in, weights, prefix, shifted, n_heads, codes):
    normed = low(layer_norm(resid_in, weights[prefix + ('norm_one',)]))
    if shifted:
        normed = jnp.pad(normed, ((0, 0), (3, 3), (0, 0), (0, 0), (0, 0)))
    windowed = to_windows(normed, shifted)
    mixed_win = attend(windowed, weights[prefix + ('qkv',)], codes[0], codes[1], n_heads)
    mixed_rows = from_windows(mixed_win, normed.shape, shifted)
    if shifted:
        mixed_rows = mixed_rows[:, 3:mixed_rows.shape[1] - 3]
    middle = resid_in + low_back(product(mixed_rows, weights[prefix + ('proj',)]))
    normed_two = low(layer_norm(middle, weights[prefix + ('norm_two',)]))
    active = low(jax.nn.gelu(low_back(product(normed_two, weights[prefix + ('up',)])), approximate=True))
    return middle + low_back(product(active, weights[prefix + ('down',)]))

def forward(working, source, goal_field, valid, plain_codes, shift_codes, valid_total):
    weights = unpack(working)
    outputs = []
    for group_id in range(GROUPS):
        group_input = source[..., group_id * PIN:(group_id + 1) * PIN]
        resid_in = low_back(product(group_input, weights['enc', group_id, -1, 'embed']))
        resid_in = block_apply(resid_in, weights, ('enc', group_id, 0), False, HEADS_ENC, plain_codes)
        resid_in = block_apply(resid_in, weights, ('enc', group_id, 1), True, HEADS_ENC, shift_codes)
        outputs.append(resid_in)
    joined = low(jnp.concatenate(outputs, -1))
    trunk = low_back(product(joined, weights['trunk', 0, -1, 'joining']))
    trunk = block_apply(trunk, weights, ('trunk', 0, 0), False, HEADS_TRUNK, plain_codes)
    trunk = block_apply(trunk, weights, ('trunk', 0, 1), True, HEADS_TRUNK, shift_codes)
    final_low = low(layer_norm(trunk, weights['trunk', 0, -1, 'final']))
    loss_sum = jnp.zeros((), jnp.float32)
    for group_id in range(GROUPS):
        raised = low_back(product(final_low, weights['top', group_id, -1, 'decode']))
        active = low(jax.nn.gelu(raised, approximate=True))
        predicted = low_back(product(active, weights['top', group_id, -1, 'head']))
        log_scale = weights['top', group_id, -1, 'scale']
        pred_error = jnp.abs(predicted - goal_field[..., group_id * PIN:(group_id + 1) * PIN])
        loss_sum = loss_sum + jnp.sum((pred_error * jnp.exp(-log_scale) + log_scale) * valid[..., None])
    return loss_sum / (valid_total * (GROUPS * PIN))

def reference(inputs, targets, crop_extent, master, moment_one, moment_two, step_count):
    working = master.astype(jnp.bfloat16).astype(jnp.float32)
    source = inputs.astype(jnp.float32)
    goal_field = targets.astype(jnp.float32)
    lat_index = lax.iota(jnp.int32, NLAT)
    level_index = lax.iota(jnp.int32, LEVELS)
    col_index = lax.iota(jnp.int32, LON)
    grid_dims = (CROPS, NLAT, LEVELS, LON)
    valid = (lat_index[None, :, None, None] < crop_extent[:, 0][:, None, None, None]) & (col_index[None, None, None, :] < crop_extent[:, 1][:, None, None, None])
    valid = jnp.broadcast_to(valid, grid_dims)
    zero_code = jnp.zeros(grid_dims, jnp.int32)
    plain_codes = (window_codes(zero_code, False), window_codes(jnp.where(valid, zero_code, -1), False))
    region = (level_index == 0).astype(jnp.int32)[None, None, :, None] * 2 + (col_index < 6).astype(jnp.int32)[None, None, None, :]
    region = jnp.broadcast_to(region, grid_dims)
    rim_pad = ((0, 0), (3, 3), (0, 0), (0, 0))
    shift_codes = (window_codes(jnp.pad(region, rim_pad), True), window_codes(jnp.pad(jnp.where(valid, region, -1), rim_pad, constant_values=-1), True))
    valid_total = jnp.sum(crop_extent[:, 0].astype(jnp.float32) * crop_extent[:, 1].astype(jnp.float32)) * LEVELS
    valid_float = valid.astype(jnp.float32)
    loss_value, pullback = jax.vjp(lambda flat_vec: forward(flat_vec, source, goal_field, valid_float, plain_codes, shift_codes, valid_total), working)
    grad_flat = pullback(jnp.ones((), jnp.float32))[0]
    grad_norm = jnp.sqrt(jnp.sum(grad_flat * grad_flat))
    factor = jnp.minimum(1.0, CLIP_LEVEL / (grad_norm + 1e-06))
    clipped = grad_flat * factor
    new_one = BETA_ONE * moment_one + (1.0 - BETA_ONE) * clipped
    new_two = BETA_TWO * moment_two + (1.0 - BETA_TWO) * clipped * clipped
    step_value = step_count[0].astype(jnp.float32)
    fix_one = 1.0 - jnp.power(BETA_ONE, step_value)
    fix_two = 1.0 - jnp.power(BETA_TWO, step_value)
    update = new_one / fix_one / (jnp.sqrt(new_two / fix_two) + ADAM_EPS) + WEIGHT_DECAY * master
    new_master = master - LEARN_RATE * update
    return (new_master, new_one, new_two, new_master.astype(jnp.bfloat16), loss_value, grad_norm)
```

```python
import math

import jax
import jax.numpy as jnp
from jax import lax
from jax.sharding import PartitionSpec as P

D_ENC = 192
HEADS_ENC = 6
D_TRUNK = 384
HEADS_TRUNK = 12
PIN = 128
GROUPS = 2


NEG_FILL = -1000000000.0
BETA_ONE = 0.5
BETA_TWO = 0.5
LEARN_RATE = 0.01
WEIGHT_DECAY = 0.1
CLIP_LEVEL = 0.07
ADAM_EPS = 1e-08


def extended_2(block, sides, width):
    for axis, dim in sides:
        count = lax.axis_size(axis)
        forward = [(i, i + 1) for i in range(count - 1)]
        backward = [(target, source) for source, target in forward]
        low = lax.ppermute(
            lax.slice_in_dim(block, block.shape[dim] - width, None, axis=dim), axis, forward
        )
        high = lax.ppermute(lax.slice_in_dim(block, 0, width, axis=dim), axis, backward)
        block = jnp.concatenate([low, block, high], axis=dim)
    return block


def block_layout(path_name, group_id, layer_id, n_width):
    prefix = (path_name, group_id, layer_id)
    return [
        (prefix + ("norm_one",), (2, n_width)),
        (prefix + ("qkv",), (n_width, 3 * n_width)),
        (prefix + ("proj",), (n_width, n_width)),
        (prefix + ("norm_two",), (2, n_width)),
        (prefix + ("up",), (n_width, 4 * n_width)),
        (prefix + ("down",), (4 * n_width, n_width)),
    ]


def layout():
    entries = []
    for group_id in range(GROUPS):
        entries.append((("enc", group_id, -1, "embed"), (PIN, D_ENC)))
        for layer_id in range(2):
            entries += block_layout("enc", group_id, layer_id, D_ENC)
        entries.append((("top", group_id, -1, "decode"), (D_TRUNK, D_ENC)))
        entries.append((("top", group_id, -1, "head"), (D_ENC, PIN)))
        entries.append((("top", group_id, -1, "scale"), (PIN,)))
    entries.append((("trunk", 0, -1, "joining"), (GROUPS * D_ENC, D_TRUNK)))
    for layer_id in range(2):
        entries += block_layout("trunk", 0, layer_id, D_TRUNK)
    entries.append((("trunk", 0, -1, "final"), (2, D_TRUNK)))
    return entries


def unpack(flat_vec):
    weights = {}
    offset = 0
    for label_key, dims_shape in layout():
        length = math.prod(dims_shape)
        weights[label_key] = flat_vec[offset : offset + length].reshape(dims_shape)
        offset += length
    return weights


def layer_norm(values, gain_shift):
    centre = values - jnp.mean(values, -1, keepdims=True)
    spread = jnp.mean(centre * centre, -1, keepdims=True)
    return centre * lax.rsqrt(spread + 1e-05) * gain_shift[0] + gain_shift[1]


def gelu_tanh(values):
    return jax.nn.gelu(values, approximate=True)


def product(left_op, right_op):
    return jnp.einsum("...w,wc->...c", left_op, right_op, preferred_element_type=jnp.float32)


def back_product(grad_low, weight):
    return jnp.einsum("...c,wc->...w", grad_low, weight, preferred_element_type=jnp.float32)


def weight_grad(left_op, right_op):
    return lax.dot_general(
        left_op.reshape(-1, left_op.shape[-1]),
        right_op.reshape(-1, right_op.shape[-1]),
        (((0,), (0,)), ((), ())),
        preferred_element_type=jnp.float32,
    )


def norm_back(resid_in, gain_shift, grad_normed):
    unused, pullback = jax.vjp(layer_norm, resid_in, gain_shift.astype(jnp.float32))
    return pullback(grad_normed)


def to_windows(grid_field, shifted):
    if shifted:
        grid_field = jnp.roll(grid_field, (-1, -6), axis=(2, 3))
    n_batch, n_rows, n_levels, n_cols, n_chans = grid_field.shape
    grid_field = grid_field.reshape(
        n_batch, n_rows // 6, 6, n_levels // 2, 2, n_cols // 12, 12, n_chans
    )
    return grid_field.transpose(0, 1, 3, 5, 2, 4, 6, 7).reshape(-1, 144, n_chans)


def from_windows(windowed, grid_shape, shifted):
    n_batch, n_rows, n_levels, n_cols, n_chans = grid_shape
    grid_field = windowed.reshape(
        n_batch, n_rows // 6, n_levels // 2, n_cols // 12, 6, 2, 12, n_chans
    )
    grid_field = grid_field.transpose(0, 1, 4, 2, 5, 3, 6, 7).reshape(grid_shape)
    if shifted:
        grid_field = jnp.roll(grid_field, (1, 6), axis=(2, 3))
    return grid_field


def make_codes(extent, first_lat, n_rows, n_levels, n_cols, shifted):
    lat_index = first_lat + lax.iota(jnp.int32, n_rows)
    level_index = lax.iota(jnp.int32, n_levels)
    col_index = lax.iota(jnp.int32, n_cols)
    inside = ((lat_index >= 0) & (lat_index < extent[0]))[:, None, None] & (col_index < extent[1])[
        None, None, :
    ]
    inside = jnp.broadcast_to(inside, (n_rows, n_levels, n_cols))
    if shifted:
        region = (level_index == 0).astype(jnp.int32)[None, :, None] * 2 + (col_index < 6).astype(
            jnp.int32
        )[None, None, :]
    else:
        region = jnp.zeros((1, n_levels, n_cols), jnp.int32)
    region = jnp.broadcast_to(region, (n_rows, n_levels, n_cols))
    key_code = jnp.where(inside, region, -1)
    query_win = to_windows(region[None, ..., None], shifted)[..., 0]
    key_win = to_windows(key_code[None, ..., None], shifted)[..., 0]
    return (inside, (query_win, key_win))


def attention_scores(queries, key_rows, codes, head_dim):
    raw_scores = jnp.einsum(
        "nihd,njhd->nhij", queries, key_rows, preferred_element_type=jnp.float32
    ) * head_dim ** (-0.5)
    allowed = codes[0][:, None, :, None] == codes[1][:, None, None, :]
    return (jnp.where(allowed, raw_scores, NEG_FILL), allowed)


def attend_forward(windowed, qkv_weight, codes, n_heads):
    n_win, n_tok, n_width = windowed.shape
    head_dim = n_width // n_heads
    packed = (
        product(windowed, qkv_weight)
        .astype(jnp.bfloat16)
        .reshape(n_win, n_tok, 3, n_heads, head_dim)
    )
    queries, key_rows, value_rows = (packed[:, :, 0], packed[:, :, 1], packed[:, :, 2])
    scores, allowed = attention_scores(queries, key_rows, codes, head_dim)
    top_score = jnp.max(scores, -1, keepdims=True)
    exp_scores = jnp.exp(scores - top_score)
    denom_sum = jnp.sum(exp_scores, -1, keepdims=True)
    attn_probs = (exp_scores / denom_sum).astype(jnp.bfloat16)
    mixed_rows = jnp.einsum(
        "nhij,njhd->nihd", attn_probs, value_rows, preferred_element_type=jnp.float32
    )
    mixed_rows = mixed_rows.reshape(n_win, n_tok, n_width).astype(jnp.bfloat16)
    return (mixed_rows, (queries, key_rows, value_rows, top_score + jnp.log(denom_sum)))


def attend_backward(windowed, qkv_weight, codes, n_heads, stored, grad_mixed):
    queries, key_rows, value_rows, log_sum = stored
    n_win, n_tok, n_width = windowed.shape
    head_dim = n_width // n_heads
    grad_heads = grad_mixed.reshape(n_win, n_tok, n_heads, head_dim)
    scores, allowed = attention_scores(queries, key_rows, codes, head_dim)
    attn_probs = jnp.exp(scores - log_sum)
    grad_values = jnp.einsum(
        "nhij,nihd->njhd",
        attn_probs.astype(jnp.bfloat16),
        grad_heads,
        preferred_element_type=jnp.float32,
    )
    grad_probs = jnp.einsum(
        "nihd,njhd->nhij", grad_heads, value_rows, preferred_element_type=jnp.float32
    )
    grad_scores = attn_probs * (grad_probs - jnp.sum(grad_probs * attn_probs, -1, keepdims=True))
    grad_scores = jnp.where(allowed, grad_scores, 0.0).astype(jnp.bfloat16)
    grad_queries = jnp.einsum(
        "nhij,njhd->nihd", grad_scores, key_rows, preferred_element_type=jnp.float32
    ) * head_dim ** (-0.5)
    grad_keys = jnp.einsum(
        "nhij,nihd->njhd", grad_scores, queries, preferred_element_type=jnp.float32
    ) * head_dim ** (-0.5)
    grad_packed = (
        jnp.stack([grad_queries, grad_keys, grad_values], 2)
        .reshape(n_win, n_tok, 3 * n_width)
        .astype(jnp.bfloat16)
    )
    return (back_product(grad_packed, qkv_weight), weight_grad(windowed, grad_packed))


def block_of(weights, prefix):
    return {
        kind_name: weights[prefix + (kind_name,)]
        for kind_name in ("norm_one", "qkv", "proj", "norm_two", "up", "down")
    }


def rest_forward(resid_in, mixed_rows, block_set):
    middle = resid_in + product(mixed_rows, block_set["proj"])
    normed_two = layer_norm(middle, block_set["norm_two"].astype(jnp.float32)).astype(jnp.bfloat16)
    raised = product(normed_two, block_set["up"])
    active = gelu_tanh(raised).astype(jnp.bfloat16)
    return (middle + product(active, block_set["down"]), (middle, normed_two, raised, active))


def rest_backward(grad_out, mixed_rows, stored, block_set):
    middle, normed_two, raised, active = stored
    grad_low = grad_out.astype(jnp.bfloat16)
    grad_down = weight_grad(active, grad_low)
    unused, pullback = jax.vjp(gelu_tanh, raised)
    grad_raised = pullback(back_product(grad_low, block_set["down"]))[0].astype(jnp.bfloat16)
    grad_up = weight_grad(normed_two, grad_raised)
    grad_middle_norm, grad_norm_two = norm_back(
        middle, block_set["norm_two"], back_product(grad_raised, block_set["up"])
    )
    grad_middle = grad_out + grad_middle_norm
    grad_branch = grad_middle.astype(jnp.bfloat16)
    grad_proj = weight_grad(mixed_rows, grad_branch)
    grad_mixed = back_product(grad_branch, block_set["proj"]).astype(jnp.bfloat16)
    return (
        grad_middle,
        grad_mixed,
        {"down": grad_down, "up": grad_up, "norm_two": grad_norm_two, "proj": grad_proj},
    )


def block_forward(resid_in, source_rows, block_set, shifted, n_heads, codes):
    windowed = to_windows(source_rows[None], shifted)
    mixed_win, attn_store = attend_forward(windowed, block_set["qkv"], codes, n_heads)
    mixed_rows = from_windows(mixed_win, (1,) + source_rows.shape, shifted)[0]
    if shifted:
        mixed_rows = mixed_rows[3 : mixed_rows.shape[0] - 3]
    new_resid, rest_store = rest_forward(resid_in, mixed_rows, block_set)
    return (new_resid, (resid_in, windowed, attn_store, mixed_rows, rest_store))


def block_backward(grad_resid, stored, block_set, shifted, n_heads, codes):
    resid_in, windowed, attn_store, mixed_rows, rest_store = stored
    grad_middle, grad_mixed, block_grads = rest_backward(
        grad_resid, mixed_rows, rest_store, block_set
    )
    if shifted:
        grad_mixed = jnp.pad(grad_mixed, ((3, 3), (0, 0), (0, 0), (0, 0)))
    grad_win, grad_qkv = attend_backward(
        windowed,
        block_set["qkv"],
        codes,
        n_heads,
        attn_store,
        to_windows(grad_mixed[None], shifted),
    )
    block_grads["qkv"] = grad_qkv
    grad_rows = from_windows(grad_win, (1,) + grad_mixed.shape, shifted)[0]
    return (grad_middle, grad_rows, block_grads)


def stack_forward(resids, weights, prefixes, n_heads, code_sets):
    stored_layers = []
    for layer_id in range(2):
        shifted = layer_id == 1
        normed = [
            layer_norm(
                resid_in, weights[prefix + (layer_id, "norm_one")].astype(jnp.float32)
            ).astype(jnp.bfloat16)
            for resid_in, prefix in zip(resids, prefixes)
        ]
        if shifted:
            extended = extended_2(jnp.concatenate(normed, -1), (("band", 0),), 3)
            sources = jnp.split(extended, len(prefixes), -1)
        else:
            sources = normed
        layer_store = []
        next_resids = []
        for resid_in, source_rows, prefix in zip(resids, sources, prefixes):
            new_resid, block_store = block_forward(
                resid_in,
                source_rows,
                block_of(weights, prefix + (layer_id,)),
                shifted,
                n_heads,
                code_sets[layer_id],
            )
            next_resids.append(new_resid)
            layer_store.append(block_store)
        resids = next_resids
        stored_layers.append(layer_store)
    return (resids, stored_layers)


def stack_backward(grad_outs, stored_layers, weights, prefixes, n_heads, code_sets, grad_table):
    for layer_id in (1, 0):
        shifted = layer_id == 1
        befores = []
        rows_grads = []
        for index_id, prefix in enumerate(prefixes):
            block_set = block_of(weights, prefix + (layer_id,))
            grad_middle, grad_rows, block_grads = block_backward(
                grad_outs[index_id],
                stored_layers[layer_id][index_id],
                block_set,
                shifted,
                n_heads,
                code_sets[layer_id],
            )
            for kind_name, grad_value in block_grads.items():
                grad_table[prefix + (layer_id, kind_name)] = grad_value
            befores.append(grad_middle)
            rows_grads.append(grad_rows)
        if shifted:
            rim_rows = jnp.concatenate(
                [
                    jnp.concatenate([row_grad[:3], row_grad[row_grad.shape[0] - 3 :]], 0)
                    for row_grad in rows_grads
                ],
                -1,
            )
            arrived = extended_2(rim_rows.astype(jnp.bfloat16), (("band", 0),), 3).astype(
                rim_rows.dtype
            )
            owned_rows = []
            for row_grad, extra_rows in zip(rows_grads, jnp.split(arrived, len(prefixes), -1)):
                inner_rows = row_grad[3 : row_grad.shape[0] - 3]
                inner_rows = inner_rows.at[:3].add(extra_rows[:3])
                inner_rows = inner_rows.at[inner_rows.shape[0] - 3 :].add(
                    extra_rows[extra_rows.shape[0] - 3 :]
                )
                owned_rows.append(inner_rows)
            rows_grads = owned_rows
        next_grads = []
        for index_id, prefix in enumerate(prefixes):
            resid_in = stored_layers[layer_id][index_id][0]
            grad_resid, grad_gain = norm_back(
                resid_in, weights[prefix + (layer_id, "norm_one")], rows_grads[index_id]
            )
            grad_table[prefix + (layer_id, "norm_one")] = grad_gain
            next_grads.append(befores[index_id] + grad_resid)
        grad_outs = next_grads
    return grad_outs


def shards(inputs, targets, crop_extent, master, moment_one, moment_two, step_count):
    n_own = master.shape[0]
    n_rows_flat = -(-n_own // 2048) * 16
    padded = jnp.pad(master.astype(jnp.bfloat16), (0, n_rows_flat * 128 - n_own))
    gathered = lax.all_gather(padded.reshape(n_rows_flat, 128), ("dp", "band"), axis=0, tiled=True)
    working = gathered.reshape(-1, n_rows_flat * 128)[:, :n_own].reshape(-1)
    weights = unpack(working)
    source = inputs[0]
    goal_field = targets[0].astype(jnp.float32)
    extent = crop_extent[0]
    n_rows, n_levels, n_cols = (source.shape[0], source.shape[1], source.shape[2])
    first_lat = lax.axis_index("band") * n_rows
    crop_cells = extent[0].astype(jnp.float32) * extent[1].astype(jnp.float32) * n_levels
    valid_total = lax.psum(crop_cells, "dp")
    norm_count = valid_total * (GROUPS * PIN)
    inside, plain_codes = make_codes(extent, first_lat, n_rows, n_levels, n_cols, False)
    unused_inside, shift_codes = make_codes(
        extent, first_lat - 3, n_rows + 6, n_levels, n_cols, True
    )
    code_sets = (plain_codes, shift_codes)
    valid = inside.astype(jnp.float32)[..., None]
    enc_prefixes = [("enc", group_id) for group_id in range(GROUPS)]
    embedded = [
        product(
            source[..., group_id * PIN : (group_id + 1) * PIN],
            weights["enc", group_id, -1, "embed"],
        )
        for group_id in range(GROUPS)
    ]
    enc_out, enc_store = stack_forward(embedded, weights, enc_prefixes, HEADS_ENC, code_sets)
    joined = jnp.concatenate(enc_out, -1).astype(jnp.bfloat16)
    joining_w = weights["trunk", 0, -1, "joining"]
    trunk_out, trunk_store = stack_forward(
        [product(joined, joining_w)], weights, [("trunk", 0)], HEADS_TRUNK, code_sets
    )
    trunk_final = trunk_out[0]
    final_gain = weights["trunk", 0, -1, "final"]
    final_low = layer_norm(trunk_final, final_gain.astype(jnp.float32)).astype(jnp.bfloat16)
    grad_table = {}
    loss_local = jnp.zeros((), jnp.float32)
    grad_final = jnp.zeros(trunk_final.shape, jnp.float32)
    for group_id in range(GROUPS):
        decode_w = weights["top", group_id, -1, "decode"]
        head_w = weights["top", group_id, -1, "head"]
        raised = product(final_low, decode_w)
        active = gelu_tanh(raised).astype(jnp.bfloat16)
        predicted = product(active, head_w)
        log_scale = weights["top", group_id, -1, "scale"].astype(jnp.float32)
        pred_error = predicted - goal_field[..., group_id * PIN : (group_id + 1) * PIN]
        inverse_scale = jnp.exp(-log_scale)
        loss_local = loss_local + jnp.sum((jnp.abs(pred_error) * inverse_scale + log_scale) * valid)
        grad_pred = (jnp.sign(pred_error) * inverse_scale * valid / norm_count).astype(jnp.bfloat16)
        grad_table["top", group_id, -1, "scale"] = (
            jnp.sum(
                ((1.0 - jnp.abs(pred_error) * inverse_scale) * valid).reshape(
                    -1, pred_error.shape[-1]
                ),
                0,
            )
            / norm_count
        )
        grad_table["top", group_id, -1, "head"] = weight_grad(active, grad_pred)
        unused, pullback = jax.vjp(gelu_tanh, raised)
        grad_raised = pullback(back_product(grad_pred, head_w))[0].astype(jnp.bfloat16)
        grad_table["top", group_id, -1, "decode"] = weight_grad(final_low, grad_raised)
        grad_final = grad_final + back_product(grad_raised, decode_w)
    loss_total = lax.psum(loss_local, ("dp", "band"))
    grad_trunk, grad_table["trunk", 0, -1, "final"] = norm_back(trunk_final, final_gain, grad_final)
    grad_trunk_in = stack_backward(
        [grad_trunk], trunk_store, weights, [("trunk", 0)], HEADS_TRUNK, code_sets, grad_table
    )[0]
    grad_join_low = grad_trunk_in.astype(jnp.bfloat16)
    grad_table["trunk", 0, -1, "joining"] = weight_grad(joined, grad_join_low)
    grad_joined = back_product(grad_join_low, joining_w)
    grad_enc = stack_backward(
        jnp.split(grad_joined, GROUPS, -1),
        enc_store,
        weights,
        enc_prefixes,
        HEADS_ENC,
        code_sets,
        grad_table,
    )
    for group_id in range(GROUPS):
        grad_table["enc", group_id, -1, "embed"] = weight_grad(
            source[..., group_id * PIN : (group_id + 1) * PIN],
            grad_enc[group_id].astype(jnp.bfloat16),
        )
    flat_grad = jnp.concatenate(
        [grad_table[label_key].reshape(-1) for label_key, dims_shape in layout()]
    )
    parts = jnp.pad(flat_grad.reshape(-1, n_own), ((0, 0), (0, n_rows_flat * 128 - n_own)))
    grad_shard = lax.psum_scatter(
        parts.reshape(-1, 128), ("dp", "band"), scatter_dimension=0, tiled=True
    ).reshape(-1)[:n_own]
    shard_square = jnp.sum(grad_shard * grad_shard)
    square_total = lax.psum(shard_square, ("dp", "band"))
    grad_norm = jnp.sqrt(square_total)
    factor_clip = jnp.minimum(1.0, CLIP_LEVEL / (grad_norm + 1e-06))
    clipped = grad_shard * factor_clip
    new_one = BETA_ONE * moment_one + (1.0 - BETA_ONE) * clipped
    new_two = BETA_TWO * moment_two + (1.0 - BETA_TWO) * clipped * clipped
    step_value = step_count[0].astype(jnp.float32)
    fix_one = 1.0 - jnp.power(BETA_ONE, step_value)
    fix_two = 1.0 - jnp.power(BETA_TWO, step_value)
    update = new_one / fix_one / (jnp.sqrt(new_two / fix_two) + ADAM_EPS) + WEIGHT_DECAY * master
    new_master = master - LEARN_RATE * update
    return (
        new_master,
        new_one,
        new_two,
        new_master.astype(jnp.bfloat16),
        loss_total / norm_count,
        grad_norm,
    )


def solution(mesh):
    in_specs = (
        P("dp", "band", None, None, None),
        P("dp", "band", None, None, None),
        P("dp", None),
        P(("dp", "band")),
        P(("dp", "band")),
        P(("dp", "band")),
        P(),
    )
    out_specs = (
        P(("dp", "band")),
        P(("dp", "band")),
        P(("dp", "band")),
        P(("dp", "band")),
        P(),
        P(),
    )
    return jax.shard_map(shards, mesh=mesh, in_specs=in_specs, out_specs=out_specs, check_vma=False)
```

```python
import functools
import math

import jax
import jax.numpy as jnp
import numpy as np
from jax import lax
from jax.experimental import pallas as pl
from jax.experimental.pallas import tpu as pltpu
from jax.sharding import PartitionSpec as P

D_ENC = 192
HEADS_ENC = 6
D_TRUNK = 384
HEADS_TRUNK = 12
PIN = 128
GROUPS = 2
HEAD_DIM = 32
SCALE = HEAD_DIM ** (-0.5)

NEG_FILL = -1000000000.0
BETA_ONE = 0.5
BETA_TWO = 0.5
LEARN_RATE = 0.01
WEIGHT_DECAY = 0.1
CLIP_LEVEL = 0.07
ADAM_EPS = 1e-08

F32 = jnp.float32
BF16 = jnp.bfloat16
TOKENS = 288
WIN = 144
ENC_SPLIT = ((0, 192, 6),)
TRUNK_SPLIT = ((0, 256, 8), (256, 128, 4))


def block_layout(path_name, group_id, layer_id, n_width):
    prefix = (path_name, group_id, layer_id)
    return [
        (prefix + ("norm_one",), (2, n_width)),
        (prefix + ("qkv",), (n_width, 3 * n_width)),
        (prefix + ("proj",), (n_width, n_width)),
        (prefix + ("norm_two",), (2, n_width)),
        (prefix + ("up",), (n_width, 4 * n_width)),
        (prefix + ("down",), (4 * n_width, n_width)),
    ]


def layout():
    entries = []
    for group_id in range(GROUPS):
        entries.append((("enc", group_id, -1, "embed"), (PIN, D_ENC)))
        for layer_id in range(2):
            entries += block_layout("enc", group_id, layer_id, D_ENC)
        entries.append((("top", group_id, -1, "decode"), (D_TRUNK, D_ENC)))
        entries.append((("top", group_id, -1, "head"), (D_ENC, PIN)))
        entries.append((("top", group_id, -1, "scale"), (PIN,)))
    entries.append((("trunk", 0, -1, "joining"), (GROUPS * D_ENC, D_TRUNK)))
    for layer_id in range(2):
        entries += block_layout("trunk", 0, layer_id, D_TRUNK)
    entries.append((("trunk", 0, -1, "final"), (2, D_TRUNK)))
    return entries


def placed():
    offset = 0
    for label_key, dims_shape in layout():
        yield label_key, dims_shape, offset
        offset += math.prod(dims_shape)


def nn(left, right):
    return jnp.dot(left, right, preferred_element_type=F32)


def nt(left, right):
    return lax.dot_general(left, right, (((1,), (1,)), ((), ())), preferred_element_type=F32)


def tn(left, right):
    return lax.dot_general(left, right, (((0,), (0,)), ((), ())), preferred_element_type=F32)


def unit_rows(values):
    centre = values - jnp.mean(values, -1, keepdims=True)
    inverse = lax.rsqrt(jnp.mean(centre * centre, -1, keepdims=True) + 1e-05)
    return centre * inverse, inverse


def norm_forward(values, gain_ref):
    unit, unused = unit_rows(values)
    return unit * gain_ref[0:1, :] + gain_ref[1:2, :]


def norm_backward(values, gain_ref, grad_normed):
    unit, inverse = unit_rows(values)
    grad_gain = jnp.sum(grad_normed * unit, 0, keepdims=True)
    grad_shift = jnp.sum(grad_normed, 0, keepdims=True)
    grad_unit = grad_normed * gain_ref[0:1, :]
    along = jnp.mean(grad_unit * unit, -1, keepdims=True)
    grad_values = inverse * (grad_unit - jnp.mean(grad_unit, -1, keepdims=True) - unit * along)
    return grad_values, jnp.concatenate([grad_gain, grad_shift], 0)


GELU_A = math.sqrt(2.0 / math.pi)
GELU_B = 0.044715


def gelu(values):
    inner = jnp.tanh(GELU_A * (values + GELU_B * (values * values * values)))
    return values * (0.5 * (1.0 + inner))


def gelu_slope(values):
    square = values * values
    inner = jnp.tanh(GELU_A * (values + GELU_B * (square * values)))
    steep = (1.0 - inner * inner) * (GELU_A + (3.0 * GELU_B * GELU_A) * square)
    return 0.5 * (1.0 + inner) + 0.5 * values * steep


def head_lanes(rows, lanes, head):
    lane = lax.broadcasted_iota(jnp.int32, (rows, lanes), 1)
    return (lane >= HEAD_DIM * head) & (lane < HEAD_DIM * (head + 1))


def columns_of(n_heads, n_query):
    return -(-n_heads * n_query // 128)


def spread_heads(rows_value, n_heads, out_ref):
    n_query, lanes = rows_value.shape
    wide = rows_value.astype(F32)
    for head in range(n_heads):
        kept = jnp.where(head_lanes(n_query, lanes, head), wide, 0.0).astype(BF16)
        out_ref[head * n_query : (head + 1) * n_query, 0:lanes] = kept
    total = 128 * columns_of(n_heads, n_query)
    if total > n_heads * n_query:
        out_ref[n_heads * n_query : total, 0:lanes] = jnp.zeros(
            (total - n_heads * n_query, lanes), BF16
        )


def join_heads(spread_ref, n_heads, n_query, lanes):
    joined = spread_ref[0:n_query, 0:lanes]
    for head in range(1, n_heads):
        part = spread_ref[head * n_query : (head + 1) * n_query, 0:lanes]
        joined = jnp.where(head_lanes(n_query, lanes, head), part, joined)
    return joined


def attend_window(queries, key_rows, value_rows, key_code, query_code, probs_ref, q_scr, o_scr, split):
    n_query = queries.shape[0]
    outs = []
    at = 0
    for lane, lanes, n_heads in split:
        spread_heads(queries[:, lane : lane + lanes], n_heads, q_scr)
        keys = key_rows[:, lane : lane + lanes]
        values = value_rows[:, lane : lane + lanes]
        for tile in range(columns_of(n_heads, n_query)):
            rows = slice(128 * tile, 128 * tile + 128)
            scores = nt(keys, q_scr[rows, 0:lanes]) * SCALE
            code = query_code[0:1, at + 128 * tile : at + 128 * tile + 128]
            scores = jnp.where(key_code == code, scores, NEG_FILL)
            raised = jnp.exp(scores - jnp.max(scores, 0, keepdims=True))
            probs = (raised * (1.0 / jnp.sum(raised, 0, keepdims=True))).astype(BF16)
            probs_ref[:, at + 128 * tile : at + 128 * tile + 128] = probs
            o_scr[rows, 0:lanes] = tn(probs, values)
        outs.append(join_heads(o_scr, n_heads, n_query, lanes))
        at += 128 * columns_of(n_heads, n_query)
    return jnp.concatenate(outs, 1) if len(outs) > 1 else outs[0]


def attend_window_back(
    queries, key_rows, value_rows, grad_rows, key_code, query_code, probs_ref, q_scr, g_scr, o_scr, s_scr, split
):
    n_query = queries.shape[0]
    out_q, out_k, out_v = [], [], []
    at = 0
    for lane, lanes, n_heads in split:
        n_col = columns_of(n_heads, n_query)
        spread_heads(queries[:, lane : lane + lanes], n_heads, q_scr)
        spread_heads(grad_rows[:, lane : lane + lanes], n_heads, g_scr)
        keys = key_rows[:, lane : lane + lanes]
        values = value_rows[:, lane : lane + lanes]
        for tile in range(n_col):
            rows = slice(128 * tile, 128 * tile + 128)
            code = query_code[0:1, at + 128 * tile : at + 128 * tile + 128]
            grad_probs = nt(values, g_scr[rows, 0:lanes])
            probs = probs_ref[:, at + 128 * tile : at + 128 * tile + 128].astype(F32)
            along = jnp.sum(grad_probs * probs, 0, keepdims=True)
            grad_scores = probs * (grad_probs - along)
            grad_scores = jnp.where(key_code == code, grad_scores, 0.0).astype(BF16)
            s_scr[:, rows] = grad_scores
            o_scr[rows, 0:lanes] = tn(grad_scores, keys)
        wide = 128 * n_col
        out_v.append(nn(probs_ref[:, at : at + wide], g_scr[0:wide, 0:lanes]))
        out_k.append(nn(s_scr[:, 0:wide], q_scr[0:wide, 0:lanes]) * SCALE)
        out_q.append(join_heads(o_scr, n_heads, n_query, lanes) * SCALE)
        at += wide
    if len(split) > 1:
        return tuple(jnp.concatenate(parts, 1) for parts in (out_q, out_k, out_v))
    return out_q[0], out_k[0], out_v[0]


def rest_forward(resid_in, mixed, proj, gain_ref, up, down, middle_ref, normed_ref, raised_ref, active_ref):
    middle = resid_in + nn(mixed, proj[...])
    middle_ref[...] = middle
    normed = norm_forward(middle, gain_ref).astype(BF16)
    normed_ref[...] = normed
    width = up.shape[1]
    for start in range(0, width, 256):
        raised_ref[:, start : start + 256] = nn(normed, up[:, start : start + 256])
        for row in range(0, TOKENS, 96):
            piece = raised_ref[row : row + 96, start : start + 256]
            active_ref[row : row + 96, start : start + 256] = gelu(piece).astype(BF16)
    return middle + nn(active_ref[...], down[...])


def rest_backward(
    grad_out, mixed_ref, middle_ref, normed_ref, raised_ref, active_ref, proj, gain_ref, up, down, raised_scr, outs
):
    d_proj, d_gain, d_up, d_down = outs
    grad_low = grad_out.astype(BF16)
    d_down[...] = tn(active_ref[...], grad_low).astype(d_down.dtype)
    width = up.shape[1]
    for start in range(0, width, 256):
        grad_active = nt(grad_low, down[start : start + 256, :])
        for row in range(0, TOKENS, 96):
            slope = gelu_slope(raised_ref[row : row + 96, start : start + 256])
            raised_scr[row : row + 96, start : start + 256] = (
                slope * grad_active[row : row + 96, :]
            ).astype(BF16)
    d_up[...] = tn(normed_ref[...], raised_scr[:, 0:width]).astype(d_up.dtype)
    grad_middle, grad_gain = norm_backward(
        middle_ref[...], gain_ref, nt(raised_scr[:, 0:width], up[...])
    )
    d_gain[...] = grad_gain
    grad_middle = grad_out + grad_middle
    grad_branch = grad_middle.astype(BF16)
    d_proj[...] = tn(mixed_ref[...], grad_branch).astype(d_proj.dtype)
    return grad_middle, nt(grad_branch, proj[...]).astype(BF16)


def plain_attention(qkv_ref, mixed_ref, key_code, query_code, probs_ref, q_scr, o_scr, split, width):
    for win in range(2):
        rows = slice(WIN * win, WIN * (win + 1))
        mixed_ref[rows, :] = attend_window(
            qkv_ref[rows, 0:width],
            qkv_ref[rows, width : 2 * width],
            qkv_ref[rows, 2 * width : 3 * width],
            key_code[rows, :],
            query_code,
            probs_ref.at[win],
            q_scr,
            o_scr,
            split,
        ).astype(BF16)


def shifted_keys(qkv_ref, far_ref, win, width):
    rows = slice(72 * win, 72 * (win + 1))
    keys = jnp.concatenate([qkv_ref[rows, width : 2 * width], far_ref[rows, 0:width]], 0)
    values = jnp.concatenate([qkv_ref[rows, 2 * width :], far_ref[rows, width:]], 0)
    return qkv_ref[rows, 0:width], keys, values


def enc_plain_kernel(
    src, key_code, query_code, to_win, embed, gain_one, qkv, proj, gain_two, up, down, gain_next,
    x_in, normed, packed, probs, mixed, middle, normed_two, raised, active, x_out, sent_a, sent_b,
    q_scr, o_scr, *, split, width,
):
    first = nn(src[...], embed[...])
    plain_body(
        first, key_code, query_code, to_win, gain_one, qkv, proj, gain_two, up, down, gain_next,
        x_in, normed, packed, probs, mixed, middle, normed_two, raised, active, x_out, sent_a, sent_b,
        q_scr, o_scr, split, width,
    )


def trunk_plain_kernel(
    left, right, key_code, query_code, to_win, joining, gain_one, qkv, proj, gain_two, up, down, gain_next,
    joined, x_in, normed, packed, probs, mixed, middle, normed_two, raised, active, x_out, sent_a, sent_b,
    q_scr, o_scr, *, split, width,
):
    joined[...] = jnp.concatenate([left[...], right[...]], 1).astype(BF16)
    first = nn(joined[...], joining[...])
    plain_body(
        first, key_code, query_code, to_win, gain_one, qkv, proj, gain_two, up, down, gain_next,
        x_in, normed, packed, probs, mixed, middle, normed_two, raised, active, x_out, sent_a, sent_b,
        q_scr, o_scr, split, width,
    )


def plain_body(
    first, key_code, query_code, to_win, gain_one, qkv, proj, gain_two, up, down, gain_next,
    x_in, normed, packed, probs, mixed, middle, normed_two, raised, active, x_out, sent_a, sent_b,
    q_scr, o_scr, split, width,
):
    x_in[...] = first
    normed[...] = norm_forward(first, gain_one).astype(BF16)
    packed[...] = nn(normed[...], qkv[...]).astype(BF16)
    plain_attention(packed, mixed, key_code, query_code, probs, q_scr, o_scr, split, width)
    last = rest_forward(
        first, mixed[...], proj, gain_two, up, down, middle, normed_two, raised, active
    )
    x_out[...] = last
    ordered = nn(to_win[...], norm_forward(last, gain_next).astype(BF16)).astype(BF16)
    sent_a[...] = ordered[0:WIN]
    sent_b[...] = ordered[WIN:]


def shifted_kernel(
    x_in, near_a, near_b, far_a, far_b, key_code, query_code, to_tok, qkv, proj, gain_two, up, down,
    packed, packed_far, probs, mixed, middle, normed_two, raised, active, x_out,
    q_scr, o_scr, m_scr, *, split, width,
):
    near = jnp.concatenate([near_a[...], near_b[...]], 0)
    far = jnp.concatenate([far_a[...], far_b[...]], 0)
    packed[...] = nn(near, qkv[...]).astype(BF16)
    packed_far[...] = nn(far, qkv[:, width:]).astype(BF16)
    for win in range(4):
        queries, keys, values = shifted_keys(packed, packed_far, win, width)
        m_scr[72 * win : 72 * (win + 1), 0:width] = attend_window(
            queries, keys, values, key_code[WIN * win : WIN * (win + 1), :],
            query_code.at[win % 2], probs.at[win], q_scr, o_scr, split,
        )
    mixed[...] = nn(to_tok[...], m_scr[:, 0:width].astype(BF16)).astype(BF16)
    x_out[...] = rest_forward(
        x_in[...], mixed[...], proj, gain_two, up, down, middle, normed_two, raised, active
    )


def loss_kernel(
    trunk, goal, key_code, count, final, decode, head, scale,
    grad_trunk, d_final, d_decode, d_head, d_scale, loss,
):
    values = trunk[...]
    low = norm_forward(values, final).astype(BF16)
    valid = key_code[...] + 1.0
    inverse_count = 1.0 / count[0, 0]
    grad_low = None
    total = None
    for group in range(GROUPS):
        raised = nn(low, decode[group])
        active = gelu(raised).astype(BF16)
        predicted = nn(active, head[group])
        log_scale = scale[group : group + 1, :]
        error = predicted - goal[:, PIN * group : PIN * (group + 1)].astype(F32)
        inverse_scale = jnp.exp(-log_scale)
        weighted = jnp.abs(error) * inverse_scale
        part = jnp.sum((weighted + log_scale) * valid, 0, keepdims=True)
        total = part if total is None else total + part
        direction = jnp.where(error > 0.0, 1.0, jnp.where(error < 0.0, -1.0, 0.0))
        grad_pred = (direction * inverse_scale * valid * inverse_count).astype(BF16)
        d_scale[group : group + 1, :] = (
            jnp.sum((1.0 - weighted) * valid, 0, keepdims=True) * inverse_count
        )
        d_head[group] = tn(active, grad_pred).astype(d_head.dtype)
        grad_raised = (gelu_slope(raised) * nt(grad_pred, head[group])).astype(BF16)
        d_decode[group] = tn(low, grad_raised).astype(d_decode.dtype)
        back = nt(grad_raised, decode[group])
        grad_low = back if grad_low is None else grad_low + back
    loss[...] = total
    grad_values, grad_final = norm_backward(values, final, grad_low)
    grad_trunk[...] = grad_values
    d_final[...] = grad_final


def shifted_back_kernel(
    grad_out, near_a, near_b, far_a, far_b, packed, packed_far, probs, mixed, middle, normed_two, raised, active,
    key_code, query_code, to_win, to_tok, qkv, proj, gain_two, up, down,
    grad_middle, grad_near, rim_a, rim_b, d_qkv, d_proj, d_gain_two, d_up, d_down,
    q_scr, g_scr, o_scr, s_scr, raised_scr, near_scr, far_scr, *, split, width,
):
    grad_mid, grad_mixed = rest_backward(
        grad_out[...], mixed, middle, normed_two, raised, active, proj, gain_two, up, down,
        raised_scr, (d_proj, d_gain_two, d_up, d_down),
    )
    grad_middle[...] = grad_mid
    grad_win = nn(to_win[...], grad_mixed).astype(BF16)
    for win in range(4):
        rows = slice(72 * win, 72 * (win + 1))
        queries, keys, values = shifted_keys(packed, packed_far, win, width)
        grad_q, grad_k, grad_v = attend_window_back(
            queries, keys, values, grad_win[rows, :], key_code[WIN * win : WIN * (win + 1), :],
            query_code.at[win % 2], probs.at[win], q_scr, g_scr, o_scr, s_scr, split,
        )
        near_scr[rows, 0:width] = grad_q.astype(BF16)
        near_scr[rows, width : 2 * width] = grad_k[0:72].astype(BF16)
        near_scr[rows, 2 * width : 3 * width] = grad_v[0:72].astype(BF16)
        far_scr[rows, 0:width] = grad_k[72:144].astype(BF16)
        far_scr[rows, width : 2 * width] = grad_v[72:144].astype(BF16)
    near_grad = near_scr[...]
    far_grad = far_scr[...]
    near = jnp.concatenate([near_a[...], near_b[...]], 0)
    far = jnp.concatenate([far_a[...], far_b[...]], 0)
    d_qkv[:, 0:width] = tn(near, near_grad[:, 0:width]).astype(d_qkv.dtype)
    d_qkv[:, width:] = (tn(near, near_grad[:, width:]) + tn(far, far_grad)).astype(d_qkv.dtype)
    rim = nt(far_grad, qkv[:, width:]).astype(BF16)
    rim_a[...] = rim[0:WIN]
    rim_b[...] = rim[WIN:]
    grad_near[...] = nt(nn(to_tok[...], near_grad).astype(BF16), qkv[...])


def plain_back_body(
    grad_middle_next, grad_near, arrived_a, arrived_b, x_out, gain_next, to_tok,
    x_in, normed, packed, probs, mixed, middle, normed_two, raised, active,
    key_code, query_code, gain_one, qkv, proj, gain_two, up, down,
    d_gain_next, d_gain_one, d_qkv, d_proj, d_gain_two, d_up, d_down,
    q_scr, g_scr, o_scr, s_scr, raised_scr, near_scr, split, width,
):
    arrived = jnp.concatenate([arrived_a[...], arrived_b[...]], 0)
    grad_normed = grad_near[...] + nn(to_tok[...], arrived)
    grad_x, grad_gain = norm_backward(x_out[...], gain_next, grad_normed)
    d_gain_next[...] = grad_gain
    grad_mid, grad_mixed = rest_backward(
        grad_middle_next[...] + grad_x, mixed, middle, normed_two, raised, active,
        proj, gain_two, up, down, raised_scr, (d_proj, d_gain_two, d_up, d_down),
    )
    for win in range(2):
        rows = slice(WIN * win, WIN * (win + 1))
        grads = attend_window_back(
            packed[rows, 0:width], packed[rows, width : 2 * width], packed[rows, 2 * width :],
            grad_mixed[rows, :], key_code[rows, :], query_code, probs.at[win],
            q_scr, g_scr, o_scr, s_scr, split,
        )
        for index, grad in enumerate(grads):
            near_scr[rows, width * index : width * (index + 1)] = grad.astype(BF16)
    near_grad = near_scr[...]
    d_qkv[...] = tn(normed[...], near_grad).astype(d_qkv.dtype)
    grad_first, grad_gain = norm_backward(x_in[...], gain_one, nt(near_grad, qkv[...]))
    d_gain_one[...] = grad_gain
    return grad_mid + grad_first


def trunk_plain_back_kernel(
    grad_middle_next, grad_near, arrived_a, arrived_b, x_out, gain_next, to_tok,
    x_in, normed, packed, probs, mixed, middle, normed_two, raised, active,
    key_code, query_code, gain_one, qkv, proj, gain_two, up, down, joined, joining,
    grad_left, grad_right, d_joining,
    d_gain_next, d_gain_one, d_qkv, d_proj, d_gain_two, d_up, d_down,
    q_scr, g_scr, o_scr, s_scr, raised_scr, near_scr, *, split, width,
):
    grad = plain_back_body(
        grad_middle_next, grad_near, arrived_a, arrived_b, x_out, gain_next, to_tok,
        x_in, normed, packed, probs, mixed, middle, normed_two, raised, active,
        key_code, query_code, gain_one, qkv, proj, gain_two, up, down,
        d_gain_next, d_gain_one, d_qkv, d_proj, d_gain_two, d_up, d_down,
        q_scr, g_scr, o_scr, s_scr, raised_scr, near_scr, split, width,
    ).astype(BF16)
    d_joining[...] = tn(joined[...], grad).astype(d_joining.dtype)
    back = nt(grad, joining[...])
    grad_left[...] = back[:, 0:D_ENC]
    grad_right[...] = back[:, D_ENC:]


def enc_plain_back_kernel(
    grad_middle_next, grad_near, arrived_a, arrived_b, x_out, gain_next, to_tok,
    x_in, normed, packed, probs, mixed, middle, normed_two, raised, active,
    key_code, query_code, gain_one, qkv, proj, gain_two, up, down, src,
    d_embed, d_gain_next, d_gain_one, d_qkv, d_proj, d_gain_two, d_up, d_down,
    q_scr, g_scr, o_scr, s_scr, raised_scr, near_scr, *, split, width,
):
    grad = plain_back_body(
        grad_middle_next, grad_near, arrived_a, arrived_b, x_out, gain_next, to_tok,
        x_in, normed, packed, probs, mixed, middle, normed_two, raised, active,
        key_code, query_code, gain_one, qkv, proj, gain_two, up, down,
        d_gain_next, d_gain_one, d_qkv, d_proj, d_gain_two, d_up, d_down,
        q_scr, g_scr, o_scr, s_scr, raised_scr, near_scr, split, width,
    ).astype(BF16)
    d_embed[...] = tn(src[...], grad).astype(d_embed.dtype)


def whole(shape):
    return pl.BlockSpec(shape, lambda g: (0,) * len(shape))


def of_group(shape, group=None):
    if group is None:
        return pl.BlockSpec((None,) + shape, lambda g: (g,) + (0,) * len(shape))
    return pl.BlockSpec((None,) + shape, lambda g: (group,) + (0,) * len(shape))


def launch(body, name, n_groups, ins, outs, scratch, limit=40 << 20):
    in_specs = [whole(array.shape) if spec is None else spec for array, spec in ins]
    out_specs = []
    out_shape = []
    for shape, dtype, grouped in outs:
        if grouped and n_groups > 1:
            out_specs.append(of_group(shape))
            out_shape.append(jax.ShapeDtypeStruct((n_groups,) + shape, dtype))
        else:
            out_specs.append(whole(shape))
            out_shape.append(jax.ShapeDtypeStruct(shape, dtype))
    return pl.pallas_call(
        body,
        grid=(n_groups,),
        in_specs=in_specs,
        out_specs=out_specs,
        out_shape=out_shape,
        scratch_shapes=scratch,
        name=name,
        compiler_params=pltpu.CompilerParams(
            dimension_semantics=("arbitrary",), vmem_limit_bytes=limit
        ),
    )(*[array for array, spec in ins])


def probs_width(split, n_query):
    return 128 * sum(columns_of(n_heads, n_query) for lane, lanes, n_heads in split)


def spread_rows(split, n_query):
    return 128 * max(columns_of(n_heads, n_query) for lane, lanes, n_heads in split)


def spread_lanes(split):
    return max(lanes for lane, lanes, n_heads in split)


def saved_outs(width, split, shifted):
    n_query, n_win = (72, 4) if shifted else (WIN, 2)
    packed = [((TOKENS, 3 * width), BF16, True)]
    if shifted:
        packed.append(((TOKENS, 2 * width), BF16, True))
    else:
        packed = [((TOKENS, width), F32, True), ((TOKENS, width), BF16, True)] + packed
    return packed + [
        ((n_win, WIN, probs_width(split, n_query)), BF16, True),
        ((TOKENS, width), BF16, True),
        ((TOKENS, width), F32, True),
        ((TOKENS, width), BF16, True),
        ((TOKENS, 4 * width), F32, True),
        ((TOKENS, 4 * width), BF16, True),
        ((TOKENS, width), F32, True),
    ]


def spread_scratch(split, n_query, dtype):
    return pltpu.VMEM((spread_rows(split, n_query), spread_lanes(split)), dtype)


def forward_scratch(width, split, shifted):
    n_query = 72 if shifted else WIN
    held = [spread_scratch(split, n_query, BF16), spread_scratch(split, n_query, F32)]
    if shifted:
        held.append(pltpu.VMEM((TOKENS, width), F32))
    return held


def backward_scratch(width, split, shifted):
    n_query = 72 if shifted else WIN
    held = [
        spread_scratch(split, n_query, BF16),
        spread_scratch(split, n_query, BF16),
        spread_scratch(split, n_query, F32),
        pltpu.VMEM((WIN, spread_rows(split, n_query)), BF16),
        pltpu.VMEM((TOKENS, 4 * width), BF16),
        pltpu.VMEM((TOKENS, 3 * width), BF16),
    ]
    if shifted:
        held.append(pltpu.VMEM((TOKENS, 2 * width), BF16))
    return held


def window_order():
    order = []
    for half in range(2):
        for pair in ((1, 2), (3, 0)):
            for level in pair:
                for row in range(3):
                    for col in range(12):
                        order.append(level * 72 + (half * 3 + row) * 12 + col)
    return np.array(order)


def fixed_tables():
    order = window_order()
    to_win = np.zeros((TOKENS, TOKENS), np.float32)
    to_win[np.arange(TOKENS), order] = 1.0
    region = np.zeros((2, 72), np.float32)
    for pair, levels in enumerate(((1, 2), (3, 0))):
        for place in range(72):
            level, col = levels[place // 36], place % 12
            region[pair, place] = 2.0 * (level == 0) + 1.0 * (col < 6)
    return to_win, region


def key_codes(extent, first_lat):
    place = lax.broadcasted_iota(jnp.int32, (TOKENS, 128), 0)
    row, col = (place // 12) % 6, place % 12
    inside = (first_lat + row < extent[0]) & (col < extent[1])
    plain = jnp.where(inside, 0.0, -1.0)
    place = lax.broadcasted_iota(jnp.int32, (2 * TOKENS, 128), 0)
    win, rest = place // WIN, place % WIN
    far, rest = rest // 72, rest % 72
    half, pair = win // 2, win % 2
    second = rest // 36
    row, col = (rest // 12) % 3, rest % 12
    near_row = 3 * half + row
    far_row = jnp.where(half == 0, row - 3, row + 6)
    lat = first_lat + jnp.where(far == 1, far_row, near_row)
    top = (pair == 1) & (second == 1)
    region = jnp.where(top, 2.0, 0.0) + jnp.where(col < 6, 1.0, 0.0)
    inside = (lat >= 0) & (lat < extent[0]) & (col < extent[1])
    return plain, jnp.where(inside, region, -1.0)


def exchange(first, second):
    count = lax.axis_size("band")
    up = [(i, i + 1) for i in range(count - 1)]
    down = [(i + 1, i) for i in range(count - 1)]
    return lax.ppermute(second, "band", up), lax.ppermute(first, "band", down)


SAVED = ("packed", "probs", "mixed", "middle", "normed_two", "raised", "active")


def compute(weights, source, goal, codes, count, grad_type):
    to_win, region = fixed_tables()
    to_tok = jnp.asarray(to_win.T, BF16)
    to_win = jnp.asarray(to_win, BF16)
    plain_code, shift_code = codes
    grads = {}

    def plain_query(split):
        return jnp.zeros((1, probs_width(split, WIN)), F32)

    def shift_query(split):
        parts = []
        for lane, lanes, n_heads in split:
            total = 128 * columns_of(n_heads, 72)
            tiled = np.tile(region, (1, n_heads))
            parts.append(np.pad(tiled, ((0, 0), (0, total - tiled.shape[1]))))
        return jnp.asarray(np.concatenate(parts, 1)[:, None, :], F32)

    def block_ins(tower, layer, names, grouped):
        found = []
        for name in names:
            array = weights[tower, layer, name]
            found.append((array, of_group(array.shape[1:]) if grouped else None))
        return found

    BLOCK = ("norm_one", "qkv", "proj", "norm_two", "up", "down")
    saved = {}
    plain_saved = ("x_in", "normed") + SAVED + ("x_out",)
    shift_saved = ("packed", "packed_far") + SAVED[1:] + ("x_out",)

    def grouped(array):
        return (array, of_group(array.shape[1:]))

    def forward_pair(tower, width, split, n_groups):
        many = n_groups > 1
        pick = grouped if many else (lambda array: (array, None))
        gain_next = block_ins(tower, 1, ("norm_one",), many)
        codes_in = [(plain_code, None), (plain_query(split), None), (to_win, None)]
        sent_outs = [((WIN, width), BF16, True)] * 2
        if many:
            ins = [(source, pl.BlockSpec((TOKENS, PIN), lambda g: (0, g)))] + codes_in
            ins += [grouped(weights[tower, -1, "embed"])]
            body, extra = enc_plain_kernel, []
        else:
            left = saved["enc", 1]["x_out"]
            ins = [(left, of_group(left.shape[1:], 0)), (left, of_group(left.shape[1:], 1))] + codes_in
            ins += [(weights[tower, -1, "joining"], None)]
            body, extra = trunk_plain_kernel, [((TOKENS, 2 * D_ENC), BF16, False)]
        ins += block_ins(tower, 0, BLOCK, many) + gain_next
        results = launch(
            functools.partial(body, split=split, width=width), tower + "_plain", n_groups, ins,
            extra + saved_outs(width, split, False) + sent_outs, forward_scratch(width, split, False),
        )
        if extra:
            saved["joined"] = results[0]
            results = results[1:]
        saved[tower, 0] = dict(zip(plain_saved, results))
        sent = results[-2:]
        far = exchange(*sent)
        ins = [pick(saved[tower, 0]["x_out"])] + [pick(array) for array in (*sent, *far)]
        ins += [(shift_code, None), (shift_query(split), None), (to_tok, None)]
        ins += block_ins(tower, 1, BLOCK[1:], many)
        results = launch(
            functools.partial(shifted_kernel, split=split, width=width), tower + "_shifted", n_groups,
            ins, saved_outs(width, split, True), forward_scratch(width, split, True),
        )
        saved[tower, 1] = dict(zip(shift_saved, results))
        saved[tower, 1]["rows"] = (*sent, *far)

    forward_pair("enc", D_ENC, ENC_SPLIT, GROUPS)
    forward_pair("trunk", D_TRUNK, TRUNK_SPLIT, 1)

    results = launch(
        loss_kernel, "loss", 1,
        [(saved["trunk", 1]["x_out"], None), (goal, None), (plain_code, None),
         (count, pl.BlockSpec(memory_space=pltpu.SMEM)),
         (weights["trunk", -1, "final"], None), (weights["top", -1, "decode"], None),
         (weights["top", -1, "head"], None), (weights["top", -1, "scale"], None)],
        [((TOKENS, D_TRUNK), F32, False), ((2, D_TRUNK), F32, False),
         ((GROUPS, D_TRUNK, D_ENC), grad_type, False), ((GROUPS, D_ENC, PIN), grad_type, False),
         ((GROUPS, PIN), F32, False), ((1, PIN), F32, False)],
        [],
    )
    grad_out, grads["trunk", -1, "final"], grads["top", -1, "decode"] = results[:3]
    grads["top", -1, "head"], grads["top", -1, "scale"], loss_row = results[3:]

    def gain_out(width):
        return ((2, width), F32, True)

    def block_grads(width):
        return [
            ((width, 3 * width), grad_type, True),
            ((width, width), grad_type, True),
            gain_out(width),
            ((width, 4 * width), grad_type, True),
            ((4 * width, width), grad_type, True),
        ]

    def backward_pair(tower, width, split, n_groups, grad_in):
        many = n_groups > 1
        pick = grouped if many else (lambda array: (array, None))
        kept = saved[tower, 1]
        ins = [grad_in] if many else [(grad_in, None)]
        ins += [pick(array) for array in kept["rows"]]
        ins += [pick(kept[name]) for name in shift_saved[:-1]]
        ins += [(shift_code, None), (shift_query(split), None), (to_win, None), (to_tok, None)]
        ins += block_ins(tower, 1, BLOCK[1:], many)
        outs = [((TOKENS, width), F32, True)] * 2 + [((WIN, width), BF16, True)] * 2
        results = launch(
            functools.partial(shifted_back_kernel, split=split, width=width), tower + "_shifted_back",
            n_groups, ins, outs + block_grads(width), backward_scratch(width, split, True),
        )
        grad_middle, grad_near, rim_a, rim_b = results[:4]
        for name, grad in zip(BLOCK[1:], results[4:]):
            grads[tower, 1, name] = grad
        from_below, from_above = exchange(rim_a, rim_b)
        kept = saved[tower, 0]
        ins = [pick(array) for array in (grad_middle, grad_near, from_below, from_above, kept["x_out"])]
        ins += block_ins(tower, 1, ("norm_one",), many) + [(to_tok, None)]
        ins += [pick(kept[name]) for name in plain_saved[:-1]]
        ins += [(plain_code, None), (plain_query(split), None)]
        ins += block_ins(tower, 0, BLOCK, many)
        tail = [gain_out(width), gain_out(width)] + block_grads(width)
        if many:
            ins += [(source, pl.BlockSpec((TOKENS, PIN), lambda g: (0, g)))]
            body, head = enc_plain_back_kernel, [((PIN, D_ENC), grad_type, True)]
        else:
            ins += [(saved["joined"], None), (weights[tower, -1, "joining"], None)]
            body = trunk_plain_back_kernel
            head = [((TOKENS, D_ENC), F32, True)] * 2 + [((width, width), grad_type, True)]
        results = launch(
            functools.partial(body, split=split, width=width), tower + "_plain_back",
            n_groups, ins, head + tail, backward_scratch(width, split, False),
        )
        grads[tower, 1, "norm_one"] = results[len(head)]
        for name, grad in zip(BLOCK, results[len(head) + 1 :]):
            grads[tower, 0, name] = grad
        return results[: len(head)]

    left, right, grads["trunk", -1, "joining"] = backward_pair(
        "trunk", D_TRUNK, TRUNK_SPLIT, 1, grad_out
    )
    stacked = jnp.stack([left, right])
    (grads["enc", -1, "embed"],) = backward_pair(
        "enc", D_ENC, ENC_SPLIT, GROUPS, grouped(stacked)
    )
    return loss_row, grads


def stacked_key(label_key):
    tower, group, layer, name = label_key
    return (tower, layer, name), (group if tower in ("enc", "top") else None)


def unpack(flat_vec):
    found = {}
    for label_key, dims_shape, offset in placed():
        piece = flat_vec[offset : offset + math.prod(dims_shape)].reshape(dims_shape)
        if label_key[3] in ("norm_one", "norm_two", "final", "scale"):
            piece = piece.astype(F32)
        key, group = stacked_key(label_key)
        found.setdefault(key, []).append(piece)
    return {
        key: jnp.stack(pieces) if key[0] in ("enc", "top") else pieces[0]
        for key, pieces in found.items()
    }


def shards(inputs, targets, crop_extent, master, moment_one, moment_two, step_count):
    n_own = master.shape[0]
    n_rows_flat = -(-n_own // 2048) * 16
    padded = jnp.pad(master.astype(jnp.bfloat16), (0, n_rows_flat * 128 - n_own))
    gathered = lax.all_gather(padded.reshape(n_rows_flat, 128), ("dp", "band"), axis=0, tiled=True)
    working = gathered.reshape(-1, n_rows_flat * 128)[:, :n_own].reshape(-1)
    weights = unpack(working)
    extent = crop_extent[0]
    n_rows, n_levels = inputs.shape[1], inputs.shape[2]
    source = inputs[0].transpose(1, 0, 2, 3).reshape(TOKENS, GROUPS * PIN)
    goal = targets[0].transpose(1, 0, 2, 3).reshape(TOKENS, GROUPS * PIN)
    first_lat = lax.axis_index("band") * n_rows
    crop_cells = extent[0].astype(F32) * extent[1].astype(F32) * n_levels
    norm_count = lax.psum(crop_cells, "dp") * (GROUPS * PIN)
    loss_row, grads = compute(
        weights, source, goal, key_codes(extent, first_lat), norm_count.reshape(1, 1), F32
    )
    loss_total = lax.psum(jnp.sum(loss_row), ("dp", "band"))
    pieces = []
    for label_key, dims_shape, offset in placed():
        key, group = stacked_key(label_key)
        piece = grads[key] if group is None else grads[key][group]
        pieces.append(piece.reshape(-1).astype(F32))
    flat_grad = jnp.concatenate(pieces)
    parts = jnp.pad(flat_grad.reshape(-1, n_own), ((0, 0), (0, n_rows_flat * 128 - n_own)))
    grad_shard = lax.psum_scatter(
        parts.reshape(-1, 128), ("dp", "band"), scatter_dimension=0, tiled=True
    ).reshape(-1)[:n_own]
    shard_square = jnp.sum(grad_shard * grad_shard)
    square_total = lax.psum(shard_square, ("dp", "band"))
    grad_norm = jnp.sqrt(square_total)
    factor_clip = jnp.minimum(1.0, CLIP_LEVEL / (grad_norm + 1e-06))
    clipped = grad_shard * factor_clip
    new_one = BETA_ONE * moment_one + (1.0 - BETA_ONE) * clipped
    new_two = BETA_TWO * moment_two + (1.0 - BETA_TWO) * clipped * clipped
    step_value = step_count[0].astype(F32)
    fix_one = 1.0 - jnp.power(BETA_ONE, step_value)
    fix_two = 1.0 - jnp.power(BETA_TWO, step_value)
    update = new_one / fix_one / (jnp.sqrt(new_two / fix_two) + ADAM_EPS) + WEIGHT_DECAY * master
    new_master = master - LEARN_RATE * update
    return (
        new_master,
        new_one,
        new_two,
        new_master.astype(jnp.bfloat16),
        loss_total / norm_count,
        grad_norm,
    )


def solution(mesh):
    in_specs = (
        P("dp", "band", None, None, None),
        P("dp", "band", None, None, None),
        P("dp", None),
        P(("dp", "band")),
        P(("dp", "band")),
        P(("dp", "band")),
        P(),
    )
    out_specs = (
        P(("dp", "band")),
        P(("dp", "band")),
        P(("dp", "band")),
        P(("dp", "band")),
        P(),
        P(),
    )
    return jax.shard_map(shards, mesh=mesh, in_specs=in_specs, out_specs=out_specs, check_vma=False)
```

```python
import functools
import math

import jax
import jax.numpy as jnp
import numpy as np
from jax import lax
from jax.experimental import pallas as pl
from jax.experimental.pallas import tpu as pltpu
from jax.sharding import PartitionSpec as P

D_ENC = 192
HEADS_ENC = 6
D_TRUNK = 384
HEADS_TRUNK = 12
PIN = 128
GROUPS = 2
HEAD_DIM = 32
SCALE = HEAD_DIM ** (-0.5)

NEG_FILL = -1000000000.0
BETA_ONE = 0.5
BETA_TWO = 0.5
LEARN_RATE = 0.01
WEIGHT_DECAY = 0.1
CLIP_LEVEL = 0.07
ADAM_EPS = 1e-08

F32 = jnp.float32
BF16 = jnp.bfloat16
TOKENS = 288
WIN = 144
ENC_SPLIT = ((0, 192, 6),)
TRUNK_SPLIT = ((0, 256, 8), (256, 128, 4))


def block_layout(path_name, group_id, layer_id, n_width):
    prefix = (path_name, group_id, layer_id)
    return [
        (prefix + ("norm_one",), (2, n_width)),
        (prefix + ("qkv",), (n_width, 3 * n_width)),
        (prefix + ("proj",), (n_width, n_width)),
        (prefix + ("norm_two",), (2, n_width)),
        (prefix + ("up",), (n_width, 4 * n_width)),
        (prefix + ("down",), (4 * n_width, n_width)),
    ]


def layout():
    entries = []
    for group_id in range(GROUPS):
        entries.append((("enc", group_id, -1, "embed"), (PIN, D_ENC)))
        for layer_id in range(2):
            entries += block_layout("enc", group_id, layer_id, D_ENC)
        entries.append((("top", group_id, -1, "decode"), (D_TRUNK, D_ENC)))
        entries.append((("top", group_id, -1, "head"), (D_ENC, PIN)))
        entries.append((("top", group_id, -1, "scale"), (PIN,)))
    entries.append((("trunk", 0, -1, "joining"), (GROUPS * D_ENC, D_TRUNK)))
    for layer_id in range(2):
        entries += block_layout("trunk", 0, layer_id, D_TRUNK)
    entries.append((("trunk", 0, -1, "final"), (2, D_TRUNK)))
    return entries


def placed():
    offset = 0
    for label_key, dims_shape in layout():
        yield label_key, dims_shape, offset
        offset += math.prod(dims_shape)


def nn(left, right):
    return jnp.dot(left, right, preferred_element_type=F32)


def nt(left, right):
    return lax.dot_general(left, right, (((1,), (1,)), ((), ())), preferred_element_type=F32)


def tn(left, right):
    return lax.dot_general(left, right, (((0,), (0,)), ((), ())), preferred_element_type=F32)


def unit_rows(values):
    centre = values - jnp.mean(values, -1, keepdims=True)
    inverse = lax.rsqrt(jnp.mean(centre * centre, -1, keepdims=True) + 1e-05)
    return centre * inverse, inverse


def norm_forward(values, gain_ref):
    unit, unused = unit_rows(values)
    return unit * gain_ref[0:1, :] + gain_ref[1:2, :]


def norm_backward(values, gain_ref, grad_normed):
    unit, inverse = unit_rows(values)
    grad_gain = jnp.sum(grad_normed * unit, 0, keepdims=True)
    grad_shift = jnp.sum(grad_normed, 0, keepdims=True)
    grad_unit = grad_normed * gain_ref[0:1, :]
    along = jnp.mean(grad_unit * unit, -1, keepdims=True)
    grad_values = inverse * (grad_unit - jnp.mean(grad_unit, -1, keepdims=True) - unit * along)
    return grad_values, jnp.concatenate([grad_gain, grad_shift], 0)


GELU_A = math.sqrt(2.0 / math.pi)
GELU_B = 0.044715


def gelu(values):
    inner = jnp.tanh(GELU_A * (values + GELU_B * (values * values * values)))
    return values * (0.5 * (1.0 + inner))


def gelu_slope(values):
    square = values * values
    inner = jnp.tanh(GELU_A * (values + GELU_B * (square * values)))
    steep = (1.0 - inner * inner) * (GELU_A + (3.0 * GELU_B * GELU_A) * square)
    return 0.5 * (1.0 + inner) + 0.5 * values * steep


def head_lanes(rows, lanes, head):
    lane = lax.broadcasted_iota(jnp.int32, (rows, lanes), 1)
    return (lane >= HEAD_DIM * head) & (lane < HEAD_DIM * (head + 1))


def columns_of(n_heads, n_query):
    return -(-n_heads * n_query // 128)


def spread_heads(rows_value, n_heads, out_ref):
    n_query, lanes = rows_value.shape
    wide = rows_value.astype(F32)
    for head in range(n_heads):
        kept = jnp.where(head_lanes(n_query, lanes, head), wide, 0.0).astype(BF16)
        out_ref[head * n_query : (head + 1) * n_query, 0:lanes] = kept
    total = 128 * columns_of(n_heads, n_query)
    if total > n_heads * n_query:
        out_ref[n_heads * n_query : total, 0:lanes] = jnp.zeros(
            (total - n_heads * n_query, lanes), BF16
        )


def join_heads(spread_ref, n_heads, n_query, lanes):
    joined = spread_ref[0:n_query, 0:lanes]
    for head in range(1, n_heads):
        part = spread_ref[head * n_query : (head + 1) * n_query, 0:lanes]
        joined = jnp.where(head_lanes(n_query, lanes, head), part, joined)
    return joined


def attend_window(queries, key_rows, value_rows, key_code, query_code, probs_ref, q_scr, o_scr, split):
    n_query = queries.shape[0]
    outs = []
    at = 0
    for lane, lanes, n_heads in split:
        spread_heads(queries[:, lane : lane + lanes], n_heads, q_scr)
        keys = key_rows[:, lane : lane + lanes]
        values = value_rows[:, lane : lane + lanes]
        for tile in range(columns_of(n_heads, n_query)):
            rows = slice(128 * tile, 128 * tile + 128)
            scores = nt(keys, q_scr[rows, 0:lanes]) * SCALE
            code = query_code[0:1, at + 128 * tile : at + 128 * tile + 128]
            scores = jnp.where(key_code == code, scores, NEG_FILL)
            raised = jnp.exp(scores - jnp.max(scores, 0, keepdims=True))
            probs = (raised * (1.0 / jnp.sum(raised, 0, keepdims=True))).astype(BF16)
            probs_ref[:, at + 128 * tile : at + 128 * tile + 128] = probs
            o_scr[rows, 0:lanes] = tn(probs, values)
        outs.append(join_heads(o_scr, n_heads, n_query, lanes))
        at += 128 * columns_of(n_heads, n_query)
    return jnp.concatenate(outs, 1) if len(outs) > 1 else outs[0]


def attend_window_back(
    queries, key_rows, value_rows, grad_rows, key_code, query_code, probs_ref, q_scr, g_scr, o_scr, s_scr, split
):
    n_query = queries.shape[0]
    out_q, out_k, out_v = [], [], []
    at = 0
    for lane, lanes, n_heads in split:
        n_col = columns_of(n_heads, n_query)
        spread_heads(queries[:, lane : lane + lanes], n_heads, q_scr)
        spread_heads(grad_rows[:, lane : lane + lanes], n_heads, g_scr)
        keys = key_rows[:, lane : lane + lanes]
        values = value_rows[:, lane : lane + lanes]
        for tile in range(n_col):
            rows = slice(128 * tile, 128 * tile + 128)
            code = query_code[0:1, at + 128 * tile : at + 128 * tile + 128]
            grad_probs = nt(values, g_scr[rows, 0:lanes])
            probs = probs_ref[:, at + 128 * tile : at + 128 * tile + 128].astype(F32)
            along = jnp.sum(grad_probs * probs, 0, keepdims=True)
            grad_scores = probs * (grad_probs - along)
            grad_scores = jnp.where(key_code == code, grad_scores, 0.0).astype(BF16)
            s_scr[:, rows] = grad_scores
            o_scr[rows, 0:lanes] = tn(grad_scores, keys)
        wide = 128 * n_col
        out_v.append(nn(probs_ref[:, at : at + wide], g_scr[0:wide, 0:lanes]))
        out_k.append(nn(s_scr[:, 0:wide], q_scr[0:wide, 0:lanes]) * SCALE)
        out_q.append(join_heads(o_scr, n_heads, n_query, lanes) * SCALE)
        at += wide
    if len(split) > 1:
        return tuple(jnp.concatenate(parts, 1) for parts in (out_q, out_k, out_v))
    return out_q[0], out_k[0], out_v[0]


def rest_forward(resid_in, mixed, proj, gain_ref, up, down, middle_ref, normed_ref, raised_ref, active_ref):
    middle = resid_in + nn(mixed, proj[...])
    middle_ref[...] = middle
    normed = norm_forward(middle, gain_ref).astype(BF16)
    normed_ref[...] = normed
    width = up.shape[1]
    for start in range(0, width, 256):
        raised_ref[:, start : start + 256] = nn(normed, up[:, start : start + 256])
        for row in range(0, TOKENS, 96):
            piece = raised_ref[row : row + 96, start : start + 256]
            active_ref[row : row + 96, start : start + 256] = gelu(piece).astype(BF16)
    return middle + nn(active_ref[...], down[...])


def rest_backward(
    grad_out, mixed_ref, middle_ref, normed_ref, raised_ref, active_ref, proj, gain_ref, up, down, raised_scr, outs
):
    d_proj, d_gain, d_up, d_down = outs
    grad_low = grad_out.astype(BF16)
    d_down[...] = tn(active_ref[...], grad_low).astype(d_down.dtype)
    width = up.shape[1]
    for start in range(0, width, 256):
        grad_active = nt(grad_low, down[start : start + 256, :])
        for row in range(0, TOKENS, 96):
            slope = gelu_slope(raised_ref[row : row + 96, start : start + 256])
            raised_scr[row : row + 96, start : start + 256] = (
                slope * grad_active[row : row + 96, :]
            ).astype(BF16)
    d_up[...] = tn(normed_ref[...], raised_scr[:, 0:width]).astype(d_up.dtype)
    grad_middle, grad_gain = norm_backward(
        middle_ref[...], gain_ref, nt(raised_scr[:, 0:width], up[...])
    )
    d_gain[...] = grad_gain
    grad_middle = grad_out + grad_middle
    grad_branch = grad_middle.astype(BF16)
    d_proj[...] = tn(mixed_ref[...], grad_branch).astype(d_proj.dtype)
    return grad_middle, nt(grad_branch, proj[...]).astype(BF16)


def plain_attention(qkv_ref, mixed_ref, key_code, query_code, probs_ref, q_scr, o_scr, split, width):
    for win in range(2):
        rows = slice(WIN * win, WIN * (win + 1))
        mixed_ref[rows, :] = attend_window(
            qkv_ref[rows, 0:width],
            qkv_ref[rows, width : 2 * width],
            qkv_ref[rows, 2 * width : 3 * width],
            key_code[rows, :],
            query_code,
            probs_ref.at[win],
            q_scr,
            o_scr,
            split,
        ).astype(BF16)


def shifted_keys(qkv_ref, far_ref, win, width):
    rows = slice(72 * win, 72 * (win + 1))
    keys = jnp.concatenate([qkv_ref[rows, width : 2 * width], far_ref[rows, 0:width]], 0)
    values = jnp.concatenate([qkv_ref[rows, 2 * width :], far_ref[rows, width:]], 0)
    return qkv_ref[rows, 0:width], keys, values


def enc_plain_kernel(
    src, key_code, query_code, to_win, embed, gain_one, qkv, proj, gain_two, up, down, gain_next,
    x_in, normed, packed, probs, mixed, middle, normed_two, raised, active, x_out, sent_a, sent_b,
    q_scr, o_scr, *, split, width,
):
    first = nn(src[...], embed[...])
    plain_body(
        first, key_code, query_code, to_win, gain_one, qkv, proj, gain_two, up, down, gain_next,
        x_in, normed, packed, probs, mixed, middle, normed_two, raised, active, x_out, sent_a, sent_b,
        q_scr, o_scr, split, width,
    )


def trunk_plain_kernel(
    left, right, key_code, query_code, to_win, joining, gain_one, qkv, proj, gain_two, up, down, gain_next,
    joined, x_in, normed, packed, probs, mixed, middle, normed_two, raised, active, x_out, sent_a, sent_b,
    q_scr, o_scr, *, split, width,
):
    joined[...] = jnp.concatenate([left[...], right[...]], 1).astype(BF16)
    first = nn(joined[...], joining[...])
    plain_body(
        first, key_code, query_code, to_win, gain_one, qkv, proj, gain_two, up, down, gain_next,
        x_in, normed, packed, probs, mixed, middle, normed_two, raised, active, x_out, sent_a, sent_b,
        q_scr, o_scr, split, width,
    )


def plain_body(
    first, key_code, query_code, to_win, gain_one, qkv, proj, gain_two, up, down, gain_next,
    x_in, normed, packed, probs, mixed, middle, normed_two, raised, active, x_out, sent_a, sent_b,
    q_scr, o_scr, split, width,
):
    x_in[...] = first
    normed[...] = norm_forward(first, gain_one).astype(BF16)
    packed[...] = nn(normed[...], qkv[...]).astype(BF16)
    plain_attention(packed, mixed, key_code, query_code, probs, q_scr, o_scr, split, width)
    last = rest_forward(
        first, mixed[...], proj, gain_two, up, down, middle, normed_two, raised, active
    )
    x_out[...] = last
    ordered = nn(to_win[...], norm_forward(last, gain_next).astype(BF16)).astype(BF16)
    sent_a[...] = ordered[0:WIN]
    sent_b[...] = ordered[WIN:]


def shifted_kernel(
    x_in, near_a, near_b, far_a, far_b, key_code, query_code, to_tok, qkv, proj, gain_two, up, down,
    packed, packed_far, probs, mixed, middle, normed_two, raised, active, x_out,
    q_scr, o_scr, m_scr, *, split, width,
):
    near = jnp.concatenate([near_a[...], near_b[...]], 0)
    far = jnp.concatenate([far_a[...], far_b[...]], 0)
    packed[...] = nn(near, qkv[...]).astype(BF16)
    packed_far[...] = nn(far, qkv[:, width:]).astype(BF16)
    for win in range(4):
        queries, keys, values = shifted_keys(packed, packed_far, win, width)
        m_scr[72 * win : 72 * (win + 1), 0:width] = attend_window(
            queries, keys, values, key_code[WIN * win : WIN * (win + 1), :],
            query_code.at[win % 2], probs.at[win], q_scr, o_scr, split,
        )
    mixed[...] = nn(to_tok[...], m_scr[:, 0:width].astype(BF16)).astype(BF16)
    x_out[...] = rest_forward(
        x_in[...], mixed[...], proj, gain_two, up, down, middle, normed_two, raised, active
    )


def loss_kernel(
    trunk, goal, key_code, count, final, decode, head, scale,
    grad_trunk, d_final, d_decode, d_head, d_scale, loss,
):
    values = trunk[...]
    low = norm_forward(values, final).astype(BF16)
    valid = key_code[...] + 1.0
    inverse_count = 1.0 / count[0, 0]
    grad_low = None
    total = None
    for group in range(GROUPS):
        raised = nn(low, decode[group])
        active = gelu(raised).astype(BF16)
        predicted = nn(active, head[group])
        log_scale = scale[group : group + 1, :]
        error = predicted - goal[:, PIN * group : PIN * (group + 1)].astype(F32)
        inverse_scale = jnp.exp(-log_scale)
        weighted = jnp.abs(error) * inverse_scale
        part = jnp.sum((weighted + log_scale) * valid, 0, keepdims=True)
        total = part if total is None else total + part
        direction = jnp.where(error > 0.0, 1.0, jnp.where(error < 0.0, -1.0, 0.0))
        grad_pred = (direction * inverse_scale * valid * inverse_count).astype(BF16)
        d_scale[group : group + 1, :] = (
            jnp.sum((1.0 - weighted) * valid, 0, keepdims=True) * inverse_count
        )
        d_head[group] = tn(active, grad_pred).astype(d_head.dtype)
        grad_raised = (gelu_slope(raised) * nt(grad_pred, head[group])).astype(BF16)
        d_decode[group] = tn(low, grad_raised).astype(d_decode.dtype)
        back = nt(grad_raised, decode[group])
        grad_low = back if grad_low is None else grad_low + back
    loss[...] = total
    grad_values, grad_final = norm_backward(values, final, grad_low)
    grad_trunk[...] = grad_values
    d_final[...] = grad_final


def shifted_back_kernel(
    grad_out, near_a, near_b, far_a, far_b, packed, packed_far, probs, mixed, middle, normed_two, raised, active,
    key_code, query_code, to_win, to_tok, qkv, proj, gain_two, up, down,
    grad_middle, grad_near, rim_a, rim_b, d_qkv, d_proj, d_gain_two, d_up, d_down,
    q_scr, g_scr, o_scr, s_scr, raised_scr, near_scr, far_scr, *, split, width,
):
    grad_mid, grad_mixed = rest_backward(
        grad_out[...], mixed, middle, normed_two, raised, active, proj, gain_two, up, down,
        raised_scr, (d_proj, d_gain_two, d_up, d_down),
    )
    grad_middle[...] = grad_mid
    grad_win = nn(to_win[...], grad_mixed).astype(BF16)
    for win in range(4):
        rows = slice(72 * win, 72 * (win + 1))
        queries, keys, values = shifted_keys(packed, packed_far, win, width)
        grad_q, grad_k, grad_v = attend_window_back(
            queries, keys, values, grad_win[rows, :], key_code[WIN * win : WIN * (win + 1), :],
            query_code.at[win % 2], probs.at[win], q_scr, g_scr, o_scr, s_scr, split,
        )
        near_scr[rows, 0:width] = grad_q.astype(BF16)
        near_scr[rows, width : 2 * width] = grad_k[0:72].astype(BF16)
        near_scr[rows, 2 * width : 3 * width] = grad_v[0:72].astype(BF16)
        far_scr[rows, 0:width] = grad_k[72:144].astype(BF16)
        far_scr[rows, width : 2 * width] = grad_v[72:144].astype(BF16)
    near_grad = near_scr[...]
    far_grad = far_scr[...]
    near = jnp.concatenate([near_a[...], near_b[...]], 0)
    far = jnp.concatenate([far_a[...], far_b[...]], 0)
    d_qkv[:, 0:width] = tn(near, near_grad[:, 0:width]).astype(d_qkv.dtype)
    d_qkv[:, width:] = (tn(near, near_grad[:, width:]) + tn(far, far_grad)).astype(d_qkv.dtype)
    rim = nt(far_grad, qkv[:, width:]).astype(BF16)
    rim_a[...] = rim[0:WIN]
    rim_b[...] = rim[WIN:]
    grad_near[...] = nt(nn(to_tok[...], near_grad).astype(BF16), qkv[...])


def plain_back_body(
    grad_middle_next, grad_near, arrived_a, arrived_b, x_out, gain_next, to_tok,
    x_in, normed, packed, probs, mixed, middle, normed_two, raised, active,
    key_code, query_code, gain_one, qkv, proj, gain_two, up, down,
    d_gain_next, d_gain_one, d_qkv, d_proj, d_gain_two, d_up, d_down,
    q_scr, g_scr, o_scr, s_scr, raised_scr, near_scr, split, width,
):
    arrived = jnp.concatenate([arrived_a[...], arrived_b[...]], 0)
    grad_normed = grad_near[...] + nn(to_tok[...], arrived)
    grad_x, grad_gain = norm_backward(x_out[...], gain_next, grad_normed)
    d_gain_next[...] = grad_gain
    grad_mid, grad_mixed = rest_backward(
        grad_middle_next[...] + grad_x, mixed, middle, normed_two, raised, active,
        proj, gain_two, up, down, raised_scr, (d_proj, d_gain_two, d_up, d_down),
    )
    for win in range(2):
        rows = slice(WIN * win, WIN * (win + 1))
        grads = attend_window_back(
            packed[rows, 0:width], packed[rows, width : 2 * width], packed[rows, 2 * width :],
            grad_mixed[rows, :], key_code[rows, :], query_code, probs.at[win],
            q_scr, g_scr, o_scr, s_scr, split,
        )
        for index, grad in enumerate(grads):
            near_scr[rows, width * index : width * (index + 1)] = grad.astype(BF16)
    near_grad = near_scr[...]
    d_qkv[...] = tn(normed[...], near_grad).astype(d_qkv.dtype)
    grad_first, grad_gain = norm_backward(x_in[...], gain_one, nt(near_grad, qkv[...]))
    d_gain_one[...] = grad_gain
    return grad_mid + grad_first


def trunk_plain_back_kernel(
    grad_middle_next, grad_near, arrived_a, arrived_b, x_out, gain_next, to_tok,
    x_in, normed, packed, probs, mixed, middle, normed_two, raised, active,
    key_code, query_code, gain_one, qkv, proj, gain_two, up, down, joined, joining,
    grad_left, grad_right, d_joining,
    d_gain_next, d_gain_one, d_qkv, d_proj, d_gain_two, d_up, d_down,
    q_scr, g_scr, o_scr, s_scr, raised_scr, near_scr, *, split, width,
):
    grad = plain_back_body(
        grad_middle_next, grad_near, arrived_a, arrived_b, x_out, gain_next, to_tok,
        x_in, normed, packed, probs, mixed, middle, normed_two, raised, active,
        key_code, query_code, gain_one, qkv, proj, gain_two, up, down,
        d_gain_next, d_gain_one, d_qkv, d_proj, d_gain_two, d_up, d_down,
        q_scr, g_scr, o_scr, s_scr, raised_scr, near_scr, split, width,
    ).astype(BF16)
    d_joining[...] = tn(joined[...], grad).astype(d_joining.dtype)
    back = nt(grad, joining[...])
    grad_left[...] = back[:, 0:D_ENC]
    grad_right[...] = back[:, D_ENC:]


def enc_plain_back_kernel(
    grad_middle_next, grad_near, arrived_a, arrived_b, x_out, gain_next, to_tok,
    x_in, normed, packed, probs, mixed, middle, normed_two, raised, active,
    key_code, query_code, gain_one, qkv, proj, gain_two, up, down, src,
    d_embed, d_gain_next, d_gain_one, d_qkv, d_proj, d_gain_two, d_up, d_down,
    q_scr, g_scr, o_scr, s_scr, raised_scr, near_scr, *, split, width,
):
    grad = plain_back_body(
        grad_middle_next, grad_near, arrived_a, arrived_b, x_out, gain_next, to_tok,
        x_in, normed, packed, probs, mixed, middle, normed_two, raised, active,
        key_code, query_code, gain_one, qkv, proj, gain_two, up, down,
        d_gain_next, d_gain_one, d_qkv, d_proj, d_gain_two, d_up, d_down,
        q_scr, g_scr, o_scr, s_scr, raised_scr, near_scr, split, width,
    ).astype(BF16)
    d_embed[...] = tn(src[...], grad).astype(d_embed.dtype)


def whole(shape):
    return pl.BlockSpec(shape, lambda g: (0,) * len(shape))


def of_group(shape, group=None):
    if group is None:
        return pl.BlockSpec((None,) + shape, lambda g: (g,) + (0,) * len(shape))
    return pl.BlockSpec((None,) + shape, lambda g: (group,) + (0,) * len(shape))


def launch(body, name, n_groups, ins, outs, scratch, limit=40 << 20):
    in_specs = [whole(array.shape) if spec is None else spec for array, spec in ins]
    out_specs = []
    out_shape = []
    for shape, dtype, grouped in outs:
        if grouped and n_groups > 1:
            out_specs.append(of_group(shape))
            out_shape.append(jax.ShapeDtypeStruct((n_groups,) + shape, dtype))
        else:
            out_specs.append(whole(shape))
            out_shape.append(jax.ShapeDtypeStruct(shape, dtype))
    return pl.pallas_call(
        body,
        grid=(n_groups,),
        in_specs=in_specs,
        out_specs=out_specs,
        out_shape=out_shape,
        scratch_shapes=scratch,
        name=name,
        compiler_params=pltpu.CompilerParams(
            dimension_semantics=("arbitrary",), vmem_limit_bytes=limit
        ),
    )(*[array for array, spec in ins])


def probs_width(split, n_query):
    return 128 * sum(columns_of(n_heads, n_query) for lane, lanes, n_heads in split)


def spread_rows(split, n_query):
    return 128 * max(columns_of(n_heads, n_query) for lane, lanes, n_heads in split)


def spread_lanes(split):
    return max(lanes for lane, lanes, n_heads in split)


def saved_outs(width, split, shifted):
    n_query, n_win = (72, 4) if shifted else (WIN, 2)
    packed = [((TOKENS, 3 * width), BF16, True)]
    if shifted:
        packed.append(((TOKENS, 2 * width), BF16, True))
    else:
        packed = [((TOKENS, width), F32, True), ((TOKENS, width), BF16, True)] + packed
    return packed + [
        ((n_win, WIN, probs_width(split, n_query)), BF16, True),
        ((TOKENS, width), BF16, True),
        ((TOKENS, width), F32, True),
        ((TOKENS, width), BF16, True),
        ((TOKENS, 4 * width), F32, True),
        ((TOKENS, 4 * width), BF16, True),
        ((TOKENS, width), F32, True),
    ]


def spread_scratch(split, n_query, dtype):
    return pltpu.VMEM((spread_rows(split, n_query), spread_lanes(split)), dtype)


def forward_scratch(width, split, shifted):
    n_query = 72 if shifted else WIN
    held = [spread_scratch(split, n_query, BF16), spread_scratch(split, n_query, F32)]
    if shifted:
        held.append(pltpu.VMEM((TOKENS, width), F32))
    return held


def backward_scratch(width, split, shifted):
    n_query = 72 if shifted else WIN
    held = [
        spread_scratch(split, n_query, BF16),
        spread_scratch(split, n_query, BF16),
        spread_scratch(split, n_query, F32),
        pltpu.VMEM((WIN, spread_rows(split, n_query)), BF16),
        pltpu.VMEM((TOKENS, 4 * width), BF16),
        pltpu.VMEM((TOKENS, 3 * width), BF16),
    ]
    if shifted:
        held.append(pltpu.VMEM((TOKENS, 2 * width), BF16))
    return held


def window_order():
    order = []
    for half in range(2):
        for pair in ((1, 2), (3, 0)):
            for level in pair:
                for row in range(3):
                    for col in range(12):
                        order.append(level * 72 + (half * 3 + row) * 12 + col)
    return np.array(order)


def fixed_tables():
    order = window_order()
    to_win = np.zeros((TOKENS, TOKENS), np.float32)
    to_win[np.arange(TOKENS), order] = 1.0
    region = np.zeros((2, 72), np.float32)
    for pair, levels in enumerate(((1, 2), (3, 0))):
        for place in range(72):
            level, col = levels[place // 36], place % 12
            region[pair, place] = 2.0 * (level == 0) + 1.0 * (col < 6)
    return to_win, region


def key_codes(extent, first_lat):
    place = lax.broadcasted_iota(jnp.int32, (TOKENS, 128), 0)
    row, col = (place // 12) % 6, place % 12
    inside = (first_lat + row < extent[0]) & (col < extent[1])
    plain = jnp.where(inside, 0.0, -1.0)
    place = lax.broadcasted_iota(jnp.int32, (2 * TOKENS, 128), 0)
    win, rest = place // WIN, place % WIN
    far, rest = rest // 72, rest % 72
    half, pair = win // 2, win % 2
    second = rest // 36
    row, col = (rest // 12) % 3, rest % 12
    near_row = 3 * half + row
    far_row = jnp.where(half == 0, row - 3, row + 6)
    lat = first_lat + jnp.where(far == 1, far_row, near_row)
    top = (pair == 1) & (second == 1)
    region = jnp.where(top, 2.0, 0.0) + jnp.where(col < 6, 1.0, 0.0)
    inside = (lat >= 0) & (lat < extent[0]) & (col < extent[1])
    return plain, jnp.where(inside, region, -1.0)


def exchange(first, second):
    count = lax.axis_size("band")
    up = [(i, i + 1) for i in range(count - 1)]
    down = [(i + 1, i) for i in range(count - 1)]
    return lax.ppermute(second, "band", up), lax.ppermute(first, "band", down)


SAVED = ("packed", "probs", "mixed", "middle", "normed_two", "raised", "active")


def compute(weights, source, goal, codes, count, grad_type):
    to_win, region = fixed_tables()
    to_tok = jnp.asarray(to_win.T, BF16)
    to_win = jnp.asarray(to_win, BF16)
    plain_code, shift_code = codes
    grads = {}

    def plain_query(split):
        return jnp.zeros((1, probs_width(split, WIN)), F32)

    def shift_query(split):
        parts = []
        for lane, lanes, n_heads in split:
            total = 128 * columns_of(n_heads, 72)
            tiled = np.tile(region, (1, n_heads))
            parts.append(np.pad(tiled, ((0, 0), (0, total - tiled.shape[1]))))
        return jnp.asarray(np.concatenate(parts, 1)[:, None, :], F32)

    def block_ins(tower, layer, names, grouped):
        found = []
        for name in names:
            array = weights[tower, layer, name]
            found.append((array, of_group(array.shape[1:]) if grouped else None))
        return found

    BLOCK = ("norm_one", "qkv", "proj", "norm_two", "up", "down")
    saved = {}
    plain_saved = ("x_in", "normed") + SAVED + ("x_out",)
    shift_saved = ("packed", "packed_far") + SAVED[1:] + ("x_out",)

    def grouped(array):
        return (array, of_group(array.shape[1:]))

    def forward_pair(tower, width, split, n_groups):
        many = n_groups > 1
        pick = grouped if many else (lambda array: (array, None))
        gain_next = block_ins(tower, 1, ("norm_one",), many)
        codes_in = [(plain_code, None), (plain_query(split), None), (to_win, None)]
        sent_outs = [((WIN, width), BF16, True)] * 2
        if many:
            ins = [(source, pl.BlockSpec((TOKENS, PIN), lambda g: (0, g)))] + codes_in
            ins += [grouped(weights[tower, -1, "embed"])]
            body, extra = enc_plain_kernel, []
        else:
            left = saved["enc", 1]["x_out"]
            ins = [(left, of_group(left.shape[1:], 0)), (left, of_group(left.shape[1:], 1))] + codes_in
            ins += [(weights[tower, -1, "joining"], None)]
            body, extra = trunk_plain_kernel, [((TOKENS, 2 * D_ENC), BF16, False)]
        ins += block_ins(tower, 0, BLOCK, many) + gain_next
        results = launch(
            functools.partial(body, split=split, width=width), tower + "_plain", n_groups, ins,
            extra + saved_outs(width, split, False) + sent_outs, forward_scratch(width, split, False),
        )
        if extra:
            saved["joined"] = results[0]
            results = results[1:]
        saved[tower, 0] = dict(zip(plain_saved, results))
        sent = results[-2:]
        far = exchange(*sent)
        ins = [pick(saved[tower, 0]["x_out"])] + [pick(array) for array in (*sent, *far)]
        ins += [(shift_code, None), (shift_query(split), None), (to_tok, None)]
        ins += block_ins(tower, 1, BLOCK[1:], many)
        results = launch(
            functools.partial(shifted_kernel, split=split, width=width), tower + "_shifted", n_groups,
            ins, saved_outs(width, split, True), forward_scratch(width, split, True),
        )
        saved[tower, 1] = dict(zip(shift_saved, results))
        saved[tower, 1]["rows"] = (*sent, *far)

    forward_pair("enc", D_ENC, ENC_SPLIT, GROUPS)
    forward_pair("trunk", D_TRUNK, TRUNK_SPLIT, 1)

    results = launch(
        loss_kernel, "loss", 1,
        [(saved["trunk", 1]["x_out"], None), (goal, None), (plain_code, None),
         (count, pl.BlockSpec(memory_space=pltpu.SMEM)),
         (weights["trunk", -1, "final"], None), (weights["top", -1, "decode"], None),
         (weights["top", -1, "head"], None), (weights["top", -1, "scale"], None)],
        [((TOKENS, D_TRUNK), F32, False), ((2, D_TRUNK), F32, False),
         ((GROUPS, D_TRUNK, D_ENC), grad_type, False), ((GROUPS, D_ENC, PIN), grad_type, False),
         ((GROUPS, PIN), F32, False), ((1, PIN), F32, False)],
        [],
    )
    grad_out, grads["trunk", -1, "final"], grads["top", -1, "decode"] = results[:3]
    grads["top", -1, "head"], grads["top", -1, "scale"], loss_row = results[3:]

    def gain_out(width):
        return ((2, width), F32, True)

    def block_grads(width):
        return [
            ((width, 3 * width), grad_type, True),
            ((width, width), grad_type, True),
            gain_out(width),
            ((width, 4 * width), grad_type, True),
            ((4 * width, width), grad_type, True),
        ]

    def backward_pair(tower, width, split, n_groups, grad_in):
        many = n_groups > 1
        pick = grouped if many else (lambda array: (array, None))
        kept = saved[tower, 1]
        ins = [grad_in] if many else [(grad_in, None)]
        ins += [pick(array) for array in kept["rows"]]
        ins += [pick(kept[name]) for name in shift_saved[:-1]]
        ins += [(shift_code, None), (shift_query(split), None), (to_win, None), (to_tok, None)]
        ins += block_ins(tower, 1, BLOCK[1:], many)
        outs = [((TOKENS, width), F32, True)] * 2 + [((WIN, width), BF16, True)] * 2
        results = launch(
            functools.partial(shifted_back_kernel, split=split, width=width), tower + "_shifted_back",
            n_groups, ins, outs + block_grads(width), backward_scratch(width, split, True),
        )
        grad_middle, grad_near, rim_a, rim_b = results[:4]
        for name, grad in zip(BLOCK[1:], results[4:]):
            grads[tower, 1, name] = grad
        from_below, from_above = exchange(rim_a, rim_b)
        kept = saved[tower, 0]
        ins = [pick(array) for array in (grad_middle, grad_near, from_below, from_above, kept["x_out"])]
        ins += block_ins(tower, 1, ("norm_one",), many) + [(to_tok, None)]
        ins += [pick(kept[name]) for name in plain_saved[:-1]]
        ins += [(plain_code, None), (plain_query(split), None)]
        ins += block_ins(tower, 0, BLOCK, many)
        tail = [gain_out(width), gain_out(width)] + block_grads(width)
        if many:
            ins += [(source, pl.BlockSpec((TOKENS, PIN), lambda g: (0, g)))]
            body, head = enc_plain_back_kernel, [((PIN, D_ENC), grad_type, True)]
        else:
            ins += [(saved["joined"], None), (weights[tower, -1, "joining"], None)]
            body = trunk_plain_back_kernel
            head = [((TOKENS, D_ENC), F32, True)] * 2 + [((width, width), grad_type, True)]
        results = launch(
            functools.partial(body, split=split, width=width), tower + "_plain_back",
            n_groups, ins, head + tail, backward_scratch(width, split, False),
        )
        grads[tower, 1, "norm_one"] = results[len(head)]
        for name, grad in zip(BLOCK, results[len(head) + 1 :]):
            grads[tower, 0, name] = grad
        return results[: len(head)]

    left, right, grads["trunk", -1, "joining"] = backward_pair(
        "trunk", D_TRUNK, TRUNK_SPLIT, 1, grad_out
    )
    stacked = jnp.stack([left, right])
    (grads["enc", -1, "embed"],) = backward_pair(
        "enc", D_ENC, ENC_SPLIT, GROUPS, grouped(stacked)
    )
    return loss_row, grads


def stacked_key(label_key):
    tower, group, layer, name = label_key
    return (tower, layer, name), (group if tower in ("enc", "top") else None)


BLOCK_ELEMENTS = 2048


def share_rows(n_own):
    blocks = -(-(n_own + BLOCK_ELEMENTS - 1) // BLOCK_ELEMENTS) + 1
    return 16 * 3 * (-(-blocks // 3))


def first_row(n_own, device):
    return (n_own * device // BLOCK_ELEMENTS) * 16


def grouped_pieces():
    found = {}
    for label_key, dims_shape, offset in placed():
        key, group = stacked_key(label_key)
        found.setdefault(key, (dims_shape, []))[1].append((group, offset // 128))
    return [(key, places, dims_shape) for key, (dims_shape, places) in found.items()]


def is_gain(key):
    return key[2] in ("norm_one", "norm_two", "final")


def stacked_shape(places, dims_shape):
    if len(dims_shape) == 1:
        return (len(places),) + dims_shape
    return dims_shape if places[0][0] is None else (len(places),) + dims_shape


def turned(values):
    return pltpu.roll(values, 64, 1)


def lower_half(values):
    return lax.broadcasted_iota(jnp.int32, values.shape, 1) < 64


def read_gain(flat, offset, width, out):
    if width % 128 == 0:
        count = width // 128
        for row in range(2):
            for tile in range(count):
                at = offset + row * count + tile
                out[row : row + 1, 128 * tile : 128 * tile + 128] = flat[at : at + 1, :]
        return
    rows = [flat[offset + place : offset + place + 1, :] for place in range(3)]
    out[0:1, 0:128] = rows[0]
    out[0:1, 128:192] = rows[1][:, 0:64]
    out[1:2, 0:128] = jnp.where(lower_half(rows[1]), turned(rows[1]), turned(rows[2]))
    out[1:2, 128:192] = rows[2][:, 64:128]


def read_matrix(flat, offset, shape, out, wide_scr):
    height, width = shape
    step = 64
    if width % 128 == 0:
        count = width // 128

        def body(index, carry):
            row = pl.multiple_of(index * step, step)
            for tile in range(count):
                start = offset + tile + row * count
                piece = flat[pl.ds(start, step, stride=count), :]
                out[pl.ds(row, step), 128 * tile : 128 * tile + 128] = piece.astype(BF16)
            return carry

        lax.fori_loop(0, height // step, body, 0)
        return
    half = width // 128
    period = 2 * half + 1

    def body(index, carry):
        row = pl.multiple_of(index * step, step)
        start = offset + (row // 2) * period
        rows = [flat[pl.ds(start + place, step // 2, stride=period), :] for place in range(period)]
        late = [turned(rows[half + place]) for place in range(half + 1)]
        for tile in range(half + 1):
            odd_rows = late[tile]
            if tile < half:
                odd_rows = jnp.where(lower_half(late[tile]), late[tile], late[tile + 1])
            wide_scr[pl.ds(step * tile, step // 2, stride=2), :] = rows[tile]
            wide_scr[pl.ds(step * tile + 1, step // 2, stride=2), :] = odd_rows
            end = min(128, width - 128 * tile)
            tile_rows = wide_scr[step * tile : step * (tile + 1), 0:end]
            out[pl.ds(row, step), 128 * tile : 128 * tile + end] = tile_rows.astype(BF16)
        return carry

    lax.fori_loop(0, height // step, body, 0)


def write_gain(flat, offset, width, values):
    if width % 128 == 0:
        count = width // 128
        for row in range(2):
            for tile in range(count):
                at = offset + row * count + tile
                flat[at : at + 1, :] = values[row : row + 1, 128 * tile : 128 * tile + 128]
        return
    flat[offset : offset + 1, :] = values[0:1, 0:128]
    first, second = values[1:2, 0:64], values[1:2, 64:192]
    flat[offset + 1 : offset + 2, :] = jnp.concatenate([values[0:1, 128:192], first], 1)
    flat[offset + 2 : offset + 3, :] = second


def write_matrix(flat, offset, shape, source, wide_scr):
    height, width = shape
    step = 64
    if width % 128 == 0:
        count = width // 128

        def body(index, carry):
            row = pl.multiple_of(index * step, step)
            for tile in range(count):
                start = offset + tile + row * count
                piece = source[pl.ds(row, step), 128 * tile : 128 * tile + 128]
                flat[pl.ds(start, step, stride=count), :] = piece.astype(F32)
            return carry

        lax.fori_loop(0, height // step, body, 0)
        return
    half = width // 128
    period = 2 * half + 1

    def body(index, carry):
        row = pl.multiple_of(index * step, step)
        start = offset + (row // 2) * period
        for tile in range(half + 1):
            end = min(128, width - 128 * tile)
            tile_rows = source[pl.ds(row, step), 128 * tile : 128 * tile + end].astype(F32)
            wide_scr[step * tile : step * (tile + 1), 0:end] = tile_rows
        early = [wide_scr[pl.ds(step * tile, step // 2, stride=2), :] for tile in range(half + 1)]
        late = [
            turned(wide_scr[pl.ds(step * tile + 1, step // 2, stride=2), :])
            for tile in range(half + 1)
        ]
        low = lower_half(late[0])
        rows = early[:half] + [jnp.where(low, early[half], late[0])]
        rows += [jnp.where(low, late[tile], late[tile + 1]) for tile in range(half)]
        for place, value in enumerate(rows):
            flat[pl.ds(start + place, step // 2, stride=period), :] = value
        return carry

    lax.fori_loop(0, height // step, body, 0)


def unpack_kernel(shares, *refs, pieces, n_own):
    outs, (flat, wide_scr) = refs[:-2], refs[-2:]
    n_devices, rows, unused = shares.shape
    step = rows // 6

    def place(device, carry):
        start = pl.multiple_of((n_own * device // BLOCK_ELEMENTS) * 16, 16)
        kept = jnp.where(device > 0, flat[pl.ds(start, 16), :], 0.0)
        flat[pl.ds(start, 16), :] = kept + shares[device, 0:16, :].astype(F32)
        flat[pl.ds(start + 16, step - 16), :] = shares[device, 16:step, :].astype(F32)
        for part in range(1, 6):
            at = pl.ds(start + part * step, step)
            flat[at, :] = shares[device, part * step : (part + 1) * step, :].astype(F32)
        return carry

    lax.fori_loop(0, n_devices, place, 0)
    for (key, places, dims_shape), out in zip(pieces, outs):
        for group, offset in places:
            view = out if group is None or len(dims_shape) == 1 else out.at[group]
            if len(dims_shape) == 1:
                view[group : group + 1, :] = flat[offset : offset + 1, :]
            elif is_gain(key):
                read_gain(flat, offset, dims_shape[1], view)
            else:
                read_matrix(flat, offset, dims_shape, view, wide_scr)


def flat_rows(n_own, n_devices):
    return first_row(n_own, n_devices - 1) + share_rows(n_own)


def unpack_weights(gathered, n_own):
    pieces = grouped_pieces()
    n_devices, rows, unused = gathered.shape
    outs = []
    for key, places, dims_shape in pieces:
        small = is_gain(key) or len(dims_shape) == 1
        outs.append(jax.ShapeDtypeStruct(stacked_shape(places, dims_shape), F32 if small else BF16))
    results = pl.pallas_call(
        functools.partial(unpack_kernel, pieces=pieces, n_own=n_own),
        out_shape=outs,
        scratch_shapes=[
            pltpu.VMEM((flat_rows(n_own, n_devices), 128), F32),
            pltpu.VMEM((5 * 64, 128), F32),
        ],
        name="unpack",
        compiler_params=pltpu.CompilerParams(vmem_limit_bytes=56 << 20),
    )(gathered)
    return {piece[0]: result for piece, result in zip(pieces, results)}


def pack_kernel(*refs, pieces, n_own):
    ins, (shares, flat, wide_scr) = refs[:-3], refs[-3:]
    n_devices, rows, unused = shares.shape
    step = rows // 6
    used = sum(len(places) * math.prod(dims_shape) for key, places, dims_shape in pieces) // 128
    flat[used:, :] = jnp.zeros((flat.shape[0] - used, 128), F32)
    for (key, places, dims_shape), source in zip(pieces, ins):
        for group, offset in places:
            view = source if group is None or len(dims_shape) == 1 else source.at[group]
            if len(dims_shape) == 1:
                flat[offset : offset + 1, :] = view[group : group + 1, :]
            elif is_gain(key):
                write_gain(flat, offset, dims_shape[1], view)
            else:
                write_matrix(flat, offset, dims_shape, view, wide_scr)

    def send(device, carry):
        start = pl.multiple_of((n_own * device // BLOCK_ELEMENTS) * 16, 16)
        for part in range(6):
            at = pl.ds(start + part * step, step)
            shares[device, part * step : (part + 1) * step, :] = flat[at, :].astype(BF16)
        return carry

    lax.fori_loop(0, n_devices, send, 0)


def pack_grads(grads, n_own, n_devices):
    pieces = grouped_pieces()
    rows = share_rows(n_own)
    return pl.pallas_call(
        functools.partial(pack_kernel, pieces=pieces, n_own=n_own),
        out_shape=jax.ShapeDtypeStruct((n_devices, rows, 128), BF16),
        scratch_shapes=[
            pltpu.VMEM((flat_rows(n_own, n_devices), 128), F32),
            pltpu.VMEM((5 * 64, 128), F32),
        ],
        name="pack",
        compiler_params=pltpu.CompilerParams(vmem_limit_bytes=56 << 20),
    )(*[grads[key] for key, places, dims_shape in pieces])


def all_sum(values):
    for axis in ("band", "dp"):
        count = lax.axis_size(axis)
        bit = 1
        while bit < count:
            pairs = [(i, i ^ bit) for i in range(count)]
            values = values + lax.ppermute(values, axis, pairs)
            bit *= 2
    return values


def shards(inputs, targets, crop_extent, master, moment_one, moment_two, step_count):
    n_own = master.shape[0]
    n_bands = lax.axis_size("band")
    n_devices = lax.axis_size("dp") * n_bands
    rows = share_rows(n_own)
    device = lax.axis_index("dp") * n_bands + lax.axis_index("band")
    shift = (n_own * device) % BLOCK_ELEMENTS
    extent = crop_extent[0]
    share = lax.dynamic_update_slice(jnp.zeros((rows * 128,), BF16), master.astype(BF16), (shift,))
    share = lax.dynamic_update_slice(share, extent.astype(BF16), ((rows - 1) * 128,))
    gathered = lax.all_gather(share.reshape(rows, 128), ("dp", "band"), axis=0, tiled=False)
    extents = gathered[::n_bands, rows - 1, 0:2].astype(F32)
    weights = unpack_weights(gathered, n_own)
    n_rows, n_levels = inputs.shape[1], inputs.shape[2]
    source = inputs[0].transpose(1, 0, 2, 3).reshape(TOKENS, GROUPS * PIN)
    goal = targets[0].transpose(1, 0, 2, 3).reshape(TOKENS, GROUPS * PIN)
    first_lat = lax.axis_index("band") * n_rows
    norm_count = jnp.sum(extents[:, 0] * extents[:, 1]) * (n_levels * GROUPS * PIN)
    loss_row, grads = compute(
        weights, source, goal, key_codes(extent, first_lat), norm_count.reshape(1, 1), BF16
    )
    packed = pack_grads(grads, n_own, n_devices)
    owned = lax.psum_scatter(packed, ("dp", "band"), scatter_dimension=0, tiled=False)
    grad_shard = lax.dynamic_slice(owned.reshape(-1), (shift,), (n_own,)).astype(F32)
    shard_square = jnp.sum(grad_shard * grad_shard)
    lanes = lax.broadcasted_iota(jnp.int32, (8, 128), 1)
    both = jnp.where(lanes < 64, shard_square, jnp.sum(loss_row))
    both = all_sum(both)
    grad_norm = jnp.sqrt(both[0, 0])
    loss_total = both[0, 64]
    factor_clip = jnp.minimum(1.0, CLIP_LEVEL / (grad_norm + 1e-06))
    clipped = grad_shard * factor_clip
    new_one = BETA_ONE * moment_one + (1.0 - BETA_ONE) * clipped
    new_two = BETA_TWO * moment_two + (1.0 - BETA_TWO) * clipped * clipped
    step_value = step_count[0].astype(F32)
    fix_one = 1.0 - jnp.power(BETA_ONE, step_value)
    fix_two = 1.0 - jnp.power(BETA_TWO, step_value)
    update = new_one / fix_one / (jnp.sqrt(new_two / fix_two) + ADAM_EPS) + WEIGHT_DECAY * master
    new_master = master - LEARN_RATE * update
    return (
        new_master,
        new_one,
        new_two,
        new_master.astype(BF16),
        loss_total / norm_count,
        grad_norm,
    )


def solution(mesh):
    in_specs = (
        P("dp", "band", None, None, None),
        P("dp", "band", None, None, None),
        P("dp", None),
        P(("dp", "band")),
        P(("dp", "band")),
        P(("dp", "band")),
        P(),
    )
    out_specs = (
        P(("dp", "band")),
        P(("dp", "band")),
        P(("dp", "band")),
        P(("dp", "band")),
        P(),
        P(),
    )
    return jax.shard_map(shards, mesh=mesh, in_specs=in_specs, out_specs=out_specs, check_vma=False)
```

```python
import functools
import math

import jax
import jax.numpy as jnp
import numpy as np
from jax import lax
from jax.experimental import pallas as pl
from jax.experimental.pallas import tpu as pltpu
from jax.sharding import PartitionSpec as P

D_ENC = 192
HEADS_ENC = 6
D_TRUNK = 384
HEADS_TRUNK = 12
PIN = 128
GROUPS = 2
HEAD_DIM = 32
SCALE = HEAD_DIM ** (-0.5)

NEG_FILL = -1000000000.0
BETA_ONE = 0.5
BETA_TWO = 0.5
LEARN_RATE = 0.01
WEIGHT_DECAY = 0.1
CLIP_LEVEL = 0.07
ADAM_EPS = 1e-08

F32 = jnp.float32
BF16 = jnp.bfloat16
TOKENS = 288
WIN = 144
ENC_SPLIT = ((0, 192, 6),)
TRUNK_SPLIT = ((0, 256, 8), (256, 128, 4))


def block_layout(path_name, group_id, layer_id, n_width):
    prefix = (path_name, group_id, layer_id)
    return [
        (prefix + ("norm_one",), (2, n_width)),
        (prefix + ("qkv",), (n_width, 3 * n_width)),
        (prefix + ("proj",), (n_width, n_width)),
        (prefix + ("norm_two",), (2, n_width)),
        (prefix + ("up",), (n_width, 4 * n_width)),
        (prefix + ("down",), (4 * n_width, n_width)),
    ]


def layout():
    entries = []
    for group_id in range(GROUPS):
        entries.append((("enc", group_id, -1, "embed"), (PIN, D_ENC)))
        for layer_id in range(2):
            entries += block_layout("enc", group_id, layer_id, D_ENC)
        entries.append((("top", group_id, -1, "decode"), (D_TRUNK, D_ENC)))
        entries.append((("top", group_id, -1, "head"), (D_ENC, PIN)))
        entries.append((("top", group_id, -1, "scale"), (PIN,)))
    entries.append((("trunk", 0, -1, "joining"), (GROUPS * D_ENC, D_TRUNK)))
    for layer_id in range(2):
        entries += block_layout("trunk", 0, layer_id, D_TRUNK)
    entries.append((("trunk", 0, -1, "final"), (2, D_TRUNK)))
    return entries


def placed():
    offset = 0
    for label_key, dims_shape in layout():
        yield label_key, dims_shape, offset
        offset += math.prod(dims_shape)


def nn(left, right):
    return jnp.dot(left, right, preferred_element_type=F32)


def nt(left, right):
    return lax.dot_general(left, right, (((1,), (1,)), ((), ())), preferred_element_type=F32)


def tn(left, right):
    return lax.dot_general(left, right, (((0,), (0,)), ((), ())), preferred_element_type=F32)


def unit_rows(values):
    centre = values - jnp.mean(values, -1, keepdims=True)
    inverse = lax.rsqrt(jnp.mean(centre * centre, -1, keepdims=True) + 1e-05)
    return centre * inverse, inverse


def norm_forward(values, gain_ref):
    unit, unused = unit_rows(values)
    return unit * gain_ref[0:1, :] + gain_ref[1:2, :]


def norm_backward(values, gain_ref, grad_normed):
    unit, inverse = unit_rows(values)
    grad_gain = jnp.sum(grad_normed * unit, 0, keepdims=True)
    grad_shift = jnp.sum(grad_normed, 0, keepdims=True)
    grad_unit = grad_normed * gain_ref[0:1, :]
    along = jnp.mean(grad_unit * unit, -1, keepdims=True)
    grad_values = inverse * (grad_unit - jnp.mean(grad_unit, -1, keepdims=True) - unit * along)
    return grad_values, jnp.concatenate([grad_gain, grad_shift], 0)


GELU_A = math.sqrt(2.0 / math.pi)
GELU_B = 0.044715


def gelu(values):
    inner = jnp.tanh(GELU_A * (values + GELU_B * (values * values * values)))
    return values * (0.5 * (1.0 + inner))


def gelu_slope(values):
    square = values * values
    inner = jnp.tanh(GELU_A * (values + GELU_B * (square * values)))
    steep = (1.0 - inner * inner) * (GELU_A + (3.0 * GELU_B * GELU_A) * square)
    return 0.5 * (1.0 + inner) + 0.5 * values * steep


def head_lanes(rows, lanes, head):
    lane = lax.broadcasted_iota(jnp.int32, (rows, lanes), 1)
    return (lane >= HEAD_DIM * head) & (lane < HEAD_DIM * (head + 1))


def columns_of(n_heads, n_query):
    return -(-n_heads * n_query // 128)


def spread_heads(rows_value, n_heads, out_ref):
    n_query, lanes = rows_value.shape
    wide = rows_value.astype(F32)
    for head in range(n_heads):
        kept = jnp.where(head_lanes(n_query, lanes, head), wide, 0.0).astype(BF16)
        out_ref[head * n_query : (head + 1) * n_query, 0:lanes] = kept
    total = 128 * columns_of(n_heads, n_query)
    if total > n_heads * n_query:
        out_ref[n_heads * n_query : total, 0:lanes] = jnp.zeros(
            (total - n_heads * n_query, lanes), BF16
        )


def join_heads(spread_ref, n_heads, n_query, lanes):
    joined = spread_ref[0:n_query, 0:lanes]
    for head in range(1, n_heads):
        part = spread_ref[head * n_query : (head + 1) * n_query, 0:lanes]
        joined = jnp.where(head_lanes(n_query, lanes, head), part, joined)
    return joined


def attend_window(queries, key_rows, value_rows, key_code, query_code, probs_ref, q_scr, o_scr, split):
    n_query = queries.shape[0]
    outs = []
    at = 0
    for lane, lanes, n_heads in split:
        spread_heads(queries[:, lane : lane + lanes], n_heads, q_scr)
        keys = key_rows[:, lane : lane + lanes]
        values = value_rows[:, lane : lane + lanes]
        for tile in range(columns_of(n_heads, n_query)):
            rows = slice(128 * tile, 128 * tile + 128)
            scores = nt(keys, q_scr[rows, 0:lanes]) * SCALE
            code = query_code[0:1, at + 128 * tile : at + 128 * tile + 128]
            scores = jnp.where(key_code == code, scores, NEG_FILL)
            raised = jnp.exp(scores - jnp.max(scores, 0, keepdims=True))
            probs = (raised * (1.0 / jnp.sum(raised, 0, keepdims=True))).astype(BF16)
            probs_ref[:, at + 128 * tile : at + 128 * tile + 128] = probs
            o_scr[rows, 0:lanes] = tn(probs, values)
        outs.append(join_heads(o_scr, n_heads, n_query, lanes))
        at += 128 * columns_of(n_heads, n_query)
    return jnp.concatenate(outs, 1) if len(outs) > 1 else outs[0]


def attend_window_back(
    queries, key_rows, value_rows, grad_rows, key_code, query_code, probs_ref, q_scr, g_scr, o_scr, s_scr, split
):
    n_query = queries.shape[0]
    out_q, out_k, out_v = [], [], []
    at = 0
    for lane, lanes, n_heads in split:
        n_col = columns_of(n_heads, n_query)
        spread_heads(queries[:, lane : lane + lanes], n_heads, q_scr)
        spread_heads(grad_rows[:, lane : lane + lanes], n_heads, g_scr)
        keys = key_rows[:, lane : lane + lanes]
        values = value_rows[:, lane : lane + lanes]
        for tile in range(n_col):
            rows = slice(128 * tile, 128 * tile + 128)
            code = query_code[0:1, at + 128 * tile : at + 128 * tile + 128]
            grad_probs = nt(values, g_scr[rows, 0:lanes])
            probs = probs_ref[:, at + 128 * tile : at + 128 * tile + 128].astype(F32)
            along = jnp.sum(grad_probs * probs, 0, keepdims=True)
            grad_scores = probs * (grad_probs - along)
            grad_scores = jnp.where(key_code == code, grad_scores, 0.0).astype(BF16)
            s_scr[:, rows] = grad_scores
            o_scr[rows, 0:lanes] = tn(grad_scores, keys)
        wide = 128 * n_col
        out_v.append(nn(probs_ref[:, at : at + wide], g_scr[0:wide, 0:lanes]))
        out_k.append(nn(s_scr[:, 0:wide], q_scr[0:wide, 0:lanes]) * SCALE)
        out_q.append(join_heads(o_scr, n_heads, n_query, lanes) * SCALE)
        at += wide
    if len(split) > 1:
        return tuple(jnp.concatenate(parts, 1) for parts in (out_q, out_k, out_v))
    return out_q[0], out_k[0], out_v[0]


def rest_forward(resid_in, mixed, proj, gain_ref, up, down, middle_ref, normed_ref, raised_ref, active_ref):
    middle = resid_in + nn(mixed, proj[...])
    middle_ref[...] = middle
    normed = norm_forward(middle, gain_ref).astype(BF16)
    normed_ref[...] = normed
    width = up.shape[1]
    for start in range(0, width, 256):
        raised_ref[:, start : start + 256] = nn(normed, up[:, start : start + 256])
        for row in range(0, TOKENS, 96):
            piece = raised_ref[row : row + 96, start : start + 256]
            active_ref[row : row + 96, start : start + 256] = gelu(piece).astype(BF16)
    return middle + nn(active_ref[...], down[...])


def rest_backward(
    grad_out, mixed_ref, middle_ref, normed_ref, raised_ref, active_ref, proj, gain_ref, up, down, raised_scr, outs
):
    d_proj, d_gain, d_up, d_down = outs
    grad_low = grad_out.astype(BF16)
    d_down[...] = tn(active_ref[...], grad_low).astype(d_down.dtype)
    width = up.shape[1]
    for start in range(0, width, 256):
        grad_active = nt(grad_low, down[start : start + 256, :])
        for row in range(0, TOKENS, 96):
            slope = gelu_slope(raised_ref[row : row + 96, start : start + 256])
            raised_scr[row : row + 96, start : start + 256] = (
                slope * grad_active[row : row + 96, :]
            ).astype(BF16)
    d_up[...] = tn(normed_ref[...], raised_scr[:, 0:width]).astype(d_up.dtype)
    grad_middle, grad_gain = norm_backward(
        middle_ref[...], gain_ref, nt(raised_scr[:, 0:width], up[...])
    )
    d_gain[...] = grad_gain
    grad_middle = grad_out + grad_middle
    grad_branch = grad_middle.astype(BF16)
    d_proj[...] = tn(mixed_ref[...], grad_branch).astype(d_proj.dtype)
    return grad_middle, nt(grad_branch, proj[...]).astype(BF16)


def plain_attention(qkv_ref, mixed_ref, key_code, query_code, probs_ref, q_scr, o_scr, split, width):
    for win in range(2):
        rows = slice(WIN * win, WIN * (win + 1))
        mixed_ref[rows, :] = attend_window(
            qkv_ref[rows, 0:width],
            qkv_ref[rows, width : 2 * width],
            qkv_ref[rows, 2 * width : 3 * width],
            key_code[rows, :],
            query_code,
            probs_ref.at[win],
            q_scr,
            o_scr,
            split,
        ).astype(BF16)


def shifted_keys(qkv_ref, far_ref, win, width):
    rows = slice(72 * win, 72 * (win + 1))
    keys = jnp.concatenate([qkv_ref[rows, width : 2 * width], far_ref[rows, 0:width]], 0)
    values = jnp.concatenate([qkv_ref[rows, 2 * width :], far_ref[rows, width:]], 0)
    return qkv_ref[rows, 0:width], keys, values


def enc_plain_kernel(
    src, key_code, query_code, to_win, embed, gain_one, qkv, proj, gain_two, up, down, gain_next,
    x_in, normed, packed, probs, mixed, middle, normed_two, raised, active, x_out, sent_a, sent_b,
    q_scr, o_scr, *, split, width,
):
    first = nn(src[...], embed[...])
    plain_body(
        first, key_code, query_code, to_win, gain_one, qkv, proj, gain_two, up, down, gain_next,
        x_in, normed, packed, probs, mixed, middle, normed_two, raised, active, x_out, sent_a, sent_b,
        q_scr, o_scr, split, width,
    )


def trunk_plain_kernel(
    left, right, key_code, query_code, to_win, joining, gain_one, qkv, proj, gain_two, up, down, gain_next,
    joined, x_in, normed, packed, probs, mixed, middle, normed_two, raised, active, x_out, sent_a, sent_b,
    q_scr, o_scr, *, split, width,
):
    joined[...] = jnp.concatenate([left[...], right[...]], 1).astype(BF16)
    first = nn(joined[...], joining[...])
    plain_body(
        first, key_code, query_code, to_win, gain_one, qkv, proj, gain_two, up, down, gain_next,
        x_in, normed, packed, probs, mixed, middle, normed_two, raised, active, x_out, sent_a, sent_b,
        q_scr, o_scr, split, width,
    )


def plain_body(
    first, key_code, query_code, to_win, gain_one, qkv, proj, gain_two, up, down, gain_next,
    x_in, normed, packed, probs, mixed, middle, normed_two, raised, active, x_out, sent_a, sent_b,
    q_scr, o_scr, split, width,
):
    x_in[...] = first
    normed[...] = norm_forward(first, gain_one).astype(BF16)
    packed[...] = nn(normed[...], qkv[...]).astype(BF16)
    plain_attention(packed, mixed, key_code, query_code, probs, q_scr, o_scr, split, width)
    last = rest_forward(
        first, mixed[...], proj, gain_two, up, down, middle, normed_two, raised, active
    )
    x_out[...] = last
    ordered = nn(to_win[...], norm_forward(last, gain_next).astype(BF16)).astype(BF16)
    sent_a[...] = ordered[0:WIN]
    sent_b[...] = ordered[WIN:]


def shifted_kernel(
    x_in, near_a, near_b, far_a, far_b, key_code, query_code, to_tok, qkv, proj, gain_two, up, down,
    packed, packed_far, probs, mixed, middle, normed_two, raised, active, x_out,
    q_scr, o_scr, m_scr, *, split, width,
):
    near = jnp.concatenate([near_a[...], near_b[...]], 0)
    far = jnp.concatenate([far_a[...], far_b[...]], 0)
    packed[...] = nn(near, qkv[...]).astype(BF16)
    packed_far[...] = nn(far, qkv[:, width:]).astype(BF16)
    for win in range(4):
        queries, keys, values = shifted_keys(packed, packed_far, win, width)
        m_scr[72 * win : 72 * (win + 1), 0:width] = attend_window(
            queries, keys, values, key_code[WIN * win : WIN * (win + 1), :],
            query_code.at[win % 2], probs.at[win], q_scr, o_scr, split,
        )
    mixed[...] = nn(to_tok[...], m_scr[:, 0:width].astype(BF16)).astype(BF16)
    x_out[...] = rest_forward(
        x_in[...], mixed[...], proj, gain_two, up, down, middle, normed_two, raised, active
    )


def loss_kernel(
    trunk, goal, key_code, count, final, decode, head, scale,
    grad_trunk, d_final, d_decode, d_head, d_scale, loss,
):
    values = trunk[...]
    low = norm_forward(values, final).astype(BF16)
    valid = key_code[...] + 1.0
    inverse_count = 1.0 / count[0, 0]
    grad_low = None
    total = None
    for group in range(GROUPS):
        raised = nn(low, decode[group])
        active = gelu(raised).astype(BF16)
        predicted = nn(active, head[group])
        log_scale = scale[group : group + 1, :]
        error = predicted - goal[:, PIN * group : PIN * (group + 1)].astype(F32)
        inverse_scale = jnp.exp(-log_scale)
        weighted = jnp.abs(error) * inverse_scale
        part = jnp.sum((weighted + log_scale) * valid, 0, keepdims=True)
        total = part if total is None else total + part
        direction = jnp.where(error > 0.0, 1.0, jnp.where(error < 0.0, -1.0, 0.0))
        grad_pred = (direction * inverse_scale * valid * inverse_count).astype(BF16)
        d_scale[group : group + 1, :] = (
            jnp.sum((1.0 - weighted) * valid, 0, keepdims=True) * inverse_count
        )
        d_head[group] = tn(active, grad_pred).astype(d_head.dtype)
        grad_raised = (gelu_slope(raised) * nt(grad_pred, head[group])).astype(BF16)
        d_decode[group] = tn(low, grad_raised).astype(d_decode.dtype)
        back = nt(grad_raised, decode[group])
        grad_low = back if grad_low is None else grad_low + back
    loss[...] = total
    grad_values, grad_final = norm_backward(values, final, grad_low)
    grad_trunk[...] = grad_values
    d_final[...] = grad_final


def shifted_back_kernel(
    grad_out, near_a, near_b, far_a, far_b, packed, packed_far, probs, mixed, middle, normed_two, raised, active,
    key_code, query_code, to_win, to_tok, qkv, proj, gain_two, up, down,
    grad_middle, grad_near, rim_a, rim_b, d_qkv, d_proj, d_gain_two, d_up, d_down,
    q_scr, g_scr, o_scr, s_scr, raised_scr, near_scr, far_scr, *, split, width,
):
    grad_mid, grad_mixed = rest_backward(
        grad_out[...], mixed, middle, normed_two, raised, active, proj, gain_two, up, down,
        raised_scr, (d_proj, d_gain_two, d_up, d_down),
    )
    grad_middle[...] = grad_mid
    grad_win = nn(to_win[...], grad_mixed).astype(BF16)
    for win in range(4):
        rows = slice(72 * win, 72 * (win + 1))
        queries, keys, values = shifted_keys(packed, packed_far, win, width)
        grad_q, grad_k, grad_v = attend_window_back(
            queries, keys, values, grad_win[rows, :], key_code[WIN * win : WIN * (win + 1), :],
            query_code.at[win % 2], probs.at[win], q_scr, g_scr, o_scr, s_scr, split,
        )
        near_scr[rows, 0:width] = grad_q.astype(BF16)
        near_scr[rows, width : 2 * width] = grad_k[0:72].astype(BF16)
        near_scr[rows, 2 * width : 3 * width] = grad_v[0:72].astype(BF16)
        far_scr[rows, 0:width] = grad_k[72:144].astype(BF16)
        far_scr[rows, width : 2 * width] = grad_v[72:144].astype(BF16)
    near_grad = near_scr[...]
    far_grad = far_scr[...]
    near = jnp.concatenate([near_a[...], near_b[...]], 0)
    far = jnp.concatenate([far_a[...], far_b[...]], 0)
    d_qkv[:, 0:width] = tn(near, near_grad[:, 0:width]).astype(d_qkv.dtype)
    d_qkv[:, width:] = (tn(near, near_grad[:, width:]) + tn(far, far_grad)).astype(d_qkv.dtype)
    rim = nt(far_grad, qkv[:, width:]).astype(BF16)
    rim_a[...] = rim[0:WIN]
    rim_b[...] = rim[WIN:]
    grad_near[...] = nt(nn(to_tok[...], near_grad).astype(BF16), qkv[...])


def plain_back_body(
    grad_middle_next, grad_near, arrived_a, arrived_b, x_out, gain_next, to_tok,
    x_in, normed, packed, probs, mixed, middle, normed_two, raised, active,
    key_code, query_code, gain_one, qkv, proj, gain_two, up, down,
    d_gain_next, d_gain_one, d_qkv, d_proj, d_gain_two, d_up, d_down,
    q_scr, g_scr, o_scr, s_scr, raised_scr, near_scr, split, width,
):
    arrived = jnp.concatenate([arrived_a[...], arrived_b[...]], 0)
    grad_normed = grad_near[...] + nn(to_tok[...], arrived)
    grad_x, grad_gain = norm_backward(x_out[...], gain_next, grad_normed)
    d_gain_next[...] = grad_gain
    grad_mid, grad_mixed = rest_backward(
        grad_middle_next[...] + grad_x, mixed, middle, normed_two, raised, active,
        proj, gain_two, up, down, raised_scr, (d_proj, d_gain_two, d_up, d_down),
    )
    for win in range(2):
        rows = slice(WIN * win, WIN * (win + 1))
        grads = attend_window_back(
            packed[rows, 0:width], packed[rows, width : 2 * width], packed[rows, 2 * width :],
            grad_mixed[rows, :], key_code[rows, :], query_code, probs.at[win],
            q_scr, g_scr, o_scr, s_scr, split,
        )
        for index, grad in enumerate(grads):
            near_scr[rows, width * index : width * (index + 1)] = grad.astype(BF16)
    near_grad = near_scr[...]
    d_qkv[...] = tn(normed[...], near_grad).astype(d_qkv.dtype)
    grad_first, grad_gain = norm_backward(x_in[...], gain_one, nt(near_grad, qkv[...]))
    d_gain_one[...] = grad_gain
    return grad_mid + grad_first


def trunk_plain_back_kernel(
    grad_middle_next, grad_near, arrived_a, arrived_b, x_out, gain_next, to_tok,
    x_in, normed, packed, probs, mixed, middle, normed_two, raised, active,
    key_code, query_code, gain_one, qkv, proj, gain_two, up, down, joined, joining,
    grad_left, grad_right, d_joining,
    d_gain_next, d_gain_one, d_qkv, d_proj, d_gain_two, d_up, d_down,
    q_scr, g_scr, o_scr, s_scr, raised_scr, near_scr, *, split, width,
):
    grad = plain_back_body(
        grad_middle_next, grad_near, arrived_a, arrived_b, x_out, gain_next, to_tok,
        x_in, normed, packed, probs, mixed, middle, normed_two, raised, active,
        key_code, query_code, gain_one, qkv, proj, gain_two, up, down,
        d_gain_next, d_gain_one, d_qkv, d_proj, d_gain_two, d_up, d_down,
        q_scr, g_scr, o_scr, s_scr, raised_scr, near_scr, split, width,
    ).astype(BF16)
    d_joining[...] = tn(joined[...], grad).astype(d_joining.dtype)
    back = nt(grad, joining[...])
    grad_left[...] = back[:, 0:D_ENC]
    grad_right[...] = back[:, D_ENC:]


def enc_plain_back_kernel(
    grad_middle_next, grad_near, arrived_a, arrived_b, x_out, gain_next, to_tok,
    x_in, normed, packed, probs, mixed, middle, normed_two, raised, active,
    key_code, query_code, gain_one, qkv, proj, gain_two, up, down, src,
    d_embed, d_gain_next, d_gain_one, d_qkv, d_proj, d_gain_two, d_up, d_down,
    q_scr, g_scr, o_scr, s_scr, raised_scr, near_scr, *, split, width,
):
    grad = plain_back_body(
        grad_middle_next, grad_near, arrived_a, arrived_b, x_out, gain_next, to_tok,
        x_in, normed, packed, probs, mixed, middle, normed_two, raised, active,
        key_code, query_code, gain_one, qkv, proj, gain_two, up, down,
        d_gain_next, d_gain_one, d_qkv, d_proj, d_gain_two, d_up, d_down,
        q_scr, g_scr, o_scr, s_scr, raised_scr, near_scr, split, width,
    ).astype(BF16)
    d_embed[...] = tn(src[...], grad).astype(d_embed.dtype)


OUT = pltpu.HBM


def held(array):
    return array if array.size == 1 else pltpu.with_memory_space_constraint(array, pltpu.HBM)


def whole(shape):
    return pl.BlockSpec(shape, lambda g: (0,) * len(shape))


def of_group(shape, group=None):
    if group is None:
        return pl.BlockSpec((None,) + shape, lambda g: (g,) + (0,) * len(shape))
    return pl.BlockSpec((None,) + shape, lambda g: (group,) + (0,) * len(shape))


def launch(body, name, n_groups, ins, outs, scratch, limit=40 << 20):
    in_specs = [whole(array.shape) if spec is None else spec for array, spec in ins]
    out_specs = []
    out_shape = []
    for shape, dtype, grouped in outs:
        if grouped and n_groups > 1:
            out_specs.append(of_group(shape))
            out_shape.append(OUT((n_groups,) + shape, dtype))
        else:
            out_specs.append(whole(shape))
            out_shape.append(OUT(shape, dtype))
    return pl.pallas_call(
        body,
        grid=(n_groups,),
        in_specs=in_specs,
        out_specs=out_specs,
        out_shape=out_shape,
        scratch_shapes=scratch,
        name=name,
        compiler_params=pltpu.CompilerParams(
            dimension_semantics=("arbitrary",), vmem_limit_bytes=limit
        ),
    )(*[held(array) for array, spec in ins])


def probs_width(split, n_query):
    return 128 * sum(columns_of(n_heads, n_query) for lane, lanes, n_heads in split)


def spread_rows(split, n_query):
    return 128 * max(columns_of(n_heads, n_query) for lane, lanes, n_heads in split)


def spread_lanes(split):
    return max(lanes for lane, lanes, n_heads in split)


def saved_outs(width, split, shifted):
    n_query, n_win = (72, 4) if shifted else (WIN, 2)
    packed = [((TOKENS, 3 * width), BF16, True)]
    if shifted:
        packed.append(((TOKENS, 2 * width), BF16, True))
    else:
        packed = [((TOKENS, width), F32, True), ((TOKENS, width), BF16, True)] + packed
    return packed + [
        ((n_win, WIN, probs_width(split, n_query)), BF16, True),
        ((TOKENS, width), BF16, True),
        ((TOKENS, width), F32, True),
        ((TOKENS, width), BF16, True),
        ((TOKENS, 4 * width), F32, True),
        ((TOKENS, 4 * width), BF16, True),
        ((TOKENS, width), F32, True),
    ]


def spread_scratch(split, n_query, dtype):
    return pltpu.VMEM((spread_rows(split, n_query), spread_lanes(split)), dtype)


def forward_scratch(width, split, shifted):
    n_query = 72 if shifted else WIN
    held = [spread_scratch(split, n_query, BF16), spread_scratch(split, n_query, F32)]
    if shifted:
        held.append(pltpu.VMEM((TOKENS, width), F32))
    return held


def backward_scratch(width, split, shifted):
    n_query = 72 if shifted else WIN
    held = [
        spread_scratch(split, n_query, BF16),
        spread_scratch(split, n_query, BF16),
        spread_scratch(split, n_query, F32),
        pltpu.VMEM((WIN, spread_rows(split, n_query)), BF16),
        pltpu.VMEM((TOKENS, 4 * width), BF16),
        pltpu.VMEM((TOKENS, 3 * width), BF16),
    ]
    if shifted:
        held.append(pltpu.VMEM((TOKENS, 2 * width), BF16))
    return held


def window_order():
    order = []
    for half in range(2):
        for pair in ((1, 2), (3, 0)):
            for level in pair:
                for row in range(3):
                    for col in range(12):
                        order.append(level * 72 + (half * 3 + row) * 12 + col)
    return np.array(order)


def fixed_tables():
    order = window_order()
    to_win = np.zeros((TOKENS, TOKENS), np.float32)
    to_win[np.arange(TOKENS), order] = 1.0
    region = np.zeros((2, 72), np.float32)
    for pair, levels in enumerate(((1, 2), (3, 0))):
        for place in range(72):
            level, col = levels[place // 36], place % 12
            region[pair, place] = 2.0 * (level == 0) + 1.0 * (col < 6)
    return to_win, region


def key_codes(extent, first_lat):
    place = lax.broadcasted_iota(jnp.int32, (TOKENS, 128), 0)
    row, col = (place // 12) % 6, place % 12
    inside = (first_lat + row < extent[0]) & (col < extent[1])
    plain = jnp.where(inside, 0.0, -1.0)
    place = lax.broadcasted_iota(jnp.int32, (2 * TOKENS, 128), 0)
    win, rest = place // WIN, place % WIN
    far, rest = rest // 72, rest % 72
    half, pair = win // 2, win % 2
    second = rest // 36
    row, col = (rest // 12) % 3, rest % 12
    near_row = 3 * half + row
    far_row = jnp.where(half == 0, row - 3, row + 6)
    lat = first_lat + jnp.where(far == 1, far_row, near_row)
    top = (pair == 1) & (second == 1)
    region = jnp.where(top, 2.0, 0.0) + jnp.where(col < 6, 1.0, 0.0)
    inside = (lat >= 0) & (lat < extent[0]) & (col < extent[1])
    return plain, jnp.where(inside, region, -1.0)


def exchange(first, second):
    count = lax.axis_size("band")
    up = [(i, i + 1) for i in range(count - 1)]
    down = [(i + 1, i) for i in range(count - 1)]
    return lax.ppermute(second, "band", up), lax.ppermute(first, "band", down)


SAVED = ("packed", "probs", "mixed", "middle", "normed_two", "raised", "active")


def compute(weights, source, goal, codes, count, grad_type):
    to_win, region = fixed_tables()
    to_tok = jnp.asarray(to_win.T, BF16)
    to_win = jnp.asarray(to_win, BF16)
    plain_code, shift_code = codes
    grads = {}

    def plain_query(split):
        return jnp.zeros((1, probs_width(split, WIN)), F32)

    def shift_query(split):
        parts = []
        for lane, lanes, n_heads in split:
            total = 128 * columns_of(n_heads, 72)
            tiled = np.tile(region, (1, n_heads))
            parts.append(np.pad(tiled, ((0, 0), (0, total - tiled.shape[1]))))
        return jnp.asarray(np.concatenate(parts, 1)[:, None, :], F32)

    def block_ins(tower, layer, names, grouped):
        found = []
        for name in names:
            array = weights[tower, layer, name]
            found.append((array, of_group(array.shape[1:]) if grouped else None))
        return found

    BLOCK = ("norm_one", "qkv", "proj", "norm_two", "up", "down")
    saved = {}
    plain_saved = ("x_in", "normed") + SAVED + ("x_out",)
    shift_saved = ("packed", "packed_far") + SAVED[1:] + ("x_out",)

    def grouped(array):
        return (array, of_group(array.shape[1:]))

    def forward_pair(tower, width, split, n_groups):
        many = n_groups > 1
        pick = grouped if many else (lambda array: (array, None))
        gain_next = block_ins(tower, 1, ("norm_one",), many)
        codes_in = [(plain_code, None), (plain_query(split), None), (to_win, None)]
        sent_outs = [((WIN, width), BF16, True)] * 2
        if many:
            ins = [(source, pl.BlockSpec((TOKENS, PIN), lambda g: (0, g)))] + codes_in
            ins += [grouped(weights[tower, -1, "embed"])]
            body, extra = enc_plain_kernel, []
        else:
            left = saved["enc", 1]["x_out"]
            ins = [(left, of_group(left.shape[1:], 0)), (left, of_group(left.shape[1:], 1))] + codes_in
            ins += [(weights[tower, -1, "joining"], None)]
            body, extra = trunk_plain_kernel, [((TOKENS, 2 * D_ENC), BF16, False)]
        ins += block_ins(tower, 0, BLOCK, many) + gain_next
        results = launch(
            functools.partial(body, split=split, width=width), tower + "_plain", n_groups, ins,
            extra + saved_outs(width, split, False) + sent_outs, forward_scratch(width, split, False),
        )
        if extra:
            saved["joined"] = results[0]
            results = results[1:]
        saved[tower, 0] = dict(zip(plain_saved, results))
        sent = results[-2:]
        far = exchange(*sent)
        ins = [pick(saved[tower, 0]["x_out"])] + [pick(array) for array in (*sent, *far)]
        ins += [(shift_code, None), (shift_query(split), None), (to_tok, None)]
        ins += block_ins(tower, 1, BLOCK[1:], many)
        results = launch(
            functools.partial(shifted_kernel, split=split, width=width), tower + "_shifted", n_groups,
            ins, saved_outs(width, split, True), forward_scratch(width, split, True),
        )
        saved[tower, 1] = dict(zip(shift_saved, results))
        saved[tower, 1]["rows"] = (*sent, *far)

    forward_pair("enc", D_ENC, ENC_SPLIT, GROUPS)
    forward_pair("trunk", D_TRUNK, TRUNK_SPLIT, 1)

    results = launch(
        loss_kernel, "loss", 1,
        [(saved["trunk", 1]["x_out"], None), (goal, None), (plain_code, None),
         (count, pl.BlockSpec(memory_space=pltpu.SMEM)),
         (weights["trunk", -1, "final"], None), (weights["top", -1, "decode"], None),
         (weights["top", -1, "head"], None), (weights["top", -1, "scale"], None)],
        [((TOKENS, D_TRUNK), F32, False), ((2, D_TRUNK), F32, False),
         ((GROUPS, D_TRUNK, D_ENC), grad_type, False), ((GROUPS, D_ENC, PIN), grad_type, False),
         ((GROUPS, PIN), F32, False), ((1, PIN), F32, False)],
        [],
    )
    grad_out, grads["trunk", -1, "final"], grads["top", -1, "decode"] = results[:3]
    grads["top", -1, "head"], grads["top", -1, "scale"], loss_row = results[3:]

    def gain_out(width):
        return ((2, width), F32, True)

    def block_grads(width):
        return [
            ((width, 3 * width), grad_type, True),
            ((width, width), grad_type, True),
            gain_out(width),
            ((width, 4 * width), grad_type, True),
            ((4 * width, width), grad_type, True),
        ]

    def backward_pair(tower, width, split, n_groups, grad_in):
        many = n_groups > 1
        pick = grouped if many else (lambda array: (array, None))
        kept = saved[tower, 1]
        ins = [grad_in] if many else [(grad_in, None)]
        ins += [pick(array) for array in kept["rows"]]
        ins += [pick(kept[name]) for name in shift_saved[:-1]]
        ins += [(shift_code, None), (shift_query(split), None), (to_win, None), (to_tok, None)]
        ins += block_ins(tower, 1, BLOCK[1:], many)
        outs = [((TOKENS, width), F32, True)] * 2 + [((WIN, width), BF16, True)] * 2
        results = launch(
            functools.partial(shifted_back_kernel, split=split, width=width), tower + "_shifted_back",
            n_groups, ins, outs + block_grads(width), backward_scratch(width, split, True),
        )
        grad_middle, grad_near, rim_a, rim_b = results[:4]
        for name, grad in zip(BLOCK[1:], results[4:]):
            grads[tower, 1, name] = grad
        from_below, from_above = exchange(rim_a, rim_b)
        kept = saved[tower, 0]
        ins = [pick(array) for array in (grad_middle, grad_near, from_below, from_above, kept["x_out"])]
        ins += block_ins(tower, 1, ("norm_one",), many) + [(to_tok, None)]
        ins += [pick(kept[name]) for name in plain_saved[:-1]]
        ins += [(plain_code, None), (plain_query(split), None)]
        ins += block_ins(tower, 0, BLOCK, many)
        tail = [gain_out(width), gain_out(width)] + block_grads(width)
        if many:
            ins += [(source, pl.BlockSpec((TOKENS, PIN), lambda g: (0, g)))]
            body, head = enc_plain_back_kernel, [((PIN, D_ENC), grad_type, True)]
        else:
            ins += [(saved["joined"], None), (weights[tower, -1, "joining"], None)]
            body = trunk_plain_back_kernel
            head = [((TOKENS, D_ENC), F32, True)] * 2 + [((width, width), grad_type, True)]
        results = launch(
            functools.partial(body, split=split, width=width), tower + "_plain_back",
            n_groups, ins, head + tail, backward_scratch(width, split, False),
        )
        grads[tower, 1, "norm_one"] = results[len(head)]
        for name, grad in zip(BLOCK, results[len(head) + 1 :]):
            grads[tower, 0, name] = grad
        return results[: len(head)]

    left, right, grads["trunk", -1, "joining"] = backward_pair(
        "trunk", D_TRUNK, TRUNK_SPLIT, 1, grad_out
    )
    stacked = jnp.stack([left, right])
    (grads["enc", -1, "embed"],) = backward_pair(
        "enc", D_ENC, ENC_SPLIT, GROUPS, grouped(stacked)
    )
    return loss_row, grads


def stacked_key(label_key):
    tower, group, layer, name = label_key
    return (tower, layer, name), (group if tower in ("enc", "top") else None)


BLOCK_ELEMENTS = 2048


def share_rows(n_own):
    blocks = -(-(n_own + BLOCK_ELEMENTS - 1) // BLOCK_ELEMENTS) + 1
    return 16 * 3 * (-(-blocks // 3))


def first_row(n_own, device):
    return (n_own * device // BLOCK_ELEMENTS) * 16


def grouped_pieces():
    found = {}
    for label_key, dims_shape, offset in placed():
        key, group = stacked_key(label_key)
        found.setdefault(key, (dims_shape, []))[1].append((group, offset // 128))
    return [(key, places, dims_shape) for key, (dims_shape, places) in found.items()]


def is_gain(key):
    return key[2] in ("norm_one", "norm_two", "final")


def stacked_shape(places, dims_shape):
    if len(dims_shape) == 1:
        return (len(places),) + dims_shape
    return dims_shape if places[0][0] is None else (len(places),) + dims_shape


def turned(values):
    return pltpu.roll(values, 64, 1)


def lower_half(values):
    return lax.broadcasted_iota(jnp.int32, values.shape, 1) < 64


def read_gain(flat, offset, width, out):
    if width % 128 == 0:
        count = width // 128
        for row in range(2):
            for tile in range(count):
                at = offset + row * count + tile
                out[row : row + 1, 128 * tile : 128 * tile + 128] = flat[at : at + 1, :]
        return
    rows = [flat[offset + place : offset + place + 1, :] for place in range(3)]
    out[0:1, 0:128] = rows[0]
    out[0:1, 128:192] = rows[1][:, 0:64]
    out[1:2, 0:128] = jnp.where(lower_half(rows[1]), turned(rows[1]), turned(rows[2]))
    out[1:2, 128:192] = rows[2][:, 64:128]


def read_matrix(flat, offset, shape, out, wide_scr):
    height, width = shape
    step = 64
    if width % 128 == 0:
        count = width // 128

        def body(index, carry):
            row = pl.multiple_of(index * step, step)
            for tile in range(count):
                start = offset + tile + row * count
                piece = flat[pl.ds(start, step, stride=count), :]
                out[pl.ds(row, step), 128 * tile : 128 * tile + 128] = piece.astype(BF16)
            return carry

        lax.fori_loop(0, height // step, body, 0)
        return
    half = width // 128
    period = 2 * half + 1

    def body(index, carry):
        row = pl.multiple_of(index * step, step)
        start = offset + (row // 2) * period
        rows = [flat[pl.ds(start + place, step // 2, stride=period), :] for place in range(period)]
        late = [turned(rows[half + place]) for place in range(half + 1)]
        for tile in range(half + 1):
            odd_rows = late[tile]
            if tile < half:
                odd_rows = jnp.where(lower_half(late[tile]), late[tile], late[tile + 1])
            wide_scr[pl.ds(step * tile, step // 2, stride=2), :] = rows[tile]
            wide_scr[pl.ds(step * tile + 1, step // 2, stride=2), :] = odd_rows
            end = min(128, width - 128 * tile)
            tile_rows = wide_scr[step * tile : step * (tile + 1), 0:end]
            out[pl.ds(row, step), 128 * tile : 128 * tile + end] = tile_rows.astype(BF16)
        return carry

    lax.fori_loop(0, height // step, body, 0)


def write_gain(flat, offset, width, values):
    if width % 128 == 0:
        count = width // 128
        for row in range(2):
            for tile in range(count):
                at = offset + row * count + tile
                flat[at : at + 1, :] = values[row : row + 1, 128 * tile : 128 * tile + 128]
        return
    flat[offset : offset + 1, :] = values[0:1, 0:128]
    first, second = values[1:2, 0:64], values[1:2, 64:192]
    flat[offset + 1 : offset + 2, :] = jnp.concatenate([values[0:1, 128:192], first], 1)
    flat[offset + 2 : offset + 3, :] = second


def write_matrix(flat, offset, shape, source, wide_scr):
    height, width = shape
    step = 64
    if width % 128 == 0:
        count = width // 128

        def body(index, carry):
            row = pl.multiple_of(index * step, step)
            for tile in range(count):
                start = offset + tile + row * count
                piece = source[pl.ds(row, step), 128 * tile : 128 * tile + 128]
                flat[pl.ds(start, step, stride=count), :] = piece.astype(F32)
            return carry

        lax.fori_loop(0, height // step, body, 0)
        return
    half = width // 128
    period = 2 * half + 1

    def body(index, carry):
        row = pl.multiple_of(index * step, step)
        start = offset + (row // 2) * period
        for tile in range(half + 1):
            end = min(128, width - 128 * tile)
            tile_rows = source[pl.ds(row, step), 128 * tile : 128 * tile + end].astype(F32)
            wide_scr[step * tile : step * (tile + 1), 0:end] = tile_rows
        early = [wide_scr[pl.ds(step * tile, step // 2, stride=2), :] for tile in range(half + 1)]
        late = [
            turned(wide_scr[pl.ds(step * tile + 1, step // 2, stride=2), :])
            for tile in range(half + 1)
        ]
        low = lower_half(late[0])
        rows = early[:half] + [jnp.where(low, early[half], late[0])]
        rows += [jnp.where(low, late[tile], late[tile + 1]) for tile in range(half)]
        for place, value in enumerate(rows):
            flat[pl.ds(start + place, step // 2, stride=period), :] = value
        return carry

    lax.fori_loop(0, height // step, body, 0)


def unpack_kernel(shares, *refs, pieces, n_own):
    outs, (flat, wide_scr) = refs[:-2], refs[-2:]
    n_devices, rows, unused = shares.shape
    step = rows // 6

    def place(device, carry):
        start = pl.multiple_of((n_own * device // BLOCK_ELEMENTS) * 16, 16)
        kept = jnp.where(device > 0, flat[pl.ds(start, 16), :], 0.0)
        flat[pl.ds(start, 16), :] = kept + shares[device, 0:16, :].astype(F32)
        flat[pl.ds(start + 16, step - 16), :] = shares[device, 16:step, :].astype(F32)
        for part in range(1, 6):
            at = pl.ds(start + part * step, step)
            flat[at, :] = shares[device, part * step : (part + 1) * step, :].astype(F32)
        return carry

    lax.fori_loop(0, n_devices, place, 0)
    for (key, places, dims_shape), out in zip(pieces, outs):
        for group, offset in places:
            view = out if group is None or len(dims_shape) == 1 else out.at[group]
            if len(dims_shape) == 1:
                view[group : group + 1, :] = flat[offset : offset + 1, :]
            elif is_gain(key):
                read_gain(flat, offset, dims_shape[1], view)
            else:
                read_matrix(flat, offset, dims_shape, view, wide_scr)


def flat_rows(n_own, n_devices):
    return first_row(n_own, n_devices - 1) + share_rows(n_own)


def unpack_weights(gathered, n_own):
    pieces = grouped_pieces()
    n_devices, rows, unused = gathered.shape
    outs = []
    for key, places, dims_shape in pieces:
        small = is_gain(key) or len(dims_shape) == 1
        outs.append(OUT(stacked_shape(places, dims_shape), F32 if small else BF16))
    results = pl.pallas_call(
        functools.partial(unpack_kernel, pieces=pieces, n_own=n_own),
        out_shape=outs,
        scratch_shapes=[
            pltpu.VMEM((flat_rows(n_own, n_devices), 128), F32),
            pltpu.VMEM((5 * 64, 128), F32),
        ],
        name="unpack",
        compiler_params=pltpu.CompilerParams(vmem_limit_bytes=56 << 20),
    )(gathered)
    return {piece[0]: result for piece, result in zip(pieces, results)}


def cuts_of(rows):
    blocks = rows // 16
    last = blocks // 5
    first = (blocks - last) // 2
    return 16 * first, 16 * (blocks - last - first), 16 * last


def step_of(rows):
    blocks = rows // 16
    return 16 * max(count for count in range(1, 13) if blocks % count == 0)


def pack_kernel(core, *refs, pieces, n_own):
    ins, kept, sent, (flat, wide_scr) = refs[:-8], refs[-8:-5], refs[-5:-2], refs[-2:]
    used = sum(len(places) * math.prod(dims_shape) for key, places, dims_shape in pieces) // 128
    flat[used:, :] = jnp.zeros((flat.shape[0] - used, 128), F32)
    for (key, places, dims_shape), source in zip(pieces, ins):
        for group, offset in places:
            view = source if group is None or len(dims_shape) == 1 else source.at[group]
            if len(dims_shape) == 1:
                flat[offset : offset + 1, :] = view[group : group + 1, :]
            elif is_gain(key):
                write_gain(flat, offset, dims_shape[1], view)
            else:
                write_matrix(flat, offset, dims_shape, view, wide_scr)

    def chip(index, carry):
        for outs, device in ((kept, 2 * index + core[0]), (sent, 2 * index + 1 - core[0])):
            start = pl.multiple_of((n_own * device // BLOCK_ELEMENTS) * 16, 16)
            done = 0
            for out in outs:
                step = step_of(out.shape[1])
                for row in range(0, out.shape[1], step):
                    piece = flat[pl.ds(start + done + row, step), :]
                    out[index, row : row + step, :] = piece.astype(BF16)
                done += out.shape[1]
        return carry

    lax.fori_loop(0, kept[0].shape[0], chip, 0)


def pack_grads(grads, n_own, n_devices, core):
    pieces = grouped_pieces()
    shapes = [OUT((n_devices // 2, rows, 128), BF16) for rows in cuts_of(share_rows(n_own))]
    results = pl.pallas_call(
        functools.partial(pack_kernel, pieces=pieces, n_own=n_own),
        in_specs=[pl.BlockSpec(memory_space=pltpu.SMEM)]
        + [pl.BlockSpec(memory_space=pltpu.VMEM)] * len(pieces),
        out_shape=shapes + shapes,
        scratch_shapes=[
            pltpu.VMEM((flat_rows(n_own, n_devices), 128), F32),
            pltpu.VMEM((5 * 64, 128), F32),
        ],
        name="pack",
        compiler_params=pltpu.CompilerParams(vmem_limit_bytes=58 << 20),
    )(core.reshape(1), *[grads[key] for key, places, dims_shape in pieces])
    return results[:3], results[3:]


class Torus:
    def __init__(self):
        self.totals = {"dp": lax.axis_size("dp"), "band": lax.axis_size("band")}
        depth = min(4, self.totals["dp"])
        across = self.totals["dp"] // depth
        self.axes = {
            "z": (depth, across, "dp"),
            "x": (across, 1, "dp"),
            "y": (self.totals["band"] // 2, 2, "band"),
            "core": (2, 1, "band"),
        }

    def size(self, axis):
        return self.axes[axis][0]

    def place(self, axis):
        count, stride, name = self.axes[axis]
        return lax.axis_index(name) // stride % count

    def move(self, values, axis, by):
        count, stride, name = self.axes[axis]
        pairs = []
        for place in range(self.totals[name]):
            at = place // stride % count
            pairs.append((place, place + ((at + by) % count - at) * stride))
        return lax.ppermute(values, name, pairs)


def scatter_terms(torus, terms, dims, axis):
    dim = dims.index(axis)
    place = torus.place(axis)
    arrived = []
    for by in range(1, torus.size(axis)):
        other = (place + by) % torus.size(axis)
        pieces = [lax.dynamic_index_in_dim(term, other, dim, keepdims=False) for term in terms]
        total = sum(piece.astype(F32) for piece in pieces).astype(BF16)
        arrived.append(torus.move(total, axis, by))
    own = [lax.dynamic_index_in_dim(term, place, dim, keepdims=False) for term in terms]
    return own + arrived, [name for name in dims if name != axis]


SCATTER_ORDERS = (("y", "x", "z"), ("x", "y", "z"), ("z", "x", "y"))


def scatter_sum(kept, sent):
    torus = Torus()
    dims = ["z", "x", "y"]
    shape = tuple(torus.size(axis) for axis in dims)
    sequence = (2, 0, 1)
    state = {}
    for part in sequence:
        near = kept[part].reshape(shape + kept[part].shape[1:])
        far = sent[part].reshape(shape + sent[part].shape[1:])
        state[part] = ([near, torus.move(far, "core", 1)], dims)
    for step in range(3):
        for part in sequence:
            terms, left = state[part]
            state[part] = scatter_terms(torus, terms, left, SCATTER_ORDERS[part][step])
    return [sum(term.astype(F32) for term in state[part][0]) for part in range(3)]


def all_sum(values):
    for axis in ("band", "dp"):
        count = lax.axis_size(axis)
        bit = 1
        while bit < count:
            pairs = [(i, i ^ bit) for i in range(count)]
            values = values + lax.ppermute(values, axis, pairs)
            bit *= 2
    return values


def shards(inputs, targets, crop_extent, master, moment_one, moment_two, step_count):
    n_own = master.shape[0]
    n_bands = lax.axis_size("band")
    n_devices = lax.axis_size("dp") * n_bands
    rows = share_rows(n_own)
    device = lax.axis_index("dp") * n_bands + lax.axis_index("band")
    shift = (n_own * device) % BLOCK_ELEMENTS
    extent = crop_extent[0]
    share = lax.dynamic_update_slice(jnp.zeros((rows * 128,), BF16), master.astype(BF16), (shift,))
    share = lax.dynamic_update_slice(share, extent.astype(BF16), ((rows - 1) * 128,))
    gathered = lax.all_gather(share.reshape(rows, 128), ("dp", "band"), axis=0, tiled=False)
    extents = gathered[::n_bands, rows - 1, 0:2].astype(F32)
    weights = unpack_weights(gathered, n_own)
    n_rows, n_levels = inputs.shape[1], inputs.shape[2]
    source = inputs[0].transpose(1, 0, 2, 3).reshape(TOKENS, GROUPS * PIN)
    goal = targets[0].transpose(1, 0, 2, 3).reshape(TOKENS, GROUPS * PIN)
    first_lat = lax.axis_index("band") * n_rows
    norm_count = jnp.sum(extents[:, 0] * extents[:, 1]) * (n_levels * GROUPS * PIN)
    loss_row, grads = compute(
        weights, source, goal, key_codes(extent, first_lat), norm_count.reshape(1, 1), BF16
    )
    kept, sent = pack_grads(grads, n_own, n_devices, lax.axis_index("band") % 2)
    owned = jnp.concatenate(scatter_sum(kept, sent), 0)
    grad_shard = lax.dynamic_slice(owned.reshape(-1), (shift,), (n_own,))
    shard_square = jnp.sum(grad_shard * grad_shard)
    lanes = lax.broadcasted_iota(jnp.int32, (8, 128), 1)
    both = jnp.where(lanes < 64, shard_square, jnp.sum(loss_row))
    both = all_sum(both)
    grad_norm = jnp.sqrt(both[0, 0])
    loss_total = both[0, 64]
    factor_clip = jnp.minimum(1.0, CLIP_LEVEL / (grad_norm + 1e-06))
    clipped = grad_shard * factor_clip
    new_one = BETA_ONE * moment_one + (1.0 - BETA_ONE) * clipped
    new_two = BETA_TWO * moment_two + (1.0 - BETA_TWO) * clipped * clipped
    step_value = step_count[0].astype(F32)
    fix_one = 1.0 - jnp.power(BETA_ONE, step_value)
    fix_two = 1.0 - jnp.power(BETA_TWO, step_value)
    update = new_one / fix_one / (jnp.sqrt(new_two / fix_two) + ADAM_EPS) + WEIGHT_DECAY * master
    new_master = master - LEARN_RATE * update
    return (
        new_master,
        new_one,
        new_two,
        new_master.astype(BF16),
        loss_total / norm_count,
        grad_norm,
    )


def solution(mesh):
    in_specs = (
        P("dp", "band", None, None, None),
        P("dp", "band", None, None, None),
        P("dp", None),
        P(("dp", "band")),
        P(("dp", "band")),
        P(("dp", "band")),
        P(),
    )
    out_specs = (
        P(("dp", "band")),
        P(("dp", "band")),
        P(("dp", "band")),
        P(("dp", "band")),
        P(),
        P(),
    )
    return jax.shard_map(shards, mesh=mesh, in_specs=in_specs, out_specs=out_specs, check_vma=False)
```

```python
import functools
import math

import jax
import jax.numpy as jnp
import numpy as np
from jax import lax
from jax.experimental import pallas as pl
from jax.experimental.pallas import tpu as pltpu
from jax.sharding import PartitionSpec as P

D_ENC = 192
HEADS_ENC = 6
D_TRUNK = 384
HEADS_TRUNK = 12
PIN = 128
GROUPS = 2
HEAD_DIM = 32
SCALE = HEAD_DIM ** (-0.5)

NEG_FILL = -1000000000.0
BETA_ONE = 0.5
BETA_TWO = 0.5
LEARN_RATE = 0.01
WEIGHT_DECAY = 0.1
CLIP_LEVEL = 0.07
ADAM_EPS = 1e-08

F32 = jnp.float32
BF16 = jnp.bfloat16
TOKENS = 288
AHEAD = 4 << 20
SPAN = 384
SPAN_BACK = 384
WIN = 144
ENC_SPLIT = ((0, 192, 6),)
TRUNK_SPLIT = ((0, 256, 8), (256, 128, 4))


def block_layout(path_name, group_id, layer_id, n_width):
    prefix = (path_name, group_id, layer_id)
    return [
        (prefix + ("norm_one",), (2, n_width)),
        (prefix + ("qkv",), (n_width, 3 * n_width)),
        (prefix + ("proj",), (n_width, n_width)),
        (prefix + ("norm_two",), (2, n_width)),
        (prefix + ("up",), (n_width, 4 * n_width)),
        (prefix + ("down",), (4 * n_width, n_width)),
    ]


def layout():
    entries = []
    for group_id in range(GROUPS):
        entries.append((("enc", group_id, -1, "embed"), (PIN, D_ENC)))
        for layer_id in range(2):
            entries += block_layout("enc", group_id, layer_id, D_ENC)
        entries.append((("top", group_id, -1, "decode"), (D_TRUNK, D_ENC)))
        entries.append((("top", group_id, -1, "head"), (D_ENC, PIN)))
        entries.append((("top", group_id, -1, "scale"), (PIN,)))
    entries.append((("trunk", 0, -1, "joining"), (GROUPS * D_ENC, D_TRUNK)))
    for layer_id in range(2):
        entries += block_layout("trunk", 0, layer_id, D_TRUNK)
    entries.append((("trunk", 0, -1, "final"), (2, D_TRUNK)))
    return entries


def placed():
    offset = 0
    for label_key, dims_shape in layout():
        yield label_key, dims_shape, offset
        offset += math.prod(dims_shape)


def nn(left, right):
    return jnp.dot(left, right, preferred_element_type=F32)


def nt(left, right):
    return lax.dot_general(left, right, (((1,), (1,)), ((), ())), preferred_element_type=F32)


def tn(left, right):
    return lax.dot_general(left, right, (((0,), (0,)), ((), ())), preferred_element_type=F32)


def unit_rows(values):
    centre = values - jnp.mean(values, -1, keepdims=True)
    inverse = lax.rsqrt(jnp.mean(centre * centre, -1, keepdims=True) + 1e-05)
    return centre * inverse, inverse


def norm_forward(values, gain_ref):
    unit, unused = unit_rows(values)
    return unit * gain_ref[0:1, :] + gain_ref[1:2, :]


def norm_backward(values, gain_ref, grad_normed):
    unit, inverse = unit_rows(values)
    grad_gain = jnp.sum(grad_normed * unit, 0, keepdims=True)
    grad_shift = jnp.sum(grad_normed, 0, keepdims=True)
    grad_unit = grad_normed * gain_ref[0:1, :]
    along = jnp.mean(grad_unit * unit, -1, keepdims=True)
    grad_values = inverse * (grad_unit - jnp.mean(grad_unit, -1, keepdims=True) - unit * along)
    return grad_values, jnp.concatenate([grad_gain, grad_shift], 0)


GELU_A = math.sqrt(2.0 / math.pi)
GELU_B = 0.044715


def gelu(values):
    inner = jnp.tanh(GELU_A * (values + GELU_B * (values * values * values)))
    return values * (0.5 * (1.0 + inner))


def gelu_slope(values):
    square = values * values
    inner = jnp.tanh(GELU_A * (values + GELU_B * (square * values)))
    steep = (1.0 - inner * inner) * (GELU_A + (3.0 * GELU_B * GELU_A) * square)
    return 0.5 * (1.0 + inner) + 0.5 * values * steep


def head_lanes(rows, lanes, head):
    lane = lax.broadcasted_iota(jnp.int32, (rows, lanes), 1)
    return (lane >= HEAD_DIM * head) & (lane < HEAD_DIM * (head + 1))


def columns_of(n_heads, n_query):
    return -(-n_heads * n_query // 128)


def spread_heads(rows_value, n_heads, out_ref):
    n_query, lanes = rows_value.shape
    wide = rows_value.astype(F32)
    for head in range(n_heads):
        kept = jnp.where(head_lanes(n_query, lanes, head), wide, 0.0).astype(BF16)
        out_ref[head * n_query : (head + 1) * n_query, 0:lanes] = kept
    total = 128 * columns_of(n_heads, n_query)
    if total > n_heads * n_query:
        out_ref[n_heads * n_query : total, 0:lanes] = jnp.zeros(
            (total - n_heads * n_query, lanes), BF16
        )


def join_heads(spread_ref, n_heads, n_query, lanes):
    joined = spread_ref[0:n_query, 0:lanes]
    for head in range(1, n_heads):
        part = spread_ref[head * n_query : (head + 1) * n_query, 0:lanes]
        joined = jnp.where(head_lanes(n_query, lanes, head), part, joined)
    return joined


def same_code(key_code, query_code):
    count = query_code.shape[1] // 128
    return jnp.concatenate([key_code] * count, 1) == query_code


def attend_window(queries, key_rows, value_rows, key_code, query_code, probs_ref, q_scr, o_scr, split):
    n_query = queries.shape[0]
    outs = []
    at = 0
    for lane, lanes, n_heads in split:
        spread_heads(queries[:, lane : lane + lanes], n_heads, q_scr)
        keys = key_rows[:, lane : lane + lanes]
        values = value_rows[:, lane : lane + lanes]
        wide = 128 * columns_of(n_heads, n_query)
        for start in range(0, wide, SPAN):
            rows = slice(start, min(start + SPAN, wide))
            columns = slice(at + rows.start, at + rows.stop)
            scores = nt(keys, q_scr[rows, 0:lanes]) * SCALE
            scores = jnp.where(same_code(key_code, query_code[0:1, columns]), scores, NEG_FILL)
            raised = jnp.exp(scores - jnp.max(scores, 0, keepdims=True))
            probs = (raised * (1.0 / jnp.sum(raised, 0, keepdims=True))).astype(BF16)
            probs_ref[:, columns] = probs
            o_scr[rows, 0:lanes] = tn(probs, values)
        outs.append(join_heads(o_scr, n_heads, n_query, lanes))
        at += wide
    return jnp.concatenate(outs, 1) if len(outs) > 1 else outs[0]


def attend_window_back(
    queries, key_rows, value_rows, grad_rows, key_code, query_code, probs_ref, q_scr, g_scr, o_scr, s_scr, split
):
    n_query = queries.shape[0]
    out_q, out_k, out_v = [], [], []
    at = 0
    for lane, lanes, n_heads in split:
        n_col = columns_of(n_heads, n_query)
        spread_heads(queries[:, lane : lane + lanes], n_heads, q_scr)
        spread_heads(grad_rows[:, lane : lane + lanes], n_heads, g_scr)
        keys = key_rows[:, lane : lane + lanes]
        values = value_rows[:, lane : lane + lanes]
        wide = 128 * n_col
        for start in range(0, wide, SPAN_BACK):
            rows = slice(start, min(start + SPAN_BACK, wide))
            columns = slice(at + rows.start, at + rows.stop)
            grad_probs = nt(values, g_scr[rows, 0:lanes])
            probs = probs_ref[:, columns].astype(F32)
            along = jnp.sum(grad_probs * probs, 0, keepdims=True)
            grad_scores = probs * (grad_probs - along)
            allowed = same_code(key_code, query_code[0:1, columns])
            grad_scores = jnp.where(allowed, grad_scores, 0.0).astype(BF16)
            s_scr[:, rows] = grad_scores
            o_scr[rows, 0:lanes] = tn(grad_scores, keys)
        out_v.append(nn(probs_ref[:, at : at + wide], g_scr[0:wide, 0:lanes]))
        out_k.append(nn(s_scr[:, 0:wide], q_scr[0:wide, 0:lanes]) * SCALE)
        out_q.append(join_heads(o_scr, n_heads, n_query, lanes) * SCALE)
        at += wide
    if len(split) > 1:
        return tuple(jnp.concatenate(parts, 1) for parts in (out_q, out_k, out_v))
    return out_q[0], out_k[0], out_v[0]


class Queue:
    def __init__(self, copies, sizes, ahead):
        self.copies, self.sizes, self.ahead = copies, sizes, ahead
        self.started, self.reach = 0, 0
        self.advance(-1)

    def advance(self, index):
        limit = sum(self.sizes[: index + 1]) + self.ahead
        while self.started < len(self.copies) and (self.started <= index or self.reach < limit):
            self.copies[self.started].start()
            self.reach += self.sizes[self.started]
            self.started += 1


class Held:
    def __init__(self, ref, queue, index):
        self.ref, self.queue, self.index = ref, queue, index

    def ready(self):
        if self.queue is not None:
            self.queue.advance(self.index)
            self.queue.copies[self.index].wait()
            self.queue = None
        return self.ref

    def __getitem__(self, index):
        return self.ready()[index]

    @property
    def at(self):
        return self.ready().at

    @property
    def shape(self):
        return self.ref.shape


class Made:
    def __init__(self, ref, copy):
        self.ref, self.copy, self.sent = ref, copy, False

    def __getitem__(self, index):
        return self.ref[index]

    def __setitem__(self, index, value):
        self.ref[index] = value

    @property
    def at(self):
        return self.ref.at

    @property
    def shape(self):
        return self.ref.shape

    @property
    def dtype(self):
        return self.ref.dtype

    def send(self):
        if not self.sent:
            self.copy.start()
            self.sent = True


class Refs:
    def __init__(self, **refs):
        self.__dict__.update(refs)


def send(*refs):
    for ref in refs:
        if isinstance(ref, Made):
            ref.send()


def rest_forward(resid_in, w, s):
    middle = resid_in + nn(s.mixed[...], w.proj[...])
    s.middle[...] = middle
    normed = norm_forward(middle, w.norm_two).astype(BF16)
    s.normed_two[...] = normed
    send(s.mixed, s.middle, s.normed_two)
    for start in range(0, w.up.shape[1], 256):
        columns = slice(start, start + 256)
        s.raised[:, columns] = nn(normed, w.up[:, columns])
        for row in range(0, TOKENS, 96):
            piece = s.raised[row : row + 96, columns]
            s.active[row : row + 96, columns] = gelu(piece).astype(BF16)
    send(s.raised, s.active)
    return middle + nn(s.active[...], w.down[...])


def rest_backward(grad_out, w, s, flow, d_norm_two):
    grad_low = grad_out.astype(BF16)
    flow.low[...] = grad_low
    width = w.up.shape[1]
    for start in range(0, width, 256):
        columns = slice(start, start + 256)
        grad_active = nt(grad_low, w.down[start : start + 256, :])
        for row in range(0, TOKENS, 96):
            slope = gelu_slope(s.raised[row : row + 96, columns])
            flow.raised[row : row + 96, columns] = (
                slope * grad_active[row : row + 96, :]
            ).astype(BF16)
    grad_middle, grad_gain = norm_backward(
        s.middle[...], w.norm_two, nt(flow.raised[...], w.up[...])
    )
    d_norm_two[...] = grad_gain
    grad_middle = grad_out + grad_middle
    grad_branch = grad_middle.astype(BF16)
    flow.branch[...] = grad_branch
    send(flow.low, flow.raised, flow.branch, d_norm_two)
    return grad_middle, nt(grad_branch, w.proj[...]).astype(BF16)


def rest_weights(s, flow, d):
    for out, left, right in (
        (d.down, s.active, flow.low),
        (d.up, s.normed_two, flow.raised),
        (d.proj, s.mixed, flow.branch),
    ):
        out[...] = tn(left[...], right[...]).astype(out.dtype)
        send(out)


def plain_forward(first, w, s, tables, t, split, width):
    s.x_in[...] = first
    s.normed[...] = norm_forward(first, w.norm_one).astype(BF16)
    s.packed[...] = nn(s.normed[...], w.qkv[...]).astype(BF16)
    send(s.x_in, s.normed, s.packed)
    for win in range(2):
        rows = slice(WIN * win, WIN * (win + 1))
        s.mixed[rows, :] = attend_window(
            s.packed[rows, 0:width],
            s.packed[rows, width : 2 * width],
            s.packed[rows, 2 * width : 3 * width],
            tables.plain_key[rows, :],
            tables.plain_query,
            s.probs.at[win],
            t.q,
            t.o,
            split,
        ).astype(BF16)
    send(s.probs)
    last = rest_forward(first, w, s)
    s.x_out[...] = last
    ordered = nn(tables.to_win[...], norm_forward(last, w.norm_next).astype(BF16)).astype(BF16)
    s.near_a[...] = ordered[0:WIN]
    s.near_b[...] = ordered[WIN:]
    send(s.x_out, s.near_a, s.near_b)


def both(first, second):
    return jnp.concatenate([first[...], second[...]], 0)


def shifted_keys(s, win, width):
    rows = slice(72 * win, 72 * (win + 1))
    keys = jnp.concatenate([s.packed[rows, width : 2 * width], s.packed_far[rows, 0:width]], 0)
    values = jnp.concatenate([s.packed[rows, 2 * width :], s.packed_far[rows, width:]], 0)
    return s.packed[rows, 0:width], keys, values


def shifted_forward(x_in, near, far, w, s, tables, t, split, width):
    s.packed[...] = nn(both(*near), w.qkv[...]).astype(BF16)
    s.packed_far[...] = nn(both(*far), w.qkv[:, width:]).astype(BF16)
    send(s.packed, s.packed_far)
    for win in range(4):
        queries, keys, values = shifted_keys(s, win, width)
        t.m[72 * win : 72 * (win + 1), 0:width] = attend_window(
            queries, keys, values, tables.shift_key[WIN * win : WIN * (win + 1), :],
            tables.shift_query.at[win % 2], s.probs.at[win], t.q, t.o, split,
        )
    send(s.probs)
    s.mixed[...] = nn(tables.to_tok[...], t.m[:, 0:width].astype(BF16)).astype(BF16)
    return rest_forward(x_in[...], w, s)


def loss_part(values, goal, tables, count, w, d):
    low = norm_forward(values, w.final).astype(BF16)
    valid = tables.plain_key[...] + 1.0
    inverse_count = 1.0 / count[0:1, :]
    grad_low = None
    total = None
    for group in range(GROUPS):
        decode, head = w.decode[group], w.head[group]
        raised = nn(low, decode)
        active = gelu(raised).astype(BF16)
        predicted = nn(active, head)
        log_scale = w.scale[group : group + 1, :]
        error = predicted - goal[:, PIN * group : PIN * (group + 1)].astype(F32)
        inverse_scale = jnp.exp(-log_scale)
        weighted = jnp.abs(error) * inverse_scale
        part = jnp.sum((weighted + log_scale) * valid, 0, keepdims=True)
        total = part if total is None else total + part
        direction = jnp.where(error > 0.0, 1.0, jnp.where(error < 0.0, -1.0, 0.0))
        grad_pred = (direction * inverse_scale * valid * inverse_count).astype(BF16)
        d.scale[group : group + 1, :] = (
            jnp.sum((1.0 - weighted) * valid, 0, keepdims=True) * inverse_count
        )
        d.head[group] = tn(active, grad_pred).astype(BF16)
        grad_raised = (gelu_slope(raised) * nt(grad_pred, head)).astype(BF16)
        d.decode[group] = tn(low, grad_raised).astype(BF16)
        back = nt(grad_raised, decode)
        grad_low = back if grad_low is None else grad_low + back
    d.loss[...] = total
    grad_values, d.final[...] = norm_backward(values, w.final, grad_low)
    send(d.scale, d.head, d.decode, d.loss, d.final)
    return grad_values


def shifted_backward(grad_out, w, s, flow, outs, tables, t, split, width):
    outs.grad_middle[...], grad_mixed = rest_backward(grad_out, w, s, flow, outs.norm_two)
    send(outs.grad_middle)
    grad_win = nn(tables.to_win[...], grad_mixed).astype(BF16)
    for win in range(4):
        rows = slice(72 * win, 72 * (win + 1))
        queries, keys, values = shifted_keys(s, win, width)
        grad_q, grad_k, grad_v = attend_window_back(
            queries, keys, values, grad_win[rows, :],
            tables.shift_key[WIN * win : WIN * (win + 1), :], tables.shift_query.at[win % 2],
            s.probs.at[win], t.q, t.g, t.o, t.s, split,
        )
        flow.near[rows, 0:width] = grad_q.astype(BF16)
        flow.near[rows, width : 2 * width] = grad_k[0:72].astype(BF16)
        flow.near[rows, 2 * width : 3 * width] = grad_v[0:72].astype(BF16)
        flow.far[rows, 0:width] = grad_k[72:144].astype(BF16)
        flow.far[rows, width : 2 * width] = grad_v[72:144].astype(BF16)
    rim = nt(flow.far[...], w.qkv[:, width:]).astype(BF16)
    outs.rim_a[...] = rim[0:WIN]
    outs.rim_b[...] = rim[WIN:]
    send(outs.rim_a, outs.rim_b, flow.near, flow.far)
    outs.grad_near[...] = nt(nn(tables.to_tok[...], flow.near[...]).astype(BF16), w.qkv[...])
    send(outs.grad_near)


def shifted_weights(near, far, s, flow, d, width):
    rest_weights(s, flow, d)
    near_rows, far_rows = both(*near), both(*far)
    d.qkv[:, 0:width] = tn(near_rows, flow.near[:, 0:width]).astype(BF16)
    d.qkv[:, width:] = (
        tn(near_rows, flow.near[:, width:]) + tn(far_rows, flow.far[...])
    ).astype(BF16)
    send(d.qkv)


def plain_backward(grad, arrived, w, s, flow, d, tables, t, split, width):
    grad_normed = grad.near[...] + nn(tables.to_tok[...], both(*arrived))
    grad_x, d.norm_next[...] = norm_backward(s.x_out[...], w.norm_next, grad_normed)
    grad_mid, grad_mixed = rest_backward(grad.middle[...] + grad_x, w, s, flow, d.norm_two)
    rest_weights(s, flow, d)
    for win in range(2):
        rows = slice(WIN * win, WIN * (win + 1))
        grads = attend_window_back(
            s.packed[rows, 0:width], s.packed[rows, width : 2 * width], s.packed[rows, 2 * width :],
            grad_mixed[rows, :], tables.plain_key[rows, :], tables.plain_query, s.probs.at[win],
            t.q, t.g, t.o, t.s, split,
        )
        for index, part in enumerate(grads):
            flow.near[rows, width * index : width * (index + 1)] = part.astype(BF16)
    near_grad = flow.near[...]
    d.qkv[...] = tn(s.normed[...], near_grad).astype(BF16)
    grad_first, d.norm_one[...] = norm_backward(s.x_in[...], w.norm_one, nt(near_grad, w.qkv[...]))
    send(d.norm_next, d.qkv, d.norm_one)
    return grad_mid + grad_first


def held(array):
    return pltpu.with_memory_space_constraint(array, pltpu.HBM)


def launch(name, body, ins, outs, scratch, limit=52 << 20, scalars=(), raw=(), sems=0):
    sources, views, shapes = [], [], []
    for value in ins.values():
        array, view, shape = value if isinstance(value, tuple) else (value, None, value.shape)
        sources.append(array)
        views.append(view)
        shapes.append(pltpu.VMEM(shape, array.dtype))
    n_in, n_out = len(ins), len(outs)
    n_first = len(scalars) + len(raw)
    own_sems = sems

    def kernel(*refs):
        named = {"scalars": refs[: len(scalars)], "raw": refs[len(scalars) : n_first]}
        refs = refs[n_first:]
        far_in, far_out = refs[:n_in], refs[n_in : n_in + n_out]
        near = refs[n_in + n_out :]
        near_in, near_out = near[:n_in], near[n_in : n_in + n_out]
        spare, flags = near[n_in + n_out : -1], near[-1]
        named["sems"] = [flags.at[n_in + n_out + index] for index in range(own_sems)]
        copies, sizes = [], []
        for index, key in enumerate(ins):
            source = far_in[index] if views[index] is None else views[index](far_in[index])
            copies.append(pltpu.make_async_copy(source, near_in[index], flags.at[index]))
            sizes.append(math.prod(near_in[index].shape) * near_in[index].dtype.itemsize)
        queue = Queue(copies, sizes, AHEAD)
        for index, key in enumerate(ins):
            named[key] = Held(near_in[index], queue, index)
        for index, key in enumerate(outs):
            copy = pltpu.make_async_copy(near_out[index], far_out[index], flags.at[n_in + index])
            named[key] = Made(near_out[index], copy)
            named[key].far, named[key].sem = far_out[index], flags.at[n_in + index]
        named.update(zip(scratch, spare))
        body(named)
        for key in ins:
            named[key].ready()
        for key in outs:
            named[key].send()
        for key in outs:
            named[key].copy.wait()

    results = pl.pallas_call(
        kernel,
        in_specs=[pl.BlockSpec(memory_space=pltpu.SMEM)] * len(scalars)
        + [pl.BlockSpec(memory_space=pl.ANY)] * (len(raw) + n_in),
        out_specs=[pl.BlockSpec(memory_space=pl.ANY)] * n_out,
        out_shape=[pltpu.HBM(shape, dtype) for shape, dtype in outs.values()],
        scratch_shapes=shapes
        + [pltpu.VMEM(shape, dtype) for shape, dtype in outs.values()]
        + [pltpu.VMEM(shape, dtype) for shape, dtype in scratch.values()]
        + [pltpu.SemaphoreType.DMA((n_in + n_out + sems,))],
        name=name,
        compiler_params=pltpu.CompilerParams(vmem_limit_bytes=limit),
    )(*scalars, *[held(array) for array in (*raw, *sources)])
    return dict(zip(outs, results))


def part(named, prefix):
    return Refs(**{key[len(prefix) :]: ref for key, ref in named.items() if key.startswith(prefix)})


def prefixed(prefix, values):
    return {prefix + key: value for key, value in values.items()}


def probs_width(split, n_query):
    return 128 * sum(columns_of(n_heads, n_query) for lane, lanes, n_heads in split)


def spread_shape(split, n_query):
    rows = 128 * max(columns_of(n_heads, n_query) for lane, lanes, n_heads in split)
    return (rows, max(lanes for lane, lanes, n_heads in split))


def saved_outs(width, split, shifted):
    n_query, n_win = (72, 4) if shifted else (WIN, 2)
    found = {"packed": ((TOKENS, 3 * width), BF16)}
    if shifted:
        found["packed_far"] = ((TOKENS, 2 * width), BF16)
    else:
        found["x_in"] = ((TOKENS, width), F32)
        found["normed"] = ((TOKENS, width), BF16)
    found["probs"] = ((n_win, WIN, probs_width(split, n_query)), BF16)
    found["mixed"] = ((TOKENS, width), BF16)
    found["middle"] = ((TOKENS, width), F32)
    found["normed_two"] = ((TOKENS, width), BF16)
    found["raised"] = ((TOKENS, 4 * width), F32)
    found["active"] = ((TOKENS, 4 * width), BF16)
    return found


def flow_shapes(width, shifted):
    found = {
        "low": ((TOKENS, width), BF16),
        "raised": ((TOKENS, 4 * width), BF16),
        "branch": ((TOKENS, width), BF16),
        "near": ((TOKENS, 3 * width), BF16),
    }
    if shifted:
        found["far"] = ((TOKENS, 2 * width), BF16)
    return found


def spare(width, split, shifted, backward):
    n_query = 72 if shifted else WIN
    shape = spread_shape(split, n_query)
    found = {"q": (shape, BF16), "o": (shape, F32)}
    if shifted:
        found["m"] = ((TOKENS, width), F32)
    if backward:
        found["g"] = (shape, BF16)
        found["s"] = ((WIN, shape[0]), BF16)
    return found


def rim_outs(width):
    found = {"grad_middle": ((TOKENS, width), F32), "grad_near": ((TOKENS, width), F32)}
    found["rim_a"] = found["rim_b"] = ((WIN, width), BF16)
    found["norm_two"] = ((2, width), F32)
    return found


def weight_grads(width):
    return {
        "down": ((4 * width, width), BF16),
        "up": ((width, 4 * width), BF16),
        "proj": ((width, width), BF16),
        "qkv": ((width, 3 * width), BF16),
    }


def window_order():
    order = []
    for half in range(2):
        for pair in ((1, 2), (3, 0)):
            for level in pair:
                for row in range(3):
                    for col in range(12):
                        order.append(level * 72 + (half * 3 + row) * 12 + col)
    return np.array(order)


def fixed_tables():
    order = window_order()
    to_win = np.zeros((TOKENS, TOKENS), np.float32)
    to_win[np.arange(TOKENS), order] = 1.0
    region = np.zeros((2, 72), np.float32)
    for pair, levels in enumerate(((1, 2), (3, 0))):
        for place in range(72):
            level, col = levels[place // 36], place % 12
            region[pair, place] = 2.0 * (level == 0) + 1.0 * (col < 6)
    return to_win, region


def key_codes(extent, first_lat):
    place = lax.broadcasted_iota(jnp.int32, (TOKENS, 128), 0)
    row, col = (place // 12) % 6, place % 12
    inside = (first_lat + row < extent[0]) & (col < extent[1])
    plain = jnp.where(inside, 0.0, -1.0)
    place = lax.broadcasted_iota(jnp.int32, (2 * TOKENS, 128), 0)
    win, rest = place // WIN, place % WIN
    far, rest = rest // 72, rest % 72
    half, pair = win // 2, win % 2
    second = rest // 36
    row, col = (rest // 12) % 3, rest % 12
    near_row = 3 * half + row
    far_row = jnp.where(half == 0, row - 3, row + 6)
    lat = first_lat + jnp.where(far == 1, far_row, near_row)
    top = (pair == 1) & (second == 1)
    region = jnp.where(top, 2.0, 0.0) + jnp.where(col < 6, 1.0, 0.0)
    inside = (lat >= 0) & (lat < extent[0]) & (col < extent[1])
    return plain, jnp.where(inside, region, -1.0)


def exchange(first, second):
    count = lax.axis_size("band")
    up = [(i, i + 1) for i in range(count - 1)]
    down = [(i + 1, i) for i in range(count - 1)]
    return lax.ppermute(second, "band", up), lax.ppermute(first, "band", down)


def shift_query_codes(region, split):
    parts = []
    for lane, lanes, n_heads in split:
        total = 128 * columns_of(n_heads, 72)
        tiled = np.tile(region, (1, n_heads))
        parts.append(np.pad(tiled, ((0, 0), (0, total - tiled.shape[1]))))
    return jnp.asarray(np.concatenate(parts, 1)[:, None, :], F32)


WIDTHS = {"enc": (D_ENC, ENC_SPLIT), "trunk": (D_TRUNK, TRUNK_SPLIT)}
FORWARD_ORDER = ("norm_one", "qkv", "proj", "norm_two", "up", "down")
BACKWARD_ORDER = ("down", "up", "norm_two", "proj", "qkv", "norm_one")


def compute(weights, source, goal, codes, count):
    to_win, region = fixed_tables()
    order = {"to_win": jnp.asarray(to_win, BF16), "to_tok": jnp.asarray(to_win.T, BF16)}
    grads = {}

    def tables(tower, names):
        split = WIDTHS[tower][1]
        found = {
            "plain_key": codes[0],
            "shift_key": codes[1],
            "plain_query": jnp.zeros((1, probs_width(split, WIN)), F32),
            "shift_query": shift_query_codes(region, split),
        } | order
        return prefixed("c_", {name: found[name] for name in names})

    PLAIN = ("plain_key", "plain_query", "to_win")
    SHIFTED = ("shift_key", "shift_query", "to_tok")

    def of(key, group):
        array = weights[key]
        if group is None:
            return array
        return (array, lambda ref: ref.at[group], array.shape[1:])

    def block(tower, layer, group, names, with_next=False):
        found = {name: of((tower, layer, name), group) for name in names}
        if with_next:
            found["norm_next"] = of((tower, layer + 1, "norm_one"), group)
        return prefixed("w_", found)

    def src(group):
        lanes = pl.ds(PIN * group, PIN)
        return (source, lambda ref: ref.at[:, lanes], (TOKENS, PIN))

    def plain_out(width, split):
        return saved_outs(width, split, False) | {
            "x_out": ((TOKENS, width), F32),
            "near_a": ((WIN, width), BF16),
            "near_b": ((WIN, width), BF16),
        }

    def enc_plain(group):
        width, split = WIDTHS["enc"]

        def body(r):
            first = nn(r["src"][...], r["embed"][...])
            plain_forward(
                first, part(r, "w_"), part(r, "s_"), part(r, "c_"), part(r, "t_"), split, width
            )

        found = launch(
            "enc_plain", body,
            {"src": src(group), "embed": of(("enc", -1, "embed"), group)}
            | block("enc", 0, group, FORWARD_ORDER, True) | tables("enc", PLAIN),
            prefixed("s_", plain_out(width, split)), prefixed("t_", spare(width, split, False, False)),
        )
        return {key[2:]: value for key, value in found.items()}

    def enc_shifted(group, before, far):
        width, split = WIDTHS["enc"]

        def body(r):
            r["x_out"][...] = shifted_forward(
                r["x_in"], (r["near_a"], r["near_b"]), (r["far_a"], r["far_b"]),
                part(r, "w_"), part(r, "s_"), part(r, "c_"), part(r, "t_"), split, width,
            )

        found = launch(
            "enc_shifted", body,
            {"near_a": before["near_a"], "near_b": before["near_b"], "far_a": far[0], "far_b": far[1]}
            | block("enc", 1, group, FORWARD_ORDER[1:]) | tables("enc", SHIFTED)
            | {"x_in": before["x_out"]},
            prefixed("s_", saved_outs(width, split, True)) | {"x_out": ((TOKENS, width), F32)},
            prefixed("t_", spare(width, split, True, False)),
        )
        saved = {key[2:]: value for key, value in found.items() if key.startswith("s_")}
        return saved, found["x_out"]

    def trunk_plain(left, right):
        width, split = WIDTHS["trunk"]

        def body(r):
            joined = jnp.concatenate([r["left"][...], r["right"][...]], 1).astype(BF16)
            r["joined"][...] = joined
            plain_forward(
                nn(joined, r["joining"][...]), part(r, "w_"), part(r, "s_"), part(r, "c_"),
                part(r, "t_"), split, width,
            )

        found = launch(
            "trunk_plain", body,
            {"left": left, "right": right, "joining": weights["trunk", -1, "joining"]}
            | block("trunk", 0, None, FORWARD_ORDER, True) | tables("trunk", PLAIN),
            {"joined": ((TOKENS, 2 * D_ENC), BF16)} | prefixed("s_", plain_out(width, split)),
            prefixed("t_", spare(width, split, False, False)),
        )
        return {key.removeprefix("s_"): value for key, value in found.items()}

    def trunk_top(before, far):
        width, split = WIDTHS["trunk"]

        def body(r):
            w, s, c, t = part(r, "w_"), part(r, "s_"), part(r, "c_"), part(r, "t_")
            last = shifted_forward(
                r["x_in"], (r["near_a"], r["near_b"]), (r["far_a"], r["far_b"]),
                w, s, c, t, split, width,
            )
            grad = loss_part(last, r["goal"], c, r["count"], part(r, "h_"), part(r, "d_"))
            shifted_backward(grad, w, s, part(r, "f_"), part(r, "b_"), c, t, split, width)

        kept = saved_outs(width, split, True)
        reused = ("mixed", "normed_two", "active")
        top = {name: weights["top", -1, name] for name in ("decode", "head", "scale")}
        found = launch(
            "trunk_top", body,
            {"near_a": before["near_a"], "near_b": before["near_b"], "far_a": far[0], "far_b": far[1]}
            | block("trunk", 1, None, FORWARD_ORDER[1:])
            | tables("trunk", SHIFTED + ("to_win", "plain_key"))
            | {"x_in": before["x_out"]}
            | prefixed("h_", {"final": weights["trunk", -1, "final"]} | top)
            | {"goal": goal, "count": count},
            prefixed("s_", {name: kept[name] for name in reused})
            | prefixed("f_", flow_shapes(width, True)) | prefixed("b_", rim_outs(width))
            | prefixed("d_", {
                "final": ((2, width), F32), "decode": ((GROUPS, D_TRUNK, D_ENC), BF16),
                "head": ((GROUPS, D_ENC, PIN), BF16), "scale": ((GROUPS, PIN), F32),
                "loss": ((1, PIN), F32),
            }),
            prefixed("s_", {name: kept[name] for name in kept if name not in reused})
            | prefixed("t_", spare(width, split, True, True)),
        )
        grads["trunk", -1, "final", None] = found["d_final"]
        for name in ("decode", "head", "scale"):
            grads["top", -1, name, "all"] = found["d_" + name]
        grads["trunk", 1, "norm_two", None] = found["b_norm_two"]
        return found

    def trunk_top_weights(before, far, found):
        width, split = WIDTHS["trunk"]

        def body(r):
            shifted_weights(
                (r["near_a"], r["near_b"]), (r["far_a"], r["far_b"]), part(r, "s_"), part(r, "f_"),
                part(r, "d_"), width,
            )

        results = launch(
            "trunk_top_weights", body,
            {key: found[key] for key in found if key[:2] in ("s_", "f_")}
            | {"near_a": before["near_a"], "near_b": before["near_b"], "far_a": far[0], "far_b": far[1]},
            prefixed("d_", weight_grads(width)), {},
        )
        for key, grad in results.items():
            grads["trunk", 1, key[2:], None] = grad

    def enc_shifted_back(group, grad, before, far, saved):
        width, split = WIDTHS["enc"]

        def body(r):
            s, f = part(r, "s_"), part(r, "f_")
            shifted_backward(
                r["grad"][...], part(r, "w_"), s, f, part(r, "b_"), part(r, "c_"), part(r, "t_"),
                split, width,
            )
            shifted_weights(
                (r["near_a"], r["near_b"]), (r["far_a"], r["far_b"]), s, f, part(r, "d_"), width
            )

        found = launch(
            "enc_shifted_back", body,
            {"grad": grad} | block("enc", 1, group, BACKWARD_ORDER[:-1])
            | prefixed("s_", {name: saved[name] for name in (
                "raised", "middle", "packed", "packed_far", "probs", "active", "normed_two", "mixed")})
            | tables("enc", SHIFTED + ("to_win",))
            | {"near_a": before["near_a"], "near_b": before["near_b"], "far_a": far[0], "far_b": far[1]},
            prefixed("b_", rim_outs(width)) | prefixed("d_", weight_grads(width)),
            prefixed("t_", spare(width, split, True, True)) | prefixed("f_", flow_shapes(width, True)),
        )
        grads["enc", 1, "norm_two", group] = found["b_norm_two"]
        for name in weight_grads(width):
            grads["enc", 1, name, group] = found["d_" + name]
        return found

    def plain_back(tower, group, back, arrived, saved, extra_ins, extra_outs, tail):
        width, split = WIDTHS[tower]

        def body(r):
            grad = plain_backward(
                part(r, "g_"), (r["arrived_a"], r["arrived_b"]), part(r, "w_"), part(r, "s_"),
                part(r, "f_"), part(r, "d_"), part(r, "c_"), part(r, "t_"), split, width,
            )
            tail(r, grad.astype(BF16))

        gains = {name: ((2, width), F32) for name in ("norm_next", "norm_one", "norm_two")}
        found = launch(
            tower + "_plain_back", body,
            {"g_near": back["b_grad_near"], "c_to_tok": order["to_tok"]}
            | {"arrived_a": arrived[0], "arrived_b": arrived[1], "s_x_out": saved["x_out"]}
            | {"g_middle": back["b_grad_middle"]}
            | {"w_norm_next": of((tower, 1, "norm_one"), group)}
            | block(tower, 0, group, BACKWARD_ORDER)
            | prefixed("s_", {name: saved[name] for name in (
                "raised", "middle", "active", "normed_two", "mixed", "packed", "probs", "normed", "x_in")})
            | tables(tower, ("plain_key", "plain_query")) | extra_ins,
            prefixed("d_", gains | weight_grads(width)) | extra_outs,
            prefixed("t_", spare(width, split, False, True)) | prefixed("f_", flow_shapes(width, False)),
        )
        grads[tower, 1, "norm_one", group] = found["d_norm_next"]
        for name in tuple(weight_grads(width)) + ("norm_one", "norm_two"):
            grads[tower, 0, name, group] = found["d_" + name]
        return found

    def join_tail(r, grad):
        r["d_joining"][...] = tn(r["joined"][...], grad).astype(BF16)
        back = nt(grad, r["joining"][...])
        r["left"][...] = back[:, 0:D_ENC]
        r["right"][...] = back[:, D_ENC:]

    def embed_tail(r, grad):
        r["d_embed"][...] = tn(r["src"][...], grad).astype(BF16)

    groups = range(GROUPS)
    plain = [enc_plain(group) for group in groups]
    far = [exchange(plain[group]["near_a"], plain[group]["near_b"]) for group in groups]
    shifted = [enc_shifted(group, plain[group], far[group]) for group in groups]
    trunk = trunk_plain(shifted[0][1], shifted[1][1])
    trunk_far = exchange(trunk["near_a"], trunk["near_b"])
    top = trunk_top(trunk, trunk_far)
    arrived = exchange(top["b_rim_a"], top["b_rim_b"])
    trunk_top_weights(trunk, trunk_far, top)
    joined = plain_back(
        "trunk", None, top, arrived, trunk,
        {"joined": trunk["joined"], "joining": weights["trunk", -1, "joining"]},
        {"left": ((TOKENS, D_ENC), F32), "right": ((TOKENS, D_ENC), F32),
         "d_joining": ((GROUPS * D_ENC, D_TRUNK), BF16)},
        join_tail,
    )
    grads["trunk", -1, "joining", None] = joined["d_joining"]
    backs = [
        enc_shifted_back(group, joined[side], plain[group], far[group], shifted[group][0])
        for group, side in zip(groups, ("left", "right"))
    ]
    for group in groups:
        arrived = exchange(backs[group]["b_rim_a"], backs[group]["b_rim_b"])
        found = plain_back(
            "enc", group, backs[group], arrived, plain[group], {"src": src(group)},
            {"d_embed": ((PIN, D_ENC), BF16)}, embed_tail,
        )
        grads["enc", -1, "embed", group] = found["d_embed"]
    return top["d_loss"], grads


def stacked_key(label_key):
    tower, group, layer, name = label_key
    return (tower, layer, name), (group if tower in ("enc", "top") else None)


BLOCK_ELEMENTS = 2048


def share_rows(n_own):
    blocks = -(-(n_own + BLOCK_ELEMENTS - 1) // BLOCK_ELEMENTS) + 1
    return 16 * 3 * (-(-blocks // 3))


def first_row(n_own, device):
    return (n_own * device // BLOCK_ELEMENTS) * 16


def grouped_pieces():
    found = {}
    for label_key, dims_shape, offset in placed():
        key, group = stacked_key(label_key)
        found.setdefault(key, (dims_shape, []))[1].append((group, offset // 128))
    return [(key, places, dims_shape) for key, (dims_shape, places) in found.items()]


def is_gain(key):
    return key[2] in ("norm_one", "norm_two", "final")


def stacked_shape(places, dims_shape):
    if len(dims_shape) == 1:
        return (len(places),) + dims_shape
    return dims_shape if places[0][0] is None else (len(places),) + dims_shape


def turned(values):
    return pltpu.roll(values, 64, 1)


def lower_half(values):
    return lax.broadcasted_iota(jnp.int32, values.shape, 1) < 64


def read_gain(flat, offset, width, out):
    if width % 128 == 0:
        count = width // 128
        for row in range(2):
            for tile in range(count):
                at = offset + row * count + tile
                out[row : row + 1, 128 * tile : 128 * tile + 128] = flat[at : at + 1, :]
        return
    rows = [flat[offset + place : offset + place + 1, :] for place in range(3)]
    out[0:1, 0:128] = rows[0]
    out[0:1, 128:192] = rows[1][:, 0:64]
    out[1:2, 0:128] = jnp.where(lower_half(rows[1]), turned(rows[1]), turned(rows[2]))
    out[1:2, 128:192] = rows[2][:, 64:128]


def read_matrix(flat, offset, shape, out, wide_scr):
    height, width = shape
    step = 64
    if width % 128 == 0:
        count = width // 128

        def body(index, carry):
            row = pl.multiple_of(index * step, step)
            for tile in range(count):
                start = offset + tile + row * count
                piece = flat[pl.ds(start, step, stride=count), :]
                out[pl.ds(row, step), 128 * tile : 128 * tile + 128] = piece.astype(BF16)
            return carry

        lax.fori_loop(0, height // step, body, 0)
        return
    half = width // 128
    period = 2 * half + 1

    def body(index, carry):
        row = pl.multiple_of(index * step, step)
        start = offset + (row // 2) * period
        rows = [flat[pl.ds(start + place, step // 2, stride=period), :] for place in range(period)]
        late = [turned(rows[half + place]) for place in range(half + 1)]
        for tile in range(half + 1):
            odd_rows = late[tile]
            if tile < half:
                odd_rows = jnp.where(lower_half(late[tile]), late[tile], late[tile + 1])
            wide_scr[pl.ds(step * tile, step // 2, stride=2), :] = rows[tile]
            wide_scr[pl.ds(step * tile + 1, step // 2, stride=2), :] = odd_rows
            end = min(128, width - 128 * tile)
            tile_rows = wide_scr[step * tile : step * (tile + 1), 0:end]
            out[pl.ds(row, step), 128 * tile : 128 * tile + end] = tile_rows.astype(BF16)
        return carry

    lax.fori_loop(0, height // step, body, 0)


def write_gain(flat, offset, width, values):
    if width % 128 == 0:
        count = width // 128
        for row in range(2):
            for tile in range(count):
                at = offset + row * count + tile
                flat[at : at + 1, :] = values[row : row + 1, 128 * tile : 128 * tile + 128]
        return
    flat[offset : offset + 1, :] = values[0:1, 0:128]
    first, second = values[1:2, 0:64], values[1:2, 64:192]
    flat[offset + 1 : offset + 2, :] = jnp.concatenate([values[0:1, 128:192], first], 1)
    flat[offset + 2 : offset + 3, :] = second


def write_matrix(flat, offset, shape, source, wide_scr):
    height, width = shape
    step = 64
    if width % 128 == 0:
        count = width // 128

        def body(index, carry):
            row = pl.multiple_of(index * step, step)
            for tile in range(count):
                start = offset + tile + row * count
                piece = source[pl.ds(row, step), 128 * tile : 128 * tile + 128]
                flat[pl.ds(start, step, stride=count), :] = piece.astype(F32)
            return carry

        lax.fori_loop(0, height // step, body, 0)
        return
    half = width // 128
    period = 2 * half + 1

    def body(index, carry):
        row = pl.multiple_of(index * step, step)
        start = offset + (row // 2) * period
        for tile in range(half + 1):
            end = min(128, width - 128 * tile)
            tile_rows = source[pl.ds(row, step), 128 * tile : 128 * tile + end].astype(F32)
            wide_scr[step * tile : step * (tile + 1), 0:end] = tile_rows
        early = [wide_scr[pl.ds(step * tile, step // 2, stride=2), :] for tile in range(half + 1)]
        late = [
            turned(wide_scr[pl.ds(step * tile + 1, step // 2, stride=2), :])
            for tile in range(half + 1)
        ]
        low = lower_half(late[0])
        rows = early[:half] + [jnp.where(low, early[half], late[0])]
        rows += [jnp.where(low, late[tile], late[tile + 1]) for tile in range(half)]
        for place, value in enumerate(rows):
            flat[pl.ds(start + place, step // 2, stride=period), :] = value
        return carry

    lax.fori_loop(0, height // step, body, 0)


def flat_rows(n_own, n_devices):
    return first_row(n_own, n_devices - 1) + share_rows(n_own)


def flat_scratch(n_own, n_devices):
    return {"flat": ((flat_rows(n_own, n_devices), 128), F32), "wide": ((5 * 64, 128), F32)}


def unpack_weights(gathered, n_own):
    pieces = grouped_pieces()
    n_devices, rows, unused = gathered.shape
    n_batch = 8
    batch = n_devices // n_batch
    step = rows // 6
    outs = {}
    for key, places, dims_shape in pieces:
        small = is_gain(key) or len(dims_shape) == 1
        outs[key] = (stacked_shape(places, dims_shape), F32 if small else BF16)

    def body(r):
        flat, wide, shares, source = r["flat"], r["wide"], r["shares"], r["raw"][0]
        copies = []
        for index in range(n_batch):
            span = pl.ds(index * batch, batch)
            copy = pltpu.make_async_copy(source.at[span], shares.at[span], r["sems"][index])
            copy.start()
            copies.append(copy)

        def place(device, carry):
            start = pl.multiple_of((n_own * device // BLOCK_ELEMENTS) * 16, 16)
            kept = jnp.where(device > 0, flat[pl.ds(start, 16), :], 0.0)
            flat[pl.ds(start, 16), :] = kept + shares[device, 0:16, :].astype(F32)
            flat[pl.ds(start + 16, step - 16), :] = shares[device, 16:step, :].astype(F32)
            for index in range(1, 6):
                at = pl.ds(start + index * step, step)
                flat[at, :] = shares[device, index * step : (index + 1) * step, :].astype(F32)
            return carry

        for index in range(n_batch):
            copies[index].wait()
            lax.fori_loop(index * batch, (index + 1) * batch, place, 0)
        for key, places, dims_shape in pieces:
            for group, offset in places:
                view = r[key] if group is None or len(dims_shape) == 1 else r[key].at[group]
                if len(dims_shape) == 1:
                    view[group : group + 1, :] = flat[offset : offset + 1, :]
                elif is_gain(key):
                    read_gain(flat, offset, dims_shape[1], view)
                else:
                    read_matrix(flat, offset, dims_shape, view, wide)
            r[key].send()

    return launch(
        "unpack", body, {}, outs,
        {"shares": (gathered.shape, BF16)} | flat_scratch(n_own, n_devices),
        limit=60 << 20, raw=(gathered,), sems=n_batch,
    )


def cuts_of(rows):
    blocks = rows // 16
    last = blocks // 5
    first = (blocks - last) // 2
    return 16 * first, 16 * (blocks - last - first), 16 * last


def step_of(rows):
    blocks = rows // 16
    return 16 * max(count for count in range(1, 13) if blocks % count == 0)


def pack_grads(grads, n_own, n_devices, core):
    pieces = grouped_pieces()
    cuts = cuts_of(share_rows(n_own))
    n_chips = n_devices // 2
    used = sum(len(places) * math.prod(dims_shape) for key, places, dims_shape in pieces) // 128
    outs = {}
    for side in ("kept", "sent"):
        for index, rows in enumerate(cuts):
            outs[side, index] = ((n_chips, rows, 128), BF16)

    def body(r):
        flat, wide, core = r["flat"], r["wide"], r["scalars"][0]
        flat[used:, :] = jnp.zeros((flat.shape[0] - used, 128), F32)
        for key, places, dims_shape in pieces:
            for group, offset in places:
                if len(dims_shape) == 1:
                    flat[offset : offset + 1, :] = r[key + ("all",)][group : group + 1, :]
                    continue
                source = r[key + ("all",)].at[group] if key[0] == "top" else r[key + (group,)]
                source = source.ready() if isinstance(source, Held) else source
                if is_gain(key):
                    write_gain(flat, offset, dims_shape[1], source)
                else:
                    write_matrix(flat, offset, dims_shape, source, wide)

        def chip(index, carry):
            for side, device in (("sent", 2 * index + 1 - core[0]), ("kept", 2 * index + core[0])):
                start = pl.multiple_of((n_own * device // BLOCK_ELEMENTS) * 16, 16)
                done = 0
                for which, rows in enumerate(cuts):
                    out = r[side, which]
                    step = step_of(rows)
                    for row in range(0, rows, step):
                        values = flat[pl.ds(start + done + row, step), :]
                        out.ref[index, row : row + step, :] = values.astype(BF16)
                    done += rows
                    pltpu.make_async_copy(out.ref.at[index], out.far.at[index], out.sem).start()
            return carry

        lax.fori_loop(0, n_chips, chip, 0)
        for key in outs:
            r[key].sent = True

    found = launch(
        "pack", body, grads, outs, flat_scratch(n_own, n_devices),
        limit=60 << 20, scalars=(core.reshape(1),),
    )
    return [[found[side, index] for index in range(3)] for side in ("kept", "sent")]


class Torus:
    def __init__(self):
        self.totals = {"dp": lax.axis_size("dp"), "band": lax.axis_size("band")}
        depth = min(4, self.totals["dp"])
        across = self.totals["dp"] // depth
        self.axes = {
            "z": (depth, across, "dp"),
            "x": (across, 1, "dp"),
            "y": (self.totals["band"] // 2, 2, "band"),
            "core": (2, 1, "band"),
        }

    def size(self, axis):
        return self.axes[axis][0]

    def place(self, axis):
        count, stride, name = self.axes[axis]
        return lax.axis_index(name) // stride % count

    def move(self, values, axis, by):
        count, stride, name = self.axes[axis]
        pairs = []
        for place in range(self.totals[name]):
            at = place // stride % count
            pairs.append((place, place + ((at + by) % count - at) * stride))
        return lax.ppermute(values, name, pairs)


def scatter_terms(torus, terms, dims, axis):
    dim = dims.index(axis)
    place = torus.place(axis)
    arrived = []
    for by in range(1, torus.size(axis)):
        other = (place + by) % torus.size(axis)
        pieces = [lax.dynamic_index_in_dim(term, other, dim, keepdims=False) for term in terms]
        total = sum(piece.astype(F32) for piece in pieces).astype(BF16)
        arrived.append(torus.move(total, axis, by))
    own = [lax.dynamic_index_in_dim(term, place, dim, keepdims=False) for term in terms]
    return own + arrived, [name for name in dims if name != axis]


SCATTER_ORDERS = (("y", "x", "z"), ("x", "y", "z"), ("z", "x", "y"))


def scatter_sum(kept, sent):
    torus = Torus()
    dims = ["z", "x", "y"]
    shape = tuple(torus.size(axis) for axis in dims)
    sequence = (2, 0, 1)
    state = {}
    for part in sequence:
        near = kept[part].reshape(shape + kept[part].shape[1:])
        far = sent[part].reshape(shape + sent[part].shape[1:])
        state[part] = ([near, torus.move(far, "core", 1)], dims)
    for step in range(3):
        for part in sequence:
            terms, left = state[part]
            state[part] = scatter_terms(torus, terms, left, SCATTER_ORDERS[part][step])
    return [sum(term.astype(F32) for term in state[part][0]) for part in range(3)]


def all_sum(values):
    for axis in ("band", "dp"):
        count = lax.axis_size(axis)
        bit = 1
        while bit < count:
            pairs = [(i, i ^ bit) for i in range(count)]
            values = values + lax.ppermute(values, axis, pairs)
            bit *= 2
    return values


def shards(inputs, targets, crop_extent, master, moment_one, moment_two, step_count):
    n_own = master.shape[0]
    n_bands = lax.axis_size("band")
    n_devices = lax.axis_size("dp") * n_bands
    rows = share_rows(n_own)
    device = lax.axis_index("dp") * n_bands + lax.axis_index("band")
    shift = (n_own * device) % BLOCK_ELEMENTS
    extent = crop_extent[0]
    share = lax.dynamic_update_slice(jnp.zeros((rows * 128,), BF16), master.astype(BF16), (shift,))
    share = lax.dynamic_update_slice(share, extent.astype(BF16), ((rows - 1) * 128,))
    gathered = lax.all_gather(share.reshape(rows, 128), ("dp", "band"), axis=0, tiled=False)
    extents = gathered[::n_bands, rows - 1, 0:2].astype(F32)
    weights = unpack_weights(gathered, n_own)
    n_rows, n_levels = inputs.shape[1], inputs.shape[2]
    source = inputs[0].transpose(1, 0, 2, 3).reshape(TOKENS, GROUPS * PIN)
    goal = targets[0].transpose(1, 0, 2, 3).reshape(TOKENS, GROUPS * PIN)
    first_lat = lax.axis_index("band") * n_rows
    norm_count = jnp.sum(extents[:, 0] * extents[:, 1]) * (n_levels * GROUPS * PIN)
    loss_row, grads = compute(
        weights, source, goal, key_codes(extent, first_lat), jnp.full((1, PIN), norm_count)
    )
    kept, sent = pack_grads(grads, n_own, n_devices, lax.axis_index("band") % 2)
    owned = jnp.concatenate(scatter_sum(kept, sent), 0)
    grad_shard = lax.dynamic_slice(owned.reshape(-1), (shift,), (n_own,))
    shard_square = jnp.sum(grad_shard * grad_shard)
    lanes = lax.broadcasted_iota(jnp.int32, (8, 128), 1)
    both = jnp.where(lanes < 64, shard_square, jnp.sum(loss_row))
    both = all_sum(both)
    grad_norm = jnp.sqrt(both[0, 0])
    loss_total = both[0, 64]
    factor_clip = jnp.minimum(1.0, CLIP_LEVEL / (grad_norm + 1e-06))
    clipped = grad_shard * factor_clip
    new_one = BETA_ONE * moment_one + (1.0 - BETA_ONE) * clipped
    new_two = BETA_TWO * moment_two + (1.0 - BETA_TWO) * clipped * clipped
    step_value = step_count[0].astype(F32)
    fix_one = 1.0 - jnp.power(BETA_ONE, step_value)
    fix_two = 1.0 - jnp.power(BETA_TWO, step_value)
    update = new_one / fix_one / (jnp.sqrt(new_two / fix_two) + ADAM_EPS) + WEIGHT_DECAY * master
    new_master = master - LEARN_RATE * update
    return (
        new_master,
        new_one,
        new_two,
        new_master.astype(BF16),
        loss_total / norm_count,
        grad_norm,
    )


def solution(mesh):
    in_specs = (
        P("dp", "band", None, None, None),
        P("dp", "band", None, None, None),
        P("dp", None),
        P(("dp", "band")),
        P(("dp", "band")),
        P(("dp", "band")),
        P(),
    )
    out_specs = (
        P(("dp", "band")),
        P(("dp", "band")),
        P(("dp", "band")),
        P(("dp", "band")),
        P(),
        P(),
    )
    return jax.shard_map(shards, mesh=mesh, in_specs=in_specs, out_specs=out_specs, check_vma=False)
```

```python
import functools
import math

import jax
import jax.numpy as jnp
import numpy as np
from jax import lax
from jax.experimental import pallas as pl
from jax.experimental.pallas import tpu as pltpu
from jax.sharding import PartitionSpec as P

D_ENC = 192
HEADS_ENC = 6
D_TRUNK = 384
HEADS_TRUNK = 12
PIN = 128
GROUPS = 2
HEAD_DIM = 32
SCALE = HEAD_DIM ** (-0.5)

NEG_FILL = -1000000000.0
BETA_ONE = 0.5
BETA_TWO = 0.5
LEARN_RATE = 0.01
WEIGHT_DECAY = 0.1
CLIP_LEVEL = 0.07
ADAM_EPS = 1e-08

F32 = jnp.float32
BF16 = jnp.bfloat16
TOKENS = 288
AHEAD = 8 << 20
SPAN = 384
SPAN_BACK = 384
WIN = 144
ENC_SPLIT = ((0, 192, 6),)
TRUNK_SPLIT = ((0, 256, 8), (256, 128, 4))


def block_layout(path_name, group_id, layer_id, n_width):
    prefix = (path_name, group_id, layer_id)
    return [
        (prefix + ("norm_one",), (2, n_width)),
        (prefix + ("qkv",), (n_width, 3 * n_width)),
        (prefix + ("proj",), (n_width, n_width)),
        (prefix + ("norm_two",), (2, n_width)),
        (prefix + ("up",), (n_width, 4 * n_width)),
        (prefix + ("down",), (4 * n_width, n_width)),
    ]


def layout():
    entries = []
    for group_id in range(GROUPS):
        entries.append((("enc", group_id, -1, "embed"), (PIN, D_ENC)))
        for layer_id in range(2):
            entries += block_layout("enc", group_id, layer_id, D_ENC)
        entries.append((("top", group_id, -1, "decode"), (D_TRUNK, D_ENC)))
        entries.append((("top", group_id, -1, "head"), (D_ENC, PIN)))
        entries.append((("top", group_id, -1, "scale"), (PIN,)))
    entries.append((("trunk", 0, -1, "joining"), (GROUPS * D_ENC, D_TRUNK)))
    for layer_id in range(2):
        entries += block_layout("trunk", 0, layer_id, D_TRUNK)
    entries.append((("trunk", 0, -1, "final"), (2, D_TRUNK)))
    return entries


def placed():
    offset = 0
    for label_key, dims_shape in layout():
        yield label_key, dims_shape, offset
        offset += math.prod(dims_shape)


def nn(left, right):
    return jnp.dot(left, right, preferred_element_type=F32)


def nt(left, right):
    return lax.dot_general(left, right, (((1,), (1,)), ((), ())), preferred_element_type=F32)


def tn(left, right):
    return lax.dot_general(left, right, (((0,), (0,)), ((), ())), preferred_element_type=F32)


def unit_rows(values):
    centre = values - jnp.mean(values, -1, keepdims=True)
    inverse = lax.rsqrt(jnp.mean(centre * centre, -1, keepdims=True) + 1e-05)
    return centre * inverse, inverse


def norm_forward(values, gain_ref):
    unit, unused = unit_rows(values)
    return unit * gain_ref[0:1, :] + gain_ref[1:2, :]


def norm_backward(values, gain_ref, grad_normed):
    unit, inverse = unit_rows(values)
    grad_gain = jnp.sum(grad_normed * unit, 0, keepdims=True)
    grad_shift = jnp.sum(grad_normed, 0, keepdims=True)
    grad_unit = grad_normed * gain_ref[0:1, :]
    along = jnp.mean(grad_unit * unit, -1, keepdims=True)
    grad_values = inverse * (grad_unit - jnp.mean(grad_unit, -1, keepdims=True) - unit * along)
    return grad_values, jnp.concatenate([grad_gain, grad_shift], 0)


GELU_A = math.sqrt(2.0 / math.pi)
GELU_B = 0.044715


def gelu(values):
    inner = jnp.tanh(GELU_A * (values + GELU_B * (values * values * values)))
    return values * (0.5 * (1.0 + inner))


def gelu_slope(values):
    square = values * values
    inner = jnp.tanh(GELU_A * (values + GELU_B * (square * values)))
    steep = (1.0 - inner * inner) * (GELU_A + (3.0 * GELU_B * GELU_A) * square)
    return 0.5 * (1.0 + inner) + 0.5 * values * steep


def head_lanes(rows, lanes, head):
    lane = lax.broadcasted_iota(jnp.int32, (rows, lanes), 1)
    return (lane >= HEAD_DIM * head) & (lane < HEAD_DIM * (head + 1))


def columns_of(n_heads, n_query):
    return -(-n_heads * n_query // 128)


def spread_heads(rows_value, n_heads, out_ref):
    n_query, lanes = rows_value.shape
    wide = rows_value.astype(F32)
    for head in range(n_heads):
        kept = jnp.where(head_lanes(n_query, lanes, head), wide, 0.0).astype(BF16)
        out_ref[head * n_query : (head + 1) * n_query, 0:lanes] = kept
    total = 128 * columns_of(n_heads, n_query)
    if total > n_heads * n_query:
        out_ref[n_heads * n_query : total, 0:lanes] = jnp.zeros(
            (total - n_heads * n_query, lanes), BF16
        )


def join_heads(spread_ref, n_heads, n_query, lanes):
    joined = spread_ref[0:n_query, 0:lanes]
    for head in range(1, n_heads):
        part = spread_ref[head * n_query : (head + 1) * n_query, 0:lanes]
        joined = jnp.where(head_lanes(n_query, lanes, head), part, joined)
    return joined


def same_code(key_code, query_code):
    count = query_code.shape[1] // 128
    return jnp.concatenate([key_code] * count, 1) == query_code


def attend_window(queries, key_rows, value_rows, key_code, query_code, probs_ref, q_scr, o_scr, split):
    n_query = queries.shape[0]
    outs = []
    at = 0
    for lane, lanes, n_heads in split:
        spread_heads(queries[:, lane : lane + lanes], n_heads, q_scr)
        keys = key_rows[:, lane : lane + lanes]
        values = value_rows[:, lane : lane + lanes]
        wide = 128 * columns_of(n_heads, n_query)
        for start in range(0, wide, SPAN):
            rows = slice(start, min(start + SPAN, wide))
            columns = slice(at + rows.start, at + rows.stop)
            scores = nt(keys, q_scr[rows, 0:lanes]) * SCALE
            scores = jnp.where(same_code(key_code, query_code[0:1, columns]), scores, NEG_FILL)
            raised = jnp.exp(scores - jnp.max(scores, 0, keepdims=True))
            probs = (raised * (1.0 / jnp.sum(raised, 0, keepdims=True))).astype(BF16)
            probs_ref[:, columns] = probs
            o_scr[rows, 0:lanes] = tn(probs, values)
        outs.append(join_heads(o_scr, n_heads, n_query, lanes))
        at += wide
    return jnp.concatenate(outs, 1) if len(outs) > 1 else outs[0]


def attend_window_back(
    queries, key_rows, value_rows, grad_rows, key_code, query_code, probs_ref, q_scr, g_scr, o_scr, s_scr, split
):
    n_query = queries.shape[0]
    out_q, out_k, out_v = [], [], []
    at = 0
    for lane, lanes, n_heads in split:
        n_col = columns_of(n_heads, n_query)
        spread_heads(queries[:, lane : lane + lanes], n_heads, q_scr)
        spread_heads(grad_rows[:, lane : lane + lanes], n_heads, g_scr)
        keys = key_rows[:, lane : lane + lanes]
        values = value_rows[:, lane : lane + lanes]
        wide = 128 * n_col
        for start in range(0, wide, SPAN_BACK):
            rows = slice(start, min(start + SPAN_BACK, wide))
            columns = slice(at + rows.start, at + rows.stop)
            grad_probs = nt(values, g_scr[rows, 0:lanes])
            probs = probs_ref[:, columns].astype(F32)
            along = jnp.sum(grad_probs * probs, 0, keepdims=True)
            grad_scores = probs * (grad_probs - along)
            allowed = same_code(key_code, query_code[0:1, columns])
            grad_scores = jnp.where(allowed, grad_scores, 0.0).astype(BF16)
            s_scr[:, rows] = grad_scores
            o_scr[rows, 0:lanes] = tn(grad_scores, keys)
        out_v.append(nn(probs_ref[:, at : at + wide], g_scr[0:wide, 0:lanes]))
        out_k.append(nn(s_scr[:, 0:wide], q_scr[0:wide, 0:lanes]) * SCALE)
        out_q.append(join_heads(o_scr, n_heads, n_query, lanes) * SCALE)
        at += wide
    if len(split) > 1:
        return tuple(jnp.concatenate(parts, 1) for parts in (out_q, out_k, out_v))
    return out_q[0], out_k[0], out_v[0]


class Queue:
    def __init__(self, copies, sizes, ahead):
        self.copies, self.sizes, self.ahead = copies, sizes, ahead
        self.started, self.reach = 0, 0
        self.advance(-1)

    def advance(self, index):
        limit = sum(self.sizes[: index + 1]) + self.ahead
        while self.started < len(self.copies) and (self.started <= index or self.reach < limit):
            self.copies[self.started].start()
            self.reach += self.sizes[self.started]
            self.started += 1


class Held:
    def __init__(self, ref, queue, index):
        self.ref, self.queue, self.index = ref, queue, index

    def ready(self):
        if self.queue is not None:
            self.queue.advance(self.index)
            self.queue.copies[self.index].wait()
            self.queue = None
        return self.ref

    def __getitem__(self, index):
        return self.ready()[index]

    @property
    def at(self):
        return self.ready().at

    @property
    def shape(self):
        return self.ref.shape


class Made:
    def __init__(self, ref, copy):
        self.ref, self.copy, self.sent = ref, copy, False

    def __getitem__(self, index):
        return self.ref[index]

    def __setitem__(self, index, value):
        self.ref[index] = value

    @property
    def at(self):
        return self.ref.at

    @property
    def shape(self):
        return self.ref.shape

    @property
    def dtype(self):
        return self.ref.dtype

    def send(self):
        if not self.sent:
            self.copy.start()
            self.sent = True


class Refs:
    def __init__(self, **refs):
        self.__dict__.update(refs)


def send(*refs):
    for ref in refs:
        if isinstance(ref, Made):
            ref.send()


def rest_forward(resid_in, w, s):
    middle = resid_in + nn(s.mixed[...], w.proj[...])
    s.middle[...] = middle
    normed = norm_forward(middle, w.norm_two).astype(BF16)
    s.normed_two[...] = normed
    send(s.mixed, s.middle, s.normed_two)
    for start in range(0, w.up.shape[1], 256):
        columns = slice(start, start + 256)
        s.raised[:, columns] = nn(normed, w.up[:, columns])
        for row in range(0, TOKENS, 96):
            piece = s.raised[row : row + 96, columns]
            s.active[row : row + 96, columns] = gelu(piece).astype(BF16)
    send(s.raised, s.active)
    return middle + nn(s.active[...], w.down[...])


def rest_backward(grad_out, w, s, flow, d_norm_two):
    grad_low = grad_out.astype(BF16)
    flow.low[...] = grad_low
    width = w.up.shape[1]
    for start in range(0, width, 256):
        columns = slice(start, start + 256)
        grad_active = nt(grad_low, w.down[start : start + 256, :])
        for row in range(0, TOKENS, 96):
            slope = gelu_slope(s.raised[row : row + 96, columns])
            flow.raised[row : row + 96, columns] = (
                slope * grad_active[row : row + 96, :]
            ).astype(BF16)
    grad_middle, grad_gain = norm_backward(
        s.middle[...], w.norm_two, nt(flow.raised[...], w.up[...])
    )
    d_norm_two[...] = grad_gain
    grad_middle = grad_out + grad_middle
    grad_branch = grad_middle.astype(BF16)
    flow.branch[...] = grad_branch
    send(flow.low, flow.raised, flow.branch, d_norm_two)
    return grad_middle, nt(grad_branch, w.proj[...]).astype(BF16)


def rest_weights(s, flow, d):
    for out, left, right in (
        (d.down, s.active, flow.low),
        (d.up, s.normed_two, flow.raised),
        (d.proj, s.mixed, flow.branch),
    ):
        out[...] = tn(left[...], right[...]).astype(out.dtype)
        send(out)


def plain_forward(first, w, s, tables, t, split, width):
    s.x_in[...] = first
    s.normed[...] = norm_forward(first, w.norm_one).astype(BF16)
    s.packed[...] = nn(s.normed[...], w.qkv[...]).astype(BF16)
    send(s.x_in, s.normed, s.packed)
    for win in range(2):
        rows = slice(WIN * win, WIN * (win + 1))
        s.mixed[rows, :] = attend_window(
            s.packed[rows, 0:width],
            s.packed[rows, width : 2 * width],
            s.packed[rows, 2 * width : 3 * width],
            tables.plain_key[rows, :],
            tables.plain_query,
            s.probs.at[win],
            t.q,
            t.o,
            split,
        ).astype(BF16)
    send(s.probs)
    last = rest_forward(first, w, s)
    s.x_out[...] = last
    ordered = nn(tables.to_win[...], norm_forward(last, w.norm_next).astype(BF16)).astype(BF16)
    s.near_a[...] = ordered[0:WIN]
    s.near_b[...] = ordered[WIN:]
    send(s.x_out, s.near_a, s.near_b)


def both(first, second):
    return jnp.concatenate([first[...], second[...]], 0)


def shifted_keys(s, win, width):
    rows = slice(72 * win, 72 * (win + 1))
    keys = jnp.concatenate([s.packed[rows, width : 2 * width], s.packed_far[rows, 0:width]], 0)
    values = jnp.concatenate([s.packed[rows, 2 * width :], s.packed_far[rows, width:]], 0)
    return s.packed[rows, 0:width], keys, values


def shifted_forward(x_in, near, far, w, s, tables, t, split, width):
    s.packed[...] = nn(both(*near), w.qkv[...]).astype(BF16)
    s.packed_far[...] = nn(both(*far), w.qkv[:, width:]).astype(BF16)
    send(s.packed, s.packed_far)
    for win in range(4):
        queries, keys, values = shifted_keys(s, win, width)
        t.m[72 * win : 72 * (win + 1), 0:width] = attend_window(
            queries, keys, values, tables.shift_key[WIN * win : WIN * (win + 1), :],
            tables.shift_query.at[win % 2], s.probs.at[win], t.q, t.o, split,
        )
    send(s.probs)
    s.mixed[...] = nn(tables.to_tok[...], t.m[:, 0:width].astype(BF16)).astype(BF16)
    return rest_forward(x_in[...], w, s)


def loss_part(values, goal, tables, count, w, d):
    low = norm_forward(values, w.final).astype(BF16)
    valid = tables.plain_key[...] + 1.0
    inverse_count = 1.0 / count[0:1, :]
    grad_low = None
    total = None
    for group in range(GROUPS):
        decode, head = w.decode[group], w.head[group]
        raised = nn(low, decode)
        active = gelu(raised).astype(BF16)
        predicted = nn(active, head)
        log_scale = w.scale[group : group + 1, :]
        error = predicted - goal[:, PIN * group : PIN * (group + 1)].astype(F32)
        inverse_scale = jnp.exp(-log_scale)
        weighted = jnp.abs(error) * inverse_scale
        part = jnp.sum((weighted + log_scale) * valid, 0, keepdims=True)
        total = part if total is None else total + part
        direction = jnp.where(error > 0.0, 1.0, jnp.where(error < 0.0, -1.0, 0.0))
        grad_pred = (direction * inverse_scale * valid * inverse_count).astype(BF16)
        d.scale[group : group + 1, :] = (
            jnp.sum((1.0 - weighted) * valid, 0, keepdims=True) * inverse_count
        )
        d.head[group] = tn(active, grad_pred).astype(BF16)
        grad_raised = (gelu_slope(raised) * nt(grad_pred, head)).astype(BF16)
        d.decode[group] = tn(low, grad_raised).astype(BF16)
        back = nt(grad_raised, decode)
        grad_low = back if grad_low is None else grad_low + back
    d.loss[...] = total
    grad_values, d.final[...] = norm_backward(values, w.final, grad_low)
    send(d.scale, d.head, d.decode, d.loss, d.final)
    return grad_values


def shifted_backward(grad_out, w, s, flow, outs, tables, t, split, width):
    outs.grad_middle[...], grad_mixed = rest_backward(grad_out, w, s, flow, outs.norm_two)
    send(outs.grad_middle)
    grad_win = nn(tables.to_win[...], grad_mixed).astype(BF16)
    for win in range(4):
        rows = slice(72 * win, 72 * (win + 1))
        queries, keys, values = shifted_keys(s, win, width)
        grad_q, grad_k, grad_v = attend_window_back(
            queries, keys, values, grad_win[rows, :],
            tables.shift_key[WIN * win : WIN * (win + 1), :], tables.shift_query.at[win % 2],
            s.probs.at[win], t.q, t.g, t.o, t.s, split,
        )
        flow.near[rows, 0:width] = grad_q.astype(BF16)
        flow.near[rows, width : 2 * width] = grad_k[0:72].astype(BF16)
        flow.near[rows, 2 * width : 3 * width] = grad_v[0:72].astype(BF16)
        flow.far[rows, 0:width] = grad_k[72:144].astype(BF16)
        flow.far[rows, width : 2 * width] = grad_v[72:144].astype(BF16)
    rim = nt(flow.far[...], w.qkv[:, width:]).astype(BF16)
    outs.rim_a[...] = rim[0:WIN]
    outs.rim_b[...] = rim[WIN:]
    send(outs.rim_a, outs.rim_b, flow.near, flow.far)
    outs.grad_near[...] = nt(nn(tables.to_tok[...], flow.near[...]).astype(BF16), w.qkv[...])
    send(outs.grad_near)


def shifted_weights(near, far, s, flow, d, width):
    rest_weights(s, flow, d)
    near_rows, far_rows = both(*near), both(*far)
    d.qkv[:, 0:width] = tn(near_rows, flow.near[:, 0:width]).astype(BF16)
    d.qkv[:, width:] = (
        tn(near_rows, flow.near[:, width:]) + tn(far_rows, flow.far[...])
    ).astype(BF16)
    send(d.qkv)


def plain_backward(grad, arrived, w, s, flow, d, tables, t, split, width):
    grad_normed = grad.near[...] + nn(tables.to_tok[...], both(*arrived))
    grad_x, d.norm_next[...] = norm_backward(s.x_out[...], w.norm_next, grad_normed)
    grad_mid, grad_mixed = rest_backward(grad.middle[...] + grad_x, w, s, flow, d.norm_two)
    rest_weights(s, flow, d)
    for win in range(2):
        rows = slice(WIN * win, WIN * (win + 1))
        grads = attend_window_back(
            s.packed[rows, 0:width], s.packed[rows, width : 2 * width], s.packed[rows, 2 * width :],
            grad_mixed[rows, :], tables.plain_key[rows, :], tables.plain_query, s.probs.at[win],
            t.q, t.g, t.o, t.s, split,
        )
        for index, part in enumerate(grads):
            flow.near[rows, width * index : width * (index + 1)] = part.astype(BF16)
    near_grad = flow.near[...]
    d.qkv[...] = tn(s.normed[...], near_grad).astype(BF16)
    grad_first, d.norm_one[...] = norm_backward(s.x_in[...], w.norm_one, nt(near_grad, w.qkv[...]))
    send(d.norm_next, d.qkv, d.norm_one)
    return grad_mid + grad_first


def held(array):
    return pltpu.with_memory_space_constraint(array, pltpu.HBM)


def launch(name, body, ins, outs, scratch, limit=52 << 20, scalars=(), raw=(), sems=0, in_place=False):
    sources, views, shapes = [], [], []
    for value in ins.values():
        array, view, shape = value if isinstance(value, tuple) else (value, None, value.shape)
        sources.append(array)
        views.append(view)
        shapes.append(pltpu.VMEM(shape, array.dtype))
    n_in, n_out = len(ins), len(outs)
    n_first = len(scalars) + len(raw)
    own_sems = sems
    n_held = 0 if in_place else n_out

    def kernel(*refs):
        named = {"scalars": refs[: len(scalars)], "raw": refs[len(scalars) : n_first]}
        refs = refs[n_first:]
        far_in, far_out = refs[:n_in], refs[n_in : n_in + n_out]
        near = refs[n_in + n_out :]
        near_in, near_out = near[:n_in], near[n_in : n_in + n_held]
        spare, flags = near[n_in + n_held : -1], near[-1]
        named["sems"] = [flags.at[n_in + n_out + index] for index in range(own_sems)]
        copies, sizes = [], []
        for index, key in enumerate(ins):
            source = far_in[index] if views[index] is None else views[index](far_in[index])
            copies.append(pltpu.make_async_copy(source, near_in[index], flags.at[index]))
            sizes.append(math.prod(near_in[index].shape) * near_in[index].dtype.itemsize)
        queue = Queue(copies, sizes, AHEAD)
        for index, key in enumerate(ins):
            named[key] = Held(near_in[index], queue, index)
        for index, key in enumerate(outs):
            if in_place:
                named[key] = Made(None, None)
            else:
                copy = pltpu.make_async_copy(near_out[index], far_out[index], flags.at[n_in + index])
                named[key] = Made(near_out[index], copy)
            named[key].far, named[key].sem = far_out[index], flags.at[n_in + index]
        named.update(zip(scratch, spare))
        body(named)
        for key in ins:
            named[key].ready()
        for key in outs:
            named[key].send()
        for key in outs:
            named[key].copy.wait()

    results = pl.pallas_call(
        kernel,
        in_specs=[pl.BlockSpec(memory_space=pltpu.SMEM)] * len(scalars)
        + [pl.BlockSpec(memory_space=pl.ANY)] * (len(raw) + n_in),
        out_specs=[pl.BlockSpec(memory_space=pl.ANY)] * n_out,
        out_shape=[pltpu.HBM(shape, dtype) for shape, dtype in outs.values()],
        scratch_shapes=shapes
        + [pltpu.VMEM(shape, dtype) for shape, dtype in list(outs.values())[:n_held]]
        + [pltpu.VMEM(shape, dtype) for shape, dtype in scratch.values()]
        + [pltpu.SemaphoreType.DMA((n_in + n_out + sems,))],
        name=name,
        input_output_aliases={len(scalars) + at: at for at in range(len(raw))} if in_place else {},
        compiler_params=pltpu.CompilerParams(vmem_limit_bytes=limit),
    )(*scalars, *[held(array) for array in (*raw, *sources)])
    return dict(zip(outs, results))


def part(named, prefix):
    return Refs(**{key[len(prefix) :]: ref for key, ref in named.items() if key.startswith(prefix)})


def prefixed(prefix, values):
    return {prefix + key: value for key, value in values.items()}


def probs_width(split, n_query):
    return 128 * sum(columns_of(n_heads, n_query) for lane, lanes, n_heads in split)


def spread_shape(split, n_query):
    rows = 128 * max(columns_of(n_heads, n_query) for lane, lanes, n_heads in split)
    return (rows, max(lanes for lane, lanes, n_heads in split))


def saved_outs(width, split, shifted):
    n_query, n_win = (72, 4) if shifted else (WIN, 2)
    found = {"packed": ((TOKENS, 3 * width), BF16)}
    if shifted:
        found["packed_far"] = ((TOKENS, 2 * width), BF16)
    else:
        found["x_in"] = ((TOKENS, width), F32)
        found["normed"] = ((TOKENS, width), BF16)
    found["probs"] = ((n_win, WIN, probs_width(split, n_query)), BF16)
    found["mixed"] = ((TOKENS, width), BF16)
    found["middle"] = ((TOKENS, width), F32)
    found["normed_two"] = ((TOKENS, width), BF16)
    found["raised"] = ((TOKENS, 4 * width), F32)
    found["active"] = ((TOKENS, 4 * width), BF16)
    return found


def flow_shapes(width, shifted):
    found = {
        "low": ((TOKENS, width), BF16),
        "raised": ((TOKENS, 4 * width), BF16),
        "branch": ((TOKENS, width), BF16),
        "near": ((TOKENS, 3 * width), BF16),
    }
    if shifted:
        found["far"] = ((TOKENS, 2 * width), BF16)
    return found


def spare(width, split, shifted, backward):
    n_query = 72 if shifted else WIN
    shape = spread_shape(split, n_query)
    found = {"q": (shape, BF16), "o": (shape, F32)}
    if shifted:
        found["m"] = ((TOKENS, width), F32)
    if backward:
        found["g"] = (shape, BF16)
        found["s"] = ((WIN, shape[0]), BF16)
    return found


def rim_outs(width):
    found = {"grad_middle": ((TOKENS, width), F32), "grad_near": ((TOKENS, width), F32)}
    found["rim_a"] = found["rim_b"] = ((WIN, width), BF16)
    found["norm_two"] = ((2, width), F32)
    return found


def weight_grads(width):
    return {
        "down": ((4 * width, width), BF16),
        "up": ((width, 4 * width), BF16),
        "proj": ((width, width), BF16),
        "qkv": ((width, 3 * width), BF16),
    }


def window_order():
    order = []
    for half in range(2):
        for pair in ((1, 2), (3, 0)):
            for level in pair:
                for row in range(3):
                    for col in range(12):
                        order.append(level * 72 + (half * 3 + row) * 12 + col)
    return np.array(order)


def fixed_tables():
    order = window_order()
    to_win = np.zeros((TOKENS, TOKENS), np.float32)
    to_win[np.arange(TOKENS), order] = 1.0
    region = np.zeros((2, 72), np.float32)
    for pair, levels in enumerate(((1, 2), (3, 0))):
        for place in range(72):
            level, col = levels[place // 36], place % 12
            region[pair, place] = 2.0 * (level == 0) + 1.0 * (col < 6)
    return to_win, region


def key_codes(extent, first_lat):
    place = lax.broadcasted_iota(jnp.int32, (TOKENS, 128), 0)
    row, col = (place // 12) % 6, place % 12
    inside = (first_lat + row < extent[0]) & (col < extent[1])
    plain = jnp.where(inside, 0.0, -1.0)
    place = lax.broadcasted_iota(jnp.int32, (2 * TOKENS, 128), 0)
    win, rest = place // WIN, place % WIN
    far, rest = rest // 72, rest % 72
    half, pair = win // 2, win % 2
    second = rest // 36
    row, col = (rest // 12) % 3, rest % 12
    near_row = 3 * half + row
    far_row = jnp.where(half == 0, row - 3, row + 6)
    lat = first_lat + jnp.where(far == 1, far_row, near_row)
    top = (pair == 1) & (second == 1)
    region = jnp.where(top, 2.0, 0.0) + jnp.where(col < 6, 1.0, 0.0)
    inside = (lat >= 0) & (lat < extent[0]) & (col < extent[1])
    return plain, jnp.where(inside, region, -1.0)


def exchange(first, second):
    count = lax.axis_size("band")
    up = [(i, i + 1) for i in range(count - 1)]
    down = [(i + 1, i) for i in range(count - 1)]
    return lax.ppermute(second, "band", up), lax.ppermute(first, "band", down)


def shift_query_codes(region, split):
    parts = []
    for lane, lanes, n_heads in split:
        total = 128 * columns_of(n_heads, 72)
        tiled = np.tile(region, (1, n_heads))
        parts.append(np.pad(tiled, ((0, 0), (0, total - tiled.shape[1]))))
    return jnp.asarray(np.concatenate(parts, 1)[:, None, :], F32)


WIDTHS = {"enc": (D_ENC, ENC_SPLIT), "trunk": (D_TRUNK, TRUNK_SPLIT)}
FORWARD_ORDER = ("norm_one", "qkv", "proj", "norm_two", "up", "down")
BACKWARD_ORDER = ("down", "up", "norm_two", "proj", "qkv", "norm_one")


def compute(weights, unpack_trunk, pack_trunk, source, goal, codes, count):
    to_win, region = fixed_tables()
    order = {"to_win": jnp.asarray(to_win, BF16), "to_tok": jnp.asarray(to_win.T, BF16)}
    grads = {}

    def tables(tower, names):
        split = WIDTHS[tower][1]
        found = {
            "plain_key": codes[0],
            "shift_key": codes[1],
            "plain_query": jnp.zeros((1, probs_width(split, WIN)), F32),
            "shift_query": shift_query_codes(region, split),
        } | order
        return prefixed("c_", {name: found[name] for name in names})

    PLAIN = ("plain_key", "plain_query", "to_win")
    SHIFTED = ("shift_key", "shift_query", "to_tok")

    def of(key, group):
        array = weights[key]
        if group is None:
            return array
        return (array, lambda ref: ref.at[group], array.shape[1:])

    def block(mark, tower, layer, group, names, with_next=False):
        found = {name: of((tower, layer, name), group) for name in names}
        if with_next:
            found["norm_next"] = of((tower, layer + 1, "norm_one"), group)
        return prefixed(mark, found)

    def src(group):
        lanes = pl.ds(PIN * group, PIN)
        return (source, lambda ref: ref.at[:, lanes], (TOKENS, PIN))

    groups = range(GROUPS)
    enc_width, enc_split = WIDTHS["enc"]
    width, split = WIDTHS["trunk"]

    def enc_plain():
        def body(r):
            for group in groups:
                s = part(r, f"s{group}_")
                s.near_a, s.near_b = r["near_a"].at[group], r["near_b"].at[group]
                plain_forward(
                    nn(r[f"src{group}"][...], r[f"embed{group}"][...]), part(r, f"w{group}_"), s,
                    part(r, "c_"), part(r, "t_"), enc_split, enc_width,
                )
            send(r["near_a"], r["near_b"])

        ins, outs = {}, {"near_a": ((GROUPS, WIN, enc_width), BF16)}
        outs["near_b"] = outs["near_a"]
        for group in groups:
            ins |= {f"src{group}": src(group), f"embed{group}": of(("enc", -1, "embed"), group)}
            ins |= block(f"w{group}_", "enc", 0, group, FORWARD_ORDER, True)
            ins |= tables("enc", PLAIN) if group == 0 else {}
            kept = saved_outs(enc_width, enc_split, False) | {"x_out": ((TOKENS, enc_width), F32)}
            outs |= prefixed(f"s{group}_", kept)
        return launch(
            "enc_plain", body, ins, outs, prefixed("t_", spare(enc_width, enc_split, False, False))
        )

    def middle(before, far):
        def body(r):
            last = []
            for group in groups:
                rows = [r[name].at[group] for name in ("near_a", "near_b", "far_a", "far_b")]
                last.append(
                    shifted_forward(
                        r[f"x_in{group}"], rows[:2], rows[2:], part(r, f"w{group}_"),
                        part(r, f"s{group}_"), part(r, "e_"), part(r, "t_"), enc_split, enc_width,
                    )
                )
            joined = jnp.concatenate(last, 1).astype(BF16)
            r["joined"][...] = joined
            s = part(r, "s_")
            s.near_a, s.near_b = r["trunk_a"], r["trunk_b"]
            plain_forward(
                nn(joined, r["joining"][...]), part(r, "w_"), s, part(r, "c_"), part(r, "u_"),
                split, width,
            )

        ins = {"near_a": before["near_a"], "near_b": before["near_b"], "far_a": far[0], "far_b": far[1]}
        outs = {}
        for group in groups:
            ins |= block(f"w{group}_", "enc", 1, group, FORWARD_ORDER[1:])
            if group == 0:
                found = tables("enc", SHIFTED)
                ins |= {"e_" + key[2:]: value for key, value in found.items()}
            ins |= {f"x_in{group}": before[f"s{group}_x_out"]}
            outs |= prefixed(f"s{group}_", saved_outs(enc_width, enc_split, True))
        ins |= {"joining": weights["trunk", -1, "joining"]}
        ins |= block("w_", "trunk", 0, None, FORWARD_ORDER, True) | tables("trunk", PLAIN)
        outs |= {"joined": ((TOKENS, 2 * D_ENC), BF16)}
        outs |= prefixed("s_", saved_outs(width, split, False) | {"x_out": ((TOKENS, width), F32)})
        outs |= {"trunk_a": ((WIN, width), BF16), "trunk_b": ((WIN, width), BF16)}
        return launch(
            "middle", body, ins, outs,
            prefixed("t_", spare(enc_width, enc_split, True, False))
            | prefixed("u_", spare(width, split, False, False)),
        )

    def trunk_top(before, far):
        def body(r):
            w, s, c, t = part(r, "w_"), part(r, "s_"), part(r, "c_"), part(r, "t_")
            last = shifted_forward(
                r["x_in"], (r["near_a"], r["near_b"]), (r["far_a"], r["far_b"]),
                w, s, c, t, split, width,
            )
            grad = loss_part(last, r["goal"], c, r["count"], part(r, "h_"), part(r, "d_"))
            shifted_backward(grad, w, s, part(r, "f_"), part(r, "b_"), c, t, split, width)

        kept = saved_outs(width, split, True)
        reused = ("mixed", "normed_two", "active")
        top = {name: weights["top", -1, name] for name in ("decode", "head", "scale")}
        found = launch(
            "trunk_top", body,
            {"near_a": before["trunk_a"], "near_b": before["trunk_b"], "far_a": far[0], "far_b": far[1]}
            | block("w_", "trunk", 1, None, FORWARD_ORDER[1:])
            | tables("trunk", SHIFTED + ("to_win", "plain_key"))
            | {"x_in": before["s_x_out"]}
            | prefixed("h_", {"final": weights["trunk", -1, "final"]} | top)
            | {"goal": goal, "count": count},
            prefixed("s_", {name: kept[name] for name in reused})
            | prefixed("f_", flow_shapes(width, True)) | prefixed("b_", rim_outs(width))
            | prefixed("d_", {
                "final": ((2, width), F32), "decode": ((GROUPS, D_TRUNK, D_ENC), BF16),
                "head": ((GROUPS, D_ENC, PIN), BF16), "scale": ((GROUPS, PIN), F32),
                "loss": ((1, PIN), F32),
            }),
            prefixed("s_", {name: kept[name] for name in kept if name not in reused})
            | prefixed("t_", spare(width, split, True, True)),
        )
        grads["trunk", -1, "final", None] = found["d_final"]
        for name in ("decode", "head", "scale"):
            grads["top", -1, name, "all"] = found["d_" + name]
        grads["trunk", 1, "norm_two", None] = found["b_norm_two"]
        return found

    def trunk_top_weights(before, far, found):
        def body(r):
            shifted_weights(
                (r["near_a"], r["near_b"]), (r["far_a"], r["far_b"]), part(r, "s_"), part(r, "f_"),
                part(r, "d_"), width,
            )

        results = launch(
            "trunk_top_weights", body,
            {key: found[key] for key in found if key[:2] in ("s_", "f_")}
            | {"near_a": before["trunk_a"], "near_b": before["trunk_b"], "far_a": far[0], "far_b": far[1]},
            prefixed("d_", weight_grads(width)), {},
        )
        for key, grad in results.items():
            grads["trunk", 1, key[2:], None] = grad
        return results["d_qkv"]

    PLAIN_KEPT = ("raised", "middle", "active", "normed_two", "mixed", "packed", "probs", "normed", "x_in")
    SHIFT_KEPT = ("raised", "middle", "packed", "packed_far", "probs", "active", "normed_two", "mixed")
    GAINS = ("norm_next", "norm_one", "norm_two")

    def plain_back_ins(mark, tower, group, kept, kept_mark):
        found = {f"w{mark}norm_next": of((tower, 1, "norm_one"), group)}
        found |= block(f"w{mark}", tower, 0, group, BACKWARD_ORDER)
        return found | {f"s{mark}{name}": kept[kept_mark + name] for name in PLAIN_KEPT}

    def keep_plain_grads(tower, group, found, mark):
        grads[tower, 1, "norm_one", group] = found[mark + "norm_next"]
        for name in ("down", "up", "proj", "qkv", "norm_one", "norm_two"):
            grads[tower, 0, name, group] = found[mark + name]

    def middle_back(top, arrived, before, first, far):
        def body(r):
            grad = plain_backward(
                part(r, "g_"), (r["arrived_a"], r["arrived_b"]), part(r, "w_"), part(r, "s_"),
                part(r, "f_"), part(r, "d_"), part(r, "c_"), part(r, "t_"), split, width,
            ).astype(BF16)
            r["d_joining"][...] = tn(r["joined"][...], grad).astype(BF16)
            send(r["d_joining"])
            r["v_grad"][...] = nt(grad, r["joining"][...])
            for group in groups:
                s, f, b = part(r, f"s{group}_"), part(r, "e_"), part(r, f"b{group}_")
                rows = [r[name].at[group] for name in ("near_a", "near_b", "far_a", "far_b")]
                b.rim_a, b.rim_b = r["rim_a"].at[group], r["rim_b"].at[group]
                shifted_backward(
                    r["v_grad"][:, enc_width * group : enc_width * (group + 1)],
                    part(r, f"w{group}_"), s, f, b, part(r, "k_"), part(r, "u_"), enc_split, enc_width,
                )
                shifted_weights(rows[:2], rows[2:], s, f, part(r, f"d{group}_"), enc_width)
            send(r["rim_a"], r["rim_b"])

        ins = {"g_near": top["b_grad_near"], "c_to_tok": order["to_tok"]}
        ins |= {"arrived_a": arrived[0], "arrived_b": arrived[1], "s_x_out": before["s_x_out"]}
        ins |= {"g_middle": top["b_grad_middle"]} | plain_back_ins("_", "trunk", None, before, "s_")
        ins |= tables("trunk", ("plain_key", "plain_query"))
        ins |= {"joined": before["joined"], "joining": weights["trunk", -1, "joining"]}
        outs = prefixed("d_", {name: ((2, width), F32) for name in GAINS} | weight_grads(width))
        outs |= {"d_joining": ((GROUPS * D_ENC, D_TRUNK), BF16)}
        outs |= {"rim_a": ((GROUPS, WIN, enc_width), BF16), "rim_b": ((GROUPS, WIN, enc_width), BF16)}
        for group in groups:
            ins |= block(f"w{group}_", "enc", 1, group, BACKWARD_ORDER[:-1])
            ins |= {f"s{group}_{name}": before[f"s{group}_{name}"] for name in SHIFT_KEPT}
            if group == 0:
                found = tables("enc", SHIFTED + ("to_win",))
                ins |= {"k_" + key[2:]: value for key, value in found.items()}
                ins |= {"near_a": first["near_a"], "near_b": first["near_b"]}
                ins |= {"far_a": far[0], "far_b": far[1]}
            found = rim_outs(enc_width)
            kept = {name: found[name] for name in ("grad_middle", "grad_near", "norm_two")}
            outs |= prefixed(f"b{group}_", kept) | prefixed(f"d{group}_", weight_grads(enc_width))
        found = launch(
            "middle_back", body, ins, outs,
            prefixed("t_", spare(width, split, False, True)) | prefixed("f_", flow_shapes(width, False))
            | prefixed("u_", spare(enc_width, enc_split, True, True))
            | prefixed("e_", flow_shapes(enc_width, True)) | {"v_grad": ((TOKENS, width), F32)},
        )
        keep_plain_grads("trunk", None, found, "d_")
        grads["trunk", -1, "joining", None] = found["d_joining"]
        for group in groups:
            grads["enc", 1, "norm_two", group] = found[f"b{group}_norm_two"]
            for name in weight_grads(enc_width):
                grads["enc", 1, name, group] = found[f"d{group}_{name}"]
        return found

    def enc_plain_back(back, arrived, first):
        def body(r):
            for group in groups:
                grad = plain_backward(
                    part(r, f"g{group}_"), (r["arrived_a"].at[group], r["arrived_b"].at[group]),
                    part(r, f"w{group}_"), part(r, f"s{group}_"), part(r, "f_"), part(r, f"d{group}_"),
                    part(r, "c_"), part(r, "t_"), enc_split, enc_width,
                ).astype(BF16)
                r[f"d{group}_embed"][...] = tn(r[f"src{group}"][...], grad).astype(BF16)
                send(r[f"d{group}_embed"])

        ins = {"arrived_a": arrived[0], "arrived_b": arrived[1], "c_to_tok": order["to_tok"]}
        outs = {}
        for group in groups:
            ins |= {f"g{group}_near": back[f"b{group}_grad_near"]}
            ins |= {f"s{group}_x_out": first[f"s{group}_x_out"]}
            ins |= {f"g{group}_middle": back[f"b{group}_grad_middle"]}
            ins |= plain_back_ins(f"{group}_", "enc", group, first, f"s{group}_")
            ins |= tables("enc", ("plain_key", "plain_query")) if group == 0 else {}
            ins |= {f"src{group}": src(group)}
            outs |= prefixed(
                f"d{group}_",
                {name: ((2, enc_width), F32) for name in GAINS}
                | weight_grads(enc_width) | {"embed": ((PIN, D_ENC), BF16)},
            )
        found = launch(
            "enc_plain_back", body, ins, outs,
            prefixed("t_", spare(enc_width, enc_split, False, True))
            | prefixed("f_", flow_shapes(enc_width, False)),
        )
        for group in groups:
            keep_plain_grads("enc", group, found, f"d{group}_")
            grads["enc", -1, "embed", group] = found[f"d{group}_embed"]

    first = enc_plain()
    far = exchange(first["near_a"], first["near_b"])
    found = unpack_trunk(first["near_a"])
    *far, found = lax.optimization_barrier((*far, found))
    weights = weights | found
    second = middle(first, far)
    trunk_far = exchange(second["trunk_a"], second["trunk_b"])
    top = trunk_top(second, trunk_far)
    arrived = exchange(top["b_rim_a"], top["b_rim_b"])
    last = trunk_top_weights(second, trunk_far, top)
    *arrived, last = lax.optimization_barrier((*arrived, last))
    grads["trunk", 1, "qkv", None] = last
    back = middle_back(top, arrived, second, first, far)
    arrived = exchange(back["rim_a"], back["rim_b"])
    packed = pack_trunk(grads)
    *arrived, packed = lax.optimization_barrier((*arrived, packed))
    enc_plain_back(back, arrived, first)
    return top["d_loss"], grads, packed


def stacked_key(label_key):
    tower, group, layer, name = label_key
    return (tower, layer, name), (group if tower in ("enc", "top") else None)


BLOCK_ELEMENTS = 2048


def share_rows(n_own):
    blocks = -(-(n_own + BLOCK_ELEMENTS - 1) // BLOCK_ELEMENTS) + 1
    return 16 * 3 * (-(-blocks // 3))


def first_row(n_own, device):
    return (n_own * device // BLOCK_ELEMENTS) * 16


def grouped_pieces():
    found = {}
    for label_key, dims_shape, offset in placed():
        key, group = stacked_key(label_key)
        found.setdefault(key, (dims_shape, []))[1].append((group, offset // 128))
    return [(key, places, dims_shape) for key, (dims_shape, places) in found.items()]


def is_gain(key):
    return key[2] in ("norm_one", "norm_two", "final")


def stacked_shape(places, dims_shape):
    if len(dims_shape) == 1:
        return (len(places),) + dims_shape
    return dims_shape if places[0][0] is None else (len(places),) + dims_shape


def turned(values):
    return pltpu.roll(values, 64, 1)


def lower_half(values):
    return lax.broadcasted_iota(jnp.int32, values.shape, 1) < 64


def read_gain(flat, offset, width, out):
    if width % 128 == 0:
        count = width // 128
        for row in range(2):
            for tile in range(count):
                at = offset + row * count + tile
                out[row : row + 1, 128 * tile : 128 * tile + 128] = flat[at : at + 1, :]
        return
    rows = [flat[offset + place : offset + place + 1, :] for place in range(3)]
    out[0:1, 0:128] = rows[0]
    out[0:1, 128:192] = rows[1][:, 0:64]
    out[1:2, 0:128] = jnp.where(lower_half(rows[1]), turned(rows[1]), turned(rows[2]))
    out[1:2, 128:192] = rows[2][:, 64:128]


def read_matrix(flat, offset, shape, out, wide_scr):
    height, width = shape
    step = 64
    if width % 128 == 0:
        count = width // 128

        def body(index, carry):
            row = pl.multiple_of(index * step, step)
            for tile in range(count):
                start = offset + tile + row * count
                piece = flat[pl.ds(start, step, stride=count), :]
                out[pl.ds(row, step), 128 * tile : 128 * tile + 128] = piece.astype(BF16)
            return carry

        lax.fori_loop(0, height // step, body, 0)
        return
    half = width // 128
    period = 2 * half + 1

    def body(index, carry):
        row = pl.multiple_of(index * step, step)
        start = offset + (row // 2) * period
        rows = [flat[pl.ds(start + place, step // 2, stride=period), :] for place in range(period)]
        late = [turned(rows[half + place]) for place in range(half + 1)]
        for tile in range(half + 1):
            odd_rows = late[tile]
            if tile < half:
                odd_rows = jnp.where(lower_half(late[tile]), late[tile], late[tile + 1])
            wide_scr[pl.ds(step * tile, step // 2, stride=2), :] = rows[tile]
            wide_scr[pl.ds(step * tile + 1, step // 2, stride=2), :] = odd_rows
            end = min(128, width - 128 * tile)
            tile_rows = wide_scr[step * tile : step * (tile + 1), 0:end]
            out[pl.ds(row, step), 128 * tile : 128 * tile + end] = tile_rows.astype(BF16)
        return carry

    lax.fori_loop(0, height // step, body, 0)


def write_gain(flat, offset, width, values):
    if width % 128 == 0:
        count = width // 128
        for row in range(2):
            for tile in range(count):
                at = offset + row * count + tile
                flat[at : at + 1, :] = values[row : row + 1, 128 * tile : 128 * tile + 128]
        return
    flat[offset : offset + 1, :] = values[0:1, 0:128]
    first, second = values[1:2, 0:64], values[1:2, 64:192]
    flat[offset + 1 : offset + 2, :] = jnp.concatenate([values[0:1, 128:192], first], 1)
    flat[offset + 2 : offset + 3, :] = second


def write_matrix(flat, offset, shape, source, wide_scr):
    height, width = shape
    step = 64
    if width % 128 == 0:
        count = width // 128

        def body(index, carry):
            row = pl.multiple_of(index * step, step)
            for tile in range(count):
                start = offset + tile + row * count
                piece = source[pl.ds(row, step), 128 * tile : 128 * tile + 128]
                flat[pl.ds(start, step, stride=count), :] = piece.astype(F32)
            return carry

        lax.fori_loop(0, height // step, body, 0)
        return
    half = width // 128
    period = 2 * half + 1

    def body(index, carry):
        row = pl.multiple_of(index * step, step)
        start = offset + (row // 2) * period
        for tile in range(half + 1):
            end = min(128, width - 128 * tile)
            tile_rows = source[pl.ds(row, step), 128 * tile : 128 * tile + end].astype(F32)
            wide_scr[step * tile : step * (tile + 1), 0:end] = tile_rows
        early = [wide_scr[pl.ds(step * tile, step // 2, stride=2), :] for tile in range(half + 1)]
        late = [
            turned(wide_scr[pl.ds(step * tile + 1, step // 2, stride=2), :])
            for tile in range(half + 1)
        ]
        low = lower_half(late[0])
        rows = early[:half] + [jnp.where(low, early[half], late[0])]
        rows += [jnp.where(low, late[tile], late[tile + 1]) for tile in range(half)]
        for place, value in enumerate(rows):
            flat[pl.ds(start + place, step // 2, stride=period), :] = value
        return carry

    lax.fori_loop(0, height // step, body, 0)


def wide_scratch(rows):
    return {"flat": ((rows, 128), F32), "wide": ((5 * 64, 128), F32)}


def trunk_row():
    return min(places[0][1] for key, places, dims_shape in grouped_pieces() if key[0] == "trunk")


def unpack_weights(gathered, n_own, trunk):
    pieces = [piece for piece in grouped_pieces() if (piece[0][0] == "trunk") == trunk]
    n_devices, rows, unused = gathered.shape
    edge = trunk_row() * 128
    low, high = (edge // n_own, n_devices) if trunk else (0, -(-edge // n_own))
    base = first_row(n_own, low)
    n_held = high - low
    cuts = [n_held * index // 8 for index in range(9)]
    step = rows // 6
    outs = {}
    for key, places, dims_shape in pieces:
        small = is_gain(key) or len(dims_shape) == 1
        outs[key] = (stacked_shape(places, dims_shape), F32 if small else BF16)

    def body(r):
        flat, wide, shares, source = r["flat"], r["wide"], r["shares"], r["raw"][0]
        copies = []
        for index, (start, stop) in enumerate(zip(cuts[:-1], cuts[1:])):
            span, held_span = pl.ds(low + start, stop - start), pl.ds(start, stop - start)
            copy = pltpu.make_async_copy(source.at[span], shares.at[held_span], r["sems"][index])
            copy.start()
            copies.append(copy)

        def place(index, carry):
            start = n_own * (low + index) // BLOCK_ELEMENTS * 16 - base
            start = pl.multiple_of(start, 16)
            kept = jnp.where(index > 0, flat[pl.ds(start, 16), :], 0.0)
            flat[pl.ds(start, 16), :] = kept + shares[index, 0:16, :].astype(F32)
            flat[pl.ds(start + 16, step - 16), :] = shares[index, 16:step, :].astype(F32)
            for number in range(1, 6):
                at = pl.ds(start + number * step, step)
                flat[at, :] = shares[index, number * step : (number + 1) * step, :].astype(F32)
            return carry

        for index in range(8):
            copies[index].wait()
            lax.fori_loop(cuts[index], cuts[index + 1], place, 0)
        for key, places, dims_shape in pieces:
            for group, offset in places:
                offset = offset - base
                view = r[key] if group is None or len(dims_shape) == 1 else r[key].at[group]
                if len(dims_shape) == 1:
                    view[group : group + 1, :] = flat[offset : offset + 1, :]
                elif is_gain(key):
                    read_gain(flat, offset, dims_shape[1], view)
                else:
                    read_matrix(flat, offset, dims_shape, view, wide)
            r[key].send()

    return launch(
        "unpack_trunk" if trunk else "unpack", body, {}, outs,
        {"shares": ((n_held,) + gathered.shape[1:], BF16)}
        | wide_scratch(first_row(n_own, high - 1) + rows - base),
        limit=60 << 20, raw=(gathered,), sems=8,
    )


def cuts_of(rows):
    blocks = rows // 16
    last = blocks // 5
    first = (blocks - last) // 2
    return 16 * first, 16 * (blocks - last - first), 16 * last


def step_of(rows):
    blocks = rows // 16
    return 16 * max(count for count in range(1, 13) if blocks % count == 0)


def pack_grads(grads, n_own, n_devices, core, before=None):
    early = before is None
    rows = share_rows(n_own)
    cuts = cuts_of(rows)
    n_chips = n_devices // 2
    middle = -(-trunk_row() * 128 // (2 * n_own))
    low, high = (middle, n_chips) if early else (0, middle)
    base = trunk_row() // 16 * 16 if early else 0
    end = first_row(n_own, 2 * high - 1) + rows
    pieces = [
        (key, group, offset, dims_shape)
        for key, places, dims_shape in grouped_pieces()
        for group, offset in places
        if (key[0] == "trunk" if early else offset < end)
    ]
    last = max(offset + math.prod(dims_shape) // 128 for key, group, offset, dims_shape in pieces)
    names = [(side, index) for side in ("kept", "sent") for index in range(3)]
    outs = {name: ((n_chips, cuts[name[1]], 128), BF16) for name in names}

    def held_as(key, group):
        return key + ("all" if key[0] == "top" else group,)

    ins = {held_as(key, group): grads[held_as(key, group)] for key, group, offset, dims_shape in pieces}

    def body(r):
        flat, wide, core = r["flat"], r["wide"], r["scalars"][0]
        if last < end:
            flat[last - base :, :] = jnp.zeros((flat.shape[0] - last + base, 128), F32)
        for key, group, offset, dims_shape in pieces:
            offset = offset - base
            held_ref = r[held_as(key, group)]
            if len(dims_shape) == 1:
                flat[offset : offset + 1, :] = held_ref[group : group + 1, :]
                continue
            source = held_ref.at[group] if key[0] == "top" else held_ref.ready()
            if is_gain(key):
                write_gain(flat, offset, dims_shape[1], source)
            else:
                write_matrix(flat, offset, dims_shape, source, wide)

        def chip(index, carry):
            for side, device in (("sent", 2 * index + 1 - core[0]), ("kept", 2 * index + core[0])):
                start = pl.multiple_of(n_own * device // BLOCK_ELEMENTS * 16 - base, 16)
                done = 0
                for which, rows in enumerate(cuts):
                    place, far, sem = r[f"{side}{which}"], r[side, which].far, r[side, which].sem
                    step = step_of(rows)
                    for row in range(0, rows, step):
                        values = flat[pl.ds(start + done + row, step), :]
                        place[index - low, row : row + step, :] = values.astype(BF16)
                    done += rows
                    pltpu.make_async_copy(place.at[index - low], far.at[index], sem).start()
            return carry

        lax.fori_loop(low, high, chip, 0)
        for side, which in names:
            place, out = r[f"{side}{which}"], r[side, which]
            out.copy = pltpu.make_async_copy(place, out.far.at[pl.ds(low, high - low)], out.sem)
            out.sent = True

    scratch = wide_scratch(max(end, last) - base)
    scratch |= {f"{side}{which}": ((high - low, cuts[which], 128), BF16) for side, which in names}
    return launch(
        "pack_trunk" if early else "pack", body, ins, outs, scratch, limit=60 << 20,
        scalars=(core.reshape(1),), raw=() if early else [before[name] for name in names], in_place=True,
    )


class Torus:
    def __init__(self):
        self.totals = {"dp": lax.axis_size("dp"), "band": lax.axis_size("band")}
        depth = min(4, self.totals["dp"])
        across = self.totals["dp"] // depth
        self.axes = {
            "z": (depth, across, "dp"),
            "x": (across, 1, "dp"),
            "y": (self.totals["band"] // 2, 2, "band"),
            "core": (2, 1, "band"),
        }

    def size(self, axis):
        return self.axes[axis][0]

    def place(self, axis):
        count, stride, name = self.axes[axis]
        return lax.axis_index(name) // stride % count

    def move(self, values, axis, by):
        count, stride, name = self.axes[axis]
        pairs = []
        for place in range(self.totals[name]):
            at = place // stride % count
            pairs.append((place, place + ((at + by) % count - at) * stride))
        return lax.ppermute(values, name, pairs)


def scatter_terms(torus, terms, dims, axis):
    dim = dims.index(axis)
    place = torus.place(axis)
    arrived = []
    for by in range(1, torus.size(axis)):
        other = (place + by) % torus.size(axis)
        pieces = [lax.dynamic_index_in_dim(term, other, dim, keepdims=False) for term in terms]
        total = sum(piece.astype(F32) for piece in pieces).astype(BF16)
        arrived.append(torus.move(total, axis, by))
    own = [lax.dynamic_index_in_dim(term, place, dim, keepdims=False) for term in terms]
    return own + arrived, [name for name in dims if name != axis]


SCATTER_ORDERS = (("y", "x", "z"), ("x", "y", "z"), ("z", "x", "y"))


def scatter_sum(packed):
    torus = Torus()
    dims = ["z", "x", "y"]
    shape = tuple(torus.size(axis) for axis in dims)
    sequence = (2, 0, 1)
    state = {}
    for part in sequence:
        near, far = packed["kept", part], packed["sent", part]
        near, far = near.reshape(shape + near.shape[1:]), far.reshape(shape + far.shape[1:])
        state[part] = ([near, torus.move(far, "core", 1)], dims)
    for step in range(3):
        for part in sequence if step < 2 else (2,):
            terms, left = state[part]
            state[part] = scatter_terms(torus, terms, left, SCATTER_ORDERS[part][step])

    def at_depth(place):
        found = []
        for part in (0, 1):
            pieces = [lax.dynamic_index_in_dim(term, place, 0, keepdims=False) for term in state[part][0]]
            found.append(sum(piece.astype(F32) for piece in pieces))
        return jnp.concatenate(found, 0)

    depth, place = torus.size("z"), torus.place("z")
    arrived = [
        torus.move(at_depth((place + by) % depth).astype(BF16), "z", by) for by in range(1, depth)
    ]
    first = at_depth(place) + sum(term.astype(F32) for term in arrived)
    return jnp.concatenate([first, sum(term.astype(F32) for term in state[2][0])], 0)


def all_sum(values):
    for axis in ("band", "dp"):
        count = lax.axis_size(axis)
        bit = 1
        while bit < count:
            pairs = [(i, i ^ bit) for i in range(count)]
            values = values + lax.ppermute(values, axis, pairs)
            bit *= 2
    return values


def shards(inputs, targets, crop_extent, master, moment_one, moment_two, step_count):
    n_own = master.shape[0]
    n_bands = lax.axis_size("band")
    n_devices = lax.axis_size("dp") * n_bands
    rows = share_rows(n_own)
    device = lax.axis_index("dp") * n_bands + lax.axis_index("band")
    shift = (n_own * device) % BLOCK_ELEMENTS
    extent = crop_extent[0]
    spread = jnp.pad(master, (BLOCK_ELEMENTS, rows * 128 - n_own))
    share = lax.dynamic_slice(spread, (BLOCK_ELEMENTS - shift,), (rows * 128,)).astype(BF16)
    share = lax.dynamic_update_slice(share, extent.astype(BF16), ((rows - 1) * 128,))
    gathered = lax.all_gather(share.reshape(rows, 128), ("dp", "band"), axis=0, tiled=False)
    extents = gathered[::n_bands, rows - 1, 0:2].astype(F32)
    weights = unpack_weights(gathered, n_own, False)
    n_rows, n_levels = inputs.shape[1], inputs.shape[2]
    source = inputs[0].transpose(1, 0, 2, 3).reshape(TOKENS, GROUPS * PIN)
    goal = targets[0].transpose(1, 0, 2, 3).reshape(TOKENS, GROUPS * PIN)
    first_lat = lax.axis_index("band") * n_rows
    norm_count = jnp.sum(extents[:, 0] * extents[:, 1]) * (n_levels * GROUPS * PIN)
    core = lax.axis_index("band") % 2

    def unpack_trunk(after):
        later, unused = lax.optimization_barrier((gathered, after))
        return unpack_weights(later, n_own, True)

    def pack_trunk(grads):
        return pack_grads(grads, n_own, n_devices, core)

    loss_row, grads, packed = compute(
        weights, unpack_trunk, pack_trunk, source, goal, key_codes(extent, first_lat),
        jnp.full((1, PIN), norm_count),
    )
    packed = pack_grads(grads, n_own, n_devices, core, packed)
    owned = scatter_sum(packed)
    grad_shard = lax.dynamic_slice(owned.reshape(-1), (shift,), (n_own,))
    shard_square = jnp.sum(grad_shard * grad_shard)
    lanes = lax.broadcasted_iota(jnp.int32, (8, 128), 1)
    both = jnp.where(lanes < 64, shard_square, jnp.sum(loss_row))
    both = all_sum(both)
    grad_norm = jnp.sqrt(both[0, 0])
    loss_total = both[0, 64]
    factor_clip = jnp.minimum(1.0, CLIP_LEVEL / (grad_norm + 1e-06))
    clipped = grad_shard * factor_clip
    new_one = BETA_ONE * moment_one + (1.0 - BETA_ONE) * clipped
    new_two = BETA_TWO * moment_two + (1.0 - BETA_TWO) * clipped * clipped
    step_value = step_count[0].astype(F32)
    fix_one = 1.0 - jnp.power(BETA_ONE, step_value)
    fix_two = 1.0 - jnp.power(BETA_TWO, step_value)
    update = new_one / fix_one / (jnp.sqrt(new_two / fix_two) + ADAM_EPS) + WEIGHT_DECAY * master
    new_master = master - LEARN_RATE * update
    return (
        new_master,
        new_one,
        new_two,
        new_master.astype(BF16),
        loss_total / norm_count,
        grad_norm,
    )


def solution(mesh):
    in_specs = (
        P("dp", "band", None, None, None),
        P("dp", "band", None, None, None),
        P("dp", None),
        P(("dp", "band")),
        P(("dp", "band")),
        P(("dp", "band")),
        P(),
    )
    out_specs = (
        P(("dp", "band")),
        P(("dp", "band")),
        P(("dp", "band")),
        P(("dp", "band")),
        P(),
        P(),
    )
    return jax.shard_map(shards, mesh=mesh, in_specs=in_specs, out_specs=out_specs, check_vma=False)
```

```python
import functools
import math

import jax
import jax.numpy as jnp
import numpy as np
from jax import lax
from jax.experimental import pallas as pl
from jax.experimental.pallas import tpu as pltpu
from jax.sharding import PartitionSpec as P

D_ENC = 192
HEADS_ENC = 6
D_TRUNK = 384
HEADS_TRUNK = 12
PIN = 128
GROUPS = 2
HEAD_DIM = 32
SCALE = HEAD_DIM ** (-0.5)

NEG_FILL = -1000000000.0
BETA_ONE = 0.5
BETA_TWO = 0.5
LEARN_RATE = 0.01
WEIGHT_DECAY = 0.1
CLIP_LEVEL = 0.07
ADAM_EPS = 1e-08

F32 = jnp.float32
BF16 = jnp.bfloat16
TOKENS = 288
AHEAD = 8 << 20
SPAN = 384
SPAN_BACK = 384
WIN = 144
ENC_SPLIT = ((0, 192, 6),)
TRUNK_SPLIT = ((0, 256, 8), (256, 128, 4))


def block_layout(path_name, group_id, layer_id, n_width):
    prefix = (path_name, group_id, layer_id)
    return [
        (prefix + ("norm_one",), (2, n_width)),
        (prefix + ("qkv",), (n_width, 3 * n_width)),
        (prefix + ("proj",), (n_width, n_width)),
        (prefix + ("norm_two",), (2, n_width)),
        (prefix + ("up",), (n_width, 4 * n_width)),
        (prefix + ("down",), (4 * n_width, n_width)),
    ]


def layout():
    entries = []
    for group_id in range(GROUPS):
        entries.append((("enc", group_id, -1, "embed"), (PIN, D_ENC)))
        for layer_id in range(2):
            entries += block_layout("enc", group_id, layer_id, D_ENC)
        entries.append((("top", group_id, -1, "decode"), (D_TRUNK, D_ENC)))
        entries.append((("top", group_id, -1, "head"), (D_ENC, PIN)))
        entries.append((("top", group_id, -1, "scale"), (PIN,)))
    entries.append((("trunk", 0, -1, "joining"), (GROUPS * D_ENC, D_TRUNK)))
    for layer_id in range(2):
        entries += block_layout("trunk", 0, layer_id, D_TRUNK)
    entries.append((("trunk", 0, -1, "final"), (2, D_TRUNK)))
    return entries


def placed():
    offset = 0
    for label_key, dims_shape in layout():
        yield label_key, dims_shape, offset
        offset += math.prod(dims_shape)


def nn(left, right):
    return jnp.dot(left, right, preferred_element_type=F32)


def nt(left, right):
    return lax.dot_general(left, right, (((1,), (1,)), ((), ())), preferred_element_type=F32)


def tn(left, right):
    return lax.dot_general(left, right, (((0,), (0,)), ((), ())), preferred_element_type=F32)


def unit_rows(values):
    centre = values - jnp.mean(values, -1, keepdims=True)
    inverse = lax.rsqrt(jnp.mean(centre * centre, -1, keepdims=True) + 1e-05)
    return centre * inverse, inverse


def norm_forward(values, gain_ref):
    unit, unused = unit_rows(values)
    return unit * gain_ref[0:1, :] + gain_ref[1:2, :]


def norm_backward(values, gain_ref, grad_normed):
    unit, inverse = unit_rows(values)
    grad_gain = jnp.sum(grad_normed * unit, 0, keepdims=True)
    grad_shift = jnp.sum(grad_normed, 0, keepdims=True)
    grad_unit = grad_normed * gain_ref[0:1, :]
    along = jnp.mean(grad_unit * unit, -1, keepdims=True)
    grad_values = inverse * (grad_unit - jnp.mean(grad_unit, -1, keepdims=True) - unit * along)
    return grad_values, jnp.concatenate([grad_gain, grad_shift], 0)


GELU_A = math.sqrt(2.0 / math.pi)
GELU_B = 0.044715


def gelu(values):
    inner = jnp.tanh(GELU_A * (values + GELU_B * (values * values * values)))
    return values * (0.5 * (1.0 + inner))


def gelu_slope(values):
    square = values * values
    inner = jnp.tanh(GELU_A * (values + GELU_B * (square * values)))
    steep = (1.0 - inner * inner) * (GELU_A + (3.0 * GELU_B * GELU_A) * square)
    return 0.5 * (1.0 + inner) + 0.5 * values * steep


def head_lanes(rows, lanes, head):
    lane = lax.broadcasted_iota(jnp.int32, (rows, lanes), 1)
    return (lane >= HEAD_DIM * head) & (lane < HEAD_DIM * (head + 1))


def columns_of(n_heads, n_query):
    return -(-n_heads * n_query // 128)


def spread_heads(rows_value, n_heads, out_ref):
    n_query, lanes = rows_value.shape
    wide = rows_value.astype(F32)
    for head in range(n_heads):
        kept = jnp.where(head_lanes(n_query, lanes, head), wide, 0.0).astype(BF16)
        out_ref[head * n_query : (head + 1) * n_query, 0:lanes] = kept
    total = 128 * columns_of(n_heads, n_query)
    if total > n_heads * n_query:
        out_ref[n_heads * n_query : total, 0:lanes] = jnp.zeros(
            (total - n_heads * n_query, lanes), BF16
        )


def join_heads(spread_ref, n_heads, n_query, lanes):
    joined = spread_ref[0:n_query, 0:lanes]
    for head in range(1, n_heads):
        part = spread_ref[head * n_query : (head + 1) * n_query, 0:lanes]
        joined = jnp.where(head_lanes(n_query, lanes, head), part, joined)
    return joined


def same_code(key_code, query_code):
    count = query_code.shape[1] // 128
    return jnp.concatenate([key_code] * count, 1) == query_code


def attend_window(queries, key_rows, value_rows, key_code, query_code, probs_ref, q_scr, o_scr, split):
    n_query = queries.shape[0]
    outs = []
    at = 0
    for lane, lanes, n_heads in split:
        spread_heads(queries[:, lane : lane + lanes], n_heads, q_scr)
        keys = key_rows[:, lane : lane + lanes]
        values = value_rows[:, lane : lane + lanes]
        wide = 128 * columns_of(n_heads, n_query)
        for start in range(0, wide, SPAN):
            rows = slice(start, min(start + SPAN, wide))
            columns = slice(at + rows.start, at + rows.stop)
            scores = nt(keys, q_scr[rows, 0:lanes]) * SCALE
            scores = jnp.where(same_code(key_code, query_code[0:1, columns]), scores, NEG_FILL)
            raised = jnp.exp(scores - jnp.max(scores, 0, keepdims=True))
            probs = (raised * (1.0 / jnp.sum(raised, 0, keepdims=True))).astype(BF16)
            probs_ref[:, columns] = probs
            o_scr[rows, 0:lanes] = tn(probs, values)
        outs.append(join_heads(o_scr, n_heads, n_query, lanes))
        at += wide
    return jnp.concatenate(outs, 1) if len(outs) > 1 else outs[0]


def attend_window_back(
    queries, key_rows, value_rows, grad_rows, key_code, query_code, probs_ref, q_scr, g_scr, o_scr, s_scr, split
):
    n_query = queries.shape[0]
    out_q, out_k, out_v = [], [], []
    at = 0
    for lane, lanes, n_heads in split:
        n_col = columns_of(n_heads, n_query)
        spread_heads(queries[:, lane : lane + lanes], n_heads, q_scr)
        spread_heads(grad_rows[:, lane : lane + lanes], n_heads, g_scr)
        keys = key_rows[:, lane : lane + lanes]
        values = value_rows[:, lane : lane + lanes]
        wide = 128 * n_col
        for start in range(0, wide, SPAN_BACK):
            rows = slice(start, min(start + SPAN_BACK, wide))
            columns = slice(at + rows.start, at + rows.stop)
            grad_probs = nt(values, g_scr[rows, 0:lanes])
            probs = probs_ref[:, columns].astype(F32)
            along = jnp.sum(grad_probs * probs, 0, keepdims=True)
            grad_scores = probs * (grad_probs - along)
            allowed = same_code(key_code, query_code[0:1, columns])
            grad_scores = jnp.where(allowed, grad_scores, 0.0).astype(BF16)
            s_scr[:, rows] = grad_scores
            o_scr[rows, 0:lanes] = tn(grad_scores, keys)
        out_v.append(nn(probs_ref[:, at : at + wide], g_scr[0:wide, 0:lanes]))
        out_k.append(nn(s_scr[:, 0:wide], q_scr[0:wide, 0:lanes]) * SCALE)
        out_q.append(join_heads(o_scr, n_heads, n_query, lanes) * SCALE)
        at += wide
    if len(split) > 1:
        return tuple(jnp.concatenate(parts, 1) for parts in (out_q, out_k, out_v))
    return out_q[0], out_k[0], out_v[0]


class Queue:
    def __init__(self, copies, sizes, ahead):
        self.copies, self.sizes, self.ahead = copies, sizes, ahead
        self.started, self.reach = 0, 0
        self.advance(-1)

    def advance(self, index):
        limit = sum(self.sizes[: index + 1]) + self.ahead
        while self.started < len(self.copies) and (self.started <= index or self.reach < limit):
            self.copies[self.started].start()
            self.reach += self.sizes[self.started]
            self.started += 1


class Held:
    def __init__(self, ref, queue, index):
        self.ref, self.queue, self.index = ref, queue, index

    def ready(self):
        if self.queue is not None:
            self.queue.advance(self.index)
            self.queue.copies[self.index].wait()
            self.queue = None
        return self.ref

    def __getitem__(self, index):
        return self.ready()[index]

    @property
    def at(self):
        return self.ready().at

    @property
    def shape(self):
        return self.ref.shape


class Made:
    def __init__(self, ref, copy):
        self.ref, self.copy, self.sent = ref, copy, False

    def __getitem__(self, index):
        return self.ref[index]

    def __setitem__(self, index, value):
        self.ref[index] = value

    @property
    def at(self):
        return self.ref.at

    @property
    def shape(self):
        return self.ref.shape

    @property
    def dtype(self):
        return self.ref.dtype

    def send(self):
        if not self.sent:
            self.copy.start()
            self.sent = True


class Refs:
    def __init__(self, **refs):
        self.__dict__.update(refs)


def send(*refs):
    for ref in refs:
        if isinstance(ref, Made):
            ref.send()


def rest_forward(resid_in, w, s):
    middle = resid_in + nn(s.mixed[...], w.proj[...])
    s.middle[...] = middle
    normed = norm_forward(middle, w.norm_two).astype(BF16)
    s.normed_two[...] = normed
    send(s.mixed, s.middle, s.normed_two)
    for start in range(0, w.up.shape[1], 256):
        columns = slice(start, start + 256)
        s.raised[:, columns] = nn(normed, w.up[:, columns])
        for row in range(0, TOKENS, 96):
            piece = s.raised[row : row + 96, columns]
            s.active[row : row + 96, columns] = gelu(piece).astype(BF16)
    send(s.raised, s.active)
    return middle + nn(s.active[...], w.down[...])


def rest_backward(grad_out, w, s, flow, d_norm_two):
    grad_low = grad_out.astype(BF16)
    flow.low[...] = grad_low
    width = w.up.shape[1]
    for start in range(0, width, 256):
        columns = slice(start, start + 256)
        grad_active = nt(grad_low, w.down[start : start + 256, :])
        for row in range(0, TOKENS, 96):
            slope = gelu_slope(s.raised[row : row + 96, columns])
            flow.raised[row : row + 96, columns] = (
                slope * grad_active[row : row + 96, :]
            ).astype(BF16)
    grad_middle, grad_gain = norm_backward(
        s.middle[...], w.norm_two, nt(flow.raised[...], w.up[...])
    )
    d_norm_two[...] = grad_gain
    grad_middle = grad_out + grad_middle
    grad_branch = grad_middle.astype(BF16)
    flow.branch[...] = grad_branch
    send(flow.low, flow.raised, flow.branch, d_norm_two)
    return grad_middle, nt(grad_branch, w.proj[...]).astype(BF16)


def rest_weights(s, flow, d):
    for out, left, right in (
        (d.down, s.active, flow.low),
        (d.up, s.normed_two, flow.raised),
        (d.proj, s.mixed, flow.branch),
    ):
        out[...] = tn(left[...], right[...]).astype(out.dtype)
        send(out)


def plain_forward(first, w, s, tables, t, split, width):
    s.x_in[...] = first
    s.normed[...] = norm_forward(first, w.norm_one).astype(BF16)
    s.packed[...] = nn(s.normed[...], w.qkv[...]).astype(BF16)
    send(s.x_in, s.normed, s.packed)
    for win in range(2):
        rows = slice(WIN * win, WIN * (win + 1))
        s.mixed[rows, :] = attend_window(
            s.packed[rows, 0:width],
            s.packed[rows, width : 2 * width],
            s.packed[rows, 2 * width : 3 * width],
            tables.plain_key[rows, :],
            tables.plain_query,
            s.probs.at[win],
            t.q,
            t.o,
            split,
        ).astype(BF16)
    send(s.probs)
    last = rest_forward(first, w, s)
    s.x_out[...] = last
    ordered = nn(tables.to_win[...], norm_forward(last, w.norm_next).astype(BF16)).astype(BF16)
    s.near_a[...] = ordered[0:WIN]
    s.near_b[...] = ordered[WIN:]
    send(s.x_out, s.near_a, s.near_b)


def both(first, second):
    return jnp.concatenate([first[...], second[...]], 0)


def shifted_keys(s, win, width):
    rows = slice(72 * win, 72 * (win + 1))
    keys = jnp.concatenate([s.packed[rows, width : 2 * width], s.packed_far[rows, 0:width]], 0)
    values = jnp.concatenate([s.packed[rows, 2 * width :], s.packed_far[rows, width:]], 0)
    return s.packed[rows, 0:width], keys, values


def shifted_forward(x_in, near, far, w, s, tables, t, split, width):
    s.packed[...] = nn(both(*near), w.qkv[...]).astype(BF16)
    s.packed_far[...] = nn(both(*far), w.qkv[:, width:]).astype(BF16)
    send(s.packed, s.packed_far)
    for win in range(4):
        queries, keys, values = shifted_keys(s, win, width)
        t.m[72 * win : 72 * (win + 1), 0:width] = attend_window(
            queries, keys, values, tables.shift_key[WIN * win : WIN * (win + 1), :],
            tables.shift_query.at[win % 2], s.probs.at[win], t.q, t.o, split,
        )
    send(s.probs)
    s.mixed[...] = nn(tables.to_tok[...], t.m[:, 0:width].astype(BF16)).astype(BF16)
    return rest_forward(x_in[...], w, s)


def loss_part(values, goal, tables, count, w, d):
    low = norm_forward(values, w.final).astype(BF16)
    valid = tables.plain_key[...] + 1.0
    inverse_count = 1.0 / count[0:1, :]
    grad_low = None
    total = None
    for group in range(GROUPS):
        decode, head = w.decode[group], w.head[group]
        raised = nn(low, decode)
        active = gelu(raised).astype(BF16)
        predicted = nn(active, head)
        log_scale = w.scale[group : group + 1, :]
        error = predicted - goal[:, PIN * group : PIN * (group + 1)].astype(F32)
        inverse_scale = jnp.exp(-log_scale)
        weighted = jnp.abs(error) * inverse_scale
        part = jnp.sum((weighted + log_scale) * valid, 0, keepdims=True)
        total = part if total is None else total + part
        direction = jnp.where(error > 0.0, 1.0, jnp.where(error < 0.0, -1.0, 0.0))
        grad_pred = (direction * inverse_scale * valid * inverse_count).astype(BF16)
        d.scale[group : group + 1, :] = (
            jnp.sum((1.0 - weighted) * valid, 0, keepdims=True) * inverse_count
        )
        d.head[group] = tn(active, grad_pred).astype(BF16)
        grad_raised = (gelu_slope(raised) * nt(grad_pred, head)).astype(BF16)
        d.decode[group] = tn(low, grad_raised).astype(BF16)
        back = nt(grad_raised, decode)
        grad_low = back if grad_low is None else grad_low + back
    d.loss[...] = total
    grad_values, d.final[...] = norm_backward(values, w.final, grad_low)
    send(d.scale, d.head, d.decode, d.loss, d.final)
    return grad_values


def shifted_backward(grad_out, w, s, flow, outs, tables, t, split, width):
    outs.grad_middle[...], grad_mixed = rest_backward(grad_out, w, s, flow, outs.norm_two)
    send(outs.grad_middle)
    grad_win = nn(tables.to_win[...], grad_mixed).astype(BF16)
    for win in range(4):
        rows = slice(72 * win, 72 * (win + 1))
        queries, keys, values = shifted_keys(s, win, width)
        grad_q, grad_k, grad_v = attend_window_back(
            queries, keys, values, grad_win[rows, :],
            tables.shift_key[WIN * win : WIN * (win + 1), :], tables.shift_query.at[win % 2],
            s.probs.at[win], t.q, t.g, t.o, t.s, split,
        )
        flow.near[rows, 0:width] = grad_q.astype(BF16)
        flow.near[rows, width : 2 * width] = grad_k[0:72].astype(BF16)
        flow.near[rows, 2 * width : 3 * width] = grad_v[0:72].astype(BF16)
        flow.far[rows, 0:width] = grad_k[72:144].astype(BF16)
        flow.far[rows, width : 2 * width] = grad_v[72:144].astype(BF16)
    rim = nt(flow.far[...], w.qkv[:, width:]).astype(BF16)
    outs.rim_a[...] = rim[0:WIN]
    outs.rim_b[...] = rim[WIN:]
    send(outs.rim_a, outs.rim_b, flow.near, flow.far)
    outs.grad_near[...] = nt(nn(tables.to_tok[...], flow.near[...]).astype(BF16), w.qkv[...])
    send(outs.grad_near)


def shifted_weights(near, far, s, flow, d, width):
    rest_weights(s, flow, d)
    near_rows, far_rows = both(*near), both(*far)
    d.qkv[:, 0:width] = tn(near_rows, flow.near[:, 0:width]).astype(BF16)
    d.qkv[:, width:] = (
        tn(near_rows, flow.near[:, width:]) + tn(far_rows, flow.far[...])
    ).astype(BF16)
    send(d.qkv)


def plain_backward(grad, arrived, w, s, flow, d, tables, t, split, width):
    grad_normed = grad.near[...] + nn(tables.to_tok[...], both(*arrived))
    grad_x, d.norm_next[...] = norm_backward(s.x_out[...], w.norm_next, grad_normed)
    grad_mid, grad_mixed = rest_backward(grad.middle[...] + grad_x, w, s, flow, d.norm_two)
    rest_weights(s, flow, d)
    for win in range(2):
        rows = slice(WIN * win, WIN * (win + 1))
        grads = attend_window_back(
            s.packed[rows, 0:width], s.packed[rows, width : 2 * width], s.packed[rows, 2 * width :],
            grad_mixed[rows, :], tables.plain_key[rows, :], tables.plain_query, s.probs.at[win],
            t.q, t.g, t.o, t.s, split,
        )
        for index, part in enumerate(grads):
            flow.near[rows, width * index : width * (index + 1)] = part.astype(BF16)
    near_grad = flow.near[...]
    d.qkv[...] = tn(s.normed[...], near_grad).astype(BF16)
    grad_first, d.norm_one[...] = norm_backward(s.x_in[...], w.norm_one, nt(near_grad, w.qkv[...]))
    send(d.norm_next, d.qkv, d.norm_one)
    return grad_mid + grad_first


def held(array):
    return pltpu.with_memory_space_constraint(array, pltpu.HBM)


def launch(name, body, ins, outs, scratch, limit=52 << 20, scalars=(), raw=(), sems=0, in_place=False):
    sources, views, shapes = [], [], []
    for value in ins.values():
        array, view, shape = value if isinstance(value, tuple) else (value, None, value.shape)
        sources.append(array)
        views.append(view)
        shapes.append(pltpu.VMEM(shape, array.dtype))
    n_in, n_out = len(ins), len(outs)
    n_first = len(scalars) + len(raw)
    own_sems = sems
    n_held = 0 if in_place else n_out

    def kernel(*refs):
        named = {"scalars": refs[: len(scalars)], "raw": refs[len(scalars) : n_first]}
        refs = refs[n_first:]
        far_in, far_out = refs[:n_in], refs[n_in : n_in + n_out]
        near = refs[n_in + n_out :]
        near_in, near_out = near[:n_in], near[n_in : n_in + n_held]
        spare, flags = near[n_in + n_held : -1], near[-1]
        named["sems"] = [flags.at[n_in + n_out + index] for index in range(own_sems)]
        copies, sizes = [], []
        for index, key in enumerate(ins):
            source = far_in[index] if views[index] is None else views[index](far_in[index])
            copies.append(pltpu.make_async_copy(source, near_in[index], flags.at[index]))
            sizes.append(math.prod(near_in[index].shape) * near_in[index].dtype.itemsize)
        queue = Queue(copies, sizes, AHEAD)
        for index, key in enumerate(ins):
            named[key] = Held(near_in[index], queue, index)
        for index, key in enumerate(outs):
            if in_place:
                named[key] = Made(None, None)
            else:
                copy = pltpu.make_async_copy(near_out[index], far_out[index], flags.at[n_in + index])
                named[key] = Made(near_out[index], copy)
            named[key].far, named[key].sem = far_out[index], flags.at[n_in + index]
        named.update(zip(scratch, spare))
        body(named)
        for key in ins:
            named[key].ready()
        for key in outs:
            named[key].send()
        for key in outs:
            named[key].copy.wait()

    results = pl.pallas_call(
        kernel,
        in_specs=[pl.BlockSpec(memory_space=pltpu.SMEM)] * len(scalars)
        + [pl.BlockSpec(memory_space=pl.ANY)] * (len(raw) + n_in),
        out_specs=[pl.BlockSpec(memory_space=pl.ANY)] * n_out,
        out_shape=[pltpu.HBM(shape, dtype) for shape, dtype in outs.values()],
        scratch_shapes=shapes
        + [pltpu.VMEM(shape, dtype) for shape, dtype in list(outs.values())[:n_held]]
        + [pltpu.VMEM(shape, dtype) for shape, dtype in scratch.values()]
        + [pltpu.SemaphoreType.DMA((n_in + n_out + sems,))],
        name=name,
        input_output_aliases={len(scalars) + at: at for at in range(len(raw))} if in_place else {},
        compiler_params=pltpu.CompilerParams(vmem_limit_bytes=limit),
    )(*scalars, *[held(array) for array in (*raw, *sources)])
    return dict(zip(outs, results))


def part(named, prefix):
    return Refs(**{key[len(prefix) :]: ref for key, ref in named.items() if key.startswith(prefix)})


def prefixed(prefix, values):
    return {prefix + key: value for key, value in values.items()}


def probs_width(split, n_query):
    return 128 * sum(columns_of(n_heads, n_query) for lane, lanes, n_heads in split)


def spread_shape(split, n_query):
    rows = 128 * max(columns_of(n_heads, n_query) for lane, lanes, n_heads in split)
    return (rows, max(lanes for lane, lanes, n_heads in split))


def saved_outs(width, split, shifted):
    n_query, n_win = (72, 4) if shifted else (WIN, 2)
    found = {"packed": ((TOKENS, 3 * width), BF16)}
    if shifted:
        found["packed_far"] = ((TOKENS, 2 * width), BF16)
    else:
        found["x_in"] = ((TOKENS, width), F32)
        found["normed"] = ((TOKENS, width), BF16)
    found["probs"] = ((n_win, WIN, probs_width(split, n_query)), BF16)
    found["mixed"] = ((TOKENS, width), BF16)
    found["middle"] = ((TOKENS, width), F32)
    found["normed_two"] = ((TOKENS, width), BF16)
    found["raised"] = ((TOKENS, 4 * width), F32)
    found["active"] = ((TOKENS, 4 * width), BF16)
    return found


def flow_shapes(width, shifted):
    found = {
        "low": ((TOKENS, width), BF16),
        "raised": ((TOKENS, 4 * width), BF16),
        "branch": ((TOKENS, width), BF16),
        "near": ((TOKENS, 3 * width), BF16),
    }
    if shifted:
        found["far"] = ((TOKENS, 2 * width), BF16)
    return found


def spare(width, split, shifted, backward):
    n_query = 72 if shifted else WIN
    shape = spread_shape(split, n_query)
    found = {"q": (shape, BF16), "o": (shape, F32)}
    if shifted:
        found["m"] = ((TOKENS, width), F32)
    if backward:
        found["g"] = (shape, BF16)
        found["s"] = ((WIN, shape[0]), BF16)
    return found


def rim_outs(width):
    found = {"grad_middle": ((TOKENS, width), F32), "grad_near": ((TOKENS, width), F32)}
    found["rim_a"] = found["rim_b"] = ((WIN, width), BF16)
    found["norm_two"] = ((2, width), F32)
    return found


def weight_grads(width):
    return {
        "down": ((4 * width, width), BF16),
        "up": ((width, 4 * width), BF16),
        "proj": ((width, width), BF16),
        "qkv": ((width, 3 * width), BF16),
    }


def window_order():
    order = []
    for half in range(2):
        for pair in ((1, 2), (3, 0)):
            for level in pair:
                for row in range(3):
                    for col in range(12):
                        order.append(level * 72 + (half * 3 + row) * 12 + col)
    return np.array(order)


def fixed_tables():
    order = window_order()
    to_win = np.zeros((TOKENS, TOKENS), np.float32)
    to_win[np.arange(TOKENS), order] = 1.0
    region = np.zeros((2, 72), np.float32)
    for pair, levels in enumerate(((1, 2), (3, 0))):
        for place in range(72):
            level, col = levels[place // 36], place % 12
            region[pair, place] = 2.0 * (level == 0) + 1.0 * (col < 6)
    return to_win, region


def key_codes(extent, first_lat):
    place = lax.broadcasted_iota(jnp.int32, (TOKENS, 128), 0)
    row, col = (place // 12) % 6, place % 12
    inside = (first_lat + row < extent[0]) & (col < extent[1])
    plain = jnp.where(inside, 0.0, -1.0)
    place = lax.broadcasted_iota(jnp.int32, (2 * TOKENS, 128), 0)
    win, rest = place // WIN, place % WIN
    far, rest = rest // 72, rest % 72
    half, pair = win // 2, win % 2
    second = rest // 36
    row, col = (rest // 12) % 3, rest % 12
    near_row = 3 * half + row
    far_row = jnp.where(half == 0, row - 3, row + 6)
    lat = first_lat + jnp.where(far == 1, far_row, near_row)
    top = (pair == 1) & (second == 1)
    region = jnp.where(top, 2.0, 0.0) + jnp.where(col < 6, 1.0, 0.0)
    inside = (lat >= 0) & (lat < extent[0]) & (col < extent[1])
    return plain, jnp.where(inside, region, -1.0)


def exchange(first, second):
    count = lax.axis_size("band")
    up = [(i, i + 1) for i in range(count - 1)]
    down = [(i + 1, i) for i in range(count - 1)]
    return lax.ppermute(second, "band", up), lax.ppermute(first, "band", down)


def shift_query_codes(region, split):
    parts = []
    for lane, lanes, n_heads in split:
        total = 128 * columns_of(n_heads, 72)
        tiled = np.tile(region, (1, n_heads))
        parts.append(np.pad(tiled, ((0, 0), (0, total - tiled.shape[1]))))
    return jnp.asarray(np.concatenate(parts, 1)[:, None, :], F32)


WIDTHS = {"enc": (D_ENC, ENC_SPLIT), "trunk": (D_TRUNK, TRUNK_SPLIT)}
FORWARD_ORDER = ("norm_one", "qkv", "proj", "norm_two", "up", "down")
BACKWARD_ORDER = ("down", "up", "norm_two", "proj", "qkv", "norm_one")


def compute(weights, unpack_trunk, pack_trunk, source, goal, codes, count):
    to_win, region = fixed_tables()
    order = {"to_win": jnp.asarray(to_win, BF16), "to_tok": jnp.asarray(to_win.T, BF16)}
    grads = {}

    def tables(tower, names):
        split = WIDTHS[tower][1]
        found = {
            "plain_key": codes[0],
            "shift_key": codes[1],
            "plain_query": jnp.zeros((1, probs_width(split, WIN)), F32),
            "shift_query": shift_query_codes(region, split),
        } | order
        return prefixed("c_", {name: found[name] for name in names})

    PLAIN = ("plain_key", "plain_query", "to_win")
    SHIFTED = ("shift_key", "shift_query", "to_tok")

    def of(key, group):
        array = weights[key]
        if group is None:
            return array
        return (array, lambda ref: ref.at[group], array.shape[1:])

    def block(mark, tower, layer, group, names, with_next=False):
        found = {name: of((tower, layer, name), group) for name in names}
        if with_next:
            found["norm_next"] = of((tower, layer + 1, "norm_one"), group)
        return prefixed(mark, found)

    def src(group):
        lanes = pl.ds(PIN * group, PIN)
        return (source, lambda ref: ref.at[:, lanes], (TOKENS, PIN))

    groups = range(GROUPS)
    enc_width, enc_split = WIDTHS["enc"]
    width, split = WIDTHS["trunk"]

    def enc_plain():
        def body(r):
            for group in groups:
                s = part(r, f"s{group}_")
                s.near_a, s.near_b = r["near_a"].at[group], r["near_b"].at[group]
                plain_forward(
                    nn(r[f"src{group}"][...], r[f"embed{group}"][...]), part(r, f"w{group}_"), s,
                    part(r, "c_"), part(r, "t_"), enc_split, enc_width,
                )
            send(r["near_a"], r["near_b"])

        ins, outs = {}, {"near_a": ((GROUPS, WIN, enc_width), BF16)}
        outs["near_b"] = outs["near_a"]
        for group in groups:
            ins |= {f"src{group}": src(group), f"embed{group}": of(("enc", -1, "embed"), group)}
            ins |= block(f"w{group}_", "enc", 0, group, FORWARD_ORDER, True)
            ins |= tables("enc", PLAIN) if group == 0 else {}
            kept = saved_outs(enc_width, enc_split, False) | {"x_out": ((TOKENS, enc_width), F32)}
            outs |= prefixed(f"s{group}_", kept)
        return launch(
            "enc_plain", body, ins, outs, prefixed("t_", spare(enc_width, enc_split, False, False))
        )

    def middle(before, far):
        def body(r):
            last = []
            for group in groups:
                rows = [r[name].at[group] for name in ("near_a", "near_b", "far_a", "far_b")]
                last.append(
                    shifted_forward(
                        r[f"x_in{group}"], rows[:2], rows[2:], part(r, f"w{group}_"),
                        part(r, f"s{group}_"), part(r, "e_"), part(r, "t_"), enc_split, enc_width,
                    )
                )
            joined = jnp.concatenate(last, 1).astype(BF16)
            r["joined"][...] = joined
            s = part(r, "s_")
            s.near_a, s.near_b = r["trunk_a"], r["trunk_b"]
            plain_forward(
                nn(joined, r["joining"][...]), part(r, "w_"), s, part(r, "c_"), part(r, "u_"),
                split, width,
            )

        ins = {"near_a": before["near_a"], "near_b": before["near_b"], "far_a": far[0], "far_b": far[1]}
        outs = {}
        for group in groups:
            ins |= block(f"w{group}_", "enc", 1, group, FORWARD_ORDER[1:])
            if group == 0:
                found = tables("enc", SHIFTED)
                ins |= {"e_" + key[2:]: value for key, value in found.items()}
            ins |= {f"x_in{group}": before[f"s{group}_x_out"]}
            outs |= prefixed(f"s{group}_", saved_outs(enc_width, enc_split, True))
        ins |= {"joining": weights["trunk", -1, "joining"]}
        ins |= block("w_", "trunk", 0, None, FORWARD_ORDER, True) | tables("trunk", PLAIN)
        outs |= {"joined": ((TOKENS, 2 * D_ENC), BF16)}
        outs |= prefixed("s_", saved_outs(width, split, False) | {"x_out": ((TOKENS, width), F32)})
        outs |= {"trunk_a": ((WIN, width), BF16), "trunk_b": ((WIN, width), BF16)}
        return launch(
            "middle", body, ins, outs,
            prefixed("t_", spare(enc_width, enc_split, True, False))
            | prefixed("u_", spare(width, split, False, False)),
        )

    def trunk_top(before, far):
        def body(r):
            w, s, c, t = part(r, "w_"), part(r, "s_"), part(r, "c_"), part(r, "t_")
            last = shifted_forward(
                r["x_in"], (r["near_a"], r["near_b"]), (r["far_a"], r["far_b"]),
                w, s, c, t, split, width,
            )
            grad = loss_part(last, r["goal"], c, r["count"], part(r, "h_"), part(r, "d_"))
            shifted_backward(grad, w, s, part(r, "f_"), part(r, "b_"), c, t, split, width)

        kept = saved_outs(width, split, True)
        reused = ("mixed", "normed_two", "active")
        top = {name: weights["top", -1, name] for name in ("decode", "head", "scale")}
        found = launch(
            "trunk_top", body,
            {"near_a": before["trunk_a"], "near_b": before["trunk_b"], "far_a": far[0], "far_b": far[1]}
            | block("w_", "trunk", 1, None, FORWARD_ORDER[1:])
            | tables("trunk", SHIFTED + ("to_win", "plain_key"))
            | {"x_in": before["s_x_out"]}
            | prefixed("h_", {"final": weights["trunk", -1, "final"]} | top)
            | {"goal": goal, "count": count},
            prefixed("s_", {name: kept[name] for name in reused})
            | prefixed("f_", flow_shapes(width, True)) | prefixed("b_", rim_outs(width))
            | prefixed("d_", {
                "final": ((2, width), F32), "decode": ((GROUPS, D_TRUNK, D_ENC), BF16),
                "head": ((GROUPS, D_ENC, PIN), BF16), "scale": ((GROUPS, PIN), F32),
                "loss": ((1, PIN), F32),
            }),
            prefixed("s_", {name: kept[name] for name in kept if name not in reused})
            | prefixed("t_", spare(width, split, True, True)),
        )
        grads["trunk", -1, "final", None] = found["d_final"]
        for name in ("decode", "head", "scale"):
            grads["top", -1, name, "all"] = found["d_" + name]
        grads["trunk", 1, "norm_two", None] = found["b_norm_two"]
        return found

    def trunk_top_weights(before, far, found):
        def body(r):
            shifted_weights(
                (r["near_a"], r["near_b"]), (r["far_a"], r["far_b"]), part(r, "s_"), part(r, "f_"),
                part(r, "d_"), width,
            )

        results = launch(
            "trunk_top_weights", body,
            {key: found[key] for key in found if key[:2] in ("s_", "f_")}
            | {"near_a": before["trunk_a"], "near_b": before["trunk_b"], "far_a": far[0], "far_b": far[1]},
            prefixed("d_", weight_grads(width)), {},
        )
        for key, grad in results.items():
            grads["trunk", 1, key[2:], None] = grad
        return results["d_qkv"]

    PLAIN_KEPT = ("raised", "middle", "active", "normed_two", "mixed", "packed", "probs", "normed", "x_in")
    SHIFT_KEPT = ("raised", "middle", "packed", "packed_far", "probs", "active", "normed_two", "mixed")
    GAINS = ("norm_next", "norm_one", "norm_two")

    def plain_back_ins(mark, tower, group, kept, kept_mark):
        found = {f"w{mark}norm_next": of((tower, 1, "norm_one"), group)}
        found |= block(f"w{mark}", tower, 0, group, BACKWARD_ORDER)
        return found | {f"s{mark}{name}": kept[kept_mark + name] for name in PLAIN_KEPT}

    def keep_plain_grads(tower, group, found, mark):
        grads[tower, 1, "norm_one", group] = found[mark + "norm_next"]
        for name in ("down", "up", "proj", "qkv", "norm_one", "norm_two"):
            grads[tower, 0, name, group] = found[mark + name]

    def middle_back(top, arrived, before, first, far):
        def body(r):
            grad = plain_backward(
                part(r, "g_"), (r["arrived_a"], r["arrived_b"]), part(r, "w_"), part(r, "s_"),
                part(r, "f_"), part(r, "d_"), part(r, "c_"), part(r, "t_"), split, width,
            ).astype(BF16)
            r["d_joining"][...] = tn(r["joined"][...], grad).astype(BF16)
            send(r["d_joining"])
            r["v_grad"][...] = nt(grad, r["joining"][...])
            for group in groups:
                s, f, b = part(r, f"s{group}_"), part(r, "e_"), part(r, f"b{group}_")
                rows = [r[name].at[group] for name in ("near_a", "near_b", "far_a", "far_b")]
                b.rim_a, b.rim_b = r["rim_a"].at[group], r["rim_b"].at[group]
                shifted_backward(
                    r["v_grad"][:, enc_width * group : enc_width * (group + 1)],
                    part(r, f"w{group}_"), s, f, b, part(r, "k_"), part(r, "u_"), enc_split, enc_width,
                )
                shifted_weights(rows[:2], rows[2:], s, f, part(r, f"d{group}_"), enc_width)
            send(r["rim_a"], r["rim_b"])

        ins = {"g_near": top["b_grad_near"], "c_to_tok": order["to_tok"]}
        ins |= {"arrived_a": arrived[0], "arrived_b": arrived[1], "s_x_out": before["s_x_out"]}
        ins |= {"g_middle": top["b_grad_middle"]} | plain_back_ins("_", "trunk", None, before, "s_")
        ins |= tables("trunk", ("plain_key", "plain_query"))
        ins |= {"joined": before["joined"], "joining": weights["trunk", -1, "joining"]}
        outs = prefixed("d_", {name: ((2, width), F32) for name in GAINS} | weight_grads(width))
        outs |= {"d_joining": ((GROUPS * D_ENC, D_TRUNK), BF16)}
        outs |= {"rim_a": ((GROUPS, WIN, enc_width), BF16), "rim_b": ((GROUPS, WIN, enc_width), BF16)}
        for group in groups:
            ins |= block(f"w{group}_", "enc", 1, group, BACKWARD_ORDER[:-1])
            ins |= {f"s{group}_{name}": before[f"s{group}_{name}"] for name in SHIFT_KEPT}
            if group == 0:
                found = tables("enc", SHIFTED + ("to_win",))
                ins |= {"k_" + key[2:]: value for key, value in found.items()}
                ins |= {"near_a": first["near_a"], "near_b": first["near_b"]}
                ins |= {"far_a": far[0], "far_b": far[1]}
            found = rim_outs(enc_width)
            kept = {name: found[name] for name in ("grad_middle", "grad_near", "norm_two")}
            outs |= prefixed(f"b{group}_", kept) | prefixed(f"d{group}_", weight_grads(enc_width))
        found = launch(
            "middle_back", body, ins, outs,
            prefixed("t_", spare(width, split, False, True)) | prefixed("f_", flow_shapes(width, False))
            | prefixed("u_", spare(enc_width, enc_split, True, True))
            | prefixed("e_", flow_shapes(enc_width, True)) | {"v_grad": ((TOKENS, width), F32)},
        )
        keep_plain_grads("trunk", None, found, "d_")
        grads["trunk", -1, "joining", None] = found["d_joining"]
        for group in groups:
            grads["enc", 1, "norm_two", group] = found[f"b{group}_norm_two"]
            for name in weight_grads(enc_width):
                grads["enc", 1, name, group] = found[f"d{group}_{name}"]
        return found

    def enc_plain_back(back, arrived, first):
        def body(r):
            for group in groups:
                grad = plain_backward(
                    part(r, f"g{group}_"), (r["arrived_a"].at[group], r["arrived_b"].at[group]),
                    part(r, f"w{group}_"), part(r, f"s{group}_"), part(r, "f_"), part(r, f"d{group}_"),
                    part(r, "c_"), part(r, "t_"), enc_split, enc_width,
                ).astype(BF16)
                r[f"d{group}_embed"][...] = tn(r[f"src{group}"][...], grad).astype(BF16)
                send(r[f"d{group}_embed"])

        ins = {"arrived_a": arrived[0], "arrived_b": arrived[1], "c_to_tok": order["to_tok"]}
        outs = {}
        for group in groups:
            ins |= {f"g{group}_near": back[f"b{group}_grad_near"]}
            ins |= {f"s{group}_x_out": first[f"s{group}_x_out"]}
            ins |= {f"g{group}_middle": back[f"b{group}_grad_middle"]}
            ins |= plain_back_ins(f"{group}_", "enc", group, first, f"s{group}_")
            ins |= tables("enc", ("plain_key", "plain_query")) if group == 0 else {}
            ins |= {f"src{group}": src(group)}
            outs |= prefixed(
                f"d{group}_",
                {name: ((2, enc_width), F32) for name in GAINS}
                | weight_grads(enc_width) | {"embed": ((PIN, D_ENC), BF16)},
            )
        found = launch(
            "enc_plain_back", body, ins, outs,
            prefixed("t_", spare(enc_width, enc_split, False, True))
            | prefixed("f_", flow_shapes(enc_width, False)),
        )
        for group in groups:
            keep_plain_grads("enc", group, found, f"d{group}_")
            grads["enc", -1, "embed", group] = found[f"d{group}_embed"]

    first = enc_plain()
    far = exchange(first["near_a"], first["near_b"])
    found = unpack_trunk(first["near_a"])
    *far, found = lax.optimization_barrier((*far, found))
    weights = weights | found
    second = middle(first, far)
    trunk_far = exchange(second["trunk_a"], second["trunk_b"])
    top = trunk_top(second, trunk_far)
    arrived = exchange(top["b_rim_a"], top["b_rim_b"])
    last = trunk_top_weights(second, trunk_far, top)
    *arrived, last = lax.optimization_barrier((*arrived, last))
    grads["trunk", 1, "qkv", None] = last
    back = middle_back(top, arrived, second, first, far)
    arrived = exchange(back["rim_a"], back["rim_b"])
    packed = pack_trunk(grads)
    *arrived, packed = lax.optimization_barrier((*arrived, packed))
    enc_plain_back(back, arrived, first)
    return top["d_loss"], grads, packed


def stacked_key(label_key):
    tower, group, layer, name = label_key
    return (tower, layer, name), (group if tower in ("enc", "top") else None)


BLOCK_ELEMENTS = 2048


def share_rows(n_own):
    blocks = -(-(n_own + BLOCK_ELEMENTS - 1) // BLOCK_ELEMENTS) + 1
    return 16 * 3 * (-(-blocks // 3))


def first_row(n_own, device):
    return (n_own * device // BLOCK_ELEMENTS) * 16


def grouped_pieces():
    found = {}
    for label_key, dims_shape, offset in placed():
        key, group = stacked_key(label_key)
        found.setdefault(key, (dims_shape, []))[1].append((group, offset // 128))
    return [(key, places, dims_shape) for key, (dims_shape, places) in found.items()]


def is_gain(key):
    return key[2] in ("norm_one", "norm_two", "final")


def stacked_shape(places, dims_shape):
    if len(dims_shape) == 1:
        return (len(places),) + dims_shape
    return dims_shape if places[0][0] is None else (len(places),) + dims_shape


def turned(values):
    return pltpu.roll(values, 64, 1)


def lower_half(values):
    return lax.broadcasted_iota(jnp.int32, values.shape, 1) < 64


def read_gain(flat, offset, width, out):
    if width % 128 == 0:
        count = width // 128
        for row in range(2):
            for tile in range(count):
                at = offset + row * count + tile
                out[row : row + 1, 128 * tile : 128 * tile + 128] = flat[at : at + 1, :]
        return
    rows = [flat[offset + place : offset + place + 1, :] for place in range(3)]
    out[0:1, 0:128] = rows[0]
    out[0:1, 128:192] = rows[1][:, 0:64]
    out[1:2, 0:128] = jnp.where(lower_half(rows[1]), turned(rows[1]), turned(rows[2]))
    out[1:2, 128:192] = rows[2][:, 64:128]


def read_matrix(flat, offset, shape, out, wide_scr):
    height, width = shape
    step = 64
    if width % 128 == 0:
        count = width // 128

        def body(index, carry):
            row = pl.multiple_of(index * step, step)
            for tile in range(count):
                start = offset + tile + row * count
                piece = flat[pl.ds(start, step, stride=count), :]
                out[pl.ds(row, step), 128 * tile : 128 * tile + 128] = piece.astype(BF16)
            return carry

        lax.fori_loop(0, height // step, body, 0)
        return
    half = width // 128
    period = 2 * half + 1

    def body(index, carry):
        row = pl.multiple_of(index * step, step)
        start = offset + (row // 2) * period
        rows = [flat[pl.ds(start + place, step // 2, stride=period), :] for place in range(period)]
        late = [turned(rows[half + place]) for place in range(half + 1)]
        for tile in range(half + 1):
            odd_rows = late[tile]
            if tile < half:
                odd_rows = jnp.where(lower_half(late[tile]), late[tile], late[tile + 1])
            wide_scr[pl.ds(step * tile, step // 2, stride=2), :] = rows[tile]
            wide_scr[pl.ds(step * tile + 1, step // 2, stride=2), :] = odd_rows
            end = min(128, width - 128 * tile)
            tile_rows = wide_scr[step * tile : step * (tile + 1), 0:end]
            out[pl.ds(row, step), 128 * tile : 128 * tile + end] = tile_rows.astype(BF16)
        return carry

    lax.fori_loop(0, height // step, body, 0)


def write_gain(flat, offset, width, values):
    if width % 128 == 0:
        count = width // 128
        for row in range(2):
            for tile in range(count):
                at = offset + row * count + tile
                flat[at : at + 1, :] = values[row : row + 1, 128 * tile : 128 * tile + 128]
        return
    flat[offset : offset + 1, :] = values[0:1, 0:128]
    first, second = values[1:2, 0:64], values[1:2, 64:192]
    flat[offset + 1 : offset + 2, :] = jnp.concatenate([values[0:1, 128:192], first], 1)
    flat[offset + 2 : offset + 3, :] = second


def write_matrix(flat, offset, shape, source, wide_scr):
    height, width = shape
    step = 64
    if width % 128 == 0:
        count = width // 128

        def body(index, carry):
            row = pl.multiple_of(index * step, step)
            for tile in range(count):
                start = offset + tile + row * count
                piece = source[pl.ds(row, step), 128 * tile : 128 * tile + 128]
                flat[pl.ds(start, step, stride=count), :] = piece.astype(F32)
            return carry

        lax.fori_loop(0, height // step, body, 0)
        return
    half = width // 128
    period = 2 * half + 1

    def body(index, carry):
        row = pl.multiple_of(index * step, step)
        start = offset + (row // 2) * period
        for tile in range(half + 1):
            end = min(128, width - 128 * tile)
            tile_rows = source[pl.ds(row, step), 128 * tile : 128 * tile + end].astype(F32)
            wide_scr[step * tile : step * (tile + 1), 0:end] = tile_rows
        early = [wide_scr[pl.ds(step * tile, step // 2, stride=2), :] for tile in range(half + 1)]
        late = [
            turned(wide_scr[pl.ds(step * tile + 1, step // 2, stride=2), :])
            for tile in range(half + 1)
        ]
        low = lower_half(late[0])
        rows = early[:half] + [jnp.where(low, early[half], late[0])]
        rows += [jnp.where(low, late[tile], late[tile + 1]) for tile in range(half)]
        for place, value in enumerate(rows):
            flat[pl.ds(start + place, step // 2, stride=period), :] = value
        return carry

    lax.fori_loop(0, height // step, body, 0)


def wide_scratch(rows):
    return {"flat": ((rows, 128), F32), "wide": ((5 * 64, 128), F32)}


def trunk_row():
    return min(places[0][1] for key, places, dims_shape in grouped_pieces() if key[0] == "trunk")


def unpack_weights(gathered, n_own, trunk):
    pieces = [piece for piece in grouped_pieces() if (piece[0][0] == "trunk") == trunk]
    n_devices, rows, unused = gathered.shape
    edge = trunk_row() * 128
    low, high = (edge // n_own, n_devices) if trunk else (0, -(-edge // n_own))
    base = first_row(n_own, low)
    n_held = high - low
    cuts = [n_held * index // 8 for index in range(9)]
    step = rows // 6
    outs = {}
    for key, places, dims_shape in pieces:
        small = is_gain(key) or len(dims_shape) == 1
        outs[key] = (stacked_shape(places, dims_shape), F32 if small else BF16)

    def body(r):
        flat, wide, shares, source = r["flat"], r["wide"], r["shares"], r["raw"][0]
        copies = []
        for index, (start, stop) in enumerate(zip(cuts[:-1], cuts[1:])):
            span, held_span = pl.ds(low + start, stop - start), pl.ds(start, stop - start)
            copy = pltpu.make_async_copy(source.at[span], shares.at[held_span], r["sems"][index])
            copy.start()
            copies.append(copy)

        def place(index, carry):
            start = n_own * (low + index) // BLOCK_ELEMENTS * 16 - base
            start = pl.multiple_of(start, 16)
            kept = jnp.where(index > 0, flat[pl.ds(start, 16), :], 0.0)
            flat[pl.ds(start, 16), :] = kept + shares[index, 0:16, :].astype(F32)
            flat[pl.ds(start + 16, step - 16), :] = shares[index, 16:step, :].astype(F32)
            for number in range(1, 6):
                at = pl.ds(start + number * step, step)
                flat[at, :] = shares[index, number * step : (number + 1) * step, :].astype(F32)
            return carry

        for index in range(8):
            copies[index].wait()
            lax.fori_loop(cuts[index], cuts[index + 1], place, 0)
        for key, places, dims_shape in pieces:
            for group, offset in places:
                offset = offset - base
                view = r[key] if group is None or len(dims_shape) == 1 else r[key].at[group]
                if len(dims_shape) == 1:
                    view[group : group + 1, :] = flat[offset : offset + 1, :]
                elif is_gain(key):
                    read_gain(flat, offset, dims_shape[1], view)
                else:
                    read_matrix(flat, offset, dims_shape, view, wide)
            r[key].send()

    return launch(
        "unpack_trunk" if trunk else "unpack", body, {}, outs,
        {"shares": ((n_held,) + gathered.shape[1:], BF16)}
        | wide_scratch(first_row(n_own, high - 1) + rows - base),
        limit=60 << 20, raw=(gathered,), sems=8,
    )


def cuts_of(rows):
    blocks = rows // 16
    last = blocks * 11 // 45
    first = (blocks - last) // 2
    return 16 * first, 16 * (blocks - last - first), 16 * last


def step_of(rows):
    blocks = rows // 16
    return 16 * max(count for count in range(1, 13) if blocks % count == 0)


def pack_grads(grads, n_own, n_devices, core, before=None):
    early = before is None
    rows = share_rows(n_own)
    cuts = cuts_of(rows)
    n_chips = n_devices // 2
    middle = -(-trunk_row() * 128 // (2 * n_own))
    low, high = (middle, n_chips) if early else (0, middle)
    base = trunk_row() // 16 * 16 if early else 0
    end = first_row(n_own, 2 * high - 1) + rows
    pieces = [
        (key, group, offset, dims_shape)
        for key, places, dims_shape in grouped_pieces()
        for group, offset in places
        if (key[0] == "trunk" if early else offset < end)
    ]
    last = max(offset + math.prod(dims_shape) // 128 for key, group, offset, dims_shape in pieces)
    names = [(side, index) for side in ("kept", "sent") for index in range(3)]
    outs = {name: ((n_chips, cuts[name[1]], 128), BF16) for name in names}

    def held_as(key, group):
        return key + ("all" if key[0] == "top" else group,)

    ins = {held_as(key, group): grads[held_as(key, group)] for key, group, offset, dims_shape in pieces}

    def body(r):
        flat, wide, core = r["flat"], r["wide"], r["scalars"][0]
        if last < end:
            flat[last - base :, :] = jnp.zeros((flat.shape[0] - last + base, 128), F32)
        for key, group, offset, dims_shape in pieces:
            offset = offset - base
            held_ref = r[held_as(key, group)]
            if len(dims_shape) == 1:
                flat[offset : offset + 1, :] = held_ref[group : group + 1, :]
                continue
            source = held_ref.at[group] if key[0] == "top" else held_ref.ready()
            if is_gain(key):
                write_gain(flat, offset, dims_shape[1], source)
            else:
                write_matrix(flat, offset, dims_shape, source, wide)

        def chip(index, carry):
            for side, device in (("sent", 2 * index + 1 - core[0]), ("kept", 2 * index + core[0])):
                start = pl.multiple_of(n_own * device // BLOCK_ELEMENTS * 16 - base, 16)
                done = 0
                for which, rows in enumerate(cuts):
                    place, far, sem = r[f"{side}{which}"], r[side, which].far, r[side, which].sem
                    step = step_of(rows)
                    for row in range(0, rows, step):
                        values = flat[pl.ds(start + done + row, step), :]
                        place[index - low, row : row + step, :] = values.astype(BF16)
                    done += rows
                    pltpu.make_async_copy(place.at[index - low], far.at[index], sem).start()
            return carry

        lax.fori_loop(low, high, chip, 0)
        for side, which in names:
            place, out = r[f"{side}{which}"], r[side, which]
            out.copy = pltpu.make_async_copy(place, out.far.at[pl.ds(low, high - low)], out.sem)
            out.sent = True

    scratch = wide_scratch(max(end, last) - base)
    scratch |= {f"{side}{which}": ((high - low, cuts[which], 128), BF16) for side, which in names}
    return launch(
        "pack_trunk" if early else "pack", body, ins, outs, scratch, limit=60 << 20,
        scalars=(core.reshape(1),), raw=() if early else [before[name] for name in names], in_place=True,
    )


class Torus:
    def __init__(self):
        self.totals = {"dp": lax.axis_size("dp"), "band": lax.axis_size("band")}
        depth = min(4, self.totals["dp"])
        across = self.totals["dp"] // depth
        self.axes = {
            "z": (depth, across, "dp"),
            "x": (across, 1, "dp"),
            "y": (self.totals["band"] // 2, 2, "band"),
            "core": (2, 1, "band"),
        }

    def size(self, axis):
        return self.axes[axis][0]

    def place(self, axis):
        count, stride, name = self.axes[axis]
        return lax.axis_index(name) // stride % count

    def move(self, values, axis, by):
        count, stride, name = self.axes[axis]
        pairs = []
        for place in range(self.totals[name]):
            at = place // stride % count
            pairs.append((place, place + ((at + by) % count - at) * stride))
        return lax.ppermute(values, name, pairs)


def scatter_terms(torus, terms, dims, axis):
    dim = dims.index(axis)
    place = torus.place(axis)
    arrived = []
    for by in range(1, torus.size(axis)):
        other = (place + by) % torus.size(axis)
        pieces = [lax.dynamic_index_in_dim(term, other, dim, keepdims=False) for term in terms]
        total = sum(piece.astype(F32) for piece in pieces).astype(BF16)
        arrived.append(torus.move(total, axis, by))
    own = [lax.dynamic_index_in_dim(term, place, dim, keepdims=False) for term in terms]
    return own + arrived, [name for name in dims if name != axis]


SCATTER_ORDERS = (("y", "x", "z"), ("x", "y", "z"), ("z", "x", "y"))


def scatter_sum(packed):
    torus = Torus()
    dims = ["z", "x", "y"]
    shape = tuple(torus.size(axis) for axis in dims)
    sequence = (2, 0, 1)
    state = {}
    for part in sequence:
        near, far = packed["kept", part], packed["sent", part]
        near, far = near.reshape(shape + near.shape[1:]), far.reshape(shape + far.shape[1:])
        state[part] = ([near, torus.move(far, "core", 1)], dims)
    for step in range(3):
        for part in sequence if step < 2 else (2,):
            terms, left = state[part]
            state[part] = scatter_terms(torus, terms, left, SCATTER_ORDERS[part][step])

    def at_depth(place):
        found = []
        for part in (0, 1):
            pieces = [lax.dynamic_index_in_dim(term, place, 0, keepdims=False) for term in state[part][0]]
            found.append(sum(piece.astype(F32) for piece in pieces))
        return jnp.concatenate(found, 0)

    depth, place = torus.size("z"), torus.place("z")
    arrived = [
        torus.move(at_depth((place + by) % depth).astype(BF16), "z", by) for by in range(1, depth)
    ]
    first = at_depth(place) + sum(term.astype(F32) for term in arrived)
    return jnp.concatenate([first, sum(term.astype(F32) for term in state[2][0])], 0)


def all_sum(values):
    for axis in ("band", "dp"):
        count = lax.axis_size(axis)
        bit = 1
        while bit < count:
            pairs = [(i, i ^ bit) for i in range(count)]
            values = values + lax.ppermute(values, axis, pairs)
            bit *= 2
    return values


def shards(inputs, targets, crop_extent, master, moment_one, moment_two, step_count):
    n_own = master.shape[0]
    n_bands = lax.axis_size("band")
    n_devices = lax.axis_size("dp") * n_bands
    rows = share_rows(n_own)
    device = lax.axis_index("dp") * n_bands + lax.axis_index("band")
    shift = (n_own * device) % BLOCK_ELEMENTS
    extent = crop_extent[0]
    spread = jnp.pad(master, (BLOCK_ELEMENTS, rows * 128 - n_own))
    share = lax.dynamic_slice(spread, (BLOCK_ELEMENTS - shift,), (rows * 128,)).astype(BF16)
    share = lax.dynamic_update_slice(share, extent.astype(BF16), ((rows - 1) * 128,))
    gathered = lax.all_gather(share.reshape(rows, 128), ("dp", "band"), axis=0, tiled=False)
    extents = gathered[::n_bands, rows - 1, 0:2].astype(F32)
    weights = unpack_weights(gathered, n_own, False)
    n_rows, n_levels = inputs.shape[1], inputs.shape[2]
    source = inputs[0].transpose(1, 0, 2, 3).reshape(TOKENS, GROUPS * PIN)
    goal = targets[0].transpose(1, 0, 2, 3).reshape(TOKENS, GROUPS * PIN)
    first_lat = lax.axis_index("band") * n_rows
    norm_count = jnp.sum(extents[:, 0] * extents[:, 1]) * (n_levels * GROUPS * PIN)
    core = lax.axis_index("band") % 2

    def unpack_trunk(after):
        later, unused = lax.optimization_barrier((gathered, after))
        return unpack_weights(later, n_own, True)

    def pack_trunk(grads):
        return pack_grads(grads, n_own, n_devices, core)

    loss_row, grads, packed = compute(
        weights, unpack_trunk, pack_trunk, source, goal, key_codes(extent, first_lat),
        jnp.full((1, PIN), norm_count),
    )
    packed = pack_grads(grads, n_own, n_devices, core, packed)
    owned = scatter_sum(packed)
    grad_shard = lax.dynamic_slice(owned.reshape(-1), (shift,), (n_own,))
    shard_square = jnp.sum(grad_shard * grad_shard)
    lanes = lax.broadcasted_iota(jnp.int32, (8, 128), 1)
    both = jnp.where(lanes < 64, shard_square, jnp.sum(loss_row))
    both = all_sum(both)
    grad_norm = jnp.sqrt(both[0, 0])
    loss_total = both[0, 64]
    factor_clip = jnp.minimum(1.0, CLIP_LEVEL / (grad_norm + 1e-06))
    clipped = grad_shard * factor_clip
    new_one = BETA_ONE * moment_one + (1.0 - BETA_ONE) * clipped
    new_two = BETA_TWO * moment_two + (1.0 - BETA_TWO) * clipped * clipped
    step_value = step_count[0].astype(F32)
    fix_one = 1.0 - jnp.power(BETA_ONE, step_value)
    fix_two = 1.0 - jnp.power(BETA_TWO, step_value)
    update = new_one / fix_one / (jnp.sqrt(new_two / fix_two) + ADAM_EPS) + WEIGHT_DECAY * master
    new_master = master - LEARN_RATE * update
    return (
        new_master,
        new_one,
        new_two,
        new_master.astype(BF16),
        loss_total / norm_count,
        grad_norm,
    )


def solution(mesh):
    in_specs = (
        P("dp", "band", None, None, None),
        P("dp", "band", None, None, None),
        P("dp", None),
        P(("dp", "band")),
        P(("dp", "band")),
        P(("dp", "band")),
        P(),
    )
    out_specs = (
        P(("dp", "band")),
        P(("dp", "band")),
        P(("dp", "band")),
        P(("dp", "band")),
        P(),
        P(),
    )
    return jax.shard_map(shards, mesh=mesh, in_specs=in_specs, out_specs=out_specs, check_vma=False)
```

```python
import functools
import math

import jax
import jax.numpy as jnp
import numpy as np
from jax import lax
from jax.experimental import pallas as pl
from jax.experimental.pallas import tpu as pltpu
from jax.sharding import PartitionSpec as P

D_ENC = 192
HEADS_ENC = 6
D_TRUNK = 384
HEADS_TRUNK = 12
PIN = 128
GROUPS = 2
HEAD_DIM = 32
SCALE = HEAD_DIM ** (-0.5)

NEG_FILL = -1000000000.0
BETA_ONE = 0.5
BETA_TWO = 0.5
LEARN_RATE = 0.01
WEIGHT_DECAY = 0.1
CLIP_LEVEL = 0.07
ADAM_EPS = 1e-08

F32 = jnp.float32
BF16 = jnp.bfloat16
TOKENS = 288
AHEAD = 8 << 20
SPAN = 384
SPAN_BACK = 640
WIN = 144
ENC_SPLIT = ((0, 192, 6),)
TRUNK_SPLIT = ((0, 256, 8), (256, 128, 4))


def block_layout(path_name, group_id, layer_id, n_width):
    prefix = (path_name, group_id, layer_id)
    return [
        (prefix + ("norm_one",), (2, n_width)),
        (prefix + ("qkv",), (n_width, 3 * n_width)),
        (prefix + ("proj",), (n_width, n_width)),
        (prefix + ("norm_two",), (2, n_width)),
        (prefix + ("up",), (n_width, 4 * n_width)),
        (prefix + ("down",), (4 * n_width, n_width)),
    ]


def layout():
    entries = []
    for group_id in range(GROUPS):
        entries.append((("enc", group_id, -1, "embed"), (PIN, D_ENC)))
        for layer_id in range(2):
            entries += block_layout("enc", group_id, layer_id, D_ENC)
        entries.append((("top", group_id, -1, "decode"), (D_TRUNK, D_ENC)))
        entries.append((("top", group_id, -1, "head"), (D_ENC, PIN)))
        entries.append((("top", group_id, -1, "scale"), (PIN,)))
    entries.append((("trunk", 0, -1, "joining"), (GROUPS * D_ENC, D_TRUNK)))
    for layer_id in range(2):
        entries += block_layout("trunk", 0, layer_id, D_TRUNK)
    entries.append((("trunk", 0, -1, "final"), (2, D_TRUNK)))
    return entries


def placed():
    offset = 0
    for label_key, dims_shape in layout():
        yield label_key, dims_shape, offset
        offset += math.prod(dims_shape)


def nn(left, right):
    return jnp.dot(left, right, preferred_element_type=F32)


def nt(left, right):
    return lax.dot_general(left, right, (((1,), (1,)), ((), ())), preferred_element_type=F32)


def tn(left, right):
    return lax.dot_general(left, right, (((0,), (0,)), ((), ())), preferred_element_type=F32)


def unit_rows(values):
    centre = values - jnp.mean(values, -1, keepdims=True)
    inverse = lax.rsqrt(jnp.mean(centre * centre, -1, keepdims=True) + 1e-05)
    return centre * inverse, inverse


def norm_forward(values, gain_ref):
    unit, unused = unit_rows(values)
    return unit * gain_ref[0:1, :] + gain_ref[1:2, :]


def norm_backward(values, gain_ref, grad_normed):
    unit, inverse = unit_rows(values)
    grad_gain = jnp.sum(grad_normed * unit, 0, keepdims=True)
    grad_shift = jnp.sum(grad_normed, 0, keepdims=True)
    grad_unit = grad_normed * gain_ref[0:1, :]
    along = jnp.mean(grad_unit * unit, -1, keepdims=True)
    grad_values = inverse * (grad_unit - jnp.mean(grad_unit, -1, keepdims=True) - unit * along)
    return grad_values, jnp.concatenate([grad_gain, grad_shift], 0)


GELU_A = math.sqrt(2.0 / math.pi)
GELU_B = 0.044715


def gelu(values):
    inner = jnp.tanh(GELU_A * (values + GELU_B * (values * values * values)))
    return values * (0.5 * (1.0 + inner))


def gelu_slope(values):
    square = values * values
    inner = jnp.tanh(GELU_A * (values + GELU_B * (square * values)))
    steep = (1.0 - inner * inner) * (GELU_A + (3.0 * GELU_B * GELU_A) * square)
    return 0.5 * (1.0 + inner) + 0.5 * values * steep


def head_lanes(rows, lanes, head):
    lane = lax.broadcasted_iota(jnp.int32, (rows, lanes), 1)
    return (lane >= HEAD_DIM * head) & (lane < HEAD_DIM * (head + 1))


def columns_of(n_heads, n_query):
    return -(-n_heads * n_query // 128)


def spread_heads(rows_value, n_heads, out_ref):
    n_query, lanes = rows_value.shape
    wide = rows_value.astype(F32)
    for head in range(n_heads):
        kept = jnp.where(head_lanes(n_query, lanes, head), wide, 0.0).astype(BF16)
        out_ref[head * n_query : (head + 1) * n_query, 0:lanes] = kept
    total = 128 * columns_of(n_heads, n_query)
    if total > n_heads * n_query:
        out_ref[n_heads * n_query : total, 0:lanes] = jnp.zeros(
            (total - n_heads * n_query, lanes), BF16
        )


def join_heads(spread_ref, n_heads, n_query, lanes):
    joined = spread_ref[0:n_query, 0:lanes]
    for head in range(1, n_heads):
        part = spread_ref[head * n_query : (head + 1) * n_query, 0:lanes]
        joined = jnp.where(head_lanes(n_query, lanes, head), part, joined)
    return joined


def same_code(key_code, query_code):
    count = query_code.shape[1] // 128
    return jnp.concatenate([key_code] * count, 1) == query_code


def attend_window(queries, key_rows, value_rows, key_code, query_code, probs_ref, q_scr, o_scr, split):
    n_query = queries.shape[0]
    outs = []
    at = 0
    for lane, lanes, n_heads in split:
        spread_heads(queries[:, lane : lane + lanes], n_heads, q_scr)
        keys = key_rows[:, lane : lane + lanes]
        values = value_rows[:, lane : lane + lanes]
        wide = 128 * columns_of(n_heads, n_query)
        for start in range(0, wide, SPAN):
            rows = slice(start, min(start + SPAN, wide))
            columns = slice(at + rows.start, at + rows.stop)
            scores = nt(keys, q_scr[rows, 0:lanes]) * SCALE
            scores = jnp.where(same_code(key_code, query_code[0:1, columns]), scores, NEG_FILL)
            raised = jnp.exp(scores - jnp.max(scores, 0, keepdims=True))
            probs = (raised * (1.0 / jnp.sum(raised, 0, keepdims=True))).astype(BF16)
            probs_ref[:, columns] = probs
            o_scr[rows, 0:lanes] = tn(probs, values)
        outs.append(join_heads(o_scr, n_heads, n_query, lanes))
        at += wide
    return jnp.concatenate(outs, 1) if len(outs) > 1 else outs[0]


def attend_window_back(
    queries, key_rows, value_rows, grad_rows, key_code, query_code, probs_ref, q_scr, g_scr, o_scr, s_scr, split
):
    n_query = queries.shape[0]
    out_q, out_k, out_v = [], [], []
    at = 0
    for lane, lanes, n_heads in split:
        n_col = columns_of(n_heads, n_query)
        spread_heads(queries[:, lane : lane + lanes], n_heads, q_scr)
        spread_heads(grad_rows[:, lane : lane + lanes], n_heads, g_scr)
        keys = key_rows[:, lane : lane + lanes]
        values = value_rows[:, lane : lane + lanes]
        wide = 128 * n_col
        for start in range(0, wide, SPAN_BACK):
            rows = slice(start, min(start + SPAN_BACK, wide))
            columns = slice(at + rows.start, at + rows.stop)
            grad_probs = nt(values, g_scr[rows, 0:lanes])
            probs = probs_ref[:, columns].astype(F32)
            along = jnp.sum(grad_probs * probs, 0, keepdims=True)
            grad_scores = probs * (grad_probs - along)
            allowed = same_code(key_code, query_code[0:1, columns])
            grad_scores = jnp.where(allowed, grad_scores, 0.0).astype(BF16)
            s_scr[:, rows] = grad_scores
            o_scr[rows, 0:lanes] = tn(grad_scores, keys)
        out_v.append(nn(probs_ref[:, at : at + wide], g_scr[0:wide, 0:lanes]))
        out_k.append(nn(s_scr[:, 0:wide], q_scr[0:wide, 0:lanes]) * SCALE)
        out_q.append(join_heads(o_scr, n_heads, n_query, lanes) * SCALE)
        at += wide
    if len(split) > 1:
        return tuple(jnp.concatenate(parts, 1) for parts in (out_q, out_k, out_v))
    return out_q[0], out_k[0], out_v[0]


class Queue:
    def __init__(self, copies, sizes, ahead):
        self.copies, self.sizes, self.ahead = copies, sizes, ahead
        self.started, self.reach = 0, 0
        self.advance(-1)

    def advance(self, index):
        limit = sum(self.sizes[: index + 1]) + self.ahead
        while self.started < len(self.copies) and (self.started <= index or self.reach < limit):
            self.copies[self.started].start()
            self.reach += self.sizes[self.started]
            self.started += 1


class Held:
    def __init__(self, ref, queue, index):
        self.ref, self.queue, self.index = ref, queue, index

    def ready(self):
        if self.queue is not None:
            self.queue.advance(self.index)
            self.queue.copies[self.index].wait()
            self.queue = None
        return self.ref

    def __getitem__(self, index):
        return self.ready()[index]

    @property
    def at(self):
        return self.ready().at

    @property
    def shape(self):
        return self.ref.shape


class Made:
    def __init__(self, ref, copy):
        self.ref, self.copy, self.sent = ref, copy, False

    def __getitem__(self, index):
        return self.ref[index]

    def __setitem__(self, index, value):
        self.ref[index] = value

    @property
    def at(self):
        return self.ref.at

    @property
    def shape(self):
        return self.ref.shape

    @property
    def dtype(self):
        return self.ref.dtype

    def send(self):
        if not self.sent:
            self.copy.start()
            self.sent = True


class Refs:
    def __init__(self, **refs):
        self.__dict__.update(refs)


def send(*refs):
    for ref in refs:
        if isinstance(ref, Made):
            ref.send()


def rest_forward(resid_in, w, s):
    middle = resid_in + nn(s.mixed[...], w.proj[...])
    s.middle[...] = middle
    normed = norm_forward(middle, w.norm_two).astype(BF16)
    s.normed_two[...] = normed
    send(s.mixed, s.middle, s.normed_two)
    for start in range(0, w.up.shape[1], 256):
        columns = slice(start, start + 256)
        s.raised[:, columns] = nn(normed, w.up[:, columns])
        for row in range(0, TOKENS, 96):
            piece = s.raised[row : row + 96, columns]
            s.active[row : row + 96, columns] = gelu(piece).astype(BF16)
    send(s.raised, s.active)
    return middle + nn(s.active[...], w.down[...])


def rest_backward(grad_out, w, s, flow, d_norm_two):
    grad_low = grad_out.astype(BF16)
    flow.low[...] = grad_low
    width = w.up.shape[1]
    for start in range(0, width, 256):
        columns = slice(start, start + 256)
        grad_active = nt(grad_low, w.down[start : start + 256, :])
        for row in range(0, TOKENS, 96):
            slope = gelu_slope(s.raised[row : row + 96, columns])
            flow.raised[row : row + 96, columns] = (
                slope * grad_active[row : row + 96, :]
            ).astype(BF16)
    grad_middle, grad_gain = norm_backward(
        s.middle[...], w.norm_two, nt(flow.raised[...], w.up[...])
    )
    d_norm_two[...] = grad_gain
    grad_middle = grad_out + grad_middle
    grad_branch = grad_middle.astype(BF16)
    flow.branch[...] = grad_branch
    send(flow.low, flow.raised, flow.branch, d_norm_two)
    return grad_middle, nt(grad_branch, w.proj[...]).astype(BF16)


def rest_weights(s, flow, d):
    for out, left, right in (
        (d.down, s.active, flow.low),
        (d.up, s.normed_two, flow.raised),
        (d.proj, s.mixed, flow.branch),
    ):
        out[...] = tn(left[...], right[...]).astype(out.dtype)
        send(out)


def plain_forward(first, w, s, tables, t, split, width):
    s.x_in[...] = first
    s.normed[...] = norm_forward(first, w.norm_one).astype(BF16)
    s.packed[...] = nn(s.normed[...], w.qkv[...]).astype(BF16)
    send(s.x_in, s.normed, s.packed)
    for win in range(2):
        rows = slice(WIN * win, WIN * (win + 1))
        s.mixed[rows, :] = attend_window(
            s.packed[rows, 0:width],
            s.packed[rows, width : 2 * width],
            s.packed[rows, 2 * width : 3 * width],
            tables.plain_key[rows, :],
            tables.plain_query,
            s.probs.at[win],
            t.q,
            t.o,
            split,
        ).astype(BF16)
    send(s.probs)
    last = rest_forward(first, w, s)
    s.x_out[...] = last
    ordered = nn(tables.to_win[...], norm_forward(last, w.norm_next).astype(BF16)).astype(BF16)
    s.near_a[...] = ordered[0:WIN]
    s.near_b[...] = ordered[WIN:]
    send(s.x_out, s.near_a, s.near_b)


def both(first, second):
    return jnp.concatenate([first[...], second[...]], 0)


def shifted_keys(s, win, width):
    rows = slice(72 * win, 72 * (win + 1))
    keys = jnp.concatenate([s.packed[rows, width : 2 * width], s.packed_far[rows, 0:width]], 0)
    values = jnp.concatenate([s.packed[rows, 2 * width :], s.packed_far[rows, width:]], 0)
    return s.packed[rows, 0:width], keys, values


def shifted_forward(x_in, near, far, w, s, tables, t, split, width):
    s.packed[...] = nn(both(*near), w.qkv[...]).astype(BF16)
    s.packed_far[...] = nn(both(*far), w.qkv[:, width:]).astype(BF16)
    send(s.packed, s.packed_far)
    for win in range(4):
        queries, keys, values = shifted_keys(s, win, width)
        t.m[72 * win : 72 * (win + 1), 0:width] = attend_window(
            queries, keys, values, tables.shift_key[WIN * win : WIN * (win + 1), :],
            tables.shift_query.at[win % 2], s.probs.at[win], t.q, t.o, split,
        )
    send(s.probs)
    s.mixed[...] = nn(tables.to_tok[...], t.m[:, 0:width].astype(BF16)).astype(BF16)
    return rest_forward(x_in[...], w, s)


def loss_part(values, goal, tables, count, w, d):
    low = norm_forward(values, w.final).astype(BF16)
    valid = tables.plain_key[...] + 1.0
    inverse_count = 1.0 / count[0:1, :]
    grad_low = None
    total = None
    for group in range(GROUPS):
        decode, head = w.decode[group], w.head[group]
        raised = nn(low, decode)
        active = gelu(raised).astype(BF16)
        predicted = nn(active, head)
        log_scale = w.scale[group : group + 1, :]
        error = predicted - goal[:, PIN * group : PIN * (group + 1)].astype(F32)
        inverse_scale = jnp.exp(-log_scale)
        weighted = jnp.abs(error) * inverse_scale
        part = jnp.sum((weighted + log_scale) * valid, 0, keepdims=True)
        total = part if total is None else total + part
        direction = jnp.where(error > 0.0, 1.0, jnp.where(error < 0.0, -1.0, 0.0))
        grad_pred = (direction * inverse_scale * valid * inverse_count).astype(BF16)
        d.scale[group : group + 1, :] = (
            jnp.sum((1.0 - weighted) * valid, 0, keepdims=True) * inverse_count
        )
        d.head[group] = tn(active, grad_pred).astype(BF16)
        grad_raised = (gelu_slope(raised) * nt(grad_pred, head)).astype(BF16)
        d.decode[group] = tn(low, grad_raised).astype(BF16)
        back = nt(grad_raised, decode)
        grad_low = back if grad_low is None else grad_low + back
    d.loss[...] = total
    grad_values, d.final[...] = norm_backward(values, w.final, grad_low)
    send(d.scale, d.head, d.decode, d.loss, d.final)
    return grad_values


def shifted_backward(grad_out, w, s, flow, outs, tables, t, split, width):
    outs.grad_middle[...], grad_mixed = rest_backward(grad_out, w, s, flow, outs.norm_two)
    send(outs.grad_middle)
    grad_win = nn(tables.to_win[...], grad_mixed).astype(BF16)
    for win in range(4):
        rows = slice(72 * win, 72 * (win + 1))
        queries, keys, values = shifted_keys(s, win, width)
        grad_q, grad_k, grad_v = attend_window_back(
            queries, keys, values, grad_win[rows, :],
            tables.shift_key[WIN * win : WIN * (win + 1), :], tables.shift_query.at[win % 2],
            s.probs.at[win], t.q, t.g, t.o, t.s, split,
        )
        flow.near[rows, 0:width] = grad_q.astype(BF16)
        flow.near[rows, width : 2 * width] = grad_k[0:72].astype(BF16)
        flow.near[rows, 2 * width : 3 * width] = grad_v[0:72].astype(BF16)
        flow.far[rows, 0:width] = grad_k[72:144].astype(BF16)
        flow.far[rows, width : 2 * width] = grad_v[72:144].astype(BF16)
    rim = nt(flow.far[...], w.qkv[:, width:]).astype(BF16)
    outs.rim_a[...] = rim[0:WIN]
    outs.rim_b[...] = rim[WIN:]
    send(outs.rim_a, outs.rim_b, flow.near, flow.far)
    outs.grad_near[...] = nt(nn(tables.to_tok[...], flow.near[...]).astype(BF16), w.qkv[...])
    send(outs.grad_near)


def shifted_weights(near, far, s, flow, d, width):
    rest_weights(s, flow, d)
    near_rows, far_rows = both(*near), both(*far)
    d.qkv[:, 0:width] = tn(near_rows, flow.near[:, 0:width]).astype(BF16)
    d.qkv[:, width:] = (
        tn(near_rows, flow.near[:, width:]) + tn(far_rows, flow.far[...])
    ).astype(BF16)
    send(d.qkv)


def plain_backward(grad, arrived, w, s, flow, d, tables, t, split, width):
    grad_normed = grad.near[...] + nn(tables.to_tok[...], both(*arrived))
    grad_x, d.norm_next[...] = norm_backward(s.x_out[...], w.norm_next, grad_normed)
    grad_mid, grad_mixed = rest_backward(grad.middle[...] + grad_x, w, s, flow, d.norm_two)
    rest_weights(s, flow, d)
    for win in range(2):
        rows = slice(WIN * win, WIN * (win + 1))
        grads = attend_window_back(
            s.packed[rows, 0:width], s.packed[rows, width : 2 * width], s.packed[rows, 2 * width :],
            grad_mixed[rows, :], tables.plain_key[rows, :], tables.plain_query, s.probs.at[win],
            t.q, t.g, t.o, t.s, split,
        )
        for index, part in enumerate(grads):
            flow.near[rows, width * index : width * (index + 1)] = part.astype(BF16)
    near_grad = flow.near[...]
    d.qkv[...] = tn(s.normed[...], near_grad).astype(BF16)
    grad_first, d.norm_one[...] = norm_backward(s.x_in[...], w.norm_one, nt(near_grad, w.qkv[...]))
    send(d.norm_next, d.qkv, d.norm_one)
    return grad_mid + grad_first


def held(array):
    return pltpu.with_memory_space_constraint(array, pltpu.HBM)


def launch(name, body, ins, outs, scratch, limit=52 << 20, scalars=(), raw=(), sems=0, in_place=False):
    sources, views, shapes = [], [], []
    for value in ins.values():
        array, view, shape = value if isinstance(value, tuple) else (value, None, value.shape)
        sources.append(array)
        views.append(view)
        shapes.append(pltpu.VMEM(shape, array.dtype))
    n_in, n_out = len(ins), len(outs)
    n_first = len(scalars) + len(raw)
    own_sems = sems
    n_held = 0 if in_place else n_out

    def kernel(*refs):
        named = {"scalars": refs[: len(scalars)], "raw": refs[len(scalars) : n_first]}
        refs = refs[n_first:]
        far_in, far_out = refs[:n_in], refs[n_in : n_in + n_out]
        near = refs[n_in + n_out :]
        near_in, near_out = near[:n_in], near[n_in : n_in + n_held]
        spare, flags = near[n_in + n_held : -1], near[-1]
        named["sems"] = [flags.at[n_in + n_out + index] for index in range(own_sems)]
        copies, sizes = [], []
        for index, key in enumerate(ins):
            source = far_in[index] if views[index] is None else views[index](far_in[index])
            copies.append(pltpu.make_async_copy(source, near_in[index], flags.at[index]))
            sizes.append(math.prod(near_in[index].shape) * near_in[index].dtype.itemsize)
        queue = Queue(copies, sizes, AHEAD)
        for index, key in enumerate(ins):
            named[key] = Held(near_in[index], queue, index)
        for index, key in enumerate(outs):
            if in_place:
                named[key] = Made(None, None)
            else:
                copy = pltpu.make_async_copy(near_out[index], far_out[index], flags.at[n_in + index])
                named[key] = Made(near_out[index], copy)
            named[key].far, named[key].sem = far_out[index], flags.at[n_in + index]
        named.update(zip(scratch, spare))
        body(named)
        for key in ins:
            named[key].ready()
        for key in outs:
            named[key].send()
        for key in outs:
            named[key].copy.wait()

    results = pl.pallas_call(
        kernel,
        in_specs=[pl.BlockSpec(memory_space=pltpu.SMEM)] * len(scalars)
        + [pl.BlockSpec(memory_space=pl.ANY)] * (len(raw) + n_in),
        out_specs=[pl.BlockSpec(memory_space=pl.ANY)] * n_out,
        out_shape=[pltpu.HBM(shape, dtype) for shape, dtype in outs.values()],
        scratch_shapes=shapes
        + [pltpu.VMEM(shape, dtype) for shape, dtype in list(outs.values())[:n_held]]
        + [pltpu.VMEM(shape, dtype) for shape, dtype in scratch.values()]
        + [pltpu.SemaphoreType.DMA((n_in + n_out + sems,))],
        name=name,
        input_output_aliases={len(scalars) + at: at for at in range(len(raw))} if in_place else {},
        compiler_params=pltpu.CompilerParams(vmem_limit_bytes=limit),
    )(*scalars, *[held(array) for array in (*raw, *sources)])
    return dict(zip(outs, results))


def part(named, prefix):
    return Refs(**{key[len(prefix) :]: ref for key, ref in named.items() if key.startswith(prefix)})


def prefixed(prefix, values):
    return {prefix + key: value for key, value in values.items()}


def probs_width(split, n_query):
    return 128 * sum(columns_of(n_heads, n_query) for lane, lanes, n_heads in split)


def spread_shape(split, n_query):
    rows = 128 * max(columns_of(n_heads, n_query) for lane, lanes, n_heads in split)
    return (rows, max(lanes for lane, lanes, n_heads in split))


def saved_outs(width, split, shifted):
    n_query, n_win = (72, 4) if shifted else (WIN, 2)
    found = {"packed": ((TOKENS, 3 * width), BF16)}
    if shifted:
        found["packed_far"] = ((TOKENS, 2 * width), BF16)
    else:
        found["x_in"] = ((TOKENS, width), F32)
        found["normed"] = ((TOKENS, width), BF16)
    found["probs"] = ((n_win, WIN, probs_width(split, n_query)), BF16)
    found["mixed"] = ((TOKENS, width), BF16)
    found["middle"] = ((TOKENS, width), F32)
    found["normed_two"] = ((TOKENS, width), BF16)
    found["raised"] = ((TOKENS, 4 * width), F32)
    found["active"] = ((TOKENS, 4 * width), BF16)
    return found


def flow_shapes(width, shifted):
    found = {
        "low": ((TOKENS, width), BF16),
        "raised": ((TOKENS, 4 * width), BF16),
        "branch": ((TOKENS, width), BF16),
        "near": ((TOKENS, 3 * width), BF16),
    }
    if shifted:
        found["far"] = ((TOKENS, 2 * width), BF16)
    return found


def spare(width, split, shifted, backward):
    n_query = 72 if shifted else WIN
    shape = spread_shape(split, n_query)
    found = {"q": (shape, BF16), "o": (shape, F32)}
    if shifted:
        found["m"] = ((TOKENS, width), F32)
    if backward:
        found["g"] = (shape, BF16)
        found["s"] = ((WIN, shape[0]), BF16)
    return found


def rim_outs(width):
    found = {"grad_middle": ((TOKENS, width), F32), "grad_near": ((TOKENS, width), F32)}
    found["rim_a"] = found["rim_b"] = ((WIN, width), BF16)
    found["norm_two"] = ((2, width), F32)
    return found


def weight_grads(width):
    return {
        "down": ((4 * width, width), BF16),
        "up": ((width, 4 * width), BF16),
        "proj": ((width, width), BF16),
        "qkv": ((width, 3 * width), BF16),
    }


def window_order():
    order = []
    for half in range(2):
        for pair in ((1, 2), (3, 0)):
            for level in pair:
                for row in range(3):
                    for col in range(12):
                        order.append(level * 72 + (half * 3 + row) * 12 + col)
    return np.array(order)


def fixed_tables():
    order = window_order()
    to_win = np.zeros((TOKENS, TOKENS), np.float32)
    to_win[np.arange(TOKENS), order] = 1.0
    region = np.zeros((2, 72), np.float32)
    for pair, levels in enumerate(((1, 2), (3, 0))):
        for place in range(72):
            level, col = levels[place // 36], place % 12
            region[pair, place] = 2.0 * (level == 0) + 1.0 * (col < 6)
    return to_win, region


def key_codes(extent, first_lat):
    place = lax.broadcasted_iota(jnp.int32, (TOKENS, 128), 0)
    row, col = (place // 12) % 6, place % 12
    inside = (first_lat + row < extent[0]) & (col < extent[1])
    plain = jnp.where(inside, 0.0, -1.0)
    place = lax.broadcasted_iota(jnp.int32, (2 * TOKENS, 128), 0)
    win, rest = place // WIN, place % WIN
    far, rest = rest // 72, rest % 72
    half, pair = win // 2, win % 2
    second = rest // 36
    row, col = (rest // 12) % 3, rest % 12
    near_row = 3 * half + row
    far_row = jnp.where(half == 0, row - 3, row + 6)
    lat = first_lat + jnp.where(far == 1, far_row, near_row)
    top = (pair == 1) & (second == 1)
    region = jnp.where(top, 2.0, 0.0) + jnp.where(col < 6, 1.0, 0.0)
    inside = (lat >= 0) & (lat < extent[0]) & (col < extent[1])
    return plain, jnp.where(inside, region, -1.0)


def exchange(first, second):
    count = lax.axis_size("band")
    up = [(i, i + 1) for i in range(count - 1)]
    down = [(i + 1, i) for i in range(count - 1)]
    return lax.ppermute(second, "band", up), lax.ppermute(first, "band", down)


def shift_query_codes(region, split):
    parts = []
    for lane, lanes, n_heads in split:
        total = 128 * columns_of(n_heads, 72)
        tiled = np.tile(region, (1, n_heads))
        parts.append(np.pad(tiled, ((0, 0), (0, total - tiled.shape[1]))))
    return jnp.asarray(np.concatenate(parts, 1)[:, None, :], F32)


WIDTHS = {"enc": (D_ENC, ENC_SPLIT), "trunk": (D_TRUNK, TRUNK_SPLIT)}
FORWARD_ORDER = ("norm_one", "qkv", "proj", "norm_two", "up", "down")
BACKWARD_ORDER = ("down", "up", "norm_two", "proj", "qkv", "norm_one")


def compute(weights, unpack_trunk, pack_trunk, source, goal, codes, count):
    to_win, region = fixed_tables()
    order = {"to_win": jnp.asarray(to_win, BF16), "to_tok": jnp.asarray(to_win.T, BF16)}
    grads = {}

    def tables(tower, names):
        split = WIDTHS[tower][1]
        found = {
            "plain_key": codes[0],
            "shift_key": codes[1],
            "plain_query": jnp.zeros((1, probs_width(split, WIN)), F32),
            "shift_query": shift_query_codes(region, split),
        } | order
        return prefixed("c_", {name: found[name] for name in names})

    PLAIN = ("plain_key", "plain_query", "to_win")
    SHIFTED = ("shift_key", "shift_query", "to_tok")

    def of(key, group):
        array = weights[key]
        if group is None:
            return array
        return (array, lambda ref: ref.at[group], array.shape[1:])

    def block(mark, tower, layer, group, names, with_next=False):
        found = {name: of((tower, layer, name), group) for name in names}
        if with_next:
            found["norm_next"] = of((tower, layer + 1, "norm_one"), group)
        return prefixed(mark, found)

    def src(group):
        lanes = pl.ds(PIN * group, PIN)
        return (source, lambda ref: ref.at[:, lanes], (TOKENS, PIN))

    groups = range(GROUPS)
    enc_width, enc_split = WIDTHS["enc"]
    width, split = WIDTHS["trunk"]

    def enc_plain():
        def body(r):
            for group in groups:
                s = part(r, f"s{group}_")
                s.near_a, s.near_b = r["near_a"].at[group], r["near_b"].at[group]
                plain_forward(
                    nn(r[f"src{group}"][...], r[f"embed{group}"][...]), part(r, f"w{group}_"), s,
                    part(r, "c_"), part(r, "t_"), enc_split, enc_width,
                )
            send(r["near_a"], r["near_b"])

        ins, outs = {}, {"near_a": ((GROUPS, WIN, enc_width), BF16)}
        outs["near_b"] = outs["near_a"]
        for group in groups:
            ins |= {f"src{group}": src(group), f"embed{group}": of(("enc", -1, "embed"), group)}
            ins |= block(f"w{group}_", "enc", 0, group, FORWARD_ORDER, True)
            ins |= tables("enc", PLAIN) if group == 0 else {}
            kept = saved_outs(enc_width, enc_split, False) | {"x_out": ((TOKENS, enc_width), F32)}
            outs |= prefixed(f"s{group}_", kept)
        return launch(
            "enc_plain", body, ins, outs, prefixed("t_", spare(enc_width, enc_split, False, False))
        )

    def middle(before, far):
        def body(r):
            last = []
            for group in groups:
                rows = [r[name].at[group] for name in ("near_a", "near_b", "far_a", "far_b")]
                last.append(
                    shifted_forward(
                        r[f"x_in{group}"], rows[:2], rows[2:], part(r, f"w{group}_"),
                        part(r, f"s{group}_"), part(r, "e_"), part(r, "t_"), enc_split, enc_width,
                    )
                )
            joined = jnp.concatenate(last, 1).astype(BF16)
            r["joined"][...] = joined
            s = part(r, "s_")
            s.near_a, s.near_b = r["trunk_a"], r["trunk_b"]
            plain_forward(
                nn(joined, r["joining"][...]), part(r, "w_"), s, part(r, "c_"), part(r, "u_"),
                split, width,
            )

        ins = {"near_a": before["near_a"], "near_b": before["near_b"], "far_a": far[0], "far_b": far[1]}
        outs = {}
        for group in groups:
            ins |= block(f"w{group}_", "enc", 1, group, FORWARD_ORDER[1:])
            if group == 0:
                found = tables("enc", SHIFTED)
                ins |= {"e_" + key[2:]: value for key, value in found.items()}
            ins |= {f"x_in{group}": before[f"s{group}_x_out"]}
            outs |= prefixed(f"s{group}_", saved_outs(enc_width, enc_split, True))
        ins |= {"joining": weights["trunk", -1, "joining"]}
        ins |= block("w_", "trunk", 0, None, FORWARD_ORDER, True) | tables("trunk", PLAIN)
        outs |= {"joined": ((TOKENS, 2 * D_ENC), BF16)}
        outs |= prefixed("s_", saved_outs(width, split, False) | {"x_out": ((TOKENS, width), F32)})
        outs |= {"trunk_a": ((WIN, width), BF16), "trunk_b": ((WIN, width), BF16)}
        return launch(
            "middle", body, ins, outs,
            prefixed("t_", spare(enc_width, enc_split, True, False))
            | prefixed("u_", spare(width, split, False, False)),
        )

    def trunk_top(before, far):
        def body(r):
            w, s, c, t = part(r, "w_"), part(r, "s_"), part(r, "c_"), part(r, "t_")
            last = shifted_forward(
                r["x_in"], (r["near_a"], r["near_b"]), (r["far_a"], r["far_b"]),
                w, s, c, t, split, width,
            )
            grad = loss_part(last, r["goal"], c, r["count"], part(r, "h_"), part(r, "d_"))
            shifted_backward(grad, w, s, part(r, "f_"), part(r, "b_"), c, t, split, width)

        kept = saved_outs(width, split, True)
        reused = ("mixed", "normed_two", "active")
        top = {name: weights["top", -1, name] for name in ("decode", "head", "scale")}
        found = launch(
            "trunk_top", body,
            {"near_a": before["trunk_a"], "near_b": before["trunk_b"], "far_a": far[0], "far_b": far[1]}
            | block("w_", "trunk", 1, None, FORWARD_ORDER[1:])
            | tables("trunk", SHIFTED + ("to_win", "plain_key"))
            | {"x_in": before["s_x_out"]}
            | prefixed("h_", {"final": weights["trunk", -1, "final"]} | top)
            | {"goal": goal, "count": count},
            prefixed("s_", {name: kept[name] for name in reused})
            | prefixed("f_", flow_shapes(width, True)) | prefixed("b_", rim_outs(width))
            | prefixed("d_", {
                "final": ((2, width), F32), "decode": ((GROUPS, D_TRUNK, D_ENC), BF16),
                "head": ((GROUPS, D_ENC, PIN), BF16), "scale": ((GROUPS, PIN), F32),
                "loss": ((1, PIN), F32),
            }),
            prefixed("s_", {name: kept[name] for name in kept if name not in reused})
            | prefixed("t_", spare(width, split, True, True)),
        )
        grads["trunk", -1, "final", None] = found["d_final"]
        for name in ("decode", "head", "scale"):
            grads["top", -1, name, "all"] = found["d_" + name]
        grads["trunk", 1, "norm_two", None] = found["b_norm_two"]
        return found

    def trunk_top_weights(before, far, found):
        def body(r):
            shifted_weights(
                (r["near_a"], r["near_b"]), (r["far_a"], r["far_b"]), part(r, "s_"), part(r, "f_"),
                part(r, "d_"), width,
            )

        results = launch(
            "trunk_top_weights", body,
            {key: found[key] for key in found if key[:2] in ("s_", "f_")}
            | {"near_a": before["trunk_a"], "near_b": before["trunk_b"], "far_a": far[0], "far_b": far[1]},
            prefixed("d_", weight_grads(width)), {},
        )
        for key, grad in results.items():
            grads["trunk", 1, key[2:], None] = grad
        return results["d_qkv"]

    PLAIN_KEPT = ("raised", "middle", "active", "normed_two", "mixed", "packed", "probs", "normed", "x_in")
    SHIFT_KEPT = ("raised", "middle", "packed", "packed_far", "probs", "active", "normed_two", "mixed")
    GAINS = ("norm_next", "norm_one", "norm_two")

    def plain_back_ins(mark, tower, group, kept, kept_mark):
        found = {f"w{mark}norm_next": of((tower, 1, "norm_one"), group)}
        found |= block(f"w{mark}", tower, 0, group, BACKWARD_ORDER)
        return found | {f"s{mark}{name}": kept[kept_mark + name] for name in PLAIN_KEPT}

    def keep_plain_grads(tower, group, found, mark):
        grads[tower, 1, "norm_one", group] = found[mark + "norm_next"]
        for name in ("down", "up", "proj", "qkv", "norm_one", "norm_two"):
            grads[tower, 0, name, group] = found[mark + name]

    def middle_back(top, arrived, before, first, far):
        def body(r):
            grad = plain_backward(
                part(r, "g_"), (r["arrived_a"], r["arrived_b"]), part(r, "w_"), part(r, "s_"),
                part(r, "f_"), part(r, "d_"), part(r, "c_"), part(r, "t_"), split, width,
            ).astype(BF16)
            r["d_joining"][...] = tn(r["joined"][...], grad).astype(BF16)
            send(r["d_joining"])
            r["v_grad"][...] = nt(grad, r["joining"][...])
            for group in groups:
                s, f, b = part(r, f"s{group}_"), part(r, "e_"), part(r, f"b{group}_")
                rows = [r[name].at[group] for name in ("near_a", "near_b", "far_a", "far_b")]
                b.rim_a, b.rim_b = r["rim_a"].at[group], r["rim_b"].at[group]
                shifted_backward(
                    r["v_grad"][:, enc_width * group : enc_width * (group + 1)],
                    part(r, f"w{group}_"), s, f, b, part(r, "k_"), part(r, "u_"), enc_split, enc_width,
                )
                shifted_weights(rows[:2], rows[2:], s, f, part(r, f"d{group}_"), enc_width)
            send(r["rim_a"], r["rim_b"])

        ins = {"g_near": top["b_grad_near"], "c_to_tok": order["to_tok"]}
        ins |= {"arrived_a": arrived[0], "arrived_b": arrived[1], "s_x_out": before["s_x_out"]}
        ins |= {"g_middle": top["b_grad_middle"]} | plain_back_ins("_", "trunk", None, before, "s_")
        ins |= tables("trunk", ("plain_key", "plain_query"))
        ins |= {"joined": before["joined"], "joining": weights["trunk", -1, "joining"]}
        outs = prefixed("d_", {name: ((2, width), F32) for name in GAINS} | weight_grads(width))
        outs |= {"d_joining": ((GROUPS * D_ENC, D_TRUNK), BF16)}
        outs |= {"rim_a": ((GROUPS, WIN, enc_width), BF16), "rim_b": ((GROUPS, WIN, enc_width), BF16)}
        for group in groups:
            ins |= block(f"w{group}_", "enc", 1, group, BACKWARD_ORDER[:-1])
            ins |= {f"s{group}_{name}": before[f"s{group}_{name}"] for name in SHIFT_KEPT}
            if group == 0:
                found = tables("enc", SHIFTED + ("to_win",))
                ins |= {"k_" + key[2:]: value for key, value in found.items()}
                ins |= {"near_a": first["near_a"], "near_b": first["near_b"]}
                ins |= {"far_a": far[0], "far_b": far[1]}
            found = rim_outs(enc_width)
            kept = {name: found[name] for name in ("grad_middle", "grad_near", "norm_two")}
            outs |= prefixed(f"b{group}_", kept) | prefixed(f"d{group}_", weight_grads(enc_width))
        found = launch(
            "middle_back", body, ins, outs,
            prefixed("t_", spare(width, split, False, True)) | prefixed("f_", flow_shapes(width, False))
            | prefixed("u_", spare(enc_width, enc_split, True, True))
            | prefixed("e_", flow_shapes(enc_width, True)) | {"v_grad": ((TOKENS, width), F32)},
        )
        keep_plain_grads("trunk", None, found, "d_")
        grads["trunk", -1, "joining", None] = found["d_joining"]
        for group in groups:
            grads["enc", 1, "norm_two", group] = found[f"b{group}_norm_two"]
            for name in weight_grads(enc_width):
                grads["enc", 1, name, group] = found[f"d{group}_{name}"]
        return found

    def enc_plain_back(back, arrived, first):
        def body(r):
            for group in groups:
                grad = plain_backward(
                    part(r, f"g{group}_"), (r["arrived_a"].at[group], r["arrived_b"].at[group]),
                    part(r, f"w{group}_"), part(r, f"s{group}_"), part(r, "f_"), part(r, f"d{group}_"),
                    part(r, "c_"), part(r, "t_"), enc_split, enc_width,
                ).astype(BF16)
                r[f"d{group}_embed"][...] = tn(r[f"src{group}"][...], grad).astype(BF16)
                send(r[f"d{group}_embed"])

        ins = {"arrived_a": arrived[0], "arrived_b": arrived[1], "c_to_tok": order["to_tok"]}
        outs = {}
        for group in groups:
            ins |= {f"g{group}_near": back[f"b{group}_grad_near"]}
            ins |= {f"s{group}_x_out": first[f"s{group}_x_out"]}
            ins |= {f"g{group}_middle": back[f"b{group}_grad_middle"]}
            ins |= plain_back_ins(f"{group}_", "enc", group, first, f"s{group}_")
            ins |= tables("enc", ("plain_key", "plain_query")) if group == 0 else {}
            ins |= {f"src{group}": src(group)}
            outs |= prefixed(
                f"d{group}_",
                {name: ((2, enc_width), F32) for name in GAINS}
                | weight_grads(enc_width) | {"embed": ((PIN, D_ENC), BF16)},
            )
        found = launch(
            "enc_plain_back", body, ins, outs,
            prefixed("t_", spare(enc_width, enc_split, False, True))
            | prefixed("f_", flow_shapes(enc_width, False)),
        )
        for group in groups:
            keep_plain_grads("enc", group, found, f"d{group}_")
            grads["enc", -1, "embed", group] = found[f"d{group}_embed"]

    first = enc_plain()
    far = exchange(first["near_a"], first["near_b"])
    found = unpack_trunk(first["near_a"])
    *far, found = lax.optimization_barrier((*far, found))
    weights = weights | found
    second = middle(first, far)
    trunk_far = exchange(second["trunk_a"], second["trunk_b"])
    top = trunk_top(second, trunk_far)
    arrived = exchange(top["b_rim_a"], top["b_rim_b"])
    last = trunk_top_weights(second, trunk_far, top)
    *arrived, last = lax.optimization_barrier((*arrived, last))
    grads["trunk", 1, "qkv", None] = last
    back = middle_back(top, arrived, second, first, far)
    arrived = exchange(back["rim_a"], back["rim_b"])
    packed = pack_trunk(grads)
    *arrived, packed = lax.optimization_barrier((*arrived, packed))
    enc_plain_back(back, arrived, first)
    return top["d_loss"], grads, packed


def stacked_key(label_key):
    tower, group, layer, name = label_key
    return (tower, layer, name), (group if tower in ("enc", "top") else None)


BLOCK_ELEMENTS = 2048


def share_rows(n_own):
    blocks = -(-(n_own + BLOCK_ELEMENTS - 1) // BLOCK_ELEMENTS) + 1
    return 16 * 3 * (-(-blocks // 3))


def first_row(n_own, device):
    return (n_own * device // BLOCK_ELEMENTS) * 16


def grouped_pieces():
    found = {}
    for label_key, dims_shape, offset in placed():
        key, group = stacked_key(label_key)
        found.setdefault(key, (dims_shape, []))[1].append((group, offset // 128))
    return [(key, places, dims_shape) for key, (dims_shape, places) in found.items()]


def is_gain(key):
    return key[2] in ("norm_one", "norm_two", "final")


def stacked_shape(places, dims_shape):
    if len(dims_shape) == 1:
        return (len(places),) + dims_shape
    return dims_shape if places[0][0] is None else (len(places),) + dims_shape


def turned(values):
    return pltpu.roll(values, 64, 1)


def lower_half(values):
    return lax.broadcasted_iota(jnp.int32, values.shape, 1) < 64


def read_gain(flat, offset, width, out):
    if width % 128 == 0:
        count = width // 128
        for row in range(2):
            for tile in range(count):
                at = offset + row * count + tile
                out[row : row + 1, 128 * tile : 128 * tile + 128] = flat[at : at + 1, :]
        return
    rows = [flat[offset + place : offset + place + 1, :] for place in range(3)]
    out[0:1, 0:128] = rows[0]
    out[0:1, 128:192] = rows[1][:, 0:64]
    out[1:2, 0:128] = jnp.where(lower_half(rows[1]), turned(rows[1]), turned(rows[2]))
    out[1:2, 128:192] = rows[2][:, 64:128]


def read_matrix(flat, offset, shape, out, wide_scr):
    height, width = shape
    step = 64
    if width % 128 == 0:
        count = width // 128

        def body(index, carry):
            row = pl.multiple_of(index * step, step)
            for tile in range(count):
                start = offset + tile + row * count
                piece = flat[pl.ds(start, step, stride=count), :]
                out[pl.ds(row, step), 128 * tile : 128 * tile + 128] = piece.astype(BF16)
            return carry

        lax.fori_loop(0, height // step, body, 0)
        return
    half = width // 128
    period = 2 * half + 1

    def body(index, carry):
        row = pl.multiple_of(index * step, step)
        start = offset + (row // 2) * period
        rows = [flat[pl.ds(start + place, step // 2, stride=period), :] for place in range(period)]
        late = [turned(rows[half + place]) for place in range(half + 1)]
        for tile in range(half + 1):
            odd_rows = late[tile]
            if tile < half:
                odd_rows = jnp.where(lower_half(late[tile]), late[tile], late[tile + 1])
            wide_scr[pl.ds(step * tile, step // 2, stride=2), :] = rows[tile]
            wide_scr[pl.ds(step * tile + 1, step // 2, stride=2), :] = odd_rows
            end = min(128, width - 128 * tile)
            tile_rows = wide_scr[step * tile : step * (tile + 1), 0:end]
            out[pl.ds(row, step), 128 * tile : 128 * tile + end] = tile_rows.astype(BF16)
        return carry

    lax.fori_loop(0, height // step, body, 0)


def write_gain(flat, offset, width, values):
    if width % 128 == 0:
        count = width // 128
        for row in range(2):
            for tile in range(count):
                at = offset + row * count + tile
                flat[at : at + 1, :] = values[row : row + 1, 128 * tile : 128 * tile + 128]
        return
    flat[offset : offset + 1, :] = values[0:1, 0:128]
    first, second = values[1:2, 0:64], values[1:2, 64:192]
    flat[offset + 1 : offset + 2, :] = jnp.concatenate([values[0:1, 128:192], first], 1)
    flat[offset + 2 : offset + 3, :] = second


def write_matrix(flat, offset, shape, source, wide_scr):
    height, width = shape
    step = 64
    if width % 128 == 0:
        count = width // 128

        def body(index, carry):
            row = pl.multiple_of(index * step, step)
            for tile in range(count):
                start = offset + tile + row * count
                piece = source[pl.ds(row, step), 128 * tile : 128 * tile + 128]
                flat[pl.ds(start, step, stride=count), :] = piece.astype(F32)
            return carry

        lax.fori_loop(0, height // step, body, 0)
        return
    half = width // 128
    period = 2 * half + 1

    def body(index, carry):
        row = pl.multiple_of(index * step, step)
        start = offset + (row // 2) * period
        for tile in range(half + 1):
            end = min(128, width - 128 * tile)
            tile_rows = source[pl.ds(row, step), 128 * tile : 128 * tile + end].astype(F32)
            wide_scr[step * tile : step * (tile + 1), 0:end] = tile_rows
        early = [wide_scr[pl.ds(step * tile, step // 2, stride=2), :] for tile in range(half + 1)]
        late = [
            turned(wide_scr[pl.ds(step * tile + 1, step // 2, stride=2), :])
            for tile in range(half + 1)
        ]
        low = lower_half(late[0])
        rows = early[:half] + [jnp.where(low, early[half], late[0])]
        rows += [jnp.where(low, late[tile], late[tile + 1]) for tile in range(half)]
        for place, value in enumerate(rows):
            flat[pl.ds(start + place, step // 2, stride=period), :] = value
        return carry

    lax.fori_loop(0, height // step, body, 0)


def wide_scratch(rows):
    return {"flat": ((rows, 128), F32), "wide": ((5 * 64, 128), F32)}


def trunk_row():
    return min(places[0][1] for key, places, dims_shape in grouped_pieces() if key[0] == "trunk")


def unpack_weights(gathered, n_own, trunk):
    pieces = [piece for piece in grouped_pieces() if (piece[0][0] == "trunk") == trunk]
    n_devices, rows, unused = gathered.shape
    edge = trunk_row() * 128
    low, high = (edge // n_own, n_devices) if trunk else (0, -(-edge // n_own))
    base = first_row(n_own, low)
    n_held = high - low
    cuts = [n_held * index // 8 for index in range(9)]
    step = rows // 6
    outs = {}
    for key, places, dims_shape in pieces:
        small = is_gain(key) or len(dims_shape) == 1
        outs[key] = (stacked_shape(places, dims_shape), F32 if small else BF16)

    def body(r):
        flat, wide, shares, source = r["flat"], r["wide"], r["shares"], r["raw"][0]
        copies = []
        for index, (start, stop) in enumerate(zip(cuts[:-1], cuts[1:])):
            span, held_span = pl.ds(low + start, stop - start), pl.ds(start, stop - start)
            copy = pltpu.make_async_copy(source.at[span], shares.at[held_span], r["sems"][index])
            copy.start()
            copies.append(copy)

        def place(index, carry):
            start = n_own * (low + index) // BLOCK_ELEMENTS * 16 - base
            start = pl.multiple_of(start, 16)
            kept = jnp.where(index > 0, flat[pl.ds(start, 16), :], 0.0)
            flat[pl.ds(start, 16), :] = kept + shares[index, 0:16, :].astype(F32)
            flat[pl.ds(start + 16, step - 16), :] = shares[index, 16:step, :].astype(F32)
            for number in range(1, 6):
                at = pl.ds(start + number * step, step)
                flat[at, :] = shares[index, number * step : (number + 1) * step, :].astype(F32)
            return carry

        for index in range(8):
            copies[index].wait()
            lax.fori_loop(cuts[index], cuts[index + 1], place, 0)
        for key, places, dims_shape in pieces:
            for group, offset in places:
                offset = offset - base
                view = r[key] if group is None or len(dims_shape) == 1 else r[key].at[group]
                if len(dims_shape) == 1:
                    view[group : group + 1, :] = flat[offset : offset + 1, :]
                elif is_gain(key):
                    read_gain(flat, offset, dims_shape[1], view)
                else:
                    read_matrix(flat, offset, dims_shape, view, wide)
            r[key].send()

    return launch(
        "unpack_trunk" if trunk else "unpack", body, {}, outs,
        {"shares": ((n_held,) + gathered.shape[1:], BF16)}
        | wide_scratch(first_row(n_own, high - 1) + rows - base),
        limit=60 << 20, raw=(gathered,), sems=8,
    )


def cuts_of(rows):
    blocks = rows // 16
    last = blocks * 11 // 45
    first = (blocks - last) // 2
    return 16 * first, 16 * (blocks - last - first), 16 * last


def step_of(rows):
    blocks = rows // 16
    return 16 * max(count for count in range(1, 13) if blocks % count == 0)


def pack_grads(grads, n_own, n_devices, core, before=None):
    early = before is None
    rows = share_rows(n_own)
    cuts = cuts_of(rows)
    n_chips = n_devices // 2
    middle = -(-trunk_row() * 128 // (2 * n_own))
    low, high = (middle, n_chips) if early else (0, middle)
    base = trunk_row() // 16 * 16 if early else 0
    end = first_row(n_own, 2 * high - 1) + rows
    pieces = [
        (key, group, offset, dims_shape)
        for key, places, dims_shape in grouped_pieces()
        for group, offset in places
        if (key[0] == "trunk" if early else offset < end)
    ]
    last = max(offset + math.prod(dims_shape) // 128 for key, group, offset, dims_shape in pieces)
    names = [(side, index) for side in ("kept", "sent") for index in range(3)]
    outs = {name: ((n_chips, cuts[name[1]], 128), BF16) for name in names}

    def held_as(key, group):
        return key + ("all" if key[0] == "top" else group,)

    ins = {held_as(key, group): grads[held_as(key, group)] for key, group, offset, dims_shape in pieces}

    def body(r):
        flat, wide, core = r["flat"], r["wide"], r["scalars"][0]
        if last < end:
            flat[last - base :, :] = jnp.zeros((flat.shape[0] - last + base, 128), F32)
        for key, group, offset, dims_shape in pieces:
            offset = offset - base
            held_ref = r[held_as(key, group)]
            if len(dims_shape) == 1:
                flat[offset : offset + 1, :] = held_ref[group : group + 1, :]
                continue
            source = held_ref.at[group] if key[0] == "top" else held_ref.ready()
            if is_gain(key):
                write_gain(flat, offset, dims_shape[1], source)
            else:
                write_matrix(flat, offset, dims_shape, source, wide)

        def chip(index, carry):
            for side, device in (("sent", 2 * index + 1 - core[0]), ("kept", 2 * index + core[0])):
                start = pl.multiple_of(n_own * device // BLOCK_ELEMENTS * 16 - base, 16)
                done = 0
                for which, rows in enumerate(cuts):
                    place, far, sem = r[f"{side}{which}"], r[side, which].far, r[side, which].sem
                    step = step_of(rows)
                    for row in range(0, rows, step):
                        values = flat[pl.ds(start + done + row, step), :]
                        place[index - low, row : row + step, :] = values.astype(BF16)
                    done += rows
                    pltpu.make_async_copy(place.at[index - low], far.at[index], sem).start()
            return carry

        lax.fori_loop(low, high, chip, 0)
        for side, which in names:
            place, out = r[f"{side}{which}"], r[side, which]
            out.copy = pltpu.make_async_copy(place, out.far.at[pl.ds(low, high - low)], out.sem)
            out.sent = True

    scratch = wide_scratch(max(end, last) - base)
    scratch |= {f"{side}{which}": ((high - low, cuts[which], 128), BF16) for side, which in names}
    return launch(
        "pack_trunk" if early else "pack", body, ins, outs, scratch, limit=60 << 20,
        scalars=(core.reshape(1),), raw=() if early else [before[name] for name in names], in_place=True,
    )


class Torus:
    def __init__(self):
        self.totals = {"dp": lax.axis_size("dp"), "band": lax.axis_size("band")}
        depth = min(4, self.totals["dp"])
        across = self.totals["dp"] // depth
        self.axes = {
            "z": (depth, across, "dp"),
            "x": (across, 1, "dp"),
            "y": (self.totals["band"] // 2, 2, "band"),
            "core": (2, 1, "band"),
        }

    def size(self, axis):
        return self.axes[axis][0]

    def place(self, axis):
        count, stride, name = self.axes[axis]
        return lax.axis_index(name) // stride % count

    def move(self, values, axis, by):
        count, stride, name = self.axes[axis]
        pairs = []
        for place in range(self.totals[name]):
            at = place // stride % count
            pairs.append((place, place + ((at + by) % count - at) * stride))
        return lax.ppermute(values, name, pairs)


def scatter_terms(torus, terms, dims, axis):
    dim = dims.index(axis)
    place = torus.place(axis)
    arrived = []
    for by in range(1, torus.size(axis)):
        other = (place + by) % torus.size(axis)
        pieces = [lax.dynamic_index_in_dim(term, other, dim, keepdims=False) for term in terms]
        total = sum(piece.astype(F32) for piece in pieces).astype(BF16)
        arrived.append(torus.move(total, axis, by))
    own = [lax.dynamic_index_in_dim(term, place, dim, keepdims=False) for term in terms]
    return own + arrived, [name for name in dims if name != axis]


SCATTER_ORDERS = (("y", "x", "z"), ("x", "y", "z"), ("z", "x", "y"))


def scatter_sum(packed):
    torus = Torus()
    dims = ["z", "x", "y"]
    shape = tuple(torus.size(axis) for axis in dims)
    sequence = (2, 0, 1)
    state = {}
    for part in sequence:
        near, far = packed["kept", part], packed["sent", part]
        near, far = near.reshape(shape + near.shape[1:]), far.reshape(shape + far.shape[1:])
        state[part] = ([near, torus.move(far, "core", 1)], dims)
    for step in range(3):
        for part in sequence if step < 2 else (2,):
            terms, left = state[part]
            state[part] = scatter_terms(torus, terms, left, SCATTER_ORDERS[part][step])

    def at_depth(place):
        found = []
        for part in (0, 1):
            pieces = [lax.dynamic_index_in_dim(term, place, 0, keepdims=False) for term in state[part][0]]
            found.append(sum(piece.astype(F32) for piece in pieces))
        return jnp.concatenate(found, 0)

    depth, place = torus.size("z"), torus.place("z")
    arrived = [
        torus.move(at_depth((place + by) % depth).astype(BF16), "z", by) for by in range(1, depth)
    ]
    first = at_depth(place) + sum(term.astype(F32) for term in arrived)
    return jnp.concatenate([first, sum(term.astype(F32) for term in state[2][0])], 0)


def all_sum(values):
    for axis in ("band", "dp"):
        count = lax.axis_size(axis)
        bit = 1
        while bit < count:
            pairs = [(i, i ^ bit) for i in range(count)]
            values = values + lax.ppermute(values, axis, pairs)
            bit *= 2
    return values


def shards(inputs, targets, crop_extent, master, moment_one, moment_two, step_count):
    n_own = master.shape[0]
    n_bands = lax.axis_size("band")
    n_devices = lax.axis_size("dp") * n_bands
    rows = share_rows(n_own)
    device = lax.axis_index("dp") * n_bands + lax.axis_index("band")
    shift = (n_own * device) % BLOCK_ELEMENTS
    extent = crop_extent[0]
    spread = jnp.pad(master, (BLOCK_ELEMENTS, rows * 128 - n_own))
    share = lax.dynamic_slice(spread, (BLOCK_ELEMENTS - shift,), (rows * 128,)).astype(BF16)
    share = lax.dynamic_update_slice(share, extent.astype(BF16), ((rows - 1) * 128,))
    gathered = lax.all_gather(share.reshape(rows, 128), ("dp", "band"), axis=0, tiled=False)
    extents = gathered[::n_bands, rows - 1, 0:2].astype(F32)
    weights = unpack_weights(gathered, n_own, False)
    n_rows, n_levels = inputs.shape[1], inputs.shape[2]
    source = inputs[0].transpose(1, 0, 2, 3).reshape(TOKENS, GROUPS * PIN)
    goal = targets[0].transpose(1, 0, 2, 3).reshape(TOKENS, GROUPS * PIN)
    first_lat = lax.axis_index("band") * n_rows
    norm_count = jnp.sum(extents[:, 0] * extents[:, 1]) * (n_levels * GROUPS * PIN)
    core = lax.axis_index("band") % 2

    def unpack_trunk(after):
        later, unused = lax.optimization_barrier((gathered, after))
        return unpack_weights(later, n_own, True)

    def pack_trunk(grads):
        return pack_grads(grads, n_own, n_devices, core)

    loss_row, grads, packed = compute(
        weights, unpack_trunk, pack_trunk, source, goal, key_codes(extent, first_lat),
        jnp.full((1, PIN), norm_count),
    )
    packed = pack_grads(grads, n_own, n_devices, core, packed)
    owned = scatter_sum(packed)
    grad_shard = lax.dynamic_slice(owned.reshape(-1), (shift,), (n_own,))
    shard_square = jnp.sum(grad_shard * grad_shard)
    lanes = lax.broadcasted_iota(jnp.int32, (8, 128), 1)
    both = jnp.where(lanes < 64, shard_square, jnp.sum(loss_row))
    both = all_sum(both)
    grad_norm = jnp.sqrt(both[0, 0])
    loss_total = both[0, 64]
    factor_clip = jnp.minimum(1.0, CLIP_LEVEL / (grad_norm + 1e-06))
    clipped = grad_shard * factor_clip
    new_one = BETA_ONE * moment_one + (1.0 - BETA_ONE) * clipped
    new_two = BETA_TWO * moment_two + (1.0 - BETA_TWO) * clipped * clipped
    step_value = step_count[0].astype(F32)
    fix_one = 1.0 - jnp.power(BETA_ONE, step_value)
    fix_two = 1.0 - jnp.power(BETA_TWO, step_value)
    update = new_one / fix_one / (jnp.sqrt(new_two / fix_two) + ADAM_EPS) + WEIGHT_DECAY * master
    new_master = master - LEARN_RATE * update
    return (
        new_master,
        new_one,
        new_two,
        new_master.astype(BF16),
        loss_total / norm_count,
        grad_norm,
    )


def solution(mesh):
    in_specs = (
        P("dp", "band", None, None, None),
        P("dp", "band", None, None, None),
        P("dp", None),
        P(("dp", "band")),
        P(("dp", "band")),
        P(("dp", "band")),
        P(),
    )
    out_specs = (
        P(("dp", "band")),
        P(("dp", "band")),
        P(("dp", "band")),
        P(("dp", "band")),
        P(),
        P(),
    )
    return jax.shard_map(shards, mesh=mesh, in_specs=in_specs, out_specs=out_specs, check_vma=False)
```
